32 devices in a mesh: wide: 8 (over z, y), narrow: 4 (over x, core).
Axes of the slice: x: 2, y: 2, z: 4, core: 2. Of those that a mesh axis runs over, the one named last changes fastest.
Arguments:
- tokens: bfloat16 [4096, 768], P('wide'), may hold values from -6 to 6
- store: bfloat16 [8, 1664, 768], P('wide', 'narrow'), may hold values from -6 to 6
- summary_length: int32 [8], P('wide'), may hold values from 64 to 512, as said below
- top_index: int32 [4096, 12, 4, 256], P('wide', 'narrow'), may hold values from 0 to 415, as said below
- cotangent: bfloat16 [4096, 768], P('wide'), may hold values from -6 to 6
- self_qkv_weight: bfloat16 [3, 768, 768], P(None, None, 'narrow'), may hold values from -0.21875 to 0.21875
- self_qv_bias: float32 [2, 768], P(None, 'narrow'), may hold values from -3 to 3
- self_out_weight: bfloat16 [768, 768], P('narrow'), may hold values from -0.875 to 0.875
- self_out_bias: float32 [768], replicated, may hold values from -3 to 3
- qkv_weight: bfloat16 [3, 768, 768], P(None, None, 'narrow'), may hold values from -0.21875 to 0.21875
- qv_bias: float32 [2, 768], P(None, 'narrow'), may hold values from -3 to 3
- out_weight: bfloat16 [768, 768], P('narrow'), may hold values from -0.875 to 0.875
- out_bias: float32 [768], replicated, may hold values from -3 to 3
- fc1_weight: bfloat16 [768, 3072], P(None, 'narrow'), may hold values from -0.21875 to 0.21875
- fc1_bias: float32 [3072], P('narrow'), may hold values from -3 to 3
- fc2_weight: bfloat16 [3072, 768], P('narrow'), may hold values from -0.109375 to 0.109375
- fc2_bias: float32 [768], replicated, may hold values from -3 to 3
- norm_gain: float32 [3, 768], replicated, may hold values from 0.4 to 1.6
- norm_shift: float32 [3, 768], replicated, may hold values from -2 to 2
Outputs:
- mixed: bfloat16 [4096, 768], P('wide')
- tokens_grad: float32 [4096, 768], P('wide')
- store_grad: float32 [8, 1664, 768], P('wide', 'narrow')
- self_qkv_grad: float32 [3, 768, 768], P(None, 'wide', 'narrow')
- self_qv_bias_grad: float32 [2, 768], P(None, 'narrow')
- self_out_weight_grad: float32 [768, 768], P('narrow', 'wide')
- self_out_bias_grad: float32 [768], replicated
- qkv_grad: float32 [3, 768, 768], P(None, 'wide', 'narrow')
- qv_bias_grad: float32 [2, 768], P(None, 'narrow')
- out_weight_grad: float32 [768, 768], P('narrow', 'wide')
- out_bias_grad: float32 [768], replicated
- fc1_grad: float32 [768, 3072], P('wide', 'narrow')
- fc1_bias_grad: float32 [3072], P('narrow')
- fc2_grad: float32 [3072, 768], P('narrow', 'wide')
- fc2_bias_grad: float32 [768], replicated
- norm_gain_grad: float32 [3, 768], replicated
- norm_shift_grad: float32 [3, 768], replicated
The draws below stay inside these ranges and needn't reach their ends.
Inputs may be any that keep to these rules, and one draw needn't show every extreme that they name: `summary_length`: the longest summary has exactly 512 tokens and the shortest exactly 64. `top_index`: each list of 256 indices is strictly increasing, starts at 0 and ends at 415.
All inputs are finite; a program needn't handle non-finite values.
Results may differ from the reference program's by a relative error of at most 0.025.
Values may be sent and summed in bfloat16 or wider, within the bound.
No kernel may reach another device: no remote copies, remote signals or barrier semaphores. Data moves between devices by JAX's collectives and lax.ppermute only.
A program may use at most 128 MiB of HBM per device.

```python
import jax
import jax.numpy as jnp
from jax import lax

D = 768
HEADS = 12
HEAD_DIM = 64
FF = 3072
SHARD_ROWS = 416
KEEP = 256
TOK_DEV = 512
MIN_LEN = 64
SHARDS = 4
STORE_ROWS = 1664
DOCS = 8
TOKENS = 4096


def draw_summary_length(key, part):
    first, second, third = jax.random.split(jax.random.fold_in(key, 11), 3)
    base = jax.random.randint(first, (DOCS,), MIN_LEN, TOK_DEV + 1)
    longest = jax.random.randint(second, (), 0, DOCS)
    shortest = (longest + 1 + jax.random.randint(third, (), 0, DOCS - 1)) % DOCS
    position = jnp.arange(DOCS, dtype=jnp.int32)
    base = jnp.where(position == longest, TOK_DEV, base)
    return jnp.where(position == shortest, MIN_LEN, base).astype(jnp.int32)


def draw_top_index(key, part):
    shape = (TOKENS, HEADS, SHARDS, KEEP)
    steps_up = jax.random.randint(jax.random.fold_in(key, 23), shape, 0, 2)
    place = lax.broadcasted_iota(jnp.int32, shape, 3)
    steps_up = jnp.where(place == 0, 0, steps_up)
    offset = jnp.minimum(jnp.cumsum(steps_up, axis=3), SHARD_ROWS - KEEP)
    index = place + offset
    return jnp.where(place == KEEP - 1, SHARD_ROWS - 1, index).astype(jnp.int32)


def spiked(array, stream_key, source, target, blocks, factor):
    def block_of(axis_at):
        return (jnp.arange(array.shape[axis_at]) // (array.shape[axis_at] // blocks)).reshape((-1,) + (1,) * (array.ndim - 1 - axis_at))

    one_side = jax.random.permutation(stream_key, blocks)[block_of(target)]
    other_side = (block_of(target) + blocks // 2) % blocks
    return jnp.where((block_of(source) == one_side) | (block_of(source) == other_side), factor * array, array)


def levels(own_key, extent, cuts, least, high):
    factor_of = 1.0
    for dim, blocks in cuts:
        draws = jax.random.uniform(jax.random.fold_in(jax.random.fold_in(own_key, 6), dim), (blocks,), jnp.float32, least / len(cuts), high / len(cuts))
        factor_of = factor_of * jnp.repeat(jnp.exp(draws), extent[dim] // blocks).reshape((-1,) + (1,) * (len(extent) - 1 - dim))
    return factor_of


def normal_values(key, dims, scale, limit, shards=(), held_as=jnp.bfloat16):
    drawn = jax.random.normal(key, dims, jnp.float32) * scale
    if len(shards) > 0:
        drawn = levels(key, dims, shards, -0.22, 0.18) * drawn
    return jnp.clip(drawn, min=-limit, max=limit).astype(held_as)


def noise_with(key, shape, scale, limit, shards, heavy, held_as=jnp.bfloat16):
    array = scale * jax.random.normal(key, shape, jnp.float32)
    if shards:
        array = array * levels(key, shape, shards, -0.22, 0.18)
    return jnp.clip(spiked(array, jax.random.fold_in(key, 3), *heavy), -limit, limit).astype(held_as)


def setup_inputs(seed: int = 0) -> dict:
    keys = jax.random.split(jax.random.key(seed), 20)
    return {
        "tokens": normal_values(keys[0], (TOKENS, D), 1.0, 6.0, ((0, 8),)),
        "store": normal_values(keys[1], (DOCS, STORE_ROWS, D), 1.0, 6.0, ((0, 8), (1, 4))),
        "summary_length": draw_summary_length(jax.random.fold_in(keys[19], 71), 0),
        "top_index": draw_top_index(jax.random.fold_in(keys[19], 71), 0),
        "cotangent": noise_with(keys[4], (TOKENS, D), 1.0, 6.0, ((0, 8),), (0, 1, 8, 2.0)),
        "self_qkv_weight": normal_values(keys[5], (3, D, D), D ** -0.5, 0.21875, ((2, 4),)),
        "self_qv_bias": normal_values(keys[6], (2, D), 0.5, 3.0, ((1, 4),), jnp.float32),
        "self_out_weight": normal_values(keys[7], (D, D), (D // 16) ** -0.5, 0.875, ((0, 4),)),
        "self_out_bias": normal_values(keys[8], (D,), 0.5, 3.0, (), jnp.float32),
        "qkv_weight": normal_values(keys[9], (3, D, D), D ** -0.5, 0.21875, ((2, 4),)),
        "qv_bias": normal_values(keys[10], (2, D), 0.5, 3.0, ((1, 4),), jnp.float32),
        "out_weight": normal_values(keys[11], (D, D), (D // 16) ** -0.5, 0.875, ((0, 4),)),
        "out_bias": normal_values(keys[12], (D,), 0.5, 3.0, (), jnp.float32),
        "fc1_weight": normal_values(keys[13], (D, FF), D ** -0.5, 0.21875, ((1, 4),)),
        "fc1_bias": normal_values(keys[14], (FF,), 0.5, 3.0, ((0, 4),), jnp.float32),
        "fc2_weight": normal_values(keys[15], (FF, D), FF ** -0.5, 0.109375, ((0, 4),)),
        "fc2_bias": normal_values(keys[16], (D,), 0.5, 3.0, (), jnp.float32),
        "norm_gain": jnp.clip(1.0 + 0.12 * jax.random.normal(keys[17], (3, D), jnp.float32), 0.4, 1.6),
        "norm_shift": normal_values(keys[18], (3, D), 0.3, 2.0, (), jnp.float32),
    }


@jax.custom_vjp
def low(v):
    return lax.optimization_barrier(v.astype(jnp.bfloat16)).astype(jnp.float32)

@jax.custom_vjp
def low_back(v):
    return v

def low_keep(v):
    return (low(v), None)

def low_pass(kept, grad):
    return (grad,)

def back_keep(v):
    return (v, None)

def back_low(kept, grad):
    return (low(grad),)
low.defvjp(low_keep, low_pass)
low_back.defvjp(back_keep, back_low)
HIGHEST = lax.Precision.HIGHEST

def matrix_product(left, right):
    return jnp.dot(left, right, precision=HIGHEST, preferred_element_type=jnp.float32)

def layer_norm(value, gain, shift):
    centre = value - lax.optimization_barrier(jnp.mean(value, axis=-1, keepdims=True))
    spread = lax.optimization_barrier(jnp.mean(centre * centre, axis=-1, keepdims=True))
    return centre * lax.rsqrt(spread + 1e-05) * gain + shift

def head_major_layout(value):
    return jnp.moveaxis(value.reshape(value.shape[0], HEADS, HEAD_DIM), 1, 0)

def self_head(live, query_head, key_head, value_head):
    n_rows = query_head.shape[0]
    scores = low_back(matrix_product(query_head, key_head.T) * HEAD_DIM ** (-0.5))
    row_ids = jnp.arange(n_rows, dtype=jnp.int32)[:, None]
    key_ids = jnp.arange(n_rows, dtype=jnp.int32)[None, :]
    allowed = (key_ids <= row_ids) & (live[None, :] > 0)
    masked = jnp.where(allowed, scores, -1e+30)
    largest = lax.optimization_barrier(jnp.max(masked, axis=1, keepdims=True))
    log_total = largest + jnp.log(lax.optimization_barrier(jnp.sum(jnp.exp(masked - largest), axis=1, keepdims=True)))
    prob = low(jnp.exp(masked - log_total))
    return low(low_back(matrix_product(prob, value_head)))

def attend_head(store_rows, fold_head, index_head):
    n_rows = fold_head.shape[0]
    total_rows = store_rows.shape[0]
    n_shards = index_head.shape[1]
    offsets = jnp.arange(n_shards, dtype=jnp.int32) * (total_rows // n_shards)
    columns = (index_head + offsets[None, :, None]).reshape(n_rows, -1)
    scores = low_back(matrix_product(fold_head, store_rows.T))
    picked = jnp.take_along_axis(scores, columns, axis=1)
    largest = lax.optimization_barrier(jnp.max(picked, axis=1, keepdims=True))
    lse = largest + jnp.log(lax.optimization_barrier(jnp.sum(jnp.exp(picked - largest), axis=1, keepdims=True)))
    prob = low(jnp.exp(picked - lse))
    row_ids = jnp.arange(n_rows, dtype=jnp.int32)[:, None]
    dense = jnp.zeros((n_rows, total_rows), jnp.float32).at[row_ids, columns].add(prob)
    return low(low_back(matrix_product(dense, store_rows)))

def layer(tokens, store_rows, live, index, self_query_key_value, self_qv_bias, self_out_w, self_out_b, qkv, qv_bias, out_weight, out_bias, fc1_weight, fc1_bias, fc2_weight, fc2_bias, norm_gain, norm_shift):
    n_rows = tokens.shape[0]
    self_query_rows = low(low_back(matrix_product(tokens, self_query_key_value[0])) + self_qv_bias[0])
    self_key_rows = low(low_back(matrix_product(tokens, self_query_key_value[1])))
    self_value_rows = low(low_back(matrix_product(tokens, self_query_key_value[2])) + self_qv_bias[1])

    def single_self_head(triple):
        return self_head(live, triple[0], triple[1], triple[2])
    self_attention_context = lax.map(jax.checkpoint(single_self_head), (head_major_layout(self_query_rows), head_major_layout(self_key_rows), head_major_layout(self_value_rows)))
    self_attention_context = jnp.moveaxis(self_attention_context, 0, 1).reshape(n_rows, D)
    after_self = layer_norm(tokens + low_back(matrix_product(self_attention_context, self_out_w)) + self_out_b, norm_gain[0], norm_shift[0])
    query = low(low_back(matrix_product(low(after_self), qkv[0])) + qv_bias[0])
    key_w = qkv[1].reshape(D, HEADS, HEAD_DIM)
    value_w = qkv[2].reshape(D, HEADS, HEAD_DIM)
    folded = jnp.einsum('thj,dhj->htd', query.reshape(n_rows, HEADS, HEAD_DIM), key_w, precision=HIGHEST)
    folded = low(low_back(folded * HEAD_DIM ** (-0.5)))

    def one_head(pair):
        return attend_head(store_rows, pair[0], pair[1])
    context = lax.map(jax.checkpoint(one_head), (folded, jnp.moveaxis(index, 1, 0)))
    head_out = jnp.einsum('htd,dhj->thj', context, value_w, precision=HIGHEST)
    head_out = low(low_back(head_out) + qv_bias[1].reshape(HEADS, HEAD_DIM)).reshape(n_rows, D)
    mid = layer_norm(after_self + low_back(matrix_product(head_out, out_weight)) + out_bias, norm_gain[1], norm_shift[1])
    pre = low_back(matrix_product(low(mid), fc1_weight)) + fc1_bias
    hidden = low(jax.nn.gelu(pre, approximate=False))
    last = mid + low_back(matrix_product(hidden, fc2_weight)) + fc2_bias
    return layer_norm(last, norm_gain[2], norm_shift[2]) * live[:, None]

def reference(tokens, store, summary_length, top_index, cotangent, self_qkv_weight, self_qv_bias, self_out_weight, self_out_bias, qkv_weight, qv_bias, out_weight, out_bias, fc1_weight, fc1_bias, fc2_weight, fc2_bias, norm_gain, norm_shift):
    params = tuple((w.astype(jnp.float32) for w in (self_qkv_weight, self_qv_bias, self_out_weight, self_out_bias, qkv_weight, qv_bias, out_weight, out_bias, fc1_weight, fc1_bias, fc2_weight, fc2_bias, norm_gain, norm_shift)))
    n_docs = summary_length.shape[0]
    n_rows = tokens.shape[0] // n_docs
    tok_docs = tokens.astype(jnp.float32).reshape(n_docs, n_rows, D)
    cot_docs = cotangent.astype(jnp.float32).reshape(n_docs, n_rows, D)
    index_docs = top_index.reshape(n_docs, n_rows, HEADS, SHARDS, KEEP)
    store_f = store.astype(jnp.float32)

    def one_doc(totals, item):
        tok, rows, length, index, delta = item
        live = (jnp.arange(n_rows, dtype=jnp.int32) < length).astype(jnp.float32)

        def forward(tok_in, rows_in, *weights):
            return layer(tok_in, rows_in, live, index, *weights)
        result, pull = jax.vjp(forward, tok, rows, *params)
        grads = pull(delta)
        totals = tuple((a + b for a, b in zip(totals, grads[2:])))
        return (totals, (result, grads[0], grads[1]))
    zeros = tuple((jnp.zeros_like(w) for w in params))
    totals, (results, tok_grads, store_grads) = lax.scan(one_doc, zeros, (tok_docs, store_f, summary_length, index_docs, cot_docs))
    return (results.reshape(-1, D).astype(jnp.bfloat16), tok_grads.reshape(-1, D), store_grads, totals[0], totals[1], totals[2], totals[3], totals[4], totals[5], totals[6], totals[7], totals[8], totals[9], totals[10], totals[11], totals[12], totals[13])
```

```python
import functools

import jax
import jax.numpy as jnp
from jax import lax
from jax.experimental import pallas as pl
from jax.experimental.pallas import tpu as pltpu
from jax.sharding import PartitionSpec as P

F32 = jnp.float32
BF = jnp.bfloat16
NN = (((1,), (0,)), ((), ()))
NT = (((1,), (1,)), ((), ()))
TN = (((0,), (0,)), ((), ()))
EPS = 1e-05
VMEM_LIMIT = 56 << 20

CORE = [(i, i ^ 1) for i in range(4)]
ACROSS = [(i, i ^ 2) for i in range(4)]
DIAGONAL = [(i, i ^ 3) for i in range(4)]


def mm(left, right, dims=NN):
    return lax.dot_general(left, right, dims, preferred_element_type=F32)


def shape(*dims, dtype=F32):
    return jax.ShapeDtypeStruct(dims, dtype)


def whole_spec(*dims):
    return pl.BlockSpec(dims, lambda *_: (0,) * len(dims))


def params():
    return pltpu.CompilerParams(vmem_limit_bytes=VMEM_LIMIT)


def cost(flops, moved, exps=0):
    return pl.CostEstimate(flops=flops, bytes_accessed=moved, transcendentals=exps)


def norm_stats(value):
    centre = value - jnp.mean(value, axis=-1, keepdims=True)
    spread = jnp.mean(centre * centre, axis=-1, keepdims=True)
    inverse = lax.rsqrt(spread + EPS)
    return centre * inverse, inverse


def norm_backward(grad, normed, inverse, gain):
    scaled = grad * gain
    centred = scaled - jnp.mean(scaled, axis=-1, keepdims=True)
    return inverse * (centred - normed * jnp.mean(scaled * normed, axis=-1, keepdims=True))


def column_sum(value):
    return jnp.sum(value, axis=0, keepdims=True)


def erf(value):
    x = jnp.clip(value, -4.0, 4.0)
    y = x * x
    top = jnp.full_like(y, -2.72614225801306e-10)
    for factor in (
        2.77068142495902e-08,
        -2.10102402082508e-06,
        -5.69250639462346e-05,
        -7.34990630326855e-04,
        -2.95459980854025e-03,
        -1.60960333262415e-02,
    ):
        top = top * y + factor
    low = jnp.full_like(y, -1.45660718464996e-05)
    for factor in (
        -2.13374055278905e-04,
        -1.68282697438203e-03,
        -7.37332916720468e-03,
        -1.42647390514189e-02,
    ):
        low = low * y + factor
    return x * top / low


def self_forward_kernel(at, tok, w, b, wo, qkv, prob, flat, send, keep, *, nh, hd):
    core, length = at[0], at[3]
    rows = tok.shape[0]
    half = rows // 2
    scale = hd**-0.5
    x = tok[...]
    q = (mm(x, w[0]) + b[0:1]).astype(BF)
    k = mm(x, w[1]).astype(BF)
    v = (mm(x, w[2]) + b[1:2]).astype(BF)
    qkv[0] = q
    qkv[1] = k
    qkv[2] = v
    row_ids = lax.broadcasted_iota(jnp.int32, (rows, rows), 0)
    key_ids = lax.broadcasted_iota(jnp.int32, (rows, rows), 1)
    allowed = (key_ids <= row_ids) & (key_ids < length)
    outs = []
    for h in range(nh):
        part = slice(h * hd, (h + 1) * hd)
        scores = mm(q[:, part], k[:, part], NT) * scale
        scores = jnp.where(allowed, scores, -1e30)
        shifted = jnp.exp(scores - jnp.max(scores, axis=1, keepdims=True))
        weights = (shifted * (1.0 / jnp.sum(shifted, axis=1, keepdims=True))).astype(BF)
        prob[h] = weights
        outs.append(mm(weights, v[:, part]).astype(BF))
    flat[...] = jnp.concatenate(outs, axis=1)
    keep[...] = mm(flat[pl.ds(pl.multiple_of(core * half, half), half), :], wo[...])
    send[...] = mm(flat[pl.ds(pl.multiple_of((1 - core) * half, half), half), :], wo[...]).astype(BF)


def self_forward(at, tokens, w, b, wo, nh):
    rows, width = tokens.shape
    local = w.shape[2]
    half = rows // 2
    return pl.pallas_call(
        functools.partial(self_forward_kernel, nh=nh, hd=local // nh),
        in_specs=[pl.BlockSpec(memory_space=pltpu.SMEM)] + [pl.BlockSpec(memory_space=pltpu.VMEM)] * 4,
        out_specs=[pl.BlockSpec(memory_space=pltpu.VMEM)] * 5,
        out_shape=[
            shape(3, rows, local, dtype=BF),
            shape(nh, rows, rows, dtype=BF),
            shape(rows, local, dtype=BF),
            shape(half, width, dtype=BF),
            shape(half, width),
        ],
        compiler_params=params(),
        cost_estimate=cost(6 * rows * width * local, 6 << 20, nh * rows * rows),
        name="self_fwd",
    )(at, tokens, w, b, wo)


def first_norm_kernel(at, mine, other, tok, bias, gain, shift, total, after, low):
    value = tok[...].astype(F32) + (mine[...].astype(F32) + other[...].astype(F32)) + bias[...]
    total[...] = value
    normed, _ = norm_stats(value)
    result = normed * gain[0:1] + shift[0:1]
    after[...] = result
    low[...] = result.astype(BF)


def first_norm(at, mine, other, tokens, bias, gain, shift):
    half, width = mine.shape
    spec = whole_spec(half, width)
    return pl.pallas_call(
        first_norm_kernel,
        grid_spec=pltpu.PrefetchScalarGridSpec(
            num_scalar_prefetch=1,
            grid=(1,),
            in_specs=[
                spec,
                spec,
                pl.BlockSpec((half, width), lambda i, at: (at[0], 0)),
                whole_spec(1, width),
                whole_spec(3, width),
                whole_spec(3, width),
            ],
            out_specs=[spec, spec, spec],
        ),
        out_shape=[shape(half, width), shape(half, width), shape(half, width, dtype=BF)],
        compiler_params=params(),
        name="first_norm",
    )(at, mine, other, tokens, bias, gain, shift)


def mask_kernel(at, index, bias, *, nh, ns, keep, group):
    count, seg = index.shape[0] // (nh * ns * (keep // 128)), bias.shape[2] // ns
    halves = keep // 128
    per_row = nh * ns * halves
    blocks = bias.shape[2] // 128
    lane = lax.broadcasted_iota(jnp.int32, (group, 128), 1).astype(F32)
    lane_low = lane.astype(BF)
    empty = jnp.full((group, 128), -1.0, BF)
    own = at[2]
    steps = []
    step = 1
    while step <= seg - keep:
        steps.insert(0, step)
        step *= 2
    below = {s: lane_low < jnp.asarray(s, BF) for s in steps + [(seg * s) % 128 for s in range(ns)] if 0 < s < 128}

    def one_group(g, _):
        for h in range(nh):
            v = [empty] * blocks
            for slot in range(ns):
                first, turn = divmod(seg * slot, 128)
                for c in range(halves):
                    start = g * (group * per_row) + h * ns * halves + c * ns + (own ^ slot)
                    found = jnp.concatenate(
                        [index[pl.ds(start + q * 8 * per_row, 8, stride=per_row), :] for q in range(group // 8)], axis=0
                    )
                    ahead = (found.astype(F32) - (lane + float(128 * c))).astype(BF)
                    at_block = first + c
                    if turn == 0:
                        v[at_block] = ahead
                    else:
                        turned = pltpu.roll(ahead, turn, axis=1)
                        v[at_block] = jnp.where(below[turn], v[at_block], turned)
                        v[at_block + 1] = jnp.where(below[turn], turned, v[at_block + 1])
            for s in steps:
                far = jnp.asarray(s, BF)
                moved = [x - far for x in v]
                stay = [jnp.where(x >= far, empty, x) for x in v]
                if s % 128 == 0:
                    hop = s // 128
                    v = stay[:hop] + [jnp.maximum(stay[i], moved[i - hop]) for i in range(hop, blocks)]
                else:
                    turned = [pltpu.roll(x, s, axis=1) for x in moved]
                    v = [jnp.maximum(stay[i], jnp.where(below[s], turned[i - 1], turned[i])) for i in range(blocks)]
            for i in range(blocks):
                bias[h, pl.ds(pl.multiple_of(g * group, group), group), i * 128 : (i + 1) * 128] = v[i] * jnp.asarray(1e30, BF)
        return 0

    lax.fori_loop(0, count // group, one_group, 0)


def make_mask(at, top_index, seg, tile):
    rows, nh, ns, keep = top_index.shape
    halves = keep // 128
    flat = top_index.reshape(rows, nh, ns, halves, 128).transpose(0, 1, 3, 2, 4)
    flat = flat.reshape(rows * nh * halves * ns, 128)
    return pl.pallas_call(
        functools.partial(mask_kernel, nh=nh, ns=ns, keep=keep, group=32),
        grid_spec=pltpu.PrefetchScalarGridSpec(
            num_scalar_prefetch=1,
            grid=(rows // tile,),
            in_specs=[pl.BlockSpec((tile * nh * halves * ns, 128), lambda i, at: (i, 0))],
            out_specs=pl.BlockSpec((nh, tile, ns * seg), lambda i, at: (0, i, 0)),
        ),
        out_shape=shape(nh, rows, ns * seg, dtype=BF),
        compiler_params=params(),
        cost_estimate=cost(rows * nh * ns * seg * 400, 12 << 20),
        name="mask",
    )(at, flat)


def keys_values_kernel(s0, s1, s2, s3, wk, wv, keys, values, *, nh, hd):
    seg = s0.shape[0]
    for slot, rows in enumerate((s0, s1, s2, s3)):
        x = rows[...]
        span = slice(slot * seg, (slot + 1) * seg)
        for weight, out in ((wk, keys), (wv, values)):
            full = mm(x, weight[...])
            high = full.astype(BF)
            low = (full - high.astype(F32)).astype(BF)
            for h in range(nh):
                part = slice(h * hd, (h + 1) * hd)
                out[h, span, :] = jnp.concatenate([high[:, part], low[:, part]], axis=1)


def keys_values(shards, wk, wv, nh):
    seg, width = shards[0].shape
    local = wk.shape[1]
    out = shape(nh, 4 * seg, 2 * local // nh, dtype=BF)
    return pl.pallas_call(
        functools.partial(keys_values_kernel, nh=nh, hd=local // nh),
        in_specs=[pl.BlockSpec(memory_space=pltpu.VMEM)] * 6,
        out_specs=[pl.BlockSpec(memory_space=pltpu.VMEM)] * 2,
        out_shape=[out, out],
        compiler_params=params(),
        cost_estimate=cost(16 * seg * width * local, 6 << 20),
        name="keys_values",
    )(*shards, wk, wv)


def cross_forward_kernel(
    at, mine, other, bias, keys, values, wq, qb, vb, wo, keep, send, raised, inverse, query, heads, x_now, *, nh, hd
):
    step = pl.program_id(0)
    scale = hd**-0.5

    @pl.when(step == 0)
    def _():
        x_now[...] = mine[...]

    @pl.when(step == 1)
    def _():
        x_now[...] = other[...]

    q = (mm(x_now[...], wq[...]) + qb[...]).astype(BF)
    query[...] = q
    scaled = q * jnp.asarray(scale, BF)
    outs = []
    for h in range(nh):
        part = slice(h * hd, (h + 1) * hd)
        twice = jnp.concatenate([scaled[:, part], scaled[:, part]], axis=1)
        scores = mm(twice, keys[h], NT) + bias[h].astype(F32)
        e = jnp.exp(scores - jnp.max(scores, axis=1, keepdims=True))
        total = 1.0 / jnp.sum(e, axis=1, keepdims=True)
        low = e.astype(BF)
        raised[h] = low
        inverse[h] = total
        both = mm(low, values[h])
        outs.append((both[:, :hd] + both[:, hd:]) * total)
    out = (jnp.concatenate(outs, axis=1) + vb[...]).astype(BF)
    heads[...] = out
    result = mm(out, wo[...])

    @pl.when(step == 0)
    def _():
        keep[...] = result

    @pl.when(step == 1)
    def _():
        send[...] = result.astype(BF)


def cross_forward(at, mine, other, bias, keys, values, wq, qb, vb, wo, nh):
    half, width = mine.shape
    local = wq.shape[1]
    hd = local // nh
    slots = keys.shape[1]
    row_block = lambda *d: pl.BlockSpec(d, lambda i, at: (i, 0))
    head_block = lambda *d: pl.BlockSpec(d, lambda i, at: (0, i, 0))
    return pl.pallas_call(
        functools.partial(cross_forward_kernel, nh=nh, hd=hd),
        grid_spec=pltpu.PrefetchScalarGridSpec(
            num_scalar_prefetch=1,
            grid=(2,),
            in_specs=[
                whole_spec(half, width),
                whole_spec(half, width),
                pl.BlockSpec((nh, half, slots), lambda i, at: (0, (i + at[0]) % 2, 0)),
                whole_spec(nh, slots, 2 * hd),
                whole_spec(nh, slots, 2 * hd),
                whole_spec(width, local),
                whole_spec(1, local),
                whole_spec(1, local),
                whole_spec(local, width),
            ],
            out_specs=[
                whole_spec(half, width),
                whole_spec(half, width),
                head_block(nh, half, slots),
                head_block(nh, half, 1),
                row_block(half, local),
                row_block(half, local),
            ],
            scratch_shapes=[pltpu.VMEM((half, width), BF)],
        ),
        out_shape=[
            shape(half, width),
            shape(half, width, dtype=BF),
            shape(nh, 2 * half, slots, dtype=BF),
            shape(nh, 2 * half, 1),
            shape(2 * half, local, dtype=BF),
            shape(2 * half, local, dtype=BF),
        ],
        compiler_params=params(),
        cost_estimate=cost(4 * half * slots * 256 * 2 * nh, 16 << 20, nh * 2 * half * slots),
        name="cross_fwd",
    )(at, mine, other, bias, keys, values, wq, qb, vb, wo)


def feed_kernel(at, after, kept, near, far, cot, *refs):
    f1, f2, b1 = refs[0:4], refs[4:8], refs[8:12]
    out_bias, fc2_bias, gain, shift = refs[12:16]
    mixed, dsecond_low, both, d0, d1, d2, d3, sums, slope = refs[16:]
    moved = (d0, d1, d2, d3)
    rows, width = mixed.shape
    second = after[...] + (kept[...] + near[...].astype(F32) + far[...].astype(F32)) + out_bias[...]
    normed_mid, inverse_mid = norm_stats(second)
    mid = normed_mid * gain[1:2] + shift[1:2]
    mid_low = mid.astype(BF)
    both[0] = mid_low
    total = jnp.zeros((rows, width), F32)
    for slot in range(4):
        pre = mm(mid_low, f1[slot][...]) + b1[slot][...]
        phi = 0.5 * (1.0 + erf(pre * 0.7071067811865476))
        slope[slot] = phi + pre * (jnp.exp(pre * pre * -0.5) * 0.3989422804014327)
        hidden = (pre * phi).astype(BF)
        moved[slot][0] = hidden
        total = total + mm(hidden, f2[slot][...])
    last = mid + total + fc2_bias[...]
    normed_last, inverse_last = norm_stats(last)
    place = (2 * at[0] + at[1]) * rows + lax.broadcasted_iota(jnp.int32, (rows, 1), 0)
    live = (place < at[3]).astype(F32)
    mixed[...] = ((normed_last * gain[2:3] + shift[2:3]) * live).astype(BF)
    delta = cot[...].astype(F32) * live
    dlast = norm_backward(delta, normed_last, inverse_last, gain[2:3])
    dlast_low = dlast.astype(BF)
    both[1] = dlast_low
    dmid = dlast
    for slot in range(4):
        dpre = (mm(dlast_low, f2[slot][...], NT) * slope[slot]).astype(BF)
        moved[slot][1] = dpre
        dmid = dmid + mm(dpre, f1[slot][...], NT)
    dsecond = norm_backward(dmid, normed_mid, inverse_mid, gain[1:2])
    dsecond_low[...] = dsecond.astype(BF)
    sums[...] = jnp.concatenate(
        [
            column_sum(delta * normed_last),
            column_sum(delta),
            column_sum(dlast),
            column_sum(dmid * normed_mid),
            column_sum(dmid),
            column_sum(dsecond),
            jnp.zeros((2, width), F32),
        ],
        axis=0,
    )


def feed(at, after, kept, near, far, cot, f1, f2, b1, out_bias, fc2_bias, gain, shift):
    rows, width = far.shape
    units = f1[0].shape[1]
    quarter = pl.BlockSpec((rows, width), lambda i, at: (at[1], 0))
    pair = shape(2, rows, width, dtype=BF)
    moved = shape(2, rows, units, dtype=BF)
    return pl.pallas_call(
        feed_kernel,
        grid_spec=pltpu.PrefetchScalarGridSpec(
            num_scalar_prefetch=1,
            grid=(1,),
            in_specs=[
                quarter,
                quarter,
                quarter,
                whole_spec(rows, width),
                pl.BlockSpec((rows, width), lambda i, at: (2 * at[0] + at[1], 0)),
            ]
            + [whole_spec(width, units)] * 4
            + [whole_spec(units, width)] * 4
            + [whole_spec(1, units)] * 4
            + [whole_spec(1, width)] * 2
            + [whole_spec(3, width)] * 2,
            out_specs=[whole_spec(rows, width)] * 2 + [whole_spec(2, rows, width)] + [whole_spec(2, rows, units)] * 4 + [whole_spec(8, width)],
            scratch_shapes=[pltpu.VMEM((4, rows, units), F32)],
        ),
        out_shape=[shape(rows, width, dtype=BF)] * 2 + [pair] + [moved] * 4 + [shape(8, width)],
        compiler_params=params(),
        cost_estimate=cost(32 * rows * width * units * 3, 12 << 20, rows * units * 8),
        name="feed",
    )(at, after, kept, near, far, cot, *f1, *f2, *b1, out_bias, fc2_bias, gain, shift)


def cross_backward_kernel(
    at, z0, z1, z2, z3, raised, inverse, query, keys, values, wq, wo, keep, send, dquery, dkv, sums, z_now, *, nh, hd
):
    step = pl.program_id(0)
    scale = hd**-0.5
    rows = z0.shape[0]
    first = pl.ds(pl.multiple_of(at[1] * rows, rows), rows)
    second = pl.ds(pl.multiple_of((1 - at[1]) * rows, rows), rows)

    @pl.when(step == 0)
    def _():
        z_now[first, :] = z0[...]
        z_now[second, :] = z2[...]

    @pl.when(step == 1)
    def _():
        z_now[first, :] = z1[...]
        z_now[second, :] = z3[...]

    dhead = mm(z_now[...], wo[...], NT)
    scaled = query[...] * jnp.asarray(scale, BF)
    zero = jnp.zeros((2 * rows, hd), BF)
    douts = []
    for h in range(nh):
        part = slice(h * hd, (h + 1) * hd)
        total = inverse[h]
        dout = (dhead[:, part] * total).astype(BF)
        dprob = mm(jnp.concatenate([dout, dout], axis=1), values[h], NT)
        low = raised[h]
        e = low.astype(F32)
        weighed = e * dprob
        mean = jnp.sum(weighed, axis=1, keepdims=True) * total
        dscore = (weighed - e * mean).astype(BF)
        both = mm(dscore, keys[h])
        douts.append(both[:, :hd] + both[:, hd:])
        left = jnp.concatenate([dscore, low], axis=0)
        right = jnp.concatenate(
            [jnp.concatenate([scaled[:, part], zero], axis=1), jnp.concatenate([zero, dout], axis=1)], axis=0
        )
        grad = mm(left, right, TN)

        @pl.when(step == 0)
        def _():
            dkv[h] = grad

        @pl.when(step == 1)
        def _():
            dkv[h] += grad

    dq = jnp.concatenate(douts, axis=1) * scale
    dq_low = dq.astype(BF)
    dquery[...] = dq_low
    result = mm(dq_low, wq[...], NT)
    both_sums = jnp.concatenate([column_sum(dq), column_sum(dhead)], axis=0)

    @pl.when(step == 0)
    def _():
        keep[...] = result
        sums[...] = both_sums

    @pl.when(step == 1)
    def _():
        send[...] = result.astype(BF)
        sums[...] += both_sums


def cross_backward(at, z, raised, inverse, query, keys, values, wq, wo, nh):
    rows, width = z[0].shape
    half = 2 * rows
    local = wq.shape[1]
    hd = local // nh
    slots = keys.shape[1]
    row_block = lambda *d: pl.BlockSpec(d, lambda i, at: (i, 0))
    head_block = lambda *d: pl.BlockSpec(d, lambda i, at: (0, i, 0))
    return pl.pallas_call(
        functools.partial(cross_backward_kernel, nh=nh, hd=hd),
        grid_spec=pltpu.PrefetchScalarGridSpec(
            num_scalar_prefetch=1,
            grid=(2,),
            in_specs=[whole_spec(rows, width)] * 4
            + [
                head_block(nh, half, slots),
                head_block(nh, half, 1),
                row_block(half, local),
                whole_spec(nh, slots, 2 * hd),
                whole_spec(nh, slots, 2 * hd),
                whole_spec(width, local),
                whole_spec(local, width),
            ],
            out_specs=[
                whole_spec(half, width),
                whole_spec(half, width),
                row_block(half, local),
                whole_spec(nh, slots, 2 * hd),
                whole_spec(2, local),
            ],
            scratch_shapes=[pltpu.VMEM((half, width), BF)],
        ),
        out_shape=[
            shape(half, width),
            shape(half, width, dtype=BF),
            shape(2 * half, local, dtype=BF),
            shape(nh, slots, 2 * hd),
            shape(2, local),
        ],
        compiler_params=params(),
        cost_estimate=cost(8 * half * slots * 256 * 2 * nh, 16 << 20, 0),
        name="cross_bwd",
    )(at, *z, raised, inverse, query, keys, values, wq, wo)


def store_grad_kernel(dkv, wk, wv, keep, send, low, *, nh, hd):
    slots = dkv.shape[1]
    seg = slots // 4
    for h in range(nh):
        low[:, h * 2 * hd : (h + 1) * 2 * hd] = dkv[h].astype(BF)
    weights = []
    for h in range(nh):
        weights += [wk[:, h * hd : (h + 1) * hd], wv[:, h * hd : (h + 1) * hd]]
    weight = jnp.concatenate(weights, axis=1)
    for slot in range(4):
        part = mm(low[slot * seg : (slot + 1) * seg, :], weight, NT)
        if slot % 2 == 0:
            keep[slot // 2] = part
        else:
            send[slot // 2] = part.astype(BF)


def store_gradient(dkv, wk, wv):
    nh, slots, twice = dkv.shape
    width = wk.shape[0]
    seg = slots // 4
    return pl.pallas_call(
        functools.partial(store_grad_kernel, nh=nh, hd=twice // 2),
        in_specs=[pl.BlockSpec(memory_space=pltpu.VMEM)] * 3,
        out_specs=[pl.BlockSpec(memory_space=pltpu.VMEM)] * 3,
        out_shape=[shape(2, seg, width), shape(2, seg, width, dtype=BF), shape(slots, nh * twice, dtype=BF)],
        compiler_params=params(),
        cost_estimate=cost(2 * slots * width * nh * twice, 12 << 20),
        name="store_grad",
    )(dkv, wk, wv)


def emit_split(at, grad, at_column, send, keep):
    blocks, rows, _ = send.shape
    columns = slice(at_column, at_column + grad.shape[1])
    for b in range(blocks):
        mine = pl.multiple_of((2 * b + at[4]) * rows, 8)
        theirs = pl.multiple_of((2 * b + 1 - at[4]) * rows, 8)
        keep[b, :, columns] = grad[pl.ds(mine, rows), :]
        send[b, :, columns] = grad[pl.ds(theirs, rows), :].astype(BF)


def feed_grads_kernel(at, *refs, split):
    pairs, moved = refs[0:4], refs[4:8]
    outs = refs[8:-3]
    left, right, grad = refs[-3:]
    rows = pairs[0].shape[1]
    bias = jnp.zeros((1, moved[0].shape[2]), F32)
    for turn in range(2):
        for s in range(4):
            left[s * rows : (s + 1) * rows, :] = pairs[s][turn]
            block = moved[s][1 - turn]
            right[s * rows : (s + 1) * rows, :] = block
            if turn == 0:
                bias = bias + column_sum(block.astype(F32))
        if split:
            grad[...] = mm(left[...], right[...], TN)
            emit_split(at, grad, turn * grad.shape[1], outs[0], outs[1])
        else:
            outs[turn][...] = mm(left[...], right[...], TN)
    outs[2][...] = bias


def feed_grads(at, pairs, moved, blocks):
    _, rows, width = pairs[0].shape
    units = moved[0].shape[2]
    vm = pl.BlockSpec(memory_space=pltpu.VMEM)
    if blocks:
        n, r = blocks
        outs = [shape(n, r, 2 * units, dtype=BF), shape(n, r, 2 * units)]
    else:
        outs = [shape(width, units), shape(width, units)]
    return pl.pallas_call(
        functools.partial(feed_grads_kernel, split=bool(blocks)),
        in_specs=[pl.BlockSpec(memory_space=pltpu.SMEM)] + [vm] * 8,
        out_specs=[vm] * 3,
        out_shape=outs + [shape(1, units)],
        scratch_shapes=[pltpu.VMEM((4 * rows, width), BF), pltpu.VMEM((4 * rows, units), BF), pltpu.VMEM((width, units), F32)],
        compiler_params=params(),
        cost_estimate=cost(4 * 4 * rows * width * units, 12 << 20),
        name="feed_grads",
    )(at, *pairs, *moved)


def cross_grads_kernel(at, z0, z1, z2, z3, mine, other, query_grad, heads, s0, s1, s2, s3, dkv, *refs, nh, hd, split):
    outs, (z_all, grad) = refs[:-2], refs[-2:]
    rows = z0.shape[0]
    half = 2 * rows
    seg = s0.shape[0]
    for base, near, far in ((0, z0, z2), (half, z1, z3)):
        z_all[pl.ds(pl.multiple_of(base + at[1] * rows, rows), rows), :] = near[...]
        z_all[pl.ds(pl.multiple_of(base + (1 - at[1]) * rows, rows), rows), :] = far[...]
    query = mm(mine[...], query_grad[0:half], TN) + mm(other[...], query_grad[half:], TN)
    both = None
    for slot, block in enumerate((s0, s1, s2, s3)):
        part = mm(block[...], dkv[slot * seg : (slot + 1) * seg, :], TN)
        both = part if both is None else both + part
    keys = jnp.concatenate([both[:, 2 * h * hd : (2 * h + 1) * hd] for h in range(nh)], axis=1)
    values = jnp.concatenate([both[:, (2 * h + 1) * hd : (2 * h + 2) * hd] for h in range(nh)], axis=1)
    out = mm(z_all[...], heads[...], TN)
    if split:
        grad[...] = jnp.concatenate([query, keys, values, out], axis=1)
        emit_split(at, grad, 0, outs[0], outs[1])
    else:
        outs[0][0] = query
        outs[0][1] = keys
        outs[0][2] = values
        outs[1][...] = out


def cross_grads(at, z, mine, other, dquery, heads, shards, dkv, nh, blocks):
    half, width = mine.shape
    local = dquery.shape[1]
    vm = pl.BlockSpec(memory_space=pltpu.VMEM)
    if blocks:
        n, r = blocks
        outs = [shape(n, r, 4 * local, dtype=BF), shape(n, r, 4 * local)]
    else:
        outs = [shape(3, width, local), shape(width, local)]
    return pl.pallas_call(
        functools.partial(cross_grads_kernel, nh=nh, hd=local // nh, split=bool(blocks)),
        in_specs=[pl.BlockSpec(memory_space=pltpu.SMEM)] + [vm] * 13,
        out_specs=[vm] * 2,
        out_shape=outs,
        scratch_shapes=[pltpu.VMEM((2 * half, width), BF), pltpu.VMEM((width, 4 * local), F32)],
        compiler_params=params(),
        cost_estimate=cost(12 * half * width * local + 16 * shards[0].shape[0] * width * local, 12 << 20),
        name="cross_grads",
    )(at, *z, mine, other, dquery, heads, *shards, dkv)


def first_back_kernel(at, z0, z2, mine, other, total, gain, dfirst, low, sums, dafter):
    rows = z0.shape[0]
    half = 2 * rows
    own = pl.ds(pl.multiple_of(at[1] * rows, rows), rows)
    far = pl.ds(pl.multiple_of((1 - at[1]) * rows, rows), rows)
    dafter[own, :] = z0[...].astype(F32)
    dafter[far, :] = z2[...].astype(F32)
    value = dafter[...] + (mine[...].astype(F32) + other[...].astype(F32))
    normed, inverse = norm_stats(total[...])
    result = norm_backward(value, normed, inverse, gain[0:1])
    dfirst[...] = result
    low[...] = result.astype(BF)
    place = lax.broadcasted_iota(jnp.int32, (half, 1), 0)
    counted = ((place >= at[1] * rows) & (place < (at[1] + 1) * rows)).astype(F32)
    sums[...] = jnp.concatenate(
        [
            column_sum(value * normed * counted),
            column_sum(value * counted),
            column_sum(result * counted),
            jnp.zeros((5, value.shape[1]), F32),
        ],
        axis=0,
    )


def first_back(at, z0, z2, mine, other, total, gain):
    half, width = mine.shape
    vm = pl.BlockSpec(memory_space=pltpu.VMEM)
    return pl.pallas_call(
        first_back_kernel,
        in_specs=[pl.BlockSpec(memory_space=pltpu.SMEM)] + [vm] * 6,
        out_specs=[vm] * 3,
        out_shape=[shape(half, width), shape(half, width, dtype=BF), shape(8, width)],
        scratch_shapes=[pltpu.VMEM((half, width), F32)],
        compiler_params=params(),
        name="first_back",
    )(at, z0, z2, mine, other, total, gain)


def self_backward_kernel(at, mine, other, tok, w, wo, qkv, prob, flat, keep, send, *refs, nh, hd, split):
    outs = refs[:3]
    z, dqkv, grad = refs[3:]
    core = at[0]
    half, width = mine.shape
    rows = 2 * half
    scale = hd**-0.5
    own = pl.ds(pl.multiple_of(core * half, half), half)
    far = pl.ds(pl.multiple_of((1 - core) * half, half), half)
    z[own, :] = mine[...]
    z[far, :] = other[...]
    dself = mm(z[...], wo[...], NT).astype(BF)
    q, k, v = qkv[0], qkv[1], qkv[2]
    dq, dk, dv = [], [], []
    for h in range(nh):
        part = slice(h * hd, (h + 1) * hd)
        weights_low = prob[h]
        weights = weights_low.astype(F32)
        weighed = weights * mm(dself[:, part], v[:, part], NT)
        dscore = (weighed - weights * jnp.sum(weighed, axis=1, keepdims=True)).astype(BF)
        dq.append(mm(dscore, k[:, part]))
        dk.append(mm(dscore, q[:, part], TN))
        dv.append(mm(weights_low, dself[:, part], TN))
    dquery = jnp.concatenate(dq, axis=1) * scale
    dvalue = jnp.concatenate(dv, axis=1)
    outs[2][...] = jnp.concatenate([column_sum(dquery), column_sum(dvalue)], axis=0)
    dqkv[0] = dquery.astype(BF)
    dqkv[1] = (jnp.concatenate(dk, axis=1) * scale).astype(BF)
    dqkv[2] = dvalue.astype(BF)
    x = tok[...]
    local = nh * hd
    out = mm(z[...], flat[...], TN)
    if split:
        for i in range(3):
            grad[:, i * local : (i + 1) * local] = mm(x, dqkv[i], TN)
        grad[:, 3 * local :] = out
        emit_split(at, grad, 0, outs[0], outs[1])
    else:
        for i in range(3):
            outs[0][i] = mm(x, dqkv[i], TN)
        outs[1][...] = out
    for place, out in ((own, keep), (far, send)):
        total = mm(dqkv[0, place, :], w[0], NT) + mm(dqkv[1, place, :], w[1], NT) + mm(dqkv[2, place, :], w[2], NT)
        out[...] = total.astype(out.dtype)


def self_backward(at, mine, other, tokens, w, wo, qkv, prob, flat, nh, blocks):
    half, width = mine.shape
    local = wo.shape[0]
    vm = pl.BlockSpec(memory_space=pltpu.VMEM)
    if blocks:
        n, r = blocks
        outs = [shape(n, r, 4 * local, dtype=BF), shape(n, r, 4 * local)]
    else:
        outs = [shape(3, width, local), shape(width, local)]
    return pl.pallas_call(
        functools.partial(self_backward_kernel, nh=nh, hd=local // nh, split=bool(blocks)),
        in_specs=[pl.BlockSpec(memory_space=pltpu.SMEM)] + [vm] * 8,
        out_specs=[vm] * 5,
        out_shape=[shape(half, width), shape(half, width, dtype=BF)] + outs + [shape(2, local)],
        scratch_shapes=[
            pltpu.VMEM((2 * half, width), BF),
            pltpu.VMEM((3, 2 * half, local), BF),
            pltpu.VMEM((width, 4 * local), F32),
        ],
        compiler_params=params(),
        cost_estimate=cost(40 * half * width * local, 12 << 20),
        name="self_bwd",
    )(at, mine, other, tokens, w, wo, qkv, prob, flat)


def second_stage_kernel(at, keep, got, own, s1, s2, s3):
    z = at[5]
    own[...] = keep[z] + got[z].astype(F32)
    for d, out in ((1, s1), (2, s2), (3, s3)):
        out[...] = (keep[z ^ d] + got[z ^ d].astype(F32)).astype(BF)


def second_stage(at, keep, got):
    _, rows, columns = keep.shape
    vm = pl.BlockSpec(memory_space=pltpu.VMEM)
    return pl.pallas_call(
        second_stage_kernel,
        in_specs=[pl.BlockSpec(memory_space=pltpu.SMEM), vm, vm],
        out_specs=[vm] * 4,
        out_shape=[shape(rows, columns)] + [shape(rows, columns, dtype=BF)] * 3,
        compiler_params=params(),
        name="second_stage",
    )(at, keep, got)


def flip(bit, size):
    return [(i, i ^ bit) for i in range(size)]


def reduce_wide(at, send, keep):
    got = lax.ppermute(send, "wide", flip(1, 8))
    own, *sends = second_stage(at, keep, got)
    total = own
    for d, block in zip((1, 2, 3), sends):
        total = total + lax.ppermute(block, "wide", flip(2 * d, 8)).astype(F32)
    return total


def butterfly(value, axis, size):
    bit = 1
    while bit < size:
        value = value + lax.ppermute(value, axis, flip(bit, size))
        bit *= 2
    return value


def on_device(
    tokens,
    store,
    summary_length,
    top_index,
    cotangent,
    self_qkv_weight,
    self_qv_bias,
    self_out_weight,
    self_out_bias,
    qkv_weight,
    qv_bias,
    out_weight,
    out_bias,
    fc1_weight,
    fc1_bias,
    fc2_weight,
    fc2_bias,
    norm_gain,
    norm_shift,
):
    rows, width = tokens.shape
    half, quarter = rows // 2, rows // 4
    nh = top_index.shape[1]
    local = qkv_weight.shape[2]
    seg = store.shape[1]
    wide = lax.axis_size("wide")
    place = lax.axis_index("narrow")
    doc = lax.axis_index("wide")
    core, across = place % 2, place // 2
    at = jnp.stack([core, across, place, summary_length[0], doc % 2, doc // 2]).astype(jnp.int32)
    split = (wide // 2, width // wide) if wide == 8 else None
    row = lambda v: v.reshape(1, -1)

    def to_core(v):
        return lax.ppermute(v, "narrow", CORE)

    def to_across(v):
        return lax.ppermute(v, "narrow", ACROSS)

    def spread(v):
        far = to_across(v)
        return [v, to_core(v), far, to_core(far)]

    def sum_half(keep, send):
        mine = (keep + to_core(send).astype(F32)).astype(BF)
        return mine, to_across(mine)

    shards = spread(store[0])
    qkv, prob, flat, send, keep = self_forward(at, tokens, self_qkv_weight, self_qv_bias, self_out_weight, nh)
    mine, other = sum_half(keep, send)
    bias = make_mask(at, top_index, seg, 128)
    keys, values = keys_values(shards, qkv_weight[1], qkv_weight[2], nh)
    first_total, after, after_low = first_norm(at, mine, other, tokens, row(self_out_bias), norm_gain, norm_shift)
    after_other = to_core(after_low)
    f1, f2, b1 = spread(fc1_weight), spread(fc2_weight), spread(row(fc1_bias))
    keep, send, raised, inverse, query, heads = cross_forward(
        at, after_low, after_other, bias, keys, values, qkv_weight[0], row(qv_bias[0]), row(qv_bias[1]), out_weight, nh
    )
    near = to_core(send)
    theirs = (1 - across) * quarter
    far = to_across(
        (
            lax.dynamic_slice_in_dim(keep, theirs, quarter, 0) + lax.dynamic_slice_in_dim(near, theirs, quarter, 0).astype(F32)
        ).astype(BF)
    )
    mixed_own, z, pair, *moved, feed_sums = feed(
        at, after, keep, near, far, cotangent, f1, f2, b1, row(out_bias), row(fc2_bias), norm_gain, norm_shift
    )
    z_all = spread(z)
    keep, send, dquery, dkv, cross_sums = cross_backward(at, z_all, raised, inverse, query, keys, values, qkv_weight[0], out_weight, nh)
    mine, other = sum_half(keep, send)

    pairs = spread(pair)
    moved_all = [moved[0], to_core(moved[1]), to_across(moved[2]), lax.ppermute(moved[3], "narrow", DIAGONAL)]
    feed_out = feed_grads(at, pairs, moved_all, split)
    store_keep, store_send, dkv_low = store_gradient(dkv, qkv_weight[1], qkv_weight[2])
    cross_out = cross_grads(at, z_all, after_low, after_other, dquery, heads, shards, dkv_low, nh, split)
    store_near = to_core(store_send)
    store_far = to_across((store_keep[1] + store_near[1].astype(F32)).astype(BF))
    store_grad = (store_keep[0] + store_near[0].astype(F32) + store_far.astype(F32))[None]

    dfirst, dfirst_low, first_sums = first_back(at, z_all[0], z_all[2], mine, other, first_total, norm_gain)
    dfirst_other = to_core(dfirst_low)
    keep, send, *self_out = self_backward(
        at, dfirst_low, dfirst_other, tokens, self_qkv_weight, self_out_weight, qkv, prob, flat, nh, split
    )
    mine, other = sum_half(keep, send)
    tokens_half = dfirst + (mine.astype(F32) + other.astype(F32))
    tokens_other = to_core(tokens_half)
    tokens_grad = jnp.where(
        core == 0,
        jnp.concatenate([tokens_half, tokens_other], axis=0),
        jnp.concatenate([tokens_other, tokens_half], axis=0),
    )
    m = spread(mixed_own)
    ordered = jnp.where(across == 0, jnp.stack([m[0], m[2], m[1], m[3]]), jnp.stack([m[2], m[0], m[3], m[1]]))
    ordered = ordered.reshape(2, half, width)
    mixed = jnp.where(core == 0, ordered, ordered[::-1]).reshape(rows, width)

    if split:
        total = reduce_wide(at, feed_out[0], feed_out[1])
        units = fc1_weight.shape[1]
        fc1_grad, fc2_grad = total[:, :units], total[:, units:].T
        total = reduce_wide(at, cross_out[0], cross_out[1])
        qkv_grad = jnp.stack([total[:, i * local : (i + 1) * local] for i in range(3)])
        out_grad = total[:, 3 * local :].T
        total = reduce_wide(at, self_out[0], self_out[1])
        self_qkv_grad = jnp.stack([total[:, i * local : (i + 1) * local] for i in range(3)])
        self_out_grad = total[:, 3 * local :].T
    else:
        fc1_grad = lax.psum_scatter(feed_out[0], "wide", scatter_dimension=0, tiled=True)
        fc2_grad = lax.psum_scatter(feed_out[1].T, "wide", scatter_dimension=1, tiled=True)
        qkv_grad = lax.psum_scatter(cross_out[0], "wide", scatter_dimension=1, tiled=True)
        out_grad = lax.psum_scatter(cross_out[1].T, "wide", scatter_dimension=1, tiled=True)
        self_qkv_grad = lax.psum_scatter(self_out[0], "wide", scatter_dimension=1, tiled=True)
        self_out_grad = lax.psum_scatter(self_out[1].T, "wide", scatter_dimension=1, tiled=True)

    row_small = jnp.concatenate([feed_sums[:6], first_sums[:3]], axis=0)
    head_small = jnp.concatenate([self_out[2].reshape(-1), cross_sums.reshape(-1), feed_out[2].reshape(-1)])
    both = jnp.concatenate([row_small.reshape(-1), head_small])
    both = butterfly(both, "wide", wide)
    n_row = row_small.size
    summed = butterfly(both[:n_row], "narrow", 4).reshape(9, width)
    heads_flat = both[n_row:]
    gain_last, shift_last, fc2_b, gain_mid, shift_mid, out_b, gain_first, shift_first, self_out_b = summed
    self_qv = heads_flat[: 2 * local].reshape(2, local)
    qv = heads_flat[2 * local : 4 * local].reshape(2, local)
    fc1_b = heads_flat[4 * local :]
    return (
        mixed,
        tokens_grad,
        store_grad,
        self_qkv_grad,
        self_qv,
        self_out_grad,
        self_out_b,
        qkv_grad,
        qv,
        out_grad,
        out_b,
        fc1_grad,
        fc1_b,
        fc2_grad,
        fc2_b,
        jnp.stack([gain_first, gain_mid, gain_last]),
        jnp.stack([shift_first, shift_mid, shift_last]),
    )


def solution(mesh):
    placed = (
        P("wide", None),
        P("wide", "narrow", None),
        P("wide"),
        P("wide", "narrow", None, None),
        P("wide", None),
        P(None, None, "narrow"),
        P(None, "narrow"),
        P("narrow", None),
        P(),
        P(None, None, "narrow"),
        P(None, "narrow"),
        P("narrow", None),
        P(),
        P(None, "narrow"),
        P("narrow"),
        P("narrow", None),
        P(),
        P(),
        P(),
    )
    return jax.shard_map(
        on_device,
        mesh=mesh,
        in_specs=placed,
        out_specs=(
            P("wide", None),
            P("wide", None),
            P("wide", "narrow", None),
            P(None, "wide", "narrow"),
            P(None, "narrow"),
            P("narrow", "wide"),
            P(),
            P(None, "wide", "narrow"),
            P(None, "narrow"),
            P("narrow", "wide"),
            P(),
            P("wide", "narrow"),
            P("narrow"),
            P("narrow", "wide"),
            P(),
            P(),
            P(),
        ),
        check_vma=False,
    )
```

```python
import functools

import jax
import jax.numpy as jnp
from jax import lax
from jax.experimental import pallas as pl
from jax.experimental.pallas import tpu as pltpu
from jax.sharding import PartitionSpec as P

F32 = jnp.float32
BF = jnp.bfloat16
NN = (((1,), (0,)), ((), ()))
NT = (((1,), (1,)), ((), ()))
TN = (((0,), (0,)), ((), ()))
EPS = 1e-05
PACE = 1.1e8
EXTRA = 16

CORE = [(i, i ^ 1) for i in range(4)]
ACROSS = [(i, i ^ 2) for i in range(4)]


def mm(left, right, dims=NN):
    return lax.dot_general(left, right, dims, preferred_element_type=F32)


def shape(*dims, dtype=F32):
    return jax.ShapeDtypeStruct(dims, dtype)


def tie(value, *earlier):
    return lax.optimization_barrier((value, *earlier))[0]


class Operand:
    def __init__(self, source, buffer, sems, first, parts):
        self.buffer = buffer
        self.parts = parts
        if parts:
            self.copies = [
                pltpu.make_async_copy(source.at[i], buffer.at[i], sems.at[first + i]) for i in range(buffer.shape[0])
            ]
        else:
            self.copies = [pltpu.make_async_copy(source, buffer, sems.at[first])]
        self.waited = [False] * len(self.copies)
        for copy in self.copies:
            copy.start()

    def ready(self, part=None):
        for i, copy in enumerate(self.copies):
            if not self.waited[i] and (part is None or i == part):
                copy.wait()
                self.waited[i] = True

    @property
    def shape(self):
        return self.buffer.shape

    def __getitem__(self, at):
        self.ready(at if self.parts and isinstance(at, int) else None)
        return self.buffer[at]


def far(array, take, dims):
    return ("far", array, take, tuple(dims), True)


def near(array, take=None):
    return ("near", array, take, None, False)


def launch(body, name, at, ins, outs, scratch=(), mib=16, us=2.0):
    in_specs = [pl.BlockSpec(memory_space=pltpu.SMEM)]
    buffers, n_in = [], 0
    for kind, array, _, dims, parts in ins:
        in_specs.append(pl.BlockSpec(memory_space=pltpu.HBM if kind == "far" else pltpu.VMEM))
        if kind == "far":
            buffers.append(pltpu.VMEM(dims, array.dtype))
            n_in += dims[0]
    n_buffers = len(buffers)
    sems = [pltpu.SemaphoreType.DMA((n_in,))] if n_in else []

    def kernel(at_ref, *refs):
        in_refs, out_refs = refs[: len(ins)], refs[len(ins) : len(ins) + len(outs)]
        rest = refs[len(ins) + len(outs) :]
        bufs, user = list(rest[:n_buffers]), rest[n_buffers : len(rest) - len(sems)]
        place, given = 0, []
        for ref, (kind, _, take, dims, parts) in zip(in_refs, ins):
            source = take(ref, at_ref) if take else ref
            if kind == "far":
                given.append(Operand(source, bufs.pop(0), rest[-1], place, parts))
                place += dims[0]
            else:
                given.append(source)
        body(at_ref, given, out_refs, user)
        for operand in given:
            if isinstance(operand, Operand):
                operand.ready()

    return pl.pallas_call(
        kernel,
        in_specs=in_specs,
        out_specs=[pl.BlockSpec(memory_space=pltpu.VMEM)] * len(outs),
        out_shape=list(outs),
        scratch_shapes=buffers + list(scratch) + sems,
        compiler_params=pltpu.CompilerParams(vmem_limit_bytes=mib << 20),
        cost_estimate=pl.CostEstimate(flops=int(us * PACE), bytes_accessed=1000, transcendentals=0),
        name=name,
    )(at, *[entry[1] for entry in ins])


def norm_stats(value):
    centre = value - jnp.mean(value, axis=-1, keepdims=True)
    spread = jnp.mean(centre * centre, axis=-1, keepdims=True)
    inverse = lax.rsqrt(spread + EPS)
    return centre * inverse, inverse


def norm_backward(grad, normed, inverse, gain):
    scaled = grad * gain
    centred = scaled - jnp.mean(scaled, axis=-1, keepdims=True)
    return inverse * (centred - normed * jnp.mean(scaled * normed, axis=-1, keepdims=True))


def column_sum(value):
    return jnp.sum(value, axis=0, keepdims=True)


def erf(value):
    x = jnp.clip(value, -4.0, 4.0)
    y = x * x
    top = jnp.full_like(y, -2.72614225801306e-10)
    for factor in (
        2.77068142495902e-08,
        -2.10102402082508e-06,
        -5.69250639462346e-05,
        -7.34990630326855e-04,
        -2.95459980854025e-03,
        -1.60960333262415e-02,
    ):
        top = top * y + factor
    low = jnp.full_like(y, -1.45660718464996e-05)
    for factor in (
        -2.13374055278905e-04,
        -1.68282697438203e-03,
        -7.37332916720468e-03,
        -1.42647390514189e-02,
    ):
        low = low * y + factor
    return x * top / low


def gelu_pair(pre):
    phi = 0.5 * (1.0 + erf(pre * 0.7071067811865476))
    return (pre * phi).astype(BF), phi + pre * (jnp.exp(pre * pre * -0.5) * 0.3989422804014327)


def three_terms(value):
    high = value.astype(BF)
    rest = value - high.astype(F32)
    middle = rest.astype(BF)
    return jnp.concatenate([high, middle, (rest - middle.astype(F32)).astype(BF)], axis=0)


def from_terms(stacked):
    rows = stacked.shape[0] // 3
    terms = stacked.astype(F32)
    return terms[:rows] + terms[rows : 2 * rows] + terms[2 * rows :]


def rows_at(place, rows):
    return pl.ds(pl.multiple_of(place * rows, rows), rows)


def self_forward(at, tokens, w, b, wo, b1, nh):
    rows, width = tokens.shape
    local = w.shape[1]
    half = rows // 2
    hd = local // nh
    scale = hd**-0.5

    def body(at, ins, outs, _):
        tok, w, wo, b, b1 = ins
        qkv, prob, flat, send, keep = outs
        x = tok[...]
        q = (mm(x, w[0], NT) + b[0:1]).astype(BF)
        k = mm(x, w[1], NT).astype(BF)
        v = (mm(x, w[2], NT) + b[1:2]).astype(BF)
        qkv[0] = q
        qkv[1] = k
        qkv[2] = v
        row_ids = lax.broadcasted_iota(jnp.int32, (rows, rows), 0)
        key_ids = lax.broadcasted_iota(jnp.int32, (rows, rows), 1)
        allowed = (key_ids <= row_ids) & (key_ids < at[3])
        found = []
        for h in range(nh):
            part = slice(h * hd, (h + 1) * hd)
            scores = mm(q[:, part], k[:, part], NT) * scale
            scores = jnp.where(allowed, scores, -1e30)
            shifted = jnp.exp(scores - jnp.max(scores, axis=1, keepdims=True))
            weights = (shifted * (1.0 / jnp.sum(shifted, axis=1, keepdims=True))).astype(BF)
            prob[h] = weights
            found.append(mm(weights, v[:, part]).astype(BF))
        flat[...] = jnp.concatenate(found, axis=1)
        send[0:half, :] = mm(flat[rows_at(1 - at[0], half), :], wo[...]).astype(BF)
        send[half:, :] = jnp.concatenate([three_terms(b1[...]), jnp.zeros((16 - 3, width), BF)], axis=0)
        keep[...] = mm(flat[rows_at(at[0], half), :], wo[...])

    return launch(
        body,
        "self_fwd",
        at,
        [near(tokens), near(w), near(wo), near(b), near(b1)],
        [
            shape(3, rows, local, dtype=BF),
            shape(nh, rows, rows, dtype=BF),
            shape(rows, local, dtype=BF),
            shape(half + 16, width, dtype=BF),
            shape(half, width),
        ],
        us=4,
    )


def first_norm(at, mine, other, tokens, bias, gain, shift):
    half, width = mine.shape[0] - 16, mine.shape[1]

    def body(at, ins, outs, _):
        mine, other, tok, bias, gain, shift = ins
        total, after, low = outs
        value = tok[...].astype(F32) + (mine[0:half].astype(F32) + other[0:half].astype(F32)) + bias[...]
        total[...] = value
        normed, _ = norm_stats(value)
        result = normed * gain[0:1] + shift[0:1]
        after[...] = result
        low[...] = result.astype(BF)

    return launch(
        body,
        "first_norm",
        at,
        [
            near(mine),
            near(other),
            near(tokens, lambda ref, at: ref.at[rows_at(at[0], half), :]),
            near(bias),
            near(gain),
            near(shift),
        ],
        [shape(half, width), shape(half, width), shape(half, width, dtype=BF)],
        us=1.7,
    )


def index_rows(top_index):
    rows, nh, ns, keep = top_index.shape
    flat = top_index.reshape(rows, nh, ns, keep // 128, 128).transpose(0, 1, 3, 2, 4)
    return flat.reshape(rows * nh * ns * (keep // 128), 128)


def make_mask(at, flat, dims, seg, tile, turn):
    rows, nh, ns, keep = dims
    halves = keep // 128
    per_row = nh * ns * halves
    tiles = rows // 2 // tile
    columns = ns * seg
    blocks = columns // 128
    group = 32

    def body(at, ins, outs, _):
        (index,) = ins
        (bias,) = outs
        lane = lax.broadcasted_iota(jnp.int32, (group, 128), 1).astype(F32)
        lane_low = lane.astype(BF)
        empty = jnp.full((group, 128), -1.0, BF)
        own = at[2]
        steps = []
        step = 1
        while step <= seg - keep:
            steps.insert(0, step)
            step *= 2
        turns = steps + [(seg * s) % 128 for s in range(ns)]
        below = {s: lane_low < jnp.asarray(s, BF) for s in turns if 0 < s < 128}

        for t in range(tiles):
            index.ready(t)
            source = index.buffer.at[t]

            def one_group(g, _):
                for h in range(nh):
                    v = [empty] * blocks
                    for slot in range(ns):
                        first, turn = divmod(seg * slot, 128)
                        for c in range(halves):
                            start = g * (group * per_row) + h * ns * halves + c * ns + (own ^ slot)
                            found = jnp.concatenate(
                                [source[pl.ds(start + q * 8 * per_row, 8, stride=per_row), :] for q in range(group // 8)],
                                axis=0,
                            )
                            ahead = (found.astype(F32) - (lane + float(128 * c))).astype(BF)
                            at_block = first + c
                            if turn == 0:
                                v[at_block] = ahead
                            else:
                                turned = pltpu.roll(ahead, turn, axis=1)
                                v[at_block] = jnp.where(below[turn], v[at_block], turned)
                                v[at_block + 1] = jnp.where(below[turn], turned, v[at_block + 1])
                    for s in steps:
                        gap = jnp.asarray(s, BF)
                        moved = [x - gap for x in v]
                        stay = [jnp.where(x >= gap, empty, x) for x in v]
                        if s % 128 == 0:
                            hop = s // 128
                            v = stay[:hop] + [jnp.maximum(stay[i], moved[i - hop]) for i in range(hop, blocks)]
                        else:
                            turned = [pltpu.roll(x, s, axis=1) for x in moved]
                            v = [
                                jnp.maximum(stay[i], jnp.where(below[s], turned[i - 1], turned[i])) for i in range(blocks)
                            ]
                    for i in range(blocks):
                        bias[h, pl.ds(pl.multiple_of(t * tile + g * group, group), group), i * 128 : (i + 1) * 128] = v[
                            i
                        ] * jnp.asarray(1e30, BF)
                return 0

            lax.fori_loop(0, tile // group, one_group, 0)

    flat = flat.reshape(2 * tiles, tile * per_row, 128)
    return launch(
        body,
        "mask",
        at,
        [
            far(
                flat,
                lambda ref, at: ref.at[pl.ds((at[0] ^ turn) * tiles, tiles)],
                (tiles, tile * per_row, 128),
            )
        ],
        [shape(nh, rows // 2, columns, dtype=BF)],
        us=10,
    )[0]


def keys_values(at, shards, w, nh):
    seg, width = shards[0].shape
    local = w.shape[1]
    hd = local // nh

    def body(at, ins, outs, _):
        for slot in range(4):
            x = ins[slot][...]
            span = slice(slot * seg, (slot + 1) * seg)
            for i, out in enumerate(outs):
                full = mm(x, ins[4][i + 1], NT)
                high = full.astype(BF)
                low = (full - high.astype(F32)).astype(BF)
                for h in range(nh):
                    part = slice(h * hd, (h + 1) * hd)
                    out[h, span, :] = jnp.concatenate([high[:, part], low[:, part]], axis=1)

    out = shape(nh, 4 * seg, 2 * hd, dtype=BF)
    return launch(body, "keys_values", at, [near(s) for s in shards] + [near(w)], [out, out], us=2)


def cross_forward(at, mine, other, bias_mine, bias_other, keys, values, w, b, wo, nh):
    half, width = mine.shape
    rows = 2 * half
    local = w.shape[1]
    hd = local // nh
    slots = keys.shape[1]
    scale = hd**-0.5

    def body(at, ins, outs, scratch):
        mine, other, wq, keys, bias_mine, bias_other, values, wo, b = ins
        keep, send, raised, inverse, query, heads = outs
        twice, found = scratch
        for r, x in enumerate((mine, other)):
            q = (mm(x[...], wq[0], NT) + b[0:1]).astype(BF)
            query[r * half : (r + 1) * half, :] = q
            scaled = q * jnp.asarray(scale, BF)
            for h in range(nh):
                part = scaled[:, h * hd : (h + 1) * hd]
                twice[h, r * half : (r + 1) * half, :] = jnp.concatenate([part, part], axis=1)

        def one_head(h, _):
            for r, bias in enumerate((bias_mine, bias_other)):
                span = slice(r * half, (r + 1) * half)
                scores = mm(twice[h, span, :], keys[h], NT) + bias[h].astype(F32)
                e = jnp.exp(scores - jnp.max(scores, axis=1, keepdims=True))
                total = 1.0 / jnp.sum(e, axis=1, keepdims=True)
                low = e.astype(BF)
                raised[h, span, :] = low
                inverse[h, span, :] = jnp.broadcast_to(total, (half, 128))
                both = mm(low, values[h])
                found[h, span, :] = (both[:, :hd] + both[:, hd:]) * total
            return 0

        lax.fori_loop(0, nh, one_head, 0)
        for r, target in enumerate((keep, send)):
            span = slice(r * half, (r + 1) * half)
            out = (jnp.concatenate([found[h, span, :] for h in range(nh)], axis=1) + b[1:2]).astype(BF)
            heads[span, :] = out
            target[...] = mm(out, wo[...]).astype(target.dtype)

    return launch(
        body,
        "cross_fwd",
        at,
        [near(a) for a in (mine, other, w, keys, bias_mine, bias_other, values, wo, b)],
        [
            shape(half, width),
            shape(half, width, dtype=BF),
            shape(nh, rows, slots, dtype=BF),
            shape(nh, rows, 128),
            shape(rows, local, dtype=BF),
            shape(rows, local, dtype=BF),
        ],
        scratch=[pltpu.VMEM((nh, rows, 2 * hd), BF), pltpu.VMEM((nh, rows, hd), F32)],
        mib=30,
        us=9,
    )


def feed(at, after, kept, close, distant, cot, f1, f2, b1, terms, out_bias, fc2_bias, gain, shift):
    rows, width = distant.shape
    units = f1[0].shape[1]
    base = terms[0].shape[0] - 16

    def body(at, ins, outs, scratch):
        after, kept, close, distant, cot, out_bias, fc2_bias, gain, shift, b1, close_terms, far_terms = ins[:12]
        f1, f2 = ins[12:16], ins[16:20]
        biases = (
            b1[...],
            from_terms(close_terms[...][0:3]),
            from_terms(far_terms[...][0:3]),
            from_terms(far_terms[...][3:6]),
        )
        trio, dsecond_low, sums = outs
        (slope,) = scratch
        second = after[...] + (kept[...] + close[...].astype(F32) + distant[...].astype(F32)) + out_bias[...]
        normed_mid, inverse_mid = norm_stats(second)
        mid = normed_mid * gain[1:2] + shift[1:2]
        mid_low = mid.astype(BF)
        trio[0] = mid_low
        total = jnp.zeros((rows, width), F32)
        for s in range(4):
            pre = mm(mid_low, f1[s][...]) + biases[s]
            hidden, slope[s] = gelu_pair(pre)
            total = total + mm(hidden, f2[s][...])
        last = mid + total + fc2_bias[...]
        normed_last, inverse_last = norm_stats(last)
        first_row = (2 * at[0] + at[1]) * rows
        live = (first_row + lax.broadcasted_iota(jnp.int32, (rows, 1), 0) < at[3]).astype(F32)
        trio[2] = ((normed_last * gain[2:3] + shift[2:3]) * live).astype(BF)
        delta = cot[...].astype(F32) * live
        dlast = norm_backward(delta, normed_last, inverse_last, gain[2:3])
        dlast_low = dlast.astype(BF)
        trio[1] = dlast_low
        dmid = dlast
        for s in range(4):
            dpre = (mm(dlast_low, f2[s][...], NT) * slope[s]).astype(BF)
            dmid = dmid + mm(dpre, f1[s][...], NT)
        dsecond = norm_backward(dmid, normed_mid, inverse_mid, gain[1:2])
        dsecond_low[...] = dsecond.astype(BF)
        sums[...] = jnp.concatenate(
            [
                column_sum(delta * normed_last),
                column_sum(delta),
                column_sum(dlast),
                column_sum(dmid * normed_mid),
                column_sum(dmid),
                column_sum(dsecond),
                jnp.zeros((2, width), F32),
            ],
            axis=0,
        )

    quarter = lambda ref, at: ref.at[rows_at(at[1], rows), :]
    tail = lambda ref, at: ref.at[pl.ds(base, 16), :]
    return launch(
        body,
        "feed",
        at,
        [
            near(after, quarter),
            near(kept, quarter),
            near(close, quarter),
            near(distant),
            near(cot, lambda ref, at: ref.at[rows_at(2 * at[0] + at[1], rows), :]),
            near(out_bias),
            near(fc2_bias),
            near(gain),
            near(shift),
            near(b1),
            near(terms[0], tail),
            near(terms[1], tail),
        ]
        + [near(a) for a in (*f1, *f2)],
        [shape(3, rows, width, dtype=BF), shape(rows, width, dtype=BF), shape(8, width)],
        scratch=[pltpu.VMEM((4, rows, units), F32)],
        mib=18,
        us=10,
    )


def assemble(at, z, blocks):
    rows = blocks[0].shape[0]
    for base, own, distant in ((0, blocks[0], blocks[2]), (2 * rows, blocks[1], blocks[3])):
        z[pl.ds(pl.multiple_of(base + at[1] * rows, rows), rows), :] = own[...]
        z[pl.ds(pl.multiple_of(base + (1 - at[1]) * rows, rows), rows), :] = distant[...]


def cross_backward(at, z_blocks, raised, inverse, query, keys, values, w, wo, nh):
    rows, width = z_blocks[0].shape
    rows = 4 * rows
    half = rows // 2
    local = w.shape[1]
    hd = local // nh
    slots = keys.shape[1]
    scale = hd**-0.5

    def body(at, ins, outs, scratch):
        blocks, (wo, inverse, values, raised, query, keys, w) = ins[:4], ins[4:]
        keep, send, dquery, dkv, sums = outs
        z, douts, right, found = scratch
        assemble(at, z, blocks)
        zero = jnp.zeros((half, hd), BF)
        head_sum = jnp.zeros((1, local), F32)
        for r in range(2):
            span = slice(r * half, (r + 1) * half)
            dhead = mm(z[span, :], wo[...], NT)
            head_sum = head_sum + column_sum(dhead)
            scaled = query[span, :] * jnp.asarray(scale, BF)
            for h in range(nh):
                part = slice(h * hd, (h + 1) * hd)
                dout = (dhead[:, part] * inverse[h, span, 0:1]).astype(BF)
                douts[h, span, :] = jnp.concatenate([dout, dout], axis=1)
                right[h, 0, span, :] = jnp.concatenate([scaled[:, part], zero], axis=1)
                right[h, 1, span, :] = jnp.concatenate([zero, dout], axis=1)

        def one_head(h, _):
            grad = None
            for r in range(2):
                span = slice(r * half, (r + 1) * half)
                dprob = mm(douts[h, span, :], values[h], NT)
                low = raised[h, span, :]
                e = low.astype(F32)
                weighed = e * dprob
                mean = jnp.sum(weighed, axis=1, keepdims=True) * inverse[h, span, 0:1]
                dscore = (weighed - e * mean).astype(BF)
                both = mm(dscore, keys[h])
                found[h, span, :] = both[:, :hd] + both[:, hd:]
                part = mm(dscore, right[h, 0, span, :], TN) + mm(low, right[h, 1, span, :], TN)
                grad = part if grad is None else grad + part
            dkv[h] = grad.astype(BF)
            return 0

        lax.fori_loop(0, nh, one_head, 0)
        query_sum = jnp.zeros((1, local), F32)
        for r, target in enumerate((keep, send)):
            span = slice(r * half, (r + 1) * half)
            dq = jnp.concatenate([found[h, span, :] for h in range(nh)], axis=1) * scale
            query_sum = query_sum + column_sum(dq)
            dq_low = dq.astype(BF)
            dquery[span, :] = dq_low
            target[...] = mm(dq_low, w[0]).astype(target.dtype)
        sums[...] = jnp.concatenate([query_sum, head_sum], axis=0)

    return launch(
        body,
        "cross_bwd",
        at,
        [near(a) for a in (*z_blocks, wo, inverse, values, raised, query, keys, w)],
        [
            shape(half, width),
            shape(half, width, dtype=BF),
            shape(rows, local, dtype=BF),
            shape(nh, slots, 2 * hd, dtype=BF),
            shape(2, local),
        ],
        scratch=[
            pltpu.VMEM((rows, width), BF),
            pltpu.VMEM((nh, rows, 2 * hd), BF),
            pltpu.VMEM((nh, 2, rows, 2 * hd), BF),
            pltpu.VMEM((nh, rows, hd), F32),
        ],
        mib=30,
        us=11,
    )


def store_gradient(at, dkv, w, nh):
    _, slots, twice = dkv.shape
    _, local, width = w.shape
    hd = twice // 2
    seg = slots // 4

    def body(at, ins, outs, _):
        dkv, w = ins
        keep, send = outs
        weights = []
        for h in range(nh):
            part = slice(h * hd, (h + 1) * hd)
            weights += [w[1][part], w[2][part]]
        weight = jnp.concatenate(weights, axis=0)
        for slot in (1, 3, 0, 2):
            rows = jnp.concatenate([dkv[h, slot * seg : (slot + 1) * seg, :] for h in range(nh)], axis=1)
            part = mm(rows, weight)
            if slot % 2 == 0:
                keep[slot // 2] = part
            else:
                send[slot // 2] = part.astype(BF)

    return launch(
        body,
        "store_grad",
        at,
        [near(dkv), near(w)],
        [shape(2, seg, width), shape(2, seg, width, dtype=BF)],
        us=2.6,
    )


def group_outs(width, columns, blocks, extra):
    if not blocks:
        return [shape(width, columns)]
    n, r = blocks
    tail = 3 * EXTRA if extra else 0
    return [shape(n * r + tail, columns, dtype=BF), shape(n, r, columns)]


def emit_group(at, grad, outs, blocks, first, columns):
    if not blocks:
        outs[0][:, first : first + columns] = grad[...]
        return
    n, r = blocks
    span = slice(first, first + columns)
    for b in range(n):
        theirs = pl.ds(pl.multiple_of((2 * b + 1 - at[4]) * r, 8), r)
        outs[0][b * r : (b + 1) * r, span] = grad[theirs, :].astype(BF)
        outs[1][b, :, span] = grad[pl.ds(pl.multiple_of((2 * b + at[4]) * r, 8), r), :]


def turned_product(out, left, right, step=256):
    if left.shape[1] % step:
        out[...] = mm(left[...], right[...], TN)
        return

    def some(i, _):
        span = pl.ds(pl.multiple_of(i * step, step), step)
        out[span, :] = mm(left[:, span], right[...], TN)
        return 0

    lax.fori_loop(0, left.shape[1] // step, some, 0)


def feed_grads(at, trios, fc1, fc2, b1, blocks):
    _, rows, width = trios[0].shape
    units = fc1.shape[1]

    def body(at, ins, outs, scratch):
        trios, (f1, f2, b1) = ins[:4], ins[4:]
        mid, dlast, hidden, dpre, grad = scratch
        for s, block in enumerate(trios):
            mid[s * rows : (s + 1) * rows, :] = block[0]
            dlast[s * rows : (s + 1) * rows, :] = block[1]

        def some_rows(i, total):
            span = rows_at(i, 2 * rows)
            hidden[span, :], slope = gelu_pair(mm(mid[span, :], f1[...]) + b1[...])
            grad_pre = mm(dlast[span, :], f2[...], NT) * slope
            dpre[span, :] = grad_pre.astype(BF)
            return total + column_sum(grad_pre)

        outs[-1][...] = lax.fori_loop(0, 2, some_rows, jnp.zeros((1, units), F32))
        turned_product(grad, mid, dpre)
        emit_group(at, grad, outs, blocks, 0, units)
        turned_product(grad, dlast, hidden)
        emit_group(at, grad, outs, blocks, units, units)

    return launch(
        body,
        "feed_grads",
        at,
        [near(a) for a in (*trios, fc1, fc2, b1)],
        group_outs(width, 2 * units, blocks, False) + [shape(1, units)],
        scratch=[pltpu.VMEM((4 * rows, width), BF)] * 2
        + [pltpu.VMEM((4 * rows, units), BF)] * 2
        + [pltpu.VMEM((width, units), F32)],
        mib=20,
        us=6,
    )


def cross_grads(at, z_blocks, mine, other, dquery, heads, shards, dkv, first_mine, first_other, flat, small, nh, blocks):
    half, width = mine.shape
    local = dquery.shape[1]
    hd = local // nh
    seg = shards[0].shape[0]
    feed_sums, first_sums, fc1_sum, head_sums = small

    def body(at, ins, outs, scratch):
        z_blocks, shards = ins[0:4], ins[4:8]
        mine, other, dquery, heads, dkv, first_mine, first_other, flat, feed_sums, first_sums, fc1_sum, head_sums = ins[8:]
        z, grad = scratch
        extra = outs[-1]
        assemble(at, z, z_blocks)
        grad[...] = mm(mine[...], dquery[:half], TN) + mm(other[...], dquery[half:], TN)
        emit_group(at, grad, outs, blocks, 0, local)
        grad[...] = mm(z[...], heads[...], TN)
        emit_group(at, grad, outs, blocks, 3 * local, local)
        z[rows_at(at[0], half), :] = first_mine[...]
        z[rows_at(1 - at[0], half), :] = first_other[...]
        grad[...] = mm(z[...], flat[...], TN)
        emit_group(at, grad, outs, blocks, 4 * local, local)
        both = None
        for slot, block in enumerate(shards):
            rows = jnp.concatenate([dkv[h, slot * seg : (slot + 1) * seg, :] for h in range(nh)], axis=1)
            part = mm(block[...], rows, TN)
            both = part if both is None else both + part
        for i in range(2):
            grad[...] = jnp.concatenate([both[:, (2 * h + i) * hd : (2 * h + i + 1) * hd] for h in range(nh)], axis=1)
            emit_group(at, grad, outs, blocks, (1 + i) * local, local)
        line = jnp.concatenate([head_sums[0:1], head_sums[1:2], jnp.zeros((1, width - 2 * local), F32)], axis=1)
        small = jnp.concatenate(
            [feed_sums[0:6], first_sums[0:3], fc1_sum[...], line, jnp.zeros((EXTRA - 11, width), F32)], axis=0
        )
        extra[...] = small
        if blocks:
            outs[0][blocks[0] * blocks[1] :, 0:width] = three_terms(small)
            outs[0][blocks[0] * blocks[1] :, width:] = jnp.zeros((3 * EXTRA, 5 * local - width), BF)

    return launch(
        body,
        "cross_grads",
        at,
        [
            near(a)
            for a in (
                *z_blocks,
                *shards,
                mine,
                other,
                dquery,
                heads,
                dkv,
                first_mine,
                first_other,
                flat,
                feed_sums,
                first_sums,
                fc1_sum,
                head_sums,
            )
        ],
        group_outs(width, 5 * local, blocks, True) + [shape(EXTRA, width)],
        scratch=[pltpu.VMEM((2 * half, width), BF), pltpu.VMEM((width, local), F32)],
        us=4,
    )


def first_back(at, z_own, z_distant, mine, other, total, gain):
    half, width = mine.shape
    rows = half // 2

    def body(at, ins, outs, scratch):
        z_own, z_distant, mine, other, total, gain = ins
        dfirst, low, sums = outs
        (dafter,) = scratch
        dafter[rows_at(at[1], rows), :] = z_own[...].astype(F32)
        dafter[rows_at(1 - at[1], rows), :] = z_distant[...].astype(F32)
        value = dafter[...] + (mine[...].astype(F32) + other[...].astype(F32))
        normed, inverse = norm_stats(total[...])
        result = norm_backward(value, normed, inverse, gain[0:1])
        dfirst[...] = result
        low[...] = result.astype(BF)
        place = lax.broadcasted_iota(jnp.int32, (half, 1), 0)
        counted = ((place >= at[1] * rows) & (place < (at[1] + 1) * rows)).astype(F32)
        sums[...] = jnp.concatenate(
            [
                column_sum(value * normed * counted),
                column_sum(value * counted),
                column_sum(result * counted),
                jnp.zeros((5, width), F32),
            ],
            axis=0,
        )

    return launch(
        body,
        "first_back",
        at,
        [near(a) for a in (z_own, z_distant, mine, other, total, gain)],
        [shape(half, width), shape(half, width, dtype=BF), shape(8, width)],
        scratch=[pltpu.VMEM((half, width), F32)],
        us=2.8,
    )


def self_backward(at, mine, other, tokens, w, wo, qkv, prob, nh, blocks):
    half, width = mine.shape
    rows = 2 * half
    local = wo.shape[0]
    hd = local // nh
    scale = hd**-0.5

    def body(at, ins, outs, scratch):
        mine, other, wo, qkv, prob, tok, w = ins
        send, keep = outs[0:2]
        group, extra = outs[2:-1], outs[-1]
        z, dqkv, grad = scratch
        own, distant = rows_at(at[0], half), rows_at(1 - at[0], half)
        z[own, :] = mine[...]
        z[distant, :] = other[...]
        dself = mm(z[...], wo[...], NT).astype(BF)
        v, k, q = qkv[2], qkv[1], qkv[0]
        dq, dk, dv = [], [], []
        for h in range(nh):
            part = slice(h * hd, (h + 1) * hd)
            weights_low = prob[h]
            weights = weights_low.astype(F32)
            weighed = weights * mm(dself[:, part], v[:, part], NT)
            dscore = (weighed - weights * jnp.sum(weighed, axis=1, keepdims=True)).astype(BF)
            dq.append(mm(dscore, k[:, part]))
            dk.append(mm(dscore, q[:, part], TN))
            dv.append(mm(weights_low, dself[:, part], TN))
        dquery = jnp.concatenate(dq, axis=1) * scale
        dvalue = jnp.concatenate(dv, axis=1)
        dqkv[0] = dquery.astype(BF)
        dqkv[1] = (jnp.concatenate(dk, axis=1) * scale).astype(BF)
        dqkv[2] = dvalue.astype(BF)
        x = tok[...]
        for i in range(3):
            grad[...] = mm(x, dqkv[i], TN)
            emit_group(at, grad, group, blocks, i * local, local)
        line = jnp.concatenate([column_sum(dquery), column_sum(dvalue), jnp.zeros((1, local), F32)], axis=1)
        small = jnp.concatenate([line, jnp.zeros((EXTRA - 1, 3 * local), F32)], axis=0)
        extra[...] = small
        if blocks:
            group[0][blocks[0] * blocks[1] :, :] = three_terms(small)
        for place, out in ((distant, send), (own, keep)):
            total = mm(dqkv[0, place, :], w[0]) + mm(dqkv[1, place, :], w[1]) + mm(dqkv[2, place, :], w[2])
            out[...] = total.astype(out.dtype)

    return launch(
        body,
        "self_bwd",
        at,
        [near(a) for a in (mine, other, wo, qkv, prob, tokens, w)],
        [shape(half, width, dtype=BF), shape(half, width)]
        + group_outs(width, 3 * local, blocks, True)
        + [shape(EXTRA, 3 * local)],
        scratch=[
            pltpu.VMEM((rows, width), BF),
            pltpu.VMEM((3, rows, local), BF),
            pltpu.VMEM((width, local), F32),
        ],
        mib=20,
        us=6,
    )


def add_stage(at, keep, got, small, bit):
    n, rows, columns = keep.shape
    tail = 0 if small is None else 3 * EXTRA
    reach = small.shape[1] if tail else 0

    def body(at, ins, outs, _):
        keep, got = ins[:2]
        mine = at[bit]
        send, stay = outs[:2]
        for b in range(n // 2):
            for chosen, out in ((1 - mine, send), (mine, stay)):
                block = 2 * b + chosen
                value = keep[block] + got[pl.ds(pl.multiple_of(block * rows, 8), rows), :].astype(F32)
                if out is send:
                    send[b * rows : (b + 1) * rows, :] = value.astype(BF)
                else:
                    stay[b] = value
        if tail:
            total = ins[2][...] + from_terms(got[n * rows :, 0:reach])
            outs[2][...] = total
            send[n // 2 * rows :, 0:reach] = three_terms(total)
            if reach < columns:
                send[n // 2 * rows :, reach:] = jnp.zeros((tail, columns - reach), BF)

    ins = [near(keep), near(got)] + ([near(small)] if tail else [])
    outs = [shape(n // 2 * rows + tail, columns, dtype=BF), shape(n // 2, rows, columns)]
    if tail:
        outs.append(shape(EXTRA, reach))
    return launch(body, "add_stage", at, ins, outs, us=1)


def last_stage(at, keep, got, small, parts):
    _, rows, columns = keep.shape
    each = columns // sum(count for count, _ in parts)
    reach = 0 if small is None else small.shape[1]

    def body(at, ins, outs, _):
        total = ins[0][0] + ins[1][0:rows].astype(F32)
        first = 0
        for out, (count, turned) in zip(outs, parts):
            if count == 1:
                value = total[:, first * each : (first + 1) * each]
                out[...] = value.T if turned else value
            else:
                for i in range(count):
                    out[i] = total[:, (first + i) * each : (first + i + 1) * each]
            first += count
        if reach:
            outs[-1][...] = ins[2][...] + from_terms(ins[1][rows:, 0:reach])

    outs = []
    for count, turned in parts:
        dims = (rows, each) if count == 1 else (count, rows, each)
        outs.append(shape(*(dims[::-1] if turned else dims)))
    ins = [near(keep), near(got)]
    if reach:
        ins.append(near(small))
        outs.append(shape(EXTRA, reach))
    return launch(body, "last_stage", at, ins, outs, us=1)


def join_halves(at, mine, other):
    half, width = mine.shape

    def body(at, ins, outs, _):
        outs[0][rows_at(at[0], half), :] = ins[0][...]
        outs[0][rows_at(1 - at[0], half), :] = ins[1][...]

    out = shape(2 * half, width, dtype=mine.dtype)
    return launch(body, "join_halves", at, [near(mine), near(other)], [out])[0]


def join_quarters(at, trios):
    _, rows, width = trios[0].shape

    def body(at, ins, outs, _):
        for flips, block in enumerate(ins):
            place = 2 * (at[0] ^ (flips & 1)) + (at[1] ^ (flips >> 1))
            outs[0][rows_at(place, rows), :] = block[...]

    ins = [near(t, lambda ref, at: ref.at[2]) for t in trios]
    return launch(body, "join_quarters", at, ins, [shape(4 * rows, width, dtype=BF)])[0]


def flip(bit, size):
    return [(i, i ^ bit) for i in range(size)]


def butterfly(value, axis, size):
    bit = 1
    while bit < size:
        value = value + lax.ppermute(value, axis, flip(bit, size))
        bit *= 2
    return value


def on_device(
    tokens,
    store,
    summary_length,
    top_index,
    cotangent,
    self_qkv_weight,
    self_qv_bias,
    self_out_weight,
    self_out_bias,
    qkv_weight,
    qv_bias,
    out_weight,
    out_bias,
    fc1_weight,
    fc1_bias,
    fc2_weight,
    fc2_bias,
    norm_gain,
    norm_shift,
):
    rows, width = tokens.shape
    half, quarter = rows // 2, rows // 4
    nh = top_index.shape[1]
    local = qkv_weight.shape[2]
    units = fc1_weight.shape[1]
    seg = store.shape[1]
    wide = lax.axis_size("wide")
    place = lax.axis_index("narrow")
    doc = lax.axis_index("wide")
    core, across = place % 2, place // 2
    at = jnp.stack([core, across, place, summary_length[0], doc % 2, doc // 2 % 2, doc // 4]).astype(jnp.int32)
    blocks = (wide // 2, width // wide) if wide == 8 else None
    row = lambda v: v.reshape(1, -1)
    self_w = jnp.swapaxes(self_qkv_weight, 1, 2)
    cross_w = jnp.swapaxes(qkv_weight, 1, 2)

    def to_core(v):
        return lax.ppermute(v, "narrow", CORE)

    def to_across(v):
        return lax.ppermute(v, "narrow", ACROSS)

    def spread(v):
        distant = to_across(v)
        return [v, to_core(v), distant, to_core(distant)]

    def chip_sum(keep, send):
        return (keep + to_core(send).astype(F32)).astype(BF)

    store_x = to_across(store[0])
    qkv, prob, flat, send, keep = self_forward(
        at, tokens, self_w, self_qv_bias, self_out_weight, row(fc1_bias), nh
    )
    close = to_core(send)
    mine = jnp.concatenate(
        [
            (keep + close[:half].astype(F32)).astype(BF),
            send[half : half + 3],
            close[half : half + 3],
            jnp.zeros((16 - 6, width), BF),
        ],
        axis=0,
    )
    terms_close = close
    other = to_across(mine)
    f1_x = to_across(tie(fc1_weight, mine))
    f2_x = to_across(tie(fc2_weight, mine))
    index = index_rows(top_index)
    bias_mine = make_mask(tie(at, mine), index, top_index.shape, seg, 128, 0)
    store_x = tie(store_x, bias_mine)
    shards = [store[0], to_core(tie(store[0], bias_mine)), store_x, to_core(store_x)]
    bias_other = make_mask(tie(at, bias_mine), index, top_index.shape, seg, 128, 1)
    other = tie(other, bias_other)
    first_total, after, after_low = first_norm(at, mine, other, tokens, row(self_out_bias), norm_gain, norm_shift)
    after_other = to_core(after_low)

    keys, values = keys_values(tie(at, after_low), shards, cross_w, nh)
    f1_x, f2_x = tie(f1_x, keys), tie(f2_x, keys)
    f1 = [fc1_weight, to_core(tie(fc1_weight, keys)), f1_x, None]
    f2 = [fc2_weight, to_core(tie(fc2_weight, keys)), f2_x, None]
    keep, send, raised, inverse, query, heads = cross_forward(
        tie(at, keys), after_low, after_other, bias_mine, bias_other, keys, values, cross_w, qv_bias, out_weight, nh
    )
    close = to_core(send)
    theirs = (1 - across) * quarter
    distant = to_across(
        (
            lax.dynamic_slice_in_dim(keep, theirs, quarter, 0)
            + lax.dynamic_slice_in_dim(close, theirs, quarter, 0).astype(F32)
        ).astype(BF)
    )
    f1[3], f2[3] = to_core(tie(f1_x, close)), to_core(tie(f2_x, close))

    trio, z, feed_sums = feed(
        at,
        after,
        keep,
        close,
        distant,
        cotangent,
        f1,
        f2,
        row(fc1_bias),
        (terms_close, other),
        row(out_bias),
        row(fc2_bias),
        norm_gain,
        norm_shift,
    )
    z_all = spread(z)
    trios = spread(tie(trio, z_all[2]))

    keep, send, dquery, dkv, cross_sums = cross_backward(
        at, z_all, raised, inverse, query, keys, values, cross_w, out_weight, nh
    )
    mine = chip_sum(keep, send)
    other = to_across(mine)
    *feed_out, fc1_sum = feed_grads(tie(at, mine), trios, fc1_weight, fc2_weight, row(fc1_bias), blocks)
    other = tie(other, fc1_sum)
    dfirst, dfirst_low, first_sums = first_back(at, z_all[0], z_all[2], mine, other, first_total, norm_gain)
    dfirst_other = to_core(dfirst_low)
    store_keep, store_send = store_gradient(tie(at, dfirst_low), dkv, cross_w, nh)
    store_close = to_core(store_send)
    *cross_out, cross_small = cross_grads(
        tie(at, store_send),
        z_all,
        after_low,
        after_other,
        dquery,
        heads,
        shards,
        dkv,
        dfirst_low,
        dfirst_other,
        flat,
        (feed_sums, first_sums, fc1_sum, cross_sums),
        nh,
        blocks,
    )
    store_distant = to_across((store_keep[1] + tie(store_close, cross_small)[1].astype(F32)).astype(BF))

    send, keep, *self_out, self_small = self_backward(
        tie(at, cross_small), dfirst_low, dfirst_other, tokens, self_w, self_out_weight, qkv, prob, nh, blocks
    )
    mine = chip_sum(keep, send)
    tokens_half = dfirst + (mine.astype(F32) + to_across(mine).astype(F32))
    tokens_grad = join_halves(at, tokens_half, to_core(tokens_half))
    mixed = join_quarters(tie(at, mine), trios)
    store_grad = (store_keep[0] + store_close[0].astype(F32) + store_distant.astype(F32))[None]

    if blocks:
        over = lambda v, bit: lax.ppermute(v, "wide", flip(bit, 8))
        feed_send, feed_keep = add_stage(tie(at, self_small), feed_out[1], over(feed_out[0], 1), None, 5)
        cross_send, cross_keep, cross_small = add_stage(
            tie(at, feed_send), cross_out[1], over(cross_out[0], 1), cross_small, 5
        )
        feed_send, feed_keep = add_stage(tie(at, cross_send), feed_keep, over(feed_send, 2), None, 6)
        self_send, self_keep, self_small = add_stage(
            tie(at, feed_send), self_out[1], over(self_out[0], 1), self_small, 5
        )
        cross_send, cross_keep, cross_small = add_stage(
            tie(at, self_send), cross_keep, over(cross_send, 2), cross_small, 6
        )
        fc1_grad, fc2_grad = last_stage(tie(at, cross_send), feed_keep, over(feed_send, 4), None, [(1, False), (1, False)])
        fc2_grad = fc2_grad.T
        self_send, self_keep, self_small = add_stage(
            tie(at, fc1_grad), self_keep, over(self_send, 2), self_small, 6
        )
        qkv_grad, out_grad, self_out_grad, cross_small = last_stage(
            tie(at, self_send), cross_keep, over(cross_send, 4), cross_small, [(3, False), (1, True), (1, True)]
        )
        self_qkv_grad, self_small = last_stage(
            tie(at, cross_small), self_keep, over(self_send, 4), self_small, [(3, False)]
        )
    else:
        scatter = functools.partial(lax.psum_scatter, axis_name="wide", tiled=True)
        parts = lambda g: jnp.stack([g[:, i * local : (i + 1) * local] for i in range(3)])
        fc1_grad = scatter(feed_out[0][:, :units], scatter_dimension=0)
        fc2_grad = scatter(feed_out[0][:, units:].T, scatter_dimension=1)
        qkv_grad = scatter(parts(cross_out[0]), scatter_dimension=1)
        out_grad = scatter(cross_out[0][:, 3 * local : 4 * local].T, scatter_dimension=1)
        self_qkv_grad = scatter(parts(self_out[0]), scatter_dimension=1)
        self_out_grad = scatter(cross_out[0][:, 4 * local :].T, scatter_dimension=1)
        cross_small = butterfly(cross_small, "wide", wide)
        self_small = butterfly(self_small, "wide", wide)
    summed = butterfly(cross_small, "narrow", 4)
    gain_last, shift_last, fc2_b, gain_mid, shift_mid, out_b, gain_first, shift_first, self_out_b = (
        summed[i] for i in range(9)
    )
    return (
        mixed,
        tokens_grad,
        store_grad,
        self_qkv_grad,
        self_small[0, : 2 * local].reshape(2, local),
        self_out_grad,
        self_out_b,
        qkv_grad,
        cross_small[10, : 2 * local].reshape(2, local),
        out_grad,
        out_b,
        fc1_grad,
        cross_small[9],
        fc2_grad,
        fc2_b,
        jnp.stack([gain_first, gain_mid, gain_last]),
        jnp.stack([shift_first, shift_mid, shift_last]),
    )


def solution(mesh):
    placed = (
        P("wide", None),
        P("wide", "narrow", None),
        P("wide"),
        P("wide", "narrow", None, None),
        P("wide", None),
        P(None, None, "narrow"),
        P(None, "narrow"),
        P("narrow", None),
        P(),
        P(None, None, "narrow"),
        P(None, "narrow"),
        P("narrow", None),
        P(),
        P(None, "narrow"),
        P("narrow"),
        P("narrow", None),
        P(),
        P(),
        P(),
    )
    return jax.shard_map(
        on_device,
        mesh=mesh,
        in_specs=placed,
        out_specs=(
            P("wide", None),
            P("wide", None),
            P("wide", "narrow", None),
            P(None, "wide", "narrow"),
            P(None, "narrow"),
            P("narrow", "wide"),
            P(),
            P(None, "wide", "narrow"),
            P(None, "narrow"),
            P("narrow", "wide"),
            P(),
            P("wide", "narrow"),
            P("narrow"),
            P("narrow", "wide"),
            P(),
            P(),
            P(),
        ),
        check_vma=False,
    )
```

```python
import functools

import jax
import jax.numpy as jnp
from jax import lax
from jax.experimental import pallas as pl
from jax.experimental.pallas import tpu as pltpu
from jax.sharding import PartitionSpec as P

F32 = jnp.float32
BF = jnp.bfloat16
NN = (((1,), (0,)), ((), ()))
NT = (((1,), (1,)), ((), ()))
TN = (((0,), (0,)), ((), ()))
EPS = 1e-05
PACE = 1.1e8
SELF_MIB = 60
EXTRA = 16

CORE = [(i, i ^ 1) for i in range(4)]
ACROSS = [(i, i ^ 2) for i in range(4)]


def mm(left, right, dims=NN):
    return lax.dot_general(left, right, dims, preferred_element_type=F32)


def shape(*dims, dtype=F32):
    return jax.ShapeDtypeStruct(dims, dtype)


def tie(value, *earlier):
    return lax.optimization_barrier((value, *earlier))[0]


class Operand:
    def __init__(self, source, buffer, sems, first, parts):
        self.buffer = buffer
        self.parts = parts
        if parts:
            self.copies = [
                pltpu.make_async_copy(source.at[i], buffer.at[i], sems.at[first + i]) for i in range(buffer.shape[0])
            ]
        else:
            self.copies = [pltpu.make_async_copy(source, buffer, sems.at[first])]
        self.waited = [False] * len(self.copies)
        for copy in self.copies:
            copy.start()

    def ready(self, part=None):
        for i, copy in enumerate(self.copies):
            if not self.waited[i] and (part is None or i == part):
                copy.wait()
                self.waited[i] = True

    @property
    def shape(self):
        return self.buffer.shape

    def __getitem__(self, at):
        self.ready(at if self.parts and isinstance(at, int) else None)
        return self.buffer[at]


class Result:
    def __init__(self, target, buffer, sems, first, parts):
        self.buffer = buffer
        if parts:
            self.copies = [
                pltpu.make_async_copy(buffer.at[i], target.at[i], sems.at[first + i]) for i in range(buffer.shape[0])
            ]
        else:
            self.copies = [pltpu.make_async_copy(buffer, target, sems.at[first])]
        self.started = [False] * len(self.copies)

    @property
    def shape(self):
        return self.buffer.shape

    @property
    def dtype(self):
        return self.buffer.dtype

    def __setitem__(self, at, value):
        self.buffer[at] = value

    def flush(self, part=0):
        self.copies[part].start()
        self.started[part] = True

    def finish(self):
        for i in range(len(self.copies)):
            if not self.started[i]:
                self.flush(i)
        for copy in self.copies:
            copy.wait()


def far(array, take=None, dims=None, parts=False):
    return ("far", array, take, tuple(dims or array.shape), parts)


def near(array, take=None):
    return ("near", array, take, None, False)


def raw(array):
    return ("raw", array, None, None, False)


def launch(body, name, at, ins, outs, scratch=(), mib=16, us=2.0):
    in_specs = [pl.BlockSpec(memory_space=pltpu.SMEM)]
    buffers, n_in, n_out = [], 0, 0
    for kind, array, _, dims, parts in ins:
        in_specs.append(pl.BlockSpec(memory_space=pltpu.VMEM if kind == "near" else pltpu.HBM))
        if kind == "far":
            buffers.append(pltpu.VMEM(dims, array.dtype))
            n_in += dims[0] if parts else 1
    out_specs, structs = [], []
    for out in outs:
        if isinstance(out, tuple):
            struct, parts = out
            out_specs.append(pl.BlockSpec(memory_space=pltpu.HBM))
            buffers.append(pltpu.VMEM(struct.shape, struct.dtype))
            n_out += struct.shape[0] if parts else 1
        else:
            struct = out
            out_specs.append(pl.BlockSpec(memory_space=pltpu.VMEM))
        structs.append(struct)
    n_buffers = len(buffers)
    sems = [pltpu.SemaphoreType.DMA((max(n, 1),)) for n in (n_in, n_out)]

    def kernel(at_ref, *refs):
        in_refs, out_refs = refs[: len(ins)], refs[len(ins) : len(ins) + len(outs)]
        rest = refs[len(ins) + len(outs) :]
        bufs, user, (in_sems, out_sems) = list(rest[:n_buffers]), rest[n_buffers:-2], rest[-2:]
        place, given = 0, []
        for ref, (kind, _, take, dims, parts) in zip(in_refs, ins):
            source = take(ref, at_ref) if take else ref
            if kind == "far":
                given.append(Operand(source, bufs.pop(0), in_sems, place, parts))
                place += dims[0] if parts else 1
            else:
                given.append(source)
        place, results = 0, []
        for ref, out in zip(out_refs, outs):
            if isinstance(out, tuple):
                results.append(Result(ref, bufs.pop(0), out_sems, place, out[1]))
                place += out[0].shape[0] if out[1] else 1
            else:
                results.append(ref)
        body(at_ref, given, results, user)
        for operand in given:
            if isinstance(operand, Operand):
                operand.ready()
        for result in results:
            if isinstance(result, Result):
                result.finish()

    return pl.pallas_call(
        kernel,
        in_specs=in_specs,
        out_specs=out_specs,
        out_shape=structs,
        scratch_shapes=buffers + list(scratch) + sems,
        compiler_params=pltpu.CompilerParams(vmem_limit_bytes=mib << 20),
        cost_estimate=pl.CostEstimate(flops=int(us * PACE), bytes_accessed=1000, transcendentals=0),
        name=name,
    )(at, *[entry[1] for entry in ins])


def norm_stats(value):
    centre = value - jnp.mean(value, axis=-1, keepdims=True)
    spread = jnp.mean(centre * centre, axis=-1, keepdims=True)
    inverse = lax.rsqrt(spread + EPS)
    return centre * inverse, inverse


def norm_backward(grad, normed, inverse, gain):
    scaled = grad * gain
    centred = scaled - jnp.mean(scaled, axis=-1, keepdims=True)
    return inverse * (centred - normed * jnp.mean(scaled * normed, axis=-1, keepdims=True))


def column_sum(value):
    return jnp.sum(value, axis=0, keepdims=True)


def erf(value):
    x = jnp.clip(value, -4.0, 4.0)
    y = x * x
    top = jnp.full_like(y, -2.72614225801306e-10)
    for factor in (
        2.77068142495902e-08,
        -2.10102402082508e-06,
        -5.69250639462346e-05,
        -7.34990630326855e-04,
        -2.95459980854025e-03,
        -1.60960333262415e-02,
    ):
        top = top * y + factor
    low = jnp.full_like(y, -1.45660718464996e-05)
    for factor in (
        -2.13374055278905e-04,
        -1.68282697438203e-03,
        -7.37332916720468e-03,
        -1.42647390514189e-02,
    ):
        low = low * y + factor
    return x * top / low


def gelu_pair(pre):
    phi = 0.5 * (1.0 + erf(pre * 0.7071067811865476))
    return (pre * phi).astype(BF), phi + pre * (jnp.exp(pre * pre * -0.5) * 0.3989422804014327)


def three_terms(value):
    high = value.astype(BF)
    rest = value - high.astype(F32)
    middle = rest.astype(BF)
    return jnp.concatenate([high, middle, (rest - middle.astype(F32)).astype(BF)], axis=0)


def from_terms(stacked):
    rows = stacked.shape[0] // 3
    terms = stacked.astype(F32)
    return terms[:rows] + terms[rows : 2 * rows] + terms[2 * rows :]


def rows_at(place, rows):
    return pl.ds(pl.multiple_of(place * rows, rows), rows)


def self_forward(at, tokens, w, b, wo, b1, nh):
    rows, width = tokens.shape
    local = w.shape[1]
    half = rows // 2
    hd = local // nh
    scale = hd**-0.5

    def body(at, ins, outs, _):
        tok, w, wo, b, b1 = ins
        qkv, prob, flat, send, keep = outs
        x = tok[...]
        q = (mm(x, w[0], NT) + b[0:1]).astype(BF)
        k = mm(x, w[1], NT).astype(BF)
        v = (mm(x, w[2], NT) + b[1:2]).astype(BF)
        for i, value in enumerate((q, k, v)):
            qkv[i] = value
            qkv.flush(i)
        row_ids = lax.broadcasted_iota(jnp.int32, (rows, rows), 0)
        key_ids = lax.broadcasted_iota(jnp.int32, (rows, rows), 1)
        allowed = (key_ids <= row_ids) & (key_ids < at[3])
        found = []
        for h in range(nh):
            part = slice(h * hd, (h + 1) * hd)
            scores = mm(q[:, part], k[:, part], NT) * scale
            scores = jnp.where(allowed, scores, -1e30)
            shifted = jnp.exp(scores - jnp.max(scores, axis=1, keepdims=True))
            weights = (shifted * (1.0 / jnp.sum(shifted, axis=1, keepdims=True))).astype(BF)
            prob[h] = weights
            prob.flush(h)
            found.append(mm(weights, v[:, part]).astype(BF))
        flat[...] = jnp.concatenate(found, axis=1)
        flat.flush()
        send[0:half, :] = mm(flat.buffer[rows_at(1 - at[0], half), :], wo[...]).astype(BF)
        send[half:, :] = jnp.concatenate([three_terms(b1[...]), jnp.zeros((16 - 3, width), BF)], axis=0)
        send.flush()
        keep[...] = mm(flat.buffer[rows_at(at[0], half), :], wo[...])

    return launch(
        body,
        "self_fwd",
        at,
        [far(tokens), far(w, parts=True), far(wo), far(b), far(b1)],
        [
            (shape(3, rows, local, dtype=BF), True),
            (shape(nh, rows, rows, dtype=BF), True),
            (shape(rows, local, dtype=BF), False),
            (shape(half + 16, width, dtype=BF), False),
            (shape(half, width), False),
        ],
        mib=SELF_MIB,
        us=4,
    )


def first_norm(at, mine, other, tokens, bias, gain, shift):
    half, width = mine.shape[0] - 16, mine.shape[1]

    def body(at, ins, outs, _):
        mine, other, tok, bias, gain, shift = ins
        total, after, low = outs
        value = tok[...].astype(F32) + (mine[0:half].astype(F32) + other[0:half].astype(F32)) + bias[...]
        total[...] = value
        normed, _ = norm_stats(value)
        result = normed * gain[0:1] + shift[0:1]
        after[...] = result
        low[...] = result.astype(BF)

    return launch(
        body,
        "first_norm",
        at,
        [
            near(mine),
            near(other),
            near(tokens, lambda ref, at: ref.at[rows_at(at[0], half), :]),
            near(bias),
            near(gain),
            near(shift),
        ],
        [shape(half, width), shape(half, width), shape(half, width, dtype=BF)],
        us=1.7,
    )


def index_rows(top_index):
    rows, nh, ns, keep = top_index.shape
    flat = top_index.reshape(rows, nh, ns, keep // 128, 128).transpose(0, 1, 3, 2, 4)
    return flat.reshape(rows * nh * ns * (keep // 128), 128)


def make_mask(at, flat, dims, seg, tile, turn):
    rows, nh, ns, keep = dims
    halves = keep // 128
    per_row = nh * ns * halves
    tiles = rows // 2 // tile
    columns = ns * seg
    blocks = columns // 128
    group = 32

    def body(at, ins, outs, _):
        (index,) = ins
        (bias,) = outs
        lane = lax.broadcasted_iota(jnp.int32, (group, 128), 1).astype(F32)
        lane_low = lane.astype(BF)
        empty = jnp.full((group, 128), -1.0, BF)
        own = at[2]
        steps = []
        step = 1
        while step <= seg - keep:
            steps.insert(0, step)
            step *= 2
        turns = steps + [(seg * s) % 128 for s in range(ns)]
        below = {s: lane_low < jnp.asarray(s, BF) for s in turns if 0 < s < 128}

        for t in range(tiles):
            index.ready(t)
            source = index.buffer.at[t]

            def one_group(g, _):
                for h in range(nh):
                    v = [empty] * blocks
                    for slot in range(ns):
                        first, turn = divmod(seg * slot, 128)
                        for c in range(halves):
                            start = g * (group * per_row) + h * ns * halves + c * ns + (own ^ slot)
                            found = jnp.concatenate(
                                [source[pl.ds(start + q * 8 * per_row, 8, stride=per_row), :] for q in range(group // 8)],
                                axis=0,
                            )
                            ahead = (found.astype(F32) - (lane + float(128 * c))).astype(BF)
                            at_block = first + c
                            if turn == 0:
                                v[at_block] = ahead
                            else:
                                turned = pltpu.roll(ahead, turn, axis=1)
                                v[at_block] = jnp.where(below[turn], v[at_block], turned)
                                v[at_block + 1] = jnp.where(below[turn], turned, v[at_block + 1])
                    for s in steps:
                        gap = jnp.asarray(s, BF)
                        moved = [x - gap for x in v]
                        stay = [jnp.where(x >= gap, empty, x) for x in v]
                        if s % 128 == 0:
                            hop = s // 128
                            v = stay[:hop] + [jnp.maximum(stay[i], moved[i - hop]) for i in range(hop, blocks)]
                        else:
                            turned = [pltpu.roll(x, s, axis=1) for x in moved]
                            v = [
                                jnp.maximum(stay[i], jnp.where(below[s], turned[i - 1], turned[i])) for i in range(blocks)
                            ]
                    for i in range(blocks):
                        bias[h, pl.ds(pl.multiple_of(t * tile + g * group, group), group), i * 128 : (i + 1) * 128] = v[
                            i
                        ] * jnp.asarray(1e30, BF)
                return 0

            lax.fori_loop(0, tile // group, one_group, 0)

    flat = flat.reshape(2 * tiles, tile * per_row, 128)
    return launch(
        body,
        "mask",
        at,
        [
            far(
                flat,
                lambda ref, at: ref.at[pl.ds((at[0] ^ turn) * tiles, tiles)],
                (tiles, tile * per_row, 128),
                parts=True,
            )
        ],
        [shape(nh, rows // 2, columns, dtype=BF)],
        us=10,
    )[0]


def keys_values(at, shards, w, nh):
    seg, width = shards[0].shape
    local = w.shape[1]
    hd = local // nh

    def body(at, ins, outs, _):
        for slot in range(4):
            x = ins[slot][...]
            span = slice(slot * seg, (slot + 1) * seg)
            for i, out in enumerate(outs):
                full = mm(x, ins[4][i + 1], NT)
                high = full.astype(BF)
                low = (full - high.astype(F32)).astype(BF)
                for h in range(nh):
                    part = slice(h * hd, (h + 1) * hd)
                    out[h, span, :] = jnp.concatenate([high[:, part], low[:, part]], axis=1)

    out = shape(nh, 4 * seg, 2 * hd, dtype=BF)
    return launch(body, "keys_values", at, [near(s) for s in shards] + [near(w)], [out, out], us=2)


def cross_forward(at, mine, other, bias_mine, bias_other, keys, values, w, b, wo, nh):
    half, width = mine.shape
    rows = 2 * half
    local = w.shape[1]
    hd = local // nh
    slots = keys.shape[1]
    scale = hd**-0.5

    def body(at, ins, outs, scratch):
        mine, other, wq, keys, bias_mine, bias_other, values, wo, b = ins
        keep, send, raised, inverse, query, heads = outs
        twice, found = scratch
        for r, x in enumerate((mine, other)):
            q = (mm(x[...], wq[0], NT) + b[0:1]).astype(BF)
            query[r * half : (r + 1) * half, :] = q
            scaled = q * jnp.asarray(scale, BF)
            for h in range(nh):
                part = scaled[:, h * hd : (h + 1) * hd]
                twice[h, r * half : (r + 1) * half, :] = jnp.concatenate([part, part], axis=1)

        def one_head(h, _):
            for r, bias in enumerate((bias_mine, bias_other)):
                span = slice(r * half, (r + 1) * half)
                scores = mm(twice[h, span, :], keys[h], NT) + bias[h].astype(F32)
                e = jnp.exp(scores - jnp.max(scores, axis=1, keepdims=True))
                total = 1.0 / jnp.sum(e, axis=1, keepdims=True)
                low = e.astype(BF)
                raised[h, span, :] = low
                inverse[h, span, :] = jnp.broadcast_to(total, (half, 128))
                both = mm(low, values[h])
                found[h, span, :] = (both[:, :hd] + both[:, hd:]) * total
            return 0

        lax.fori_loop(0, nh, one_head, 0)
        for r, target in enumerate((keep, send)):
            span = slice(r * half, (r + 1) * half)
            out = (jnp.concatenate([found[h, span, :] for h in range(nh)], axis=1) + b[1:2]).astype(BF)
            heads[span, :] = out
            target[...] = mm(out, wo[...]).astype(target.dtype)

    return launch(
        body,
        "cross_fwd",
        at,
        [near(a) for a in (mine, other, w, keys, bias_mine, bias_other, values, wo, b)],
        [
            shape(half, width),
            shape(half, width, dtype=BF),
            shape(nh, rows, slots, dtype=BF),
            shape(nh, rows, 128),
            shape(rows, local, dtype=BF),
            shape(rows, local, dtype=BF),
        ],
        scratch=[pltpu.VMEM((nh, rows, 2 * hd), BF), pltpu.VMEM((nh, rows, hd), F32)],
        mib=30,
        us=9,
    )


def feed(at, after, kept, close, distant, cot, weights, b1, terms, out_bias, fc2_bias, gain, shift):
    rows, width = distant.shape
    units = weights[0][0].shape[1]
    base = terms[0].shape[0] - 16

    def body(at, ins, outs, scratch):
        after, kept, close, distant, cot, out_bias, fc2_bias, gain, shift, b1, close_terms, far_terms = ins[:12]
        f1, f2, slope, sems = scratch
        copies = []
        for matrix, target in enumerate((f1, f2)):
            own, core, *halves = ins[12 + 6 * matrix : 18 + 6 * matrix]
            for s, source in ((0, own), (1, core)):
                copies.append(pltpu.make_async_copy(source, target.at[s], sems.at[len(copies)]))
            for i, source in enumerate(halves):
                size = source.shape[0]
                start = pl.multiple_of((at[4] ^ (i % 2)) * size, size)
                copies.append(
                    pltpu.make_async_copy(source, target.at[2 + i // 2, pl.ds(start, size), :], sems.at[len(copies)])
                )
        for copy in copies:
            copy.start()
        needed = ((0,), (1,), (2, 3), (4, 5))
        biases = (
            b1[...],
            from_terms(close_terms[...][0:3]),
            from_terms(far_terms[...][0:3]),
            from_terms(far_terms[...][3:6]),
        )
        trio, mixed, dsecond_low, sums = outs
        second = after[...] + (kept[...] + close[...].astype(F32) + distant[...].astype(F32)) + out_bias[...]
        normed_mid, inverse_mid = norm_stats(second)
        mid = normed_mid * gain[1:2] + shift[1:2]
        mid_low = mid.astype(BF)
        trio[0] = mid_low
        total = jnp.zeros((rows, width), F32)
        for s in range(4):
            for i in needed[s]:
                copies[i].wait()
            pre = mm(mid_low, f1[s]) + biases[s]
            hidden, slope[s] = gelu_pair(pre)
            for i in needed[s]:
                copies[6 + i].wait()
            total = total + mm(hidden, f2[s])
        last = mid + total + fc2_bias[...]
        normed_last, inverse_last = norm_stats(last)
        first_row = (2 * at[0] + at[1]) * rows
        live = (first_row + lax.broadcasted_iota(jnp.int32, (rows, 1), 0) < at[3]).astype(F32)
        mixed[...] = ((normed_last * gain[2:3] + shift[2:3]) * live).astype(BF)
        delta = cot[...].astype(F32) * live
        dlast = norm_backward(delta, normed_last, inverse_last, gain[2:3])
        dlast_low = dlast.astype(BF)
        trio[1] = dlast_low
        dmid = dlast
        for s in range(4):
            dpre = (mm(dlast_low, f2[s], NT) * slope[s]).astype(BF)
            dmid = dmid + mm(dpre, f1[s], NT)
        dsecond = norm_backward(dmid, normed_mid, inverse_mid, gain[1:2])
        dsecond_low[...] = dsecond.astype(BF)
        sums[...] = jnp.concatenate(
            [
                column_sum(delta * normed_last),
                column_sum(delta),
                column_sum(dlast),
                column_sum(dmid * normed_mid),
                column_sum(dmid),
                column_sum(dsecond),
                jnp.zeros((2, width), F32),
            ],
            axis=0,
        )

    quarter = lambda ref, at: ref.at[rows_at(at[1], rows), :]
    tail = lambda ref, at: ref.at[pl.ds(base, 16), :]
    return launch(
        body,
        "feed",
        at,
        [
            near(after, quarter),
            near(kept, quarter),
            near(close, quarter),
            near(distant),
            near(cot, lambda ref, at: ref.at[rows_at(2 * at[0] + at[1], rows), :]),
            near(out_bias),
            near(fc2_bias),
            near(gain),
            near(shift),
            near(b1),
            near(terms[0], tail),
            near(terms[1], tail),
        ]
        + [raw(a) for group in weights for a in group],
        [shape(2, rows, width, dtype=BF), shape(rows, width, dtype=BF), shape(rows, width, dtype=BF), shape(8, width)],
        scratch=[
            pltpu.VMEM((4, width, units), BF),
            pltpu.VMEM((4, units, width), BF),
            pltpu.VMEM((4, rows, units), F32),
            pltpu.SemaphoreType.DMA((12,)),
        ],
        mib=20,
        us=10,
    )


def assemble(at, z, blocks):
    rows = blocks[0].shape[0]
    for base, own, distant in ((0, blocks[0], blocks[2]), (2 * rows, blocks[1], blocks[3])):
        z[pl.ds(pl.multiple_of(base + at[1] * rows, rows), rows), :] = own[...]
        z[pl.ds(pl.multiple_of(base + (1 - at[1]) * rows, rows), rows), :] = distant[...]


def cross_backward(at, z_blocks, raised, inverse, query, keys, values, w, wo, nh):
    rows, width = z_blocks[0].shape
    rows = 4 * rows
    half = rows // 2
    local = w.shape[1]
    hd = local // nh
    slots = keys.shape[1]
    scale = hd**-0.5

    def body(at, ins, outs, scratch):
        blocks, (wo, inverse, values, raised, query, keys, w) = ins[:4], ins[4:]
        keep, send, dquery, dkv, sums = outs
        z, douts, right, found = scratch
        assemble(at, z, blocks)
        zero = jnp.zeros((half, hd), BF)
        head_sum = jnp.zeros((1, local), F32)
        for r in range(2):
            span = slice(r * half, (r + 1) * half)
            dhead = mm(z[span, :], wo[...], NT)
            head_sum = head_sum + column_sum(dhead)
            scaled = query[span, :] * jnp.asarray(scale, BF)
            for h in range(nh):
                part = slice(h * hd, (h + 1) * hd)
                dout = (dhead[:, part] * inverse[h, span, 0:1]).astype(BF)
                douts[h, span, :] = jnp.concatenate([dout, dout], axis=1)
                right[h, 0, span, :] = jnp.concatenate([scaled[:, part], zero], axis=1)
                right[h, 1, span, :] = jnp.concatenate([zero, dout], axis=1)

        def one_head(h, _):
            grad = None
            for r in range(2):
                span = slice(r * half, (r + 1) * half)
                dprob = mm(douts[h, span, :], values[h], NT)
                low = raised[h, span, :]
                e = low.astype(F32)
                weighed = e * dprob
                mean = jnp.sum(weighed, axis=1, keepdims=True) * inverse[h, span, 0:1]
                dscore = (weighed - e * mean).astype(BF)
                both = mm(dscore, keys[h])
                found[h, span, :] = both[:, :hd] + both[:, hd:]
                part = mm(dscore, right[h, 0, span, :], TN) + mm(low, right[h, 1, span, :], TN)
                grad = part if grad is None else grad + part
            dkv[h] = grad.astype(BF)
            return 0

        lax.fori_loop(0, nh, one_head, 0)
        query_sum = jnp.zeros((1, local), F32)
        for r, target in enumerate((keep, send)):
            span = slice(r * half, (r + 1) * half)
            dq = jnp.concatenate([found[h, span, :] for h in range(nh)], axis=1) * scale
            query_sum = query_sum + column_sum(dq)
            dq_low = dq.astype(BF)
            dquery[span, :] = dq_low
            target[...] = mm(dq_low, w[0]).astype(target.dtype)
        sums[...] = jnp.concatenate([query_sum, head_sum], axis=0)

    return launch(
        body,
        "cross_bwd",
        at,
        [near(a) for a in (*z_blocks, wo, inverse, values, raised, query, keys, w)],
        [
            shape(half, width),
            shape(half, width, dtype=BF),
            shape(rows, local, dtype=BF),
            shape(nh, slots, 2 * hd, dtype=BF),
            shape(2, local),
        ],
        scratch=[
            pltpu.VMEM((rows, width), BF),
            pltpu.VMEM((nh, rows, 2 * hd), BF),
            pltpu.VMEM((nh, 2, rows, 2 * hd), BF),
            pltpu.VMEM((nh, rows, hd), F32),
        ],
        mib=30,
        us=11,
    )


def store_gradient(at, dkv, w, nh):
    _, slots, twice = dkv.shape
    _, local, width = w.shape
    hd = twice // 2
    seg = slots // 4

    def body(at, ins, outs, _):
        dkv, w = ins
        keep, send = outs
        weights = []
        for h in range(nh):
            part = slice(h * hd, (h + 1) * hd)
            weights += [w[1][part], w[2][part]]
        weight = jnp.concatenate(weights, axis=0)
        for slot in (1, 3, 0, 2):
            rows = jnp.concatenate([dkv[h, slot * seg : (slot + 1) * seg, :] for h in range(nh)], axis=1)
            part = mm(rows, weight)
            if slot % 2 == 0:
                keep[slot // 2] = part
            else:
                send[slot // 2] = part.astype(BF)

    return launch(
        body,
        "store_grad",
        at,
        [near(dkv), near(w)],
        [shape(2, seg, width), shape(2, seg, width, dtype=BF)],
        us=2.6,
    )


def group_outs(width, columns, blocks, extra):
    if not blocks:
        return [shape(width, columns)]
    n, r = blocks
    tail = 3 * EXTRA if extra else 0
    return [shape(n * r + tail, columns, dtype=BF), shape(n, r, columns)]


def emit_group(at, grad, outs, blocks, first, columns, late=False):
    if not blocks:
        outs[0][:, first : first + columns] = grad[...]
        return
    n, r = blocks
    span = slice(first, first + columns)
    for b in range(n):
        mine = 4 * (b % 2) + 2 * at[5] + b // 2 if late else 2 * b + at[4]
        theirs = 4 * (b % 2) + 2 * (1 - at[5]) + b // 2 if late else 2 * b + 1 - at[4]
        outs[0][b * r : (b + 1) * r, span] = grad[pl.ds(pl.multiple_of(theirs * r, 8), r), :].astype(BF)
        outs[1][b, :, span] = grad[pl.ds(pl.multiple_of(mine * r, 8), r), :]


def turned_product(out, left, right, step=256):
    if left.shape[1] % step:
        out[...] = mm(left[...], right[...], TN)
        return

    def some(i, _):
        span = pl.ds(pl.multiple_of(i * step, step), step)
        out[span, :] = mm(left[:, span], right[...], TN)
        return 0

    lax.fori_loop(0, left.shape[1] // step, some, 0)


def feed_grads(at, trios, fc1, fc2, b1, blocks):
    _, rows, width = trios[0].shape
    units = fc1.shape[1]

    def body(at, ins, outs, scratch):
        trios, (f1, f2, b1) = ins[:4], ins[4:]
        mid, dlast, hidden, dpre, grad = scratch
        for s, block in enumerate(trios):
            mid[s * rows : (s + 1) * rows, :] = block[0]
            dlast[s * rows : (s + 1) * rows, :] = block[1]

        f1.ready()
        f2.ready()

        def some_rows(i, total):
            span = rows_at(i, 2 * rows)
            hidden[span, :], slope = gelu_pair(mm(mid[span, :], f1[...]) + b1[...])
            grad_pre = mm(dlast[span, :], f2[...], NT) * slope
            dpre[span, :] = grad_pre.astype(BF)
            return total + column_sum(grad_pre)

        outs[-1][...] = lax.fori_loop(0, 2, some_rows, jnp.zeros((1, units), F32))
        turned_product(grad, mid, dpre)
        emit_group(at, grad, outs, blocks, 0, units, True)
        turned_product(grad, dlast, hidden)
        emit_group(at, grad, outs, blocks, units, units, True)

    return launch(
        body,
        "feed_grads",
        at,
        [near(a) for a in trios] + [far(fc1), far(fc2), near(b1)],
        group_outs(width, 2 * units, blocks, False) + [shape(1, units)],
        scratch=[pltpu.VMEM((4 * rows, width), BF)] * 2
        + [pltpu.VMEM((4 * rows, units), BF)] * 2
        + [pltpu.VMEM((width, units), F32)],
        mib=20,
        us=6,
    )


def cross_grads(at, z_blocks, mine, other, dquery, heads, shards, dkv, first_mine, first_other, flat, small, nh, blocks):
    half, width = mine.shape
    local = dquery.shape[1]
    hd = local // nh
    seg = shards[0].shape[0]
    feed_sums, first_sums, fc1_sum, head_sums = small

    def body(at, ins, outs, scratch):
        z_blocks, shards = ins[0:4], ins[4:8]
        mine, other, dquery, heads, dkv, first_mine, first_other, flat, feed_sums, first_sums, fc1_sum, head_sums = ins[8:]
        z, grad = scratch
        extra = outs[-1]
        assemble(at, z, z_blocks)
        grad[...] = mm(mine[...], dquery[:half], TN) + mm(other[...], dquery[half:], TN)
        emit_group(at, grad, outs, blocks, 0, local)
        grad[...] = mm(z[...], heads[...], TN)
        emit_group(at, grad, outs, blocks, 3 * local, local)
        z[rows_at(at[0], half), :] = first_mine[...]
        z[rows_at(1 - at[0], half), :] = first_other[...]
        grad[...] = mm(z[...], flat[...], TN)
        emit_group(at, grad, outs, blocks, 4 * local, local)
        both = None
        for slot, block in enumerate(shards):
            rows = jnp.concatenate([dkv[h, slot * seg : (slot + 1) * seg, :] for h in range(nh)], axis=1)
            part = mm(block[...], rows, TN)
            both = part if both is None else both + part
        for i in range(2):
            grad[...] = jnp.concatenate([both[:, (2 * h + i) * hd : (2 * h + i + 1) * hd] for h in range(nh)], axis=1)
            emit_group(at, grad, outs, blocks, (1 + i) * local, local)
        line = jnp.concatenate([head_sums[0:1], head_sums[1:2], jnp.zeros((1, width - 2 * local), F32)], axis=1)
        small = jnp.concatenate(
            [feed_sums[0:6], first_sums[0:3], fc1_sum[...], line, jnp.zeros((EXTRA - 11, width), F32)], axis=0
        )
        extra[...] = small
        if blocks:
            outs[0][blocks[0] * blocks[1] :, 0:width] = three_terms(small)
            outs[0][blocks[0] * blocks[1] :, width:] = jnp.zeros((3 * EXTRA, 5 * local - width), BF)

    return launch(
        body,
        "cross_grads",
        at,
        [
            near(a)
            for a in (
                *z_blocks,
                *shards,
                mine,
                other,
                dquery,
                heads,
                dkv,
                first_mine,
                first_other,
                flat,
                feed_sums,
                first_sums,
                fc1_sum,
                head_sums,
            )
        ],
        group_outs(width, 5 * local, blocks, True) + [shape(EXTRA, width)],
        scratch=[pltpu.VMEM((2 * half, width), BF), pltpu.VMEM((width, local), F32)],
        us=4,
    )


def first_back(at, z_own, z_distant, mine, other, total, gain):
    half, width = mine.shape
    rows = half // 2

    def body(at, ins, outs, scratch):
        z_own, z_distant, mine, other, total, gain = ins
        dfirst, low, sums = outs
        (dafter,) = scratch
        dafter[rows_at(at[1], rows), :] = z_own[...].astype(F32)
        dafter[rows_at(1 - at[1], rows), :] = z_distant[...].astype(F32)
        value = dafter[...] + (mine[...].astype(F32) + other[...].astype(F32))
        normed, inverse = norm_stats(total[...])
        result = norm_backward(value, normed, inverse, gain[0:1])
        dfirst[...] = result
        low[...] = result.astype(BF)
        place = lax.broadcasted_iota(jnp.int32, (half, 1), 0)
        counted = ((place >= at[1] * rows) & (place < (at[1] + 1) * rows)).astype(F32)
        sums[...] = jnp.concatenate(
            [
                column_sum(value * normed * counted),
                column_sum(value * counted),
                column_sum(result * counted),
                jnp.zeros((5, width), F32),
            ],
            axis=0,
        )

    return launch(
        body,
        "first_back",
        at,
        [near(a) for a in (z_own, z_distant, mine, other, total, gain)],
        [shape(half, width), shape(half, width, dtype=BF), shape(8, width)],
        scratch=[pltpu.VMEM((half, width), F32)],
        us=2.8,
    )


def self_backward(at, mine, other, tokens, w, wo, qkv, prob, mixed, nh, blocks):
    half, width = mine.shape
    rows = 2 * half
    local = wo.shape[0]
    hd = local // nh
    scale = hd**-0.5

    def body(at, ins, outs, scratch):
        mine, other, wo, qkv, prob, tok, w, mixed = ins
        send, keep = outs[0:2]
        group, extra = outs[2:-1], outs[-1]
        z, dqkv, grad = scratch
        own, distant = rows_at(at[0], half), rows_at(1 - at[0], half)
        z[own, :] = mine[...]
        z[distant, :] = other[...]
        dself = mm(z[...], wo[...], NT).astype(BF)
        v, k, q = qkv[2], qkv[1], qkv[0]
        dq, dk, dv = [], [], []
        for h in range(nh):
            part = slice(h * hd, (h + 1) * hd)
            weights_low = prob[h]
            weights = weights_low.astype(F32)
            weighed = weights * mm(dself[:, part], v[:, part], NT)
            dscore = (weighed - weights * jnp.sum(weighed, axis=1, keepdims=True)).astype(BF)
            dq.append(mm(dscore, k[:, part]))
            dk.append(mm(dscore, q[:, part], TN))
            dv.append(mm(weights_low, dself[:, part], TN))
        dquery = jnp.concatenate(dq, axis=1) * scale
        dvalue = jnp.concatenate(dv, axis=1)
        dqkv[0] = dquery.astype(BF)
        dqkv[1] = (jnp.concatenate(dk, axis=1) * scale).astype(BF)
        dqkv[2] = dvalue.astype(BF)
        x = tok[...]
        for i in range(3):
            grad[...] = mm(x, dqkv[i], TN)
            emit_group(at, grad, group, blocks, i * local, local)
        line = jnp.concatenate([column_sum(dquery), column_sum(dvalue), jnp.zeros((1, local), F32)], axis=1)
        small = jnp.concatenate([line, jnp.zeros((EXTRA - 1, 3 * local), F32)], axis=0)
        extra[...] = small
        if blocks:
            group[0][blocks[0] * blocks[1] :, :] = three_terms(small)
        send[half:, :] = mixed[...]
        for place, out in ((distant, send), (own, keep)):
            total = mm(dqkv[0, place, :], w[0]) + mm(dqkv[1, place, :], w[1]) + mm(dqkv[2, place, :], w[2])
            out[0:half, :] = total.astype(out.dtype)

    return launch(
        body,
        "self_bwd",
        at,
        [near(a) for a in (mine, other, wo, qkv, prob, tokens, w, mixed)],
        [shape(half + half // 2, width, dtype=BF), shape(half, width)]
        + group_outs(width, 3 * local, blocks, True)
        + [shape(EXTRA, 3 * local)],
        scratch=[
            pltpu.VMEM((rows, width), BF),
            pltpu.VMEM((3, rows, local), BF),
            pltpu.VMEM((width, local), F32),
        ],
        mib=20,
        us=6,
    )


def add_stage(at, keep, got, small, bit):
    n, rows, columns = keep.shape
    tail = 0 if small is None else 3 * EXTRA
    reach = small.shape[1] if tail else 0

    def body(at, ins, outs, _):
        keep, got = ins[:2]
        mine = at[bit]
        send, stay = outs[:2]
        for b in range(n // 2):
            for chosen, out in ((1 - mine, send), (mine, stay)):
                block = 2 * b + chosen
                value = keep[block] + got[pl.ds(pl.multiple_of(block * rows, 8), rows), :].astype(F32)
                if out is send:
                    send[b * rows : (b + 1) * rows, :] = value.astype(BF)
                else:
                    stay[b] = value
        if tail:
            total = ins[2][...] + from_terms(got[n * rows :, 0:reach])
            outs[2][...] = total
            send[n // 2 * rows :, 0:reach] = three_terms(total)
            if reach < columns:
                send[n // 2 * rows :, reach:] = jnp.zeros((tail, columns - reach), BF)

    ins = [near(keep), near(got)] + ([near(small)] if tail else [])
    outs = [shape(n // 2 * rows + tail, columns, dtype=BF), shape(n // 2, rows, columns)]
    if tail:
        outs.append(shape(EXTRA, reach))
    return launch(body, "add_stage", at, ins, outs, us=1)


def last_stage(at, keep, got, small, parts):
    _, rows, columns = keep.shape
    each = columns // sum(count for count, _ in parts)
    reach = 0 if small is None else small.shape[1]

    def body(at, ins, outs, _):
        total = ins[0][0] + ins[1][0:rows].astype(F32)
        first = 0
        for out, (count, turned) in zip(outs, parts):
            if count == 1:
                value = total[:, first * each : (first + 1) * each]
                out[...] = value.T if turned else value
            else:
                for i in range(count):
                    out[i] = total[:, (first + i) * each : (first + i + 1) * each]
            first += count
        if reach:
            outs[-1][...] = ins[2][...] + from_terms(ins[1][rows:, 0:reach])

    outs = []
    for count, turned in parts:
        dims = (rows, each) if count == 1 else (count, rows, each)
        outs.append(shape(*(dims[::-1] if turned else dims)))
    ins = [near(keep), near(got)]
    if reach:
        ins.append(near(small))
        outs.append(shape(EXTRA, reach))
    return launch(body, "last_stage", at, ins, outs, us=1)


def join_halves(at, mine, other):
    half, width = mine.shape

    def body(at, ins, outs, _):
        outs[0][rows_at(at[0], half), :] = ins[0][...]
        outs[0][rows_at(1 - at[0], half), :] = ins[1][...]

    out = shape(2 * half, width, dtype=mine.dtype)
    return launch(body, "join_halves", at, [near(mine), near(other)], [out])[0]


def join_quarters(at, own, close, distant):
    rows, width = own.shape

    def body(at, ins, outs, _):
        for flips, block in enumerate(ins):
            place = 2 * (at[0] ^ (flips & 1)) + (at[1] ^ (flips >> 1))
            outs[0][rows_at(place, rows), :] = block[...]

    part = lambda i: lambda ref, at: ref.at[pl.ds(i * rows, rows), :]
    ins = [near(own), near(close, part(2)), near(distant, part(2)), near(distant, part(3))]
    return launch(body, "join_quarters", at, ins, [shape(4 * rows, width, dtype=BF)])[0]


def flip(bit, size):
    return [(i, i ^ bit) for i in range(size)]


def butterfly(value, axis, size):
    bit = 1
    while bit < size:
        value = value + lax.ppermute(value, axis, flip(bit, size))
        bit *= 2
    return value


def on_device(
    tokens,
    store,
    summary_length,
    top_index,
    cotangent,
    self_qkv_weight,
    self_qv_bias,
    self_out_weight,
    self_out_bias,
    qkv_weight,
    qv_bias,
    out_weight,
    out_bias,
    fc1_weight,
    fc1_bias,
    fc2_weight,
    fc2_bias,
    norm_gain,
    norm_shift,
):
    rows, width = tokens.shape
    half, quarter = rows // 2, rows // 4
    nh = top_index.shape[1]
    local = qkv_weight.shape[2]
    units = fc1_weight.shape[1]
    seg = store.shape[1]
    wide = lax.axis_size("wide")
    place = lax.axis_index("narrow")
    doc = lax.axis_index("wide")
    core, across = place % 2, place // 2
    at = jnp.stack([core, across, place, summary_length[0], doc % 2, doc // 2 % 2, doc // 4]).astype(jnp.int32)
    blocks = (wide // 2, width // wide) if wide == 8 else None
    row = lambda v: v.reshape(1, -1)
    self_w = jnp.swapaxes(self_qkv_weight, 1, 2)
    cross_w = jnp.swapaxes(qkv_weight, 1, 2)

    def to_core(v):
        return lax.ppermute(v, "narrow", CORE)

    def to_across(v):
        return lax.ppermute(v, "narrow", ACROSS)

    def spread(v):
        distant = to_across(v)
        return [v, to_core(v), distant, to_core(distant)]

    def chip_sum(keep, send):
        return (keep + to_core(send).astype(F32)).astype(BF)

    store_x = to_across(store[0])
    qkv, prob, flat, send, keep = self_forward(
        at, tokens, self_w, self_qv_bias, self_out_weight, row(fc1_bias), nh
    )
    close = to_core(send)
    mine = jnp.concatenate(
        [
            (keep + close[:half].astype(F32)).astype(BF),
            send[half : half + 3],
            close[half : half + 3],
            jnp.zeros((16 - 6, width), BF),
        ],
        axis=0,
    )
    terms_close = close
    other = to_across(mine)
    doc_bit = doc % 2
    share = lambda v: lax.dynamic_slice_in_dim(v, doc_bit * (v.shape[0] // 2), v.shape[0] // 2, 0)
    over = lambda v, bit: lax.ppermute(v, "wide", flip(bit, wide))
    f1_half, f2_half = tie((share(fc1_weight), share(fc2_weight)), mine)
    f1_x, f2_x = to_across(f1_half), to_across(f2_half)
    index = index_rows(top_index)
    bias_mine = make_mask(tie(at, mine, f1_half, f2_half), index, top_index.shape, seg, 128, 0)
    store_x = tie(store_x, bias_mine)
    shards = [store[0], to_core(tie(store[0], bias_mine)), store_x, to_core(store_x)]
    bias_other = make_mask(tie(at, bias_mine), index, top_index.shape, seg, 128, 1)
    other, f1_x = tie((other, f1_x), bias_other)
    f1_y = over(f1_x, 1)
    first_total, after, after_low = first_norm(at, mine, other, tokens, row(self_out_bias), norm_gain, norm_shift)
    after_other = to_core(after_low)

    keys, values = keys_values(tie(at, after_low), shards, cross_w, nh)
    f1_core = to_core(tie(fc1_weight, keys))
    keep, send, raised, inverse, query, heads = cross_forward(
        tie(at, keys), after_low, after_other, bias_mine, bias_other, keys, values, cross_w, qv_bias, out_weight, nh
    )
    close = to_core(send)
    theirs = (1 - across) * quarter
    distant = to_across(
        (
            lax.dynamic_slice_in_dim(keep, theirs, quarter, 0)
            + lax.dynamic_slice_in_dim(close, theirs, quarter, 0).astype(F32)
        ).astype(BF)
    )
    f2_x = tie(f2_x, keep)
    f2_y = over(f2_x, 1)
    f2_core = to_core(tie(fc2_weight, keep))
    f1_y = tie(f1_y, close)
    f2_y = tie(f2_y, distant)
    weights = (
        (fc1_weight, f1_core, f1_x, f1_y, to_core(f1_x), to_core(f1_y)),
        (fc2_weight, f2_core, f2_x, f2_y, to_core(f2_x), to_core(f2_y)),
    )

    pair, mixed_own, z, feed_sums = feed(
        at,
        after,
        keep,
        close,
        distant,
        cotangent,
        weights,
        row(fc1_bias),
        (terms_close, other),
        row(out_bias),
        row(fc2_bias),
        norm_gain,
        norm_shift,
    )
    z_all = spread(z)
    trios = spread(tie(pair, z_all[2]))

    keep, send, dquery, dkv, cross_sums = cross_backward(
        at, z_all, raised, inverse, query, keys, values, cross_w, out_weight, nh
    )
    mine = chip_sum(keep, send)
    other = to_across(mine)
    *feed_out, fc1_sum = feed_grads(tie(at, mine), trios, fc1_weight, fc2_weight, row(fc1_bias), blocks)
    other = tie(other, fc1_sum)
    dfirst, dfirst_low, first_sums = first_back(at, z_all[0], z_all[2], mine, other, first_total, norm_gain)
    dfirst_other = to_core(dfirst_low)
    store_keep, store_send = store_gradient(tie(at, dfirst_low), dkv, cross_w, nh)
    store_close = to_core(store_send)
    *cross_out, cross_small = cross_grads(
        tie(at, store_send),
        z_all,
        after_low,
        after_other,
        dquery,
        heads,
        shards,
        dkv,
        dfirst_low,
        dfirst_other,
        flat,
        (feed_sums, first_sums, fc1_sum, cross_sums),
        nh,
        blocks,
    )
    store_distant = to_across((store_keep[1] + tie(store_close, cross_small)[1].astype(F32)).astype(BF))

    send, keep, *self_out, self_small = self_backward(
        tie(at, cross_small), dfirst_low, dfirst_other, tokens, self_w, self_out_weight, qkv, prob, mixed_own, nh, blocks
    )
    close = to_core(send)
    mine = jnp.concatenate([(keep + close[:half].astype(F32)).astype(BF), send[half:], close[half:]], axis=0)
    other = to_across(mine)
    tokens_half = dfirst + (mine[:half].astype(F32) + other[:half].astype(F32))
    tokens_grad = join_halves(at, tokens_half, to_core(tokens_half))
    mixed = join_quarters(at, mixed_own, close, other)
    store_grad = (store_keep[0] + store_close[0].astype(F32) + store_distant.astype(F32))[None]

    if blocks:
        feed_send, feed_keep = add_stage(tie(at, self_small), feed_out[1], over(feed_out[0], 2), None, 6)
        cross_send, cross_keep, cross_small = add_stage(
            tie(at, feed_send), cross_out[1], over(cross_out[0], 1), cross_small, 5
        )
        self_send, self_keep, self_small = add_stage(
            tie(at, cross_send), self_out[1], over(self_out[0], 1), self_small, 5
        )
        feed_send, feed_keep = add_stage(tie(at, self_send), feed_keep, over(feed_send, 4), None, 4)
        cross_send, cross_keep, cross_small = add_stage(
            tie(at, feed_send), cross_keep, over(cross_send, 2), cross_small, 6
        )
        self_send, self_keep, self_small = add_stage(
            tie(at, cross_send), self_keep, over(self_send, 2), self_small, 6
        )
        fc1_grad, fc2_grad = last_stage(tie(at, self_send), feed_keep, over(feed_send, 1), None, [(1, False), (1, False)])
        fc2_grad = fc2_grad.T
        qkv_grad, out_grad, self_out_grad, cross_small = last_stage(
            tie(at, fc1_grad), cross_keep, over(cross_send, 4), cross_small, [(3, False), (1, True), (1, True)]
        )
        self_qkv_grad, self_small = last_stage(
            tie(at, cross_small), self_keep, over(self_send, 4), self_small, [(3, False)]
        )
    else:
        scatter = functools.partial(lax.psum_scatter, axis_name="wide", tiled=True)
        parts = lambda g: jnp.stack([g[:, i * local : (i + 1) * local] for i in range(3)])
        fc1_grad = scatter(feed_out[0][:, :units], scatter_dimension=0)
        fc2_grad = scatter(feed_out[0][:, units:].T, scatter_dimension=1)
        qkv_grad = scatter(parts(cross_out[0]), scatter_dimension=1)
        out_grad = scatter(cross_out[0][:, 3 * local : 4 * local].T, scatter_dimension=1)
        self_qkv_grad = scatter(parts(self_out[0]), scatter_dimension=1)
        self_out_grad = scatter(cross_out[0][:, 4 * local :].T, scatter_dimension=1)
        cross_small = butterfly(cross_small, "wide", wide)
        self_small = butterfly(self_small, "wide", wide)
    summed = butterfly(cross_small, "narrow", 4)
    gain_last, shift_last, fc2_b, gain_mid, shift_mid, out_b, gain_first, shift_first, self_out_b = (
        summed[i] for i in range(9)
    )
    return (
        mixed,
        tokens_grad,
        store_grad,
        self_qkv_grad,
        self_small[0, : 2 * local].reshape(2, local),
        self_out_grad,
        self_out_b,
        qkv_grad,
        cross_small[10, : 2 * local].reshape(2, local),
        out_grad,
        out_b,
        fc1_grad,
        cross_small[9],
        fc2_grad,
        fc2_b,
        jnp.stack([gain_first, gain_mid, gain_last]),
        jnp.stack([shift_first, shift_mid, shift_last]),
    )


def solution(mesh):
    placed = (
        P("wide", None),
        P("wide", "narrow", None),
        P("wide"),
        P("wide", "narrow", None, None),
        P("wide", None),
        P(None, None, "narrow"),
        P(None, "narrow"),
        P("narrow", None),
        P(),
        P(None, None, "narrow"),
        P(None, "narrow"),
        P("narrow", None),
        P(),
        P(None, "narrow"),
        P("narrow"),
        P("narrow", None),
        P(),
        P(),
        P(),
    )
    return jax.shard_map(
        on_device,
        mesh=mesh,
        in_specs=placed,
        out_specs=(
            P("wide", None),
            P("wide", None),
            P("wide", "narrow", None),
            P(None, "wide", "narrow"),
            P(None, "narrow"),
            P("narrow", "wide"),
            P(),
            P(None, "wide", "narrow"),
            P(None, "narrow"),
            P("narrow", "wide"),
            P(),
            P("wide", "narrow"),
            P("narrow"),
            P("narrow", "wide"),
            P(),
            P(),
            P(),
        ),
        check_vma=False,
    )
```

```python
import functools

import jax
import jax.numpy as jnp
from jax import lax
from jax.experimental import pallas as pl
from jax.experimental.pallas import tpu as pltpu
from jax.sharding import PartitionSpec as P

F32 = jnp.float32
BF = jnp.bfloat16
NN = (((1,), (0,)), ((), ()))
NT = (((1,), (1,)), ((), ()))
TN = (((0,), (0,)), ((), ()))
EPS = 1e-05
PACE = 1.1e7
SELF_MIB = 60
EXTRA = 16

CORE = [(i, i ^ 1) for i in range(4)]
ACROSS = [(i, i ^ 2) for i in range(4)]


def mm(left, right, dims=NN):
    return lax.dot_general(left, right, dims, preferred_element_type=F32)


def shape(*dims, dtype=F32):
    return jax.ShapeDtypeStruct(dims, dtype)


def tie(value, *earlier):
    return lax.optimization_barrier((value, *earlier))[0]


class Operand:
    def __init__(self, source, buffer, sems, first, parts):
        self.buffer = buffer
        self.parts = parts
        if parts:
            self.copies = [
                pltpu.make_async_copy(source.at[i], buffer.at[i], sems.at[first + i]) for i in range(buffer.shape[0])
            ]
        else:
            self.copies = [pltpu.make_async_copy(source, buffer, sems.at[first])]
        self.waited = [False] * len(self.copies)
        for copy in self.copies:
            copy.start()

    def ready(self, part=None):
        for i, copy in enumerate(self.copies):
            if not self.waited[i] and (part is None or i == part):
                copy.wait()
                self.waited[i] = True

    @property
    def shape(self):
        return self.buffer.shape

    def __getitem__(self, at):
        self.ready(at if self.parts and isinstance(at, int) else None)
        return self.buffer[at]


class Result:
    def __init__(self, target, buffer, sems, first, parts):
        self.buffer = buffer
        if parts:
            self.copies = [
                pltpu.make_async_copy(buffer.at[i], target.at[i], sems.at[first + i]) for i in range(buffer.shape[0])
            ]
        else:
            self.copies = [pltpu.make_async_copy(buffer, target, sems.at[first])]
        self.started = [False] * len(self.copies)

    @property
    def shape(self):
        return self.buffer.shape

    @property
    def dtype(self):
        return self.buffer.dtype

    def __setitem__(self, at, value):
        self.buffer[at] = value

    def flush(self, part=0):
        self.copies[part].start()
        self.started[part] = True

    def finish(self):
        for i in range(len(self.copies)):
            if not self.started[i]:
                self.flush(i)
        for copy in self.copies:
            copy.wait()


def far(array, take=None, dims=None, parts=False):
    return ("far", array, take, tuple(dims or array.shape), parts)


def near(array, take=None):
    return ("near", array, take, None, False)


def raw(array):
    return ("raw", array, None, None, False)


def launch(body, name, at, ins, outs, scratch=(), mib=16, us=2.0):
    in_specs = [pl.BlockSpec(memory_space=pltpu.SMEM)]
    buffers, n_in, n_out = [], 0, 0
    for kind, array, _, dims, parts in ins:
        in_specs.append(pl.BlockSpec(memory_space=pltpu.VMEM if kind == "near" else pltpu.HBM))
        if kind == "far":
            buffers.append(pltpu.VMEM(dims, array.dtype))
            n_in += dims[0] if parts else 1
    out_specs, structs = [], []
    for out in outs:
        if isinstance(out, tuple):
            struct, parts = out
            out_specs.append(pl.BlockSpec(memory_space=pltpu.HBM))
            buffers.append(pltpu.VMEM(struct.shape, struct.dtype))
            n_out += struct.shape[0] if parts else 1
        else:
            struct = out
            out_specs.append(pl.BlockSpec(memory_space=pltpu.VMEM))
        structs.append(struct)
    n_buffers = len(buffers)
    sems = [pltpu.SemaphoreType.DMA((max(n, 1),)) for n in (n_in, n_out)]

    def kernel(at_ref, *refs):
        in_refs, out_refs = refs[: len(ins)], refs[len(ins) : len(ins) + len(outs)]
        rest = refs[len(ins) + len(outs) :]
        bufs, user, (in_sems, out_sems) = list(rest[:n_buffers]), rest[n_buffers:-2], rest[-2:]
        place, given = 0, []
        for ref, (kind, _, take, dims, parts) in zip(in_refs, ins):
            source = take(ref, at_ref) if take else ref
            if kind == "far":
                given.append(Operand(source, bufs.pop(0), in_sems, place, parts))
                place += dims[0] if parts else 1
            else:
                given.append(source)
        place, results = 0, []
        for ref, out in zip(out_refs, outs):
            if isinstance(out, tuple):
                results.append(Result(ref, bufs.pop(0), out_sems, place, out[1]))
                place += out[0].shape[0] if out[1] else 1
            else:
                results.append(ref)
        body(at_ref, given, results, user)
        for operand in given:
            if isinstance(operand, Operand):
                operand.ready()
        for result in results:
            if isinstance(result, Result):
                result.finish()

    return pl.pallas_call(
        kernel,
        in_specs=in_specs,
        out_specs=out_specs,
        out_shape=structs,
        scratch_shapes=buffers + list(scratch) + sems,
        compiler_params=pltpu.CompilerParams(vmem_limit_bytes=mib << 20),
        cost_estimate=pl.CostEstimate(flops=int(us * PACE), bytes_accessed=1000, transcendentals=0),
        name=name,
    )(at, *[entry[1] for entry in ins])


def norm_stats(value):
    centre = value - jnp.mean(value, axis=-1, keepdims=True)
    spread = jnp.mean(centre * centre, axis=-1, keepdims=True)
    inverse = lax.rsqrt(spread + EPS)
    return centre * inverse, inverse


def norm_backward(grad, normed, inverse, gain):
    scaled = grad * gain
    centred = scaled - jnp.mean(scaled, axis=-1, keepdims=True)
    return inverse * (centred - normed * jnp.mean(scaled * normed, axis=-1, keepdims=True))


def column_sum(value):
    return jnp.sum(value, axis=0, keepdims=True)


def erf(value):
    x = jnp.clip(value, -4.0, 4.0)
    y = x * x
    top = jnp.full_like(y, -2.72614225801306e-10)
    for factor in (
        2.77068142495902e-08,
        -2.10102402082508e-06,
        -5.69250639462346e-05,
        -7.34990630326855e-04,
        -2.95459980854025e-03,
        -1.60960333262415e-02,
    ):
        top = top * y + factor
    low = jnp.full_like(y, -1.45660718464996e-05)
    for factor in (
        -2.13374055278905e-04,
        -1.68282697438203e-03,
        -7.37332916720468e-03,
        -1.42647390514189e-02,
    ):
        low = low * y + factor
    return x * top / low


def gelu_pair(pre):
    phi = 0.5 * (1.0 + erf(pre * 0.7071067811865476))
    return (pre * phi).astype(BF), phi + pre * (jnp.exp(pre * pre * -0.5) * 0.3989422804014327)


def three_terms(value):
    high = value.astype(BF)
    rest = value - high.astype(F32)
    middle = rest.astype(BF)
    return jnp.concatenate([high, middle, (rest - middle.astype(F32)).astype(BF)], axis=0)


def from_terms(stacked):
    rows = stacked.shape[0] // 3
    terms = stacked.astype(F32)
    return terms[:rows] + terms[rows : 2 * rows] + terms[2 * rows :]


def rows_at(place, rows):
    return pl.ds(pl.multiple_of(place * rows, rows), rows)


def self_forward(at, tokens, w, b, wo, b1, nh):
    rows, width = tokens.shape
    local = w.shape[1]
    half = rows // 2
    hd = local // nh
    scale = hd**-0.5

    def body(at, ins, outs, _):
        tok, w, wo, b, b1 = ins
        qkv, prob, flat, send, keep = outs
        x = tok[...]
        q = (mm(x, w[0], NT) + b[0:1]).astype(BF)
        k = mm(x, w[1], NT).astype(BF)
        v = (mm(x, w[2], NT) + b[1:2]).astype(BF)
        for i, value in enumerate((q, k, v)):
            qkv[i] = value
            qkv.flush(i)
        row_ids = lax.broadcasted_iota(jnp.int32, (rows, rows), 0)
        key_ids = lax.broadcasted_iota(jnp.int32, (rows, rows), 1)
        allowed = (key_ids <= row_ids) & (key_ids < at[3])
        found = []
        for h in range(nh):
            part = slice(h * hd, (h + 1) * hd)
            scores = mm(q[:, part], k[:, part], NT) * scale
            scores = jnp.where(allowed, scores, -1e30)
            shifted = jnp.exp(scores - jnp.max(scores, axis=1, keepdims=True))
            weights = (shifted * (1.0 / jnp.sum(shifted, axis=1, keepdims=True))).astype(BF)
            prob[h] = weights
            prob.flush(h)
            found.append(mm(weights, v[:, part]).astype(BF))
        flat[...] = jnp.concatenate(found, axis=1)
        flat.flush()
        send[0:half, :] = mm(flat.buffer[rows_at(1 - at[0], half), :], wo[...]).astype(BF)
        send[half:, :] = jnp.concatenate([three_terms(b1[...]), jnp.zeros((16 - 3, width), BF)], axis=0)
        send.flush()
        keep[...] = mm(flat.buffer[rows_at(at[0], half), :], wo[...])

    return launch(
        body,
        "self_fwd",
        at,
        [far(tokens), far(w, parts=True), far(wo), far(b), far(b1)],
        [
            (shape(3, rows, local, dtype=BF), True),
            (shape(nh, rows, rows, dtype=BF), True),
            (shape(rows, local, dtype=BF), False),
            (shape(half + 16, width, dtype=BF), False),
            (shape(half, width), False),
        ],
        mib=SELF_MIB,
        us=4,
    )


def first_norm(at, mine, other, tokens, bias, gain, shift):
    half, width = mine.shape[0] - 16, mine.shape[1]

    def body(at, ins, outs, _):
        mine, other, tok, bias, gain, shift = ins
        total, after, low = outs
        value = tok[...].astype(F32) + (mine[0:half].astype(F32) + other[0:half].astype(F32)) + bias[...]
        total[...] = value
        normed, _ = norm_stats(value)
        result = normed * gain[0:1] + shift[0:1]
        after[...] = result
        low[...] = result.astype(BF)

    return launch(
        body,
        "first_norm",
        at,
        [
            near(mine),
            near(other),
            near(tokens, lambda ref, at: ref.at[rows_at(at[0], half), :]),
            near(bias),
            near(gain),
            near(shift),
        ],
        [shape(half, width), shape(half, width), shape(half, width, dtype=BF)],
        us=1.7,
    )


def index_rows(top_index):
    rows, nh, ns, keep = top_index.shape
    flat = top_index.reshape(rows, nh, ns, keep // 128, 128).transpose(0, 1, 3, 2, 4)
    return flat.reshape(rows * nh * ns * (keep // 128), 128)


def make_mask(at, flat, dims, seg, tile, turn):
    rows, nh, ns, keep = dims
    halves = keep // 128
    per_row = nh * ns * halves
    tiles = rows // 2 // tile
    columns = ns * seg
    blocks = columns // 128
    group = 32

    def body(at, ins, outs, _):
        (index,) = ins
        (bias,) = outs
        lane = lax.broadcasted_iota(jnp.int32, (group, 128), 1).astype(F32)
        lane_low = lane.astype(BF)
        empty = jnp.full((group, 128), -1.0, BF)
        own = at[2]
        steps = []
        step = 1
        while step <= seg - keep:
            steps.insert(0, step)
            step *= 2
        turns = steps + [(seg * s) % 128 for s in range(ns)]
        below = {s: lane_low < jnp.asarray(s, BF) for s in turns if 0 < s < 128}

        for t in range(tiles):
            index.ready(t)
            source = index.buffer.at[t]

            def one_group(g, _):
                for h in range(nh):
                    v = [empty] * blocks
                    for slot in range(ns):
                        first, turn = divmod(seg * slot, 128)
                        for c in range(halves):
                            start = g * (group * per_row) + h * ns * halves + c * ns + (own ^ slot)
                            found = jnp.concatenate(
                                [source[pl.ds(start + q * 8 * per_row, 8, stride=per_row), :] for q in range(group // 8)],
                                axis=0,
                            )
                            ahead = (found.astype(F32) - (lane + float(128 * c))).astype(BF)
                            at_block = first + c
                            if turn == 0:
                                v[at_block] = ahead
                            else:
                                turned = pltpu.roll(ahead, turn, axis=1)
                                v[at_block] = jnp.where(below[turn], v[at_block], turned)
                                v[at_block + 1] = jnp.where(below[turn], turned, v[at_block + 1])
                    for s in steps:
                        gap = jnp.asarray(s, BF)
                        moved = [x - gap for x in v]
                        stay = [jnp.where(x >= gap, empty, x) for x in v]
                        if s % 128 == 0:
                            hop = s // 128
                            v = stay[:hop] + [jnp.maximum(stay[i], moved[i - hop]) for i in range(hop, blocks)]
                        else:
                            turned = [pltpu.roll(x, s, axis=1) for x in moved]
                            v = [
                                jnp.maximum(stay[i], jnp.where(below[s], turned[i - 1], turned[i])) for i in range(blocks)
                            ]
                    for i in range(blocks):
                        bias[h, pl.ds(pl.multiple_of(t * tile + g * group, group), group), i * 128 : (i + 1) * 128] = v[
                            i
                        ] * jnp.asarray(1e30, BF)
                return 0

            lax.fori_loop(0, tile // group, one_group, 0)

    flat = flat.reshape(2 * tiles, tile * per_row, 128)
    return launch(
        body,
        "mask",
        at,
        [
            far(
                flat,
                lambda ref, at: ref.at[pl.ds((at[0] ^ turn) * tiles, tiles)],
                (tiles, tile * per_row, 128),
                parts=True,
            )
        ],
        [shape(nh, rows // 2, columns, dtype=BF)],
        us=10,
    )[0]


def shard_views(pairs):
    view = lambda flips: lambda ref, at: ref.at[at[1] ^ flips]
    return [near(pairs[0], view(0)), near(pairs[1], view(0)), near(pairs[0], view(1)), near(pairs[1], view(1))]


def keys_values(at, pairs, w, nh):
    _, seg, width = pairs[0].shape
    local = w.shape[1]
    hd = local // nh

    def body(at, ins, outs, _):
        for slot in range(4):
            x = ins[slot][...]
            span = slice(slot * seg, (slot + 1) * seg)
            for i, out in enumerate(outs):
                full = mm(x, ins[4][i + 1], NT)
                high = full.astype(BF)
                low = (full - high.astype(F32)).astype(BF)
                for h in range(nh):
                    part = slice(h * hd, (h + 1) * hd)
                    out[h, span, :] = jnp.concatenate([high[:, part], low[:, part]], axis=1)

    out = shape(nh, 4 * seg, 2 * hd, dtype=BF)
    return launch(body, "keys_values", at, shard_views(pairs) + [near(w)], [out, out], us=2)


def cross_forward(at, mine, other, bias_mine, bias_other, keys, values, w, b, wo, nh):
    half, width = mine.shape
    rows = 2 * half
    local = w.shape[1]
    hd = local // nh
    slots = keys.shape[1]
    scale = hd**-0.5

    def body(at, ins, outs, scratch):
        mine, other, wq, keys, bias_mine, bias_other, values, wo, b = ins
        keep, send, raised, inverse, query, heads = outs
        twice, found = scratch
        for r, x in enumerate((mine, other)):
            q = (mm(x[...], wq[0], NT) + b[0:1]).astype(BF)
            query[r * half : (r + 1) * half, :] = q
            scaled = q * jnp.asarray(scale, BF)
            for h in range(nh):
                part = scaled[:, h * hd : (h + 1) * hd]
                twice[h, r * half : (r + 1) * half, :] = jnp.concatenate([part, part], axis=1)

        def one_head(h, _):
            for r, bias in enumerate((bias_mine, bias_other)):
                span = slice(r * half, (r + 1) * half)
                scores = mm(twice[h, span, :], keys[h], NT) + bias[h].astype(F32)
                e = jnp.exp(scores - jnp.max(scores, axis=1, keepdims=True))
                total = 1.0 / jnp.sum(e, axis=1, keepdims=True)
                low = e.astype(BF)
                raised[h, span, :] = low
                inverse[h, span, :] = jnp.broadcast_to(total, (half, 128))
                both = mm(low, values[h])
                found[h, span, :] = (both[:, :hd] + both[:, hd:]) * total
            return 0

        lax.fori_loop(0, nh, one_head, 0)
        for r, target in enumerate((keep, send)):
            span = slice(r * half, (r + 1) * half)
            out = (jnp.concatenate([found[h, span, :] for h in range(nh)], axis=1) + b[1:2]).astype(BF)
            heads[span, :] = out
            target[...] = mm(out, wo[...]).astype(target.dtype)

    return launch(
        body,
        "cross_fwd",
        at,
        [near(a) for a in (mine, other, w, keys, bias_mine, bias_other, values, wo, b)],
        [
            shape(half, width),
            shape(half, width, dtype=BF),
            shape(nh, rows, slots, dtype=BF),
            shape(nh, rows, 128),
            shape(rows, local, dtype=BF),
            shape(rows, local, dtype=BF),
        ],
        scratch=[pltpu.VMEM((nh, rows, 2 * hd), BF), pltpu.VMEM((nh, rows, hd), F32)],
        mib=30,
        us=9,
    )


def feed(at, after, kept, close, distant, cot, weights, b1, terms, out_bias, fc2_bias, gain, shift):
    rows, width = distant.shape
    units = weights[0][0].shape[1]
    base = terms[0].shape[0] - 16

    def body(at, ins, outs, scratch):
        after, kept, close, distant, cot, out_bias, fc2_bias, gain, shift, b1, close_terms, far_terms = ins[:12]
        f1, f2, slope, sems = scratch
        copies = []
        for matrix, target in enumerate((f1, f2)):
            own, core, *halves = ins[12 + 6 * matrix : 18 + 6 * matrix]
            for s, source in ((0, own), (1, core)):
                copies.append(pltpu.make_async_copy(source, target.at[s], sems.at[len(copies)]))
            for i, source in enumerate(halves):
                size = source.shape[0]
                start = pl.multiple_of((at[4] ^ (i % 2)) * size, size)
                copies.append(
                    pltpu.make_async_copy(source, target.at[2 + i // 2, pl.ds(start, size), :], sems.at[len(copies)])
                )
        for copy in copies:
            copy.start()
        needed = ((0,), (1,), (2, 3), (4, 5))
        biases = (
            b1[...],
            from_terms(close_terms[...][0:3]),
            from_terms(far_terms[...][0:3]),
            from_terms(far_terms[...][3:6]),
        )
        trio, mixed, dsecond_low, sums = outs
        second = after[...] + (kept[...] + close[...].astype(F32) + distant[...].astype(F32)) + out_bias[...]
        normed_mid, inverse_mid = norm_stats(second)
        mid = normed_mid * gain[1:2] + shift[1:2]
        mid_low = mid.astype(BF)
        trio[0] = mid_low
        total = jnp.zeros((rows, width), F32)
        for s in range(4):
            for i in needed[s]:
                copies[i].wait()
            pre = mm(mid_low, f1[s]) + biases[s]
            hidden, slope[s] = gelu_pair(pre)
            for i in needed[s]:
                copies[6 + i].wait()
            total = total + mm(hidden, f2[s])
        last = mid + total + fc2_bias[...]
        normed_last, inverse_last = norm_stats(last)
        first_row = (2 * at[0] + at[1]) * rows
        live = (first_row + lax.broadcasted_iota(jnp.int32, (rows, 1), 0) < at[3]).astype(F32)
        mixed[...] = ((normed_last * gain[2:3] + shift[2:3]) * live).astype(BF)
        delta = cot[...].astype(F32) * live
        dlast = norm_backward(delta, normed_last, inverse_last, gain[2:3])
        dlast_low = dlast.astype(BF)
        trio[1] = dlast_low
        dmid = dlast
        for s in range(4):
            dpre = (mm(dlast_low, f2[s], NT) * slope[s]).astype(BF)
            dmid = dmid + mm(dpre, f1[s], NT)
        dsecond = norm_backward(dmid, normed_mid, inverse_mid, gain[1:2])
        dsecond_low[...] = dsecond.astype(BF)
        sums[...] = jnp.concatenate(
            [
                column_sum(delta * normed_last),
                column_sum(delta),
                column_sum(dlast),
                column_sum(dmid * normed_mid),
                column_sum(dmid),
                column_sum(dsecond),
                jnp.zeros((2, width), F32),
            ],
            axis=0,
        )

    quarter = lambda ref, at: ref.at[rows_at(at[1], rows), :]
    tail = lambda ref, at: ref.at[pl.ds(base, 16), :]
    return launch(
        body,
        "feed",
        at,
        [
            near(after, quarter),
            near(kept, quarter),
            near(close, quarter),
            near(distant),
            near(cot, lambda ref, at: ref.at[rows_at(2 * at[0] + at[1], rows), :]),
            near(out_bias),
            near(fc2_bias),
            near(gain),
            near(shift),
            near(b1),
            near(terms[0], tail),
            near(terms[1], tail),
        ]
        + [raw(a) for group in weights for a in group],
        [shape(2, rows, width, dtype=BF), shape(rows, width, dtype=BF), shape(rows, width, dtype=BF), shape(8, width)],
        scratch=[
            pltpu.VMEM((4, width, units), BF),
            pltpu.VMEM((4, units, width), BF),
            pltpu.VMEM((4, rows, units), F32),
            pltpu.SemaphoreType.DMA((12,)),
        ],
        mib=20,
        us=10,
    )


def assemble(at, z, blocks):
    rows = blocks[0].shape[0]
    for base, own, distant in ((0, blocks[0], blocks[2]), (2 * rows, blocks[1], blocks[3])):
        z[pl.ds(pl.multiple_of(base + at[1] * rows, rows), rows), :] = own[...]
        z[pl.ds(pl.multiple_of(base + (1 - at[1]) * rows, rows), rows), :] = distant[...]


def cross_backward(at, z_blocks, raised, inverse, query, keys, values, w, wo, nh):
    rows, width = z_blocks[0].shape
    rows = 4 * rows
    half = rows // 2
    local = w.shape[1]
    hd = local // nh
    slots = keys.shape[1]
    scale = hd**-0.5

    def body(at, ins, outs, scratch):
        blocks, (wo, inverse, values, raised, query, keys, w) = ins[:4], ins[4:]
        keep, send, dquery, dkv, sums = outs
        z, douts, right, found = scratch
        assemble(at, z, blocks)
        zero = jnp.zeros((half, hd), BF)
        head_sum = jnp.zeros((1, local), F32)
        for r in range(2):
            span = slice(r * half, (r + 1) * half)
            dhead = mm(z[span, :], wo[...], NT)
            head_sum = head_sum + column_sum(dhead)
            scaled = query[span, :] * jnp.asarray(scale, BF)
            for h in range(nh):
                part = slice(h * hd, (h + 1) * hd)
                dout = (dhead[:, part] * inverse[h, span, 0:1]).astype(BF)
                douts[h, span, :] = jnp.concatenate([dout, dout], axis=1)
                right[h, 0, span, :] = jnp.concatenate([scaled[:, part], zero], axis=1)
                right[h, 1, span, :] = jnp.concatenate([zero, dout], axis=1)

        def one_head(h, _):
            grad = None
            for r in range(2):
                span = slice(r * half, (r + 1) * half)
                dprob = mm(douts[h, span, :], values[h], NT)
                low = raised[h, span, :]
                e = low.astype(F32)
                weighed = e * dprob
                mean = jnp.sum(weighed, axis=1, keepdims=True) * inverse[h, span, 0:1]
                dscore = (weighed - e * mean).astype(BF)
                both = mm(dscore, keys[h])
                found[h, span, :] = both[:, :hd] + both[:, hd:]
                part = mm(dscore, right[h, 0, span, :], TN) + mm(low, right[h, 1, span, :], TN)
                grad = part if grad is None else grad + part
            dkv[h] = grad.astype(BF)
            return 0

        lax.fori_loop(0, nh, one_head, 0)
        query_sum = jnp.zeros((1, local), F32)
        for r, target in enumerate((keep, send)):
            span = slice(r * half, (r + 1) * half)
            dq = jnp.concatenate([found[h, span, :] for h in range(nh)], axis=1) * scale
            query_sum = query_sum + column_sum(dq)
            dq_low = dq.astype(BF)
            dquery[span, :] = dq_low
            target[...] = mm(dq_low, w[0]).astype(target.dtype)
        sums[...] = jnp.concatenate([query_sum, head_sum], axis=0)

    return launch(
        body,
        "cross_bwd",
        at,
        [near(a) for a in (*z_blocks, wo, inverse, values, raised, query, keys, w)],
        [
            shape(half, width),
            shape(half, width, dtype=BF),
            shape(rows, local, dtype=BF),
            shape(nh, slots, 2 * hd, dtype=BF),
            shape(2, local),
        ],
        scratch=[
            pltpu.VMEM((rows, width), BF),
            pltpu.VMEM((nh, rows, 2 * hd), BF),
            pltpu.VMEM((nh, 2, rows, 2 * hd), BF),
            pltpu.VMEM((nh, rows, hd), F32),
        ],
        mib=30,
        us=11,
    )


def store_gradient(at, dkv, w, nh):
    _, slots, twice = dkv.shape
    _, local, width = w.shape
    hd = twice // 2
    seg = slots // 4

    def body(at, ins, outs, _):
        dkv, w = ins
        keep, send = outs
        weights = []
        for h in range(nh):
            part = slice(h * hd, (h + 1) * hd)
            weights += [w[1][part], w[2][part]]
        weight = jnp.concatenate(weights, axis=0)
        for slot in (1, 3, 0, 2):
            rows = jnp.concatenate([dkv[h, slot * seg : (slot + 1) * seg, :] for h in range(nh)], axis=1)
            part = mm(rows, weight)
            if slot % 2 == 0:
                keep[slot // 2] = part
            else:
                send[slot // 2] = part.astype(BF)

    return launch(
        body,
        "store_grad",
        at,
        [near(dkv), near(w)],
        [shape(2, seg, width), shape(2, seg, width, dtype=BF)],
        us=2.6,
    )


def group_outs(width, columns, blocks, extra):
    if not blocks:
        return [shape(width, columns)]
    n, r = blocks
    tail = 3 * EXTRA if extra else 0
    return [shape(n * r + tail, columns, dtype=BF), shape(n, r, columns)]


def emit_group(at, grad, outs, blocks, first, columns, late=False):
    if not blocks:
        outs[0][:, first : first + columns] = grad[...]
        return
    n, r = blocks
    span = slice(first, first + columns)
    for b in range(n):
        mine = 4 * (b % 2) + 2 * at[5] + b // 2 if late else 2 * b + at[4]
        theirs = 4 * (b % 2) + 2 * (1 - at[5]) + b // 2 if late else 2 * b + 1 - at[4]
        outs[0][b * r : (b + 1) * r, span] = grad[pl.ds(pl.multiple_of(theirs * r, 8), r), :].astype(BF)
        outs[1][b, :, span] = grad[pl.ds(pl.multiple_of(mine * r, 8), r), :]


def turned_product(out, left, right, step=256):
    if left.shape[1] % step:
        out[...] = mm(left[...], right[...], TN)
        return

    def some(i, _):
        span = pl.ds(pl.multiple_of(i * step, step), step)
        out[span, :] = mm(left[:, span], right[...], TN)
        return 0

    lax.fori_loop(0, left.shape[1] // step, some, 0)


def feed_grads(at, trios, fc1, fc2, b1, blocks):
    _, rows, width = trios[0].shape
    units = fc1.shape[1]

    def body(at, ins, outs, scratch):
        trios, (f1, f2, b1) = ins[:4], ins[4:]
        mid, dlast, hidden, dpre, grad = scratch
        for s, block in enumerate(trios):
            mid[s * rows : (s + 1) * rows, :] = block[0]
            dlast[s * rows : (s + 1) * rows, :] = block[1]

        f1.ready()
        f2.ready()

        def some_rows(i, total):
            span = rows_at(i, 2 * rows)
            hidden[span, :], slope = gelu_pair(mm(mid[span, :], f1[...]) + b1[...])
            grad_pre = mm(dlast[span, :], f2[...], NT) * slope
            dpre[span, :] = grad_pre.astype(BF)
            return total + column_sum(grad_pre)

        outs[-1][...] = lax.fori_loop(0, 2, some_rows, jnp.zeros((1, units), F32))
        turned_product(grad, mid, dpre)
        emit_group(at, grad, outs, blocks, 0, units, True)
        turned_product(grad, dlast, hidden)
        emit_group(at, grad, outs, blocks, units, units, True)

    return launch(
        body,
        "feed_grads",
        at,
        [near(a) for a in trios] + [far(fc1), far(fc2), near(b1)],
        group_outs(width, 2 * units, blocks, False) + [shape(1, units)],
        scratch=[pltpu.VMEM((4 * rows, width), BF)] * 2
        + [pltpu.VMEM((4 * rows, units), BF)] * 2
        + [pltpu.VMEM((width, units), F32)],
        mib=20,
        us=6,
    )


def cross_grads(at, z_blocks, mine, other, dquery, heads, pairs, dkv, first_mine, first_other, flat, small, nh, blocks):
    half, width = mine.shape
    local = dquery.shape[1]
    hd = local // nh
    seg = pairs[0].shape[1]
    feed_sums, first_sums, fc1_sum, head_sums = small

    def body(at, ins, outs, scratch):
        z_blocks, shards = ins[0:4], ins[4:8]
        mine, other, dquery, heads, dkv, first_mine, first_other, flat, feed_sums, first_sums, fc1_sum, head_sums = ins[8:]
        z, grad = scratch
        extra = outs[-1]
        assemble(at, z, z_blocks)
        grad[...] = mm(mine[...], dquery[:half], TN) + mm(other[...], dquery[half:], TN)
        emit_group(at, grad, outs, blocks, 0, local)
        grad[...] = mm(z[...], heads[...], TN)
        emit_group(at, grad, outs, blocks, 3 * local, local)
        z[rows_at(at[0], half), :] = first_mine[...]
        z[rows_at(1 - at[0], half), :] = first_other[...]
        grad[...] = mm(z[...], flat[...], TN)
        emit_group(at, grad, outs, blocks, 4 * local, local)
        both = None
        for slot, block in enumerate(shards):
            rows = jnp.concatenate([dkv[h, slot * seg : (slot + 1) * seg, :] for h in range(nh)], axis=1)
            part = mm(block[...], rows, TN)
            both = part if both is None else both + part
        for i in range(2):
            grad[...] = jnp.concatenate([both[:, (2 * h + i) * hd : (2 * h + i + 1) * hd] for h in range(nh)], axis=1)
            emit_group(at, grad, outs, blocks, (1 + i) * local, local)
        line = jnp.concatenate([head_sums[0:1], head_sums[1:2], jnp.zeros((1, width - 2 * local), F32)], axis=1)
        small = jnp.concatenate(
            [feed_sums[0:6], first_sums[0:3], fc1_sum[...], line, jnp.zeros((EXTRA - 11, width), F32)], axis=0
        )
        extra[...] = small
        if blocks:
            outs[0][blocks[0] * blocks[1] :, 0:width] = three_terms(small)
            outs[0][blocks[0] * blocks[1] :, width:] = jnp.zeros((3 * EXTRA, 5 * local - width), BF)

    return launch(
        body,
        "cross_grads",
        at,
        [near(z) for z in z_blocks]
        + shard_views(pairs)
        + [
            near(a)
            for a in (
                mine,
                other,
                dquery,
                heads,
                dkv,
                first_mine,
                first_other,
                flat,
                feed_sums,
                first_sums,
                fc1_sum,
                head_sums,
            )
        ],
        group_outs(width, 5 * local, blocks, True) + [shape(EXTRA, width)],
        scratch=[pltpu.VMEM((2 * half, width), BF), pltpu.VMEM((width, local), F32)],
        us=4,
    )


def first_back(at, z_own, z_distant, mine, other, total, gain):
    half, width = mine.shape
    rows = half // 2

    def body(at, ins, outs, scratch):
        z_own, z_distant, mine, other, total, gain = ins
        dfirst, low, sums = outs
        (dafter,) = scratch
        dafter[rows_at(at[1], rows), :] = z_own[...].astype(F32)
        dafter[rows_at(1 - at[1], rows), :] = z_distant[...].astype(F32)
        value = dafter[...] + (mine[...].astype(F32) + other[...].astype(F32))
        normed, inverse = norm_stats(total[...])
        result = norm_backward(value, normed, inverse, gain[0:1])
        dfirst[...] = result
        low[...] = result.astype(BF)
        place = lax.broadcasted_iota(jnp.int32, (half, 1), 0)
        counted = ((place >= at[1] * rows) & (place < (at[1] + 1) * rows)).astype(F32)
        sums[...] = jnp.concatenate(
            [
                column_sum(value * normed * counted),
                column_sum(value * counted),
                column_sum(result * counted),
                jnp.zeros((5, width), F32),
            ],
            axis=0,
        )

    return launch(
        body,
        "first_back",
        at,
        [near(a) for a in (z_own, z_distant, mine, other, total, gain)],
        [shape(half, width), shape(half, width, dtype=BF), shape(8, width)],
        scratch=[pltpu.VMEM((half, width), F32)],
        us=2.8,
    )


def self_backward(at, mine, other, tokens, w, wo, qkv, prob, mixed, nh, blocks):
    half, width = mine.shape
    rows = 2 * half
    local = wo.shape[0]
    hd = local // nh
    scale = hd**-0.5

    def body(at, ins, outs, scratch):
        mine, other, wo, qkv, prob, tok, w, mixed = ins
        send, keep = outs[0:2]
        group, extra = outs[2:-1], outs[-1]
        z, dqkv, grad = scratch
        own, distant = rows_at(at[0], half), rows_at(1 - at[0], half)
        z[own, :] = mine[...]
        z[distant, :] = other[...]
        dself = mm(z[...], wo[...], NT).astype(BF)
        v, k, q = qkv[2], qkv[1], qkv[0]
        dq, dk, dv = [], [], []
        for h in range(nh):
            part = slice(h * hd, (h + 1) * hd)
            weights_low = prob[h]
            weights = weights_low.astype(F32)
            weighed = weights * mm(dself[:, part], v[:, part], NT)
            dscore = (weighed - weights * jnp.sum(weighed, axis=1, keepdims=True)).astype(BF)
            dq.append(mm(dscore, k[:, part]))
            dk.append(mm(dscore, q[:, part], TN))
            dv.append(mm(weights_low, dself[:, part], TN))
        dquery = jnp.concatenate(dq, axis=1) * scale
        dvalue = jnp.concatenate(dv, axis=1)
        dqkv[0] = dquery.astype(BF)
        dqkv[1] = (jnp.concatenate(dk, axis=1) * scale).astype(BF)
        dqkv[2] = dvalue.astype(BF)
        x = tok[...]
        for i in range(3):
            grad[...] = mm(x, dqkv[i], TN)
            emit_group(at, grad, group, blocks, i * local, local)
        line = jnp.concatenate([column_sum(dquery), column_sum(dvalue), jnp.zeros((1, local), F32)], axis=1)
        small = jnp.concatenate([line, jnp.zeros((EXTRA - 1, 3 * local), F32)], axis=0)
        extra[...] = small
        if blocks:
            group[0][blocks[0] * blocks[1] :, :] = three_terms(small)
        send[half:, :] = mixed[...]
        for place, out in ((distant, send), (own, keep)):
            total = mm(dqkv[0, place, :], w[0]) + mm(dqkv[1, place, :], w[1]) + mm(dqkv[2, place, :], w[2])
            out[0:half, :] = total.astype(out.dtype)

    return launch(
        body,
        "self_bwd",
        at,
        [near(a) for a in (mine, other, wo, qkv, prob, tokens, w, mixed)],
        [shape(half + half // 2, width, dtype=BF), shape(half, width)]
        + group_outs(width, 3 * local, blocks, True)
        + [shape(EXTRA, 3 * local)],
        scratch=[
            pltpu.VMEM((rows, width), BF),
            pltpu.VMEM((3, rows, local), BF),
            pltpu.VMEM((width, local), F32),
        ],
        mib=20,
        us=6,
    )


def add_stage(at, keep, got, small, bit):
    n, rows, columns = keep.shape
    tail = 0 if small is None else 3 * EXTRA
    reach = small.shape[1] if tail else 0

    def body(at, ins, outs, _):
        keep, got = ins[:2]
        mine = at[bit]
        send, stay = outs[:2]
        for b in range(n // 2):
            for chosen, out in ((1 - mine, send), (mine, stay)):
                block = 2 * b + chosen
                value = keep[block] + got[pl.ds(pl.multiple_of(block * rows, 8), rows), :].astype(F32)
                if out is send:
                    send[b * rows : (b + 1) * rows, :] = value.astype(BF)
                else:
                    stay[b] = value
        if tail:
            total = ins[2][...] + from_terms(got[n * rows :, 0:reach])
            outs[2][...] = total
            send[n // 2 * rows :, 0:reach] = three_terms(total)
            if reach < columns:
                send[n // 2 * rows :, reach:] = jnp.zeros((tail, columns - reach), BF)

    ins = [near(keep), near(got)] + ([near(small)] if tail else [])
    outs = [shape(n // 2 * rows + tail, columns, dtype=BF), shape(n // 2, rows, columns)]
    if tail:
        outs.append(shape(EXTRA, reach))
    return launch(body, "add_stage", at, ins, outs, us=1)


def last_stage(at, keep, got, small, parts):
    _, rows, columns = keep.shape
    each = columns // sum(count for count, _ in parts)
    reach = 0 if small is None else small.shape[1]

    def body(at, ins, outs, _):
        total = ins[0][0] + ins[1][0:rows].astype(F32)
        first = 0
        for out, (count, turned) in zip(outs, parts):
            if count == 1:
                value = total[:, first * each : (first + 1) * each]
                out[...] = value.T if turned else value
            else:
                for i in range(count):
                    out[i] = total[:, (first + i) * each : (first + i + 1) * each]
            first += count
        if reach:
            outs[-1][...] = ins[2][...] + from_terms(ins[1][rows:, 0:reach])

    outs = []
    for count, turned in parts:
        dims = (rows, each) if count == 1 else (count, rows, each)
        outs.append(shape(*(dims[::-1] if turned else dims)))
    ins = [near(keep), near(got)]
    if reach:
        ins.append(near(small))
        outs.append(shape(EXTRA, reach))
    return launch(body, "last_stage", at, ins, outs, us=1)


def join_halves(at, mine, other):
    half, width = mine.shape

    def body(at, ins, outs, _):
        outs[0][rows_at(at[0], half), :] = ins[0][...]
        outs[0][rows_at(1 - at[0], half), :] = ins[1][...]

    out = shape(2 * half, width, dtype=mine.dtype)
    return launch(body, "join_halves", at, [near(mine), near(other)], [out])[0]


def join_quarters(at, own, close, distant):
    rows, width = own.shape

    def body(at, ins, outs, _):
        for flips, block in enumerate(ins):
            place = 2 * (at[0] ^ (flips & 1)) + (at[1] ^ (flips >> 1))
            outs[0][rows_at(place, rows), :] = block[...]

    part = lambda i: lambda ref, at: ref.at[pl.ds(i * rows, rows), :]
    ins = [near(own), near(close, part(2)), near(distant, part(2)), near(distant, part(3))]
    return launch(body, "join_quarters", at, ins, [shape(4 * rows, width, dtype=BF)])[0]


def flip(bit, size):
    return [(i, i ^ bit) for i in range(size)]


def butterfly(value, axis, size):
    bit = 1
    while bit < size:
        value = value + lax.ppermute(value, axis, flip(bit, size))
        bit *= 2
    return value


def on_device(
    tokens,
    store,
    summary_length,
    top_index,
    cotangent,
    self_qkv_weight,
    self_qv_bias,
    self_out_weight,
    self_out_bias,
    qkv_weight,
    qv_bias,
    out_weight,
    out_bias,
    fc1_weight,
    fc1_bias,
    fc2_weight,
    fc2_bias,
    norm_gain,
    norm_shift,
):
    rows, width = tokens.shape
    half, quarter = rows // 2, rows // 4
    nh = top_index.shape[1]
    local = qkv_weight.shape[2]
    units = fc1_weight.shape[1]
    seg = store.shape[1]
    wide = lax.axis_size("wide")
    place = lax.axis_index("narrow")
    doc = lax.axis_index("wide")
    core, across = place % 2, place // 2
    at = jnp.stack([core, across, place, summary_length[0], doc % 2, doc // 2 % 2, doc // 4]).astype(jnp.int32)
    blocks = (wide // 2, width // wide) if wide == 8 else None
    row = lambda v: v.reshape(1, -1)
    self_w = jnp.swapaxes(self_qkv_weight, 1, 2)
    cross_w = jnp.swapaxes(qkv_weight, 1, 2)

    def to_core(v):
        return lax.ppermute(v, "narrow", CORE)

    def to_across(v):
        return lax.ppermute(v, "narrow", ACROSS)

    def spread(v):
        distant = to_across(v)
        return [v, to_core(v), distant, to_core(distant)]

    def chip_sum(keep, send):
        return (keep + to_core(send).astype(F32)).astype(BF)

    def gather_pair(v, groups):
        return lax.all_gather(v, "narrow", axis=0, axis_index_groups=groups)

    by_x, by_core = [[0, 2], [1, 3]], [[0, 1], [2, 3]]
    share = lambda v: lax.dynamic_slice_in_dim(v, doc % 2 * (v.shape[0] // 2), v.shape[0] // 2, 0)
    over = lambda v, bit: lax.ppermute(v, "wide", flip(bit, wide))
    store_pair = gather_pair(store[0], by_x)
    f2_pair = gather_pair(share(fc2_weight), by_x)
    qkv, prob, flat, send, keep = self_forward(
        at, tokens, self_w, self_qv_bias, self_out_weight, row(fc1_bias), nh
    )
    close = to_core(send)
    mine = jnp.concatenate(
        [
            (keep + close[:half].astype(F32)).astype(BF),
            send[half : half + 3],
            close[half : half + 3],
            jnp.zeros((16 - 6, width), BF),
        ],
        axis=0,
    )
    terms_close = close
    other = to_across(mine)
    index = index_rows(top_index)
    bias_mine = make_mask(tie(at, mine), index, top_index.shape, seg, 128, 0)
    other = tie(other, bias_mine)
    f1_half = share(tie(fc1_weight, bias_mine))
    f1_x = to_across(f1_half)
    first_total, after, after_low = first_norm(at, mine, other, tokens, row(self_out_bias), norm_gain, norm_shift)
    after_other = to_core(after_low)
    f1_core, f2_core = to_core(tie(fc1_weight, after_low)), to_core(tie(fc2_weight, after_low))
    bias_other = make_mask(tie(at, after_low, f1_half), index, top_index.shape, seg, 128, 1)
    store_pair = tie(store_pair, other)
    pairs = (store_pair, to_core(store_pair))
    f1_x, after_other, f1_core, f2_core = tie((f1_x, after_other, f1_core, f2_core), bias_other)
    f1_y, f1_xc = over(f1_x, 1), to_core(f1_x)

    keys, values = keys_values(tie(at, bias_other), pairs, cross_w, nh)
    keep, send, raised, inverse, query, heads = cross_forward(
        tie(at, keys), after_low, after_other, bias_mine, bias_other, keys, values, cross_w, qv_bias, out_weight, nh
    )
    close = to_core(send)
    theirs = (1 - across) * quarter
    distant = to_across(
        (
            lax.dynamic_slice_in_dim(keep, theirs, quarter, 0)
            + lax.dynamic_slice_in_dim(close, theirs, quarter, 0).astype(F32)
        ).astype(BF)
    )
    f2_x = lax.dynamic_index_in_dim(tie(f2_pair, keep), 1 - across, 0, keepdims=False)
    f2_y, f2_xc = over(f2_x, 1), to_core(f2_x)
    f1_y = tie(f1_y, close)
    f2_y = tie(f2_y, distant)
    weights = (
        (fc1_weight, f1_core, f1_x, f1_y, f1_xc, to_core(f1_y)),
        (fc2_weight, f2_core, f2_x, f2_y, f2_xc, to_core(f2_y)),
    )

    pair, mixed_own, z, feed_sums = feed(
        at,
        after,
        keep,
        close,
        distant,
        cotangent,
        weights,
        row(fc1_bias),
        (terms_close, other),
        row(out_bias),
        row(fc2_bias),
        norm_gain,
        norm_shift,
    )
    z_all = spread(z)
    trios = spread(tie(pair, z_all[2]))

    keep, send, dquery, dkv, cross_sums = cross_backward(
        at, z_all, raised, inverse, query, keys, values, cross_w, out_weight, nh
    )
    mine = chip_sum(keep, send)
    other = to_across(mine)
    *feed_out, fc1_sum = feed_grads(tie(at, mine), trios, fc1_weight, fc2_weight, row(fc1_bias), blocks)
    other = tie(other, fc1_sum)
    dfirst, dfirst_low, first_sums = first_back(at, z_all[0], z_all[2], mine, other, first_total, norm_gain)
    dfirst_other = to_core(dfirst_low)
    store_keep, store_send = store_gradient(tie(at, dfirst_low), dkv, cross_w, nh)
    store_close = to_core(store_send)
    *cross_out, cross_small = cross_grads(
        tie(at, store_send),
        z_all,
        after_low,
        after_other,
        dquery,
        heads,
        pairs,
        dkv,
        dfirst_low,
        dfirst_other,
        flat,
        (feed_sums, first_sums, fc1_sum, cross_sums),
        nh,
        blocks,
    )
    store_distant = to_across((store_keep[1] + tie(store_close, cross_small)[1].astype(F32)).astype(BF))

    send, keep, *self_out, self_small = self_backward(
        tie(at, cross_small), dfirst_low, dfirst_other, tokens, self_w, self_out_weight, qkv, prob, mixed_own, nh, blocks
    )
    close = to_core(send)
    mine = jnp.concatenate([(keep + close[:half].astype(F32)).astype(BF), send[half:], close[half:]], axis=0)
    other = to_across(mine)
    tokens_half = dfirst + (mine[:half].astype(F32) + other[:half].astype(F32))
    tokens_grad = join_halves(at, tokens_half, to_core(tokens_half))
    mixed = join_quarters(at, mixed_own, close, other)
    store_grad = (store_keep[0] + store_close[0].astype(F32) + store_distant.astype(F32))[None]

    if blocks:
        feed_send, feed_keep = add_stage(tie(at, self_small), feed_out[1], over(feed_out[0], 2), None, 6)
        cross_send, cross_keep, cross_small = add_stage(
            tie(at, feed_send), cross_out[1], over(cross_out[0], 1), cross_small, 5
        )
        self_send, self_keep, self_small = add_stage(
            tie(at, cross_send), self_out[1], over(self_out[0], 1), self_small, 5
        )
        feed_send, feed_keep = add_stage(tie(at, self_send), feed_keep, over(feed_send, 4), None, 4)
        cross_send, cross_keep, cross_small = add_stage(
            tie(at, feed_send), cross_keep, over(cross_send, 2), cross_small, 6
        )
        self_send, self_keep, self_small = add_stage(
            tie(at, cross_send), self_keep, over(self_send, 2), self_small, 6
        )
        fc1_grad, fc2_grad = last_stage(tie(at, self_send), feed_keep, over(feed_send, 1), None, [(1, False), (1, False)])
        fc2_grad = fc2_grad.T
        qkv_grad, out_grad, self_out_grad, cross_small = last_stage(
            tie(at, fc1_grad), cross_keep, over(cross_send, 4), cross_small, [(3, False), (1, True), (1, True)]
        )
        self_qkv_grad, self_small = last_stage(
            tie(at, cross_small), self_keep, over(self_send, 4), self_small, [(3, False)]
        )
    else:
        scatter = functools.partial(lax.psum_scatter, axis_name="wide", tiled=True)
        parts = lambda g: jnp.stack([g[:, i * local : (i + 1) * local] for i in range(3)])
        fc1_grad = scatter(feed_out[0][:, :units], scatter_dimension=0)
        fc2_grad = scatter(feed_out[0][:, units:].T, scatter_dimension=1)
        qkv_grad = scatter(parts(cross_out[0]), scatter_dimension=1)
        out_grad = scatter(cross_out[0][:, 3 * local : 4 * local].T, scatter_dimension=1)
        self_qkv_grad = scatter(parts(self_out[0]), scatter_dimension=1)
        self_out_grad = scatter(cross_out[0][:, 4 * local :].T, scatter_dimension=1)
        cross_small = butterfly(cross_small, "wide", wide)
        self_small = butterfly(self_small, "wide", wide)
    summed = butterfly(cross_small, "narrow", 4)
    gain_last, shift_last, fc2_b, gain_mid, shift_mid, out_b, gain_first, shift_first, self_out_b = (
        summed[i] for i in range(9)
    )
    return (
        mixed,
        tokens_grad,
        store_grad,
        self_qkv_grad,
        self_small[0, : 2 * local].reshape(2, local),
        self_out_grad,
        self_out_b,
        qkv_grad,
        cross_small[10, : 2 * local].reshape(2, local),
        out_grad,
        out_b,
        fc1_grad,
        cross_small[9],
        fc2_grad,
        fc2_b,
        jnp.stack([gain_first, gain_mid, gain_last]),
        jnp.stack([shift_first, shift_mid, shift_last]),
    )


def solution(mesh):
    placed = (
        P("wide", None),
        P("wide", "narrow", None),
        P("wide"),
        P("wide", "narrow", None, None),
        P("wide", None),
        P(None, None, "narrow"),
        P(None, "narrow"),
        P("narrow", None),
        P(),
        P(None, None, "narrow"),
        P(None, "narrow"),
        P("narrow", None),
        P(),
        P(None, "narrow"),
        P("narrow"),
        P("narrow", None),
        P(),
        P(),
        P(),
    )
    return jax.shard_map(
        on_device,
        mesh=mesh,
        in_specs=placed,
        out_specs=(
            P("wide", None),
            P("wide", None),
            P("wide", "narrow", None),
            P(None, "wide", "narrow"),
            P(None, "narrow"),
            P("narrow", "wide"),
            P(),
            P(None, "wide", "narrow"),
            P(None, "narrow"),
            P("narrow", "wide"),
            P(),
            P("wide", "narrow"),
            P("narrow"),
            P("narrow", "wide"),
            P(),
            P(),
            P(),
        ),
        check_vma=False,
    )
```

```python
import functools

import jax
import jax.numpy as jnp
from jax import lax
from jax.experimental import pallas as pl
from jax.experimental.pallas import tpu as pltpu
from jax.sharding import PartitionSpec as P

F32 = jnp.float32
BF = jnp.bfloat16
NN = (((1,), (0,)), ((), ()))
NT = (((1,), (1,)), ((), ()))
TN = (((0,), (0,)), ((), ()))
EPS = 1e-05
PACE = 1.1e8
SELF_MIB = 60
EXTRA = 16

CORE = [(i, i ^ 1) for i in range(4)]
ACROSS = [(i, i ^ 2) for i in range(4)]


def mm(left, right, dims=NN):
    return lax.dot_general(left, right, dims, preferred_element_type=F32)


def shape(*dims, dtype=F32):
    return jax.ShapeDtypeStruct(dims, dtype)


def tie(value, *earlier):
    return lax.optimization_barrier((value, *earlier))[0]


class Operand:
    def __init__(self, source, buffer, sems, first, parts):
        self.buffer = buffer
        self.parts = parts
        if parts:
            self.copies = [
                pltpu.make_async_copy(source.at[i], buffer.at[i], sems.at[first + i]) for i in range(buffer.shape[0])
            ]
        else:
            self.copies = [pltpu.make_async_copy(source, buffer, sems.at[first])]
        self.waited = [False] * len(self.copies)
        for copy in self.copies:
            copy.start()

    def ready(self, part=None):
        for i, copy in enumerate(self.copies):
            if not self.waited[i] and (part is None or i == part):
                copy.wait()
                self.waited[i] = True

    @property
    def shape(self):
        return self.buffer.shape

    def __getitem__(self, at):
        self.ready(at if self.parts and isinstance(at, int) else None)
        return self.buffer[at]


class Result:
    def __init__(self, target, buffer, sems, first, parts):
        self.buffer = buffer
        if parts:
            self.copies = [
                pltpu.make_async_copy(buffer.at[i], target.at[i], sems.at[first + i]) for i in range(buffer.shape[0])
            ]
        else:
            self.copies = [pltpu.make_async_copy(buffer, target, sems.at[first])]
        self.started = [False] * len(self.copies)

    @property
    def shape(self):
        return self.buffer.shape

    @property
    def dtype(self):
        return self.buffer.dtype

    def __setitem__(self, at, value):
        self.buffer[at] = value

    def flush(self, part=0):
        self.copies[part].start()
        self.started[part] = True

    def finish(self):
        for i in range(len(self.copies)):
            if not self.started[i]:
                self.flush(i)
        for copy in self.copies:
            copy.wait()


def far(array, take=None, dims=None, parts=False):
    return ("far", array, take, tuple(dims or array.shape), parts)


def near(array, take=None):
    return ("near", array, take, None, False)


def raw(array):
    return ("raw", array, None, None, False)


def launch(body, name, at, ins, outs, scratch=(), mib=16, us=2.0):
    in_specs = [pl.BlockSpec(memory_space=pltpu.SMEM)]
    buffers, n_in, n_out = [], 0, 0
    for kind, array, _, dims, parts in ins:
        in_specs.append(pl.BlockSpec(memory_space=pltpu.VMEM if kind == "near" else pltpu.HBM))
        if kind == "far":
            buffers.append(pltpu.VMEM(dims, array.dtype))
            n_in += dims[0] if parts else 1
    out_specs, structs = [], []
    for out in outs:
        if isinstance(out, tuple):
            struct, parts = out
            out_specs.append(pl.BlockSpec(memory_space=pltpu.HBM))
            buffers.append(pltpu.VMEM(struct.shape, struct.dtype))
            n_out += struct.shape[0] if parts else 1
        else:
            struct = out
            out_specs.append(pl.BlockSpec(memory_space=pltpu.VMEM))
        structs.append(struct)
    n_buffers = len(buffers)
    sems = [pltpu.SemaphoreType.DMA((max(n, 1),)) for n in (n_in, n_out)]

    def kernel(at_ref, *refs):
        in_refs, out_refs = refs[: len(ins)], refs[len(ins) : len(ins) + len(outs)]
        rest = refs[len(ins) + len(outs) :]
        bufs, user, (in_sems, out_sems) = list(rest[:n_buffers]), rest[n_buffers:-2], rest[-2:]
        place, given = 0, []
        for ref, (kind, _, take, dims, parts) in zip(in_refs, ins):
            source = take(ref, at_ref) if take else ref
            if kind == "far":
                given.append(Operand(source, bufs.pop(0), in_sems, place, parts))
                place += dims[0] if parts else 1
            else:
                given.append(source)
        place, results = 0, []
        for ref, out in zip(out_refs, outs):
            if isinstance(out, tuple):
                results.append(Result(ref, bufs.pop(0), out_sems, place, out[1]))
                place += out[0].shape[0] if out[1] else 1
            else:
                results.append(ref)
        body(at_ref, given, results, user)
        for operand in given:
            if isinstance(operand, Operand):
                operand.ready()
        for result in results:
            if isinstance(result, Result):
                result.finish()

    return pl.pallas_call(
        kernel,
        in_specs=in_specs,
        out_specs=out_specs,
        out_shape=structs,
        scratch_shapes=buffers + list(scratch) + sems,
        compiler_params=pltpu.CompilerParams(vmem_limit_bytes=mib << 20),
        cost_estimate=pl.CostEstimate(flops=int(us * PACE), bytes_accessed=1000, transcendentals=0),
        name=name,
    )(at, *[entry[1] for entry in ins])


def norm_stats(value):
    centre = value - jnp.mean(value, axis=-1, keepdims=True)
    spread = jnp.mean(centre * centre, axis=-1, keepdims=True)
    inverse = lax.rsqrt(spread + EPS)
    return centre * inverse, inverse


def norm_backward(grad, normed, inverse, gain):
    scaled = grad * gain
    centred = scaled - jnp.mean(scaled, axis=-1, keepdims=True)
    return inverse * (centred - normed * jnp.mean(scaled * normed, axis=-1, keepdims=True))


def column_sum(value):
    return jnp.sum(value, axis=0, keepdims=True)


def erf(value):
    x = jnp.clip(value, -4.0, 4.0)
    y = x * x
    top = jnp.full_like(y, -2.72614225801306e-10)
    for factor in (
        2.77068142495902e-08,
        -2.10102402082508e-06,
        -5.69250639462346e-05,
        -7.34990630326855e-04,
        -2.95459980854025e-03,
        -1.60960333262415e-02,
    ):
        top = top * y + factor
    low = jnp.full_like(y, -1.45660718464996e-05)
    for factor in (
        -2.13374055278905e-04,
        -1.68282697438203e-03,
        -7.37332916720468e-03,
        -1.42647390514189e-02,
    ):
        low = low * y + factor
    return x * top / low


def three_terms(value):
    high = value.astype(BF)
    rest = value - high.astype(F32)
    middle = rest.astype(BF)
    return jnp.concatenate([high, middle, (rest - middle.astype(F32)).astype(BF)], axis=0)


def from_terms(stacked):
    rows = stacked.shape[0] // 3
    terms = stacked.astype(F32)
    return terms[:rows] + terms[rows : 2 * rows] + terms[2 * rows :]


def rows_at(place, rows):
    return pl.ds(pl.multiple_of(place * rows, rows), rows)


def self_forward(at, tokens, w, b, wo, nh):
    rows, width = tokens.shape
    local = w.shape[1]
    half = rows // 2
    hd = local // nh
    scale = hd**-0.5

    def body(at, ins, outs, _):
        tok, w, wo, b = ins
        qkv, prob, flat, send, keep = outs
        x = tok[...]
        q = (mm(x, w[0], NT) + b[0:1]).astype(BF)
        k = mm(x, w[1], NT).astype(BF)
        v = (mm(x, w[2], NT) + b[1:2]).astype(BF)
        for i, value in enumerate((q, k, v)):
            qkv[i] = value
            qkv.flush(i)
        row_ids = lax.broadcasted_iota(jnp.int32, (rows, rows), 0)
        key_ids = lax.broadcasted_iota(jnp.int32, (rows, rows), 1)
        allowed = (key_ids <= row_ids) & (key_ids < at[3])
        found = []
        for h in range(nh):
            part = slice(h * hd, (h + 1) * hd)
            scores = mm(q[:, part], k[:, part], NT) * scale
            scores = jnp.where(allowed, scores, -1e30)
            shifted = jnp.exp(scores - jnp.max(scores, axis=1, keepdims=True))
            weights = (shifted * (1.0 / jnp.sum(shifted, axis=1, keepdims=True))).astype(BF)
            prob[h] = weights
            prob.flush(h)
            found.append(mm(weights, v[:, part]).astype(BF))
        flat[...] = jnp.concatenate(found, axis=1)
        flat.flush()
        send[...] = mm(flat.buffer[rows_at(1 - at[0], half), :], wo[...]).astype(BF)
        send.flush()
        keep[...] = mm(flat.buffer[rows_at(at[0], half), :], wo[...])

    return launch(
        body,
        "self_fwd",
        at,
        [far(tokens), far(w, parts=True), far(wo), far(b)],
        [
            (shape(3, rows, local, dtype=BF), True),
            (shape(nh, rows, rows, dtype=BF), True),
            (shape(rows, local, dtype=BF), False),
            (shape(half, width, dtype=BF), False),
            (shape(half, width), False),
        ],
        mib=SELF_MIB,
        us=4,
    )


def first_norm(at, mine, other, tokens, bias, gain, shift):
    half, width = mine.shape

    def body(at, ins, outs, _):
        mine, other, tok, bias, gain, shift = ins
        total, after, low = outs
        value = tok[...].astype(F32) + (mine[...].astype(F32) + other[...].astype(F32)) + bias[...]
        total[...] = value
        normed, _ = norm_stats(value)
        result = normed * gain[0:1] + shift[0:1]
        after[...] = result
        low[...] = result.astype(BF)

    return launch(
        body,
        "first_norm",
        at,
        [
            near(mine),
            near(other),
            near(tokens, lambda ref, at: ref.at[rows_at(at[0], half), :]),
            near(bias),
            near(gain),
            near(shift),
        ],
        [shape(half, width), shape(half, width), shape(half, width, dtype=BF)],
        us=1.7,
    )


def index_rows(top_index):
    rows, nh, ns, keep = top_index.shape
    flat = top_index.reshape(rows, nh, ns, keep // 128, 128).transpose(0, 1, 3, 2, 4)
    return flat.reshape(rows * nh * ns * (keep // 128), 128)


def make_mask(at, flat, dims, seg, tile, turn):
    rows, nh, ns, keep = dims
    halves = keep // 128
    per_row = nh * ns * halves
    tiles = rows // 2 // tile
    columns = ns * seg
    blocks = columns // 128
    group = 32

    def body(at, ins, outs, _):
        (index,) = ins
        (bias,) = outs
        lane = lax.broadcasted_iota(jnp.int32, (group, 128), 1).astype(F32)
        lane_low = lane.astype(BF)
        empty = jnp.full((group, 128), -1.0, BF)
        own = at[2]
        steps = []
        step = 1
        while step <= seg - keep:
            steps.insert(0, step)
            step *= 2
        turns = steps + [(seg * s) % 128 for s in range(ns)]
        below = {s: lane_low < jnp.asarray(s, BF) for s in turns if 0 < s < 128}

        for t in range(tiles):
            index.ready(t)
            source = index.buffer.at[t]

            def one_group(g, _):
                for h in range(nh):
                    v = [empty] * blocks
                    for slot in range(ns):
                        first, turn = divmod(seg * slot, 128)
                        for c in range(halves):
                            start = g * (group * per_row) + h * ns * halves + c * ns + (own ^ slot)
                            found = jnp.concatenate(
                                [source[pl.ds(start + q * 8 * per_row, 8, stride=per_row), :] for q in range(group // 8)],
                                axis=0,
                            )
                            ahead = (found.astype(F32) - (lane + float(128 * c))).astype(BF)
                            at_block = first + c
                            if turn == 0:
                                v[at_block] = ahead
                            else:
                                turned = pltpu.roll(ahead, turn, axis=1)
                                v[at_block] = jnp.where(below[turn], v[at_block], turned)
                                v[at_block + 1] = jnp.where(below[turn], turned, v[at_block + 1])
                    for s in steps:
                        gap = jnp.asarray(s, BF)
                        moved = [x - gap for x in v]
                        stay = [jnp.where(x >= gap, empty, x) for x in v]
                        if s % 128 == 0:
                            hop = s // 128
                            v = stay[:hop] + [jnp.maximum(stay[i], moved[i - hop]) for i in range(hop, blocks)]
                        else:
                            turned = [pltpu.roll(x, s, axis=1) for x in moved]
                            v = [
                                jnp.maximum(stay[i], jnp.where(below[s], turned[i - 1], turned[i])) for i in range(blocks)
                            ]
                    for i in range(blocks):
                        bias[h, pl.ds(pl.multiple_of(t * tile + g * group, group), group), i * 128 : (i + 1) * 128] = v[
                            i
                        ] * jnp.asarray(1e30, BF)
                return 0

            lax.fori_loop(0, tile // group, one_group, 0)

    flat = flat.reshape(2 * tiles, tile * per_row, 128)
    return launch(
        body,
        "mask",
        at,
        [
            far(
                flat,
                lambda ref, at: ref.at[pl.ds((at[0] ^ turn) * tiles, tiles)],
                (tiles, tile * per_row, 128),
                parts=True,
            )
        ],
        [shape(nh, rows // 2, columns, dtype=BF)],
        us=10,
    )[0]


def keys_values(at, shards, w, nh):
    seg, width = shards[0].shape
    local = w.shape[1]
    hd = local // nh

    def body(at, ins, outs, _):
        for slot in range(4):
            x = ins[slot][...]
            span = slice(slot * seg, (slot + 1) * seg)
            for i, out in enumerate(outs):
                full = mm(x, ins[4][i + 1], NT)
                high = full.astype(BF)
                low = (full - high.astype(F32)).astype(BF)
                for h in range(nh):
                    part = slice(h * hd, (h + 1) * hd)
                    out[h, span, :] = jnp.concatenate([high[:, part], low[:, part]], axis=1)

    out = shape(nh, 4 * seg, 2 * hd, dtype=BF)
    return launch(body, "keys_values", at, [near(s) for s in shards] + [near(w)], [out, out], us=2)


def cross_forward(at, mine, other, bias_mine, bias_other, keys, values, w, b, wo, nh):
    half, width = mine.shape
    rows = 2 * half
    local = w.shape[1]
    hd = local // nh
    slots = keys.shape[1]
    scale = hd**-0.5

    def body(at, ins, outs, scratch):
        mine, other, wq, keys, bias_mine, bias_other, values, wo, b = ins
        keep, send, raised, inverse, query, heads = outs
        twice, found = scratch
        for r, x in enumerate((mine, other)):
            q = (mm(x[...], wq[0], NT) + b[0:1]).astype(BF)
            query[r * half : (r + 1) * half, :] = q
            scaled = q * jnp.asarray(scale, BF)
            for h in range(nh):
                part = scaled[:, h * hd : (h + 1) * hd]
                twice[h, r * half : (r + 1) * half, :] = jnp.concatenate([part, part], axis=1)

        def one_head(h, _):
            for r, bias in enumerate((bias_mine, bias_other)):
                span = slice(r * half, (r + 1) * half)
                scores = mm(twice[h, span, :], keys[h], NT) + bias[h].astype(F32)
                e = jnp.exp(scores - jnp.max(scores, axis=1, keepdims=True))
                total = 1.0 / jnp.sum(e, axis=1, keepdims=True)
                low = e.astype(BF)
                raised[h, span, :] = low
                inverse[h, span, :] = jnp.broadcast_to(total, (half, 128))
                both = mm(low, values[h])
                found[h, span, :] = (both[:, :hd] + both[:, hd:]) * total
            return 0

        lax.fori_loop(0, nh, one_head, 0)
        for r, target in enumerate((keep, send)):
            span = slice(r * half, (r + 1) * half)
            out = (jnp.concatenate([found[h, span, :] for h in range(nh)], axis=1) + b[1:2]).astype(BF)
            heads[span, :] = out
            target[...] = mm(out, wo[...]).astype(target.dtype)

    return launch(
        body,
        "cross_fwd",
        at,
        [near(a) for a in (mine, other, w, keys, bias_mine, bias_other, values, wo, b)],
        [
            shape(half, width),
            shape(half, width, dtype=BF),
            shape(nh, rows, slots, dtype=BF),
            shape(nh, rows, 128),
            shape(rows, local, dtype=BF),
            shape(rows, local, dtype=BF),
        ],
        scratch=[pltpu.VMEM((nh, rows, 2 * hd), BF), pltpu.VMEM((nh, rows, hd), F32)],
        mib=30,
        us=9,
    )


def counted_rows(at, half):
    rows = half // 2
    place = lax.broadcasted_iota(jnp.int32, (half, 1), 0)
    return ((place >= at[1] * rows) & (place < (at[1] + 1) * rows)).astype(F32)


def stacked_sums(*values):
    sums = [column_sum(value) for value in values]
    return jnp.concatenate(sums + [jnp.zeros((8 - len(sums), values[0].shape[1]), F32)], axis=0)


def second_norm(at, after, mine, other, bias, gain, shift):
    half, width = mine.shape

    def body(at, ins, outs, _):
        after, mine, other, bias, gain, shift = ins
        total, low = outs
        value = after[...] + (mine[...].astype(F32) + other[...].astype(F32)) + bias[...]
        total[...] = value
        normed, _ = norm_stats(value)
        low[...] = (normed * gain[1:2] + shift[1:2]).astype(BF)

    ins = [near(a) for a in (after, mine, other, bias, gain, shift)]
    return launch(body, "second_norm", at, ins, [shape(half, width), shape(half, width, dtype=BF)], us=1.5)


def feed_up(at, mine, other, f1, f2, b1):
    half, width = mine.shape
    units = f1.shape[1]

    def body(at, ins, outs, _):
        mine, other, f1, f2, b1 = ins
        keep, send, hidden, slope = outs
        for r, (x, target) in enumerate(((other, send), (mine, keep))):
            span = slice((1 - r) * half, (2 - r) * half)
            low, steep = gelu_pair(mm(x[...], f1[...]) + b1[...])
            hidden[span, :] = low
            slope[span, :] = steep
            target[...] = mm(low, f2[...]).astype(target.dtype)

    ins = [near(a) for a in (mine, other, f1, f2, b1)]
    outs = [
        shape(half, width),
        shape(half, width, dtype=BF),
        shape(2 * half, units, dtype=BF),
        shape(2 * half, units),
    ]
    return launch(body, "feed_up", at, ins, outs, us=4)


def third_norm(at, total, mine, other, cot, bias, gain, shift):
    half, width = mine.shape

    def body(at, ins, outs, _):
        total, mine, other, cot, bias, gain, shift = ins
        mixed, dlast_out, low, sums = outs
        normed_mid, _ = norm_stats(total[...])
        last = normed_mid * gain[1:2] + shift[1:2] + (mine[...].astype(F32) + other[...].astype(F32)) + bias[...]
        normed, inverse = norm_stats(last)
        first_row = at[0] * half
        live = (first_row + lax.broadcasted_iota(jnp.int32, (half, 1), 0) < at[3]).astype(F32)
        mixed[...] = ((normed * gain[2:3] + shift[2:3]) * live).astype(BF)
        delta = cot[...].astype(F32) * live
        dlast = norm_backward(delta, normed, inverse, gain[2:3])
        dlast_out[...] = dlast
        low[...] = dlast.astype(BF)
        counted = counted_rows(at, half)
        sums[...] = stacked_sums(delta * normed * counted, delta * counted, dlast * counted)

    ins = [
        near(total),
        near(mine),
        near(other),
        near(cot, lambda ref, at: ref.at[rows_at(at[0], half), :]),
        near(bias),
        near(gain),
        near(shift),
    ]
    outs = [shape(half, width, dtype=BF), shape(half, width), shape(half, width, dtype=BF), shape(8, width)]
    return launch(body, "third_norm", at, ins, outs, us=2.5)


def feed_down(at, mine, other, f1, f2, slope):
    half, width = mine.shape
    units = f1.shape[1]

    def body(at, ins, outs, _):
        mine, other, f1, f2, slope = ins
        keep, send, dpre, sums = outs
        total = jnp.zeros((1, units), F32)
        for r, (x, target) in enumerate(((other, send), (mine, keep))):
            span = slice((1 - r) * half, (2 - r) * half)
            grad = mm(x[...], f2[...], NT) * slope[span, :]
            total = total + column_sum(grad)
            low = grad.astype(BF)
            dpre[span, :] = low
            target[...] = mm(low, f1[...], NT).astype(target.dtype)
        sums[...] = total

    ins = [near(a) for a in (mine, other, f1, f2, slope)]
    outs = [
        shape(half, width),
        shape(half, width, dtype=BF),
        shape(2 * half, units, dtype=BF),
        shape(1, units),
    ]
    return launch(body, "feed_down", at, ins, outs, us=3)


def second_back(at, dlast, mine, other, total, gain):
    half, width = mine.shape

    def body(at, ins, outs, _):
        dlast, mine, other, total, gain = ins
        dsecond, low, sums = outs
        dmid = dlast[...] + (mine[...].astype(F32) + other[...].astype(F32))
        normed, inverse = norm_stats(total[...])
        result = norm_backward(dmid, normed, inverse, gain[1:2])
        dsecond[...] = result
        low[...] = result.astype(BF)
        counted = counted_rows(at, half)
        sums[...] = stacked_sums(dmid * normed * counted, dmid * counted, result * counted)

    ins = [near(a) for a in (dlast, mine, other, total, gain)]
    outs = [shape(half, width), shape(half, width, dtype=BF), shape(8, width)]
    return launch(body, "second_back", at, ins, outs, us=1.8)


def gelu_pair(pre):
    phi = 0.5 * (1.0 + erf(pre * 0.7071067811865476))
    return (pre * phi).astype(BF), phi + pre * (jnp.exp(pre * pre * -0.5) * 0.3989422804014327)


def cross_backward(at, z_mine, z_other, raised, inverse, query, keys, values, w, wo, nh):
    half, width = z_mine.shape
    rows = 2 * half
    local = w.shape[1]
    hd = local // nh
    slots = keys.shape[1]
    scale = hd**-0.5

    def body(at, ins, outs, scratch):
        z_halves, (wo, inverse, values, raised, query, keys, w) = ins[:2], ins[2:]
        keep, send, dquery, dkv, sums = outs
        douts, right, found = scratch
        zero = jnp.zeros((half, hd), BF)
        head_sum = jnp.zeros((1, local), F32)
        for r in range(2):
            span = slice(r * half, (r + 1) * half)
            dhead = mm(z_halves[r][...], wo[...], NT)
            head_sum = head_sum + column_sum(dhead)
            scaled = query[span, :] * jnp.asarray(scale, BF)
            for h in range(nh):
                part = slice(h * hd, (h + 1) * hd)
                dout = (dhead[:, part] * inverse[h, span, 0:1]).astype(BF)
                douts[h, span, :] = jnp.concatenate([dout, dout], axis=1)
                right[h, 0, span, :] = jnp.concatenate([scaled[:, part], zero], axis=1)
                right[h, 1, span, :] = jnp.concatenate([zero, dout], axis=1)

        def one_head(h, _):
            grad = None
            for r in range(2):
                span = slice(r * half, (r + 1) * half)
                dprob = mm(douts[h, span, :], values[h], NT)
                low = raised[h, span, :]
                e = low.astype(F32)
                weighed = e * dprob
                mean = jnp.sum(weighed, axis=1, keepdims=True) * inverse[h, span, 0:1]
                dscore = (weighed - e * mean).astype(BF)
                both = mm(dscore, keys[h])
                found[h, span, :] = both[:, :hd] + both[:, hd:]
                part = mm(dscore, right[h, 0, span, :], TN) + mm(low, right[h, 1, span, :], TN)
                grad = part if grad is None else grad + part
            dkv[h] = grad.astype(BF)
            return 0

        lax.fori_loop(0, nh, one_head, 0)
        query_sum = jnp.zeros((1, local), F32)
        for r, target in enumerate((keep, send)):
            span = slice(r * half, (r + 1) * half)
            dq = jnp.concatenate([found[h, span, :] for h in range(nh)], axis=1) * scale
            query_sum = query_sum + column_sum(dq)
            dq_low = dq.astype(BF)
            dquery[span, :] = dq_low
            target[...] = mm(dq_low, w[0]).astype(target.dtype)
        sums[...] = jnp.concatenate([query_sum, head_sum], axis=0)

    return launch(
        body,
        "cross_bwd",
        at,
        [near(a) for a in (z_mine, z_other, wo, inverse, values, raised, query, keys, w)],
        [
            shape(half, width),
            shape(half, width, dtype=BF),
            shape(rows, local, dtype=BF),
            shape(nh, slots, 2 * hd, dtype=BF),
            shape(2, local),
        ],
        scratch=[
            pltpu.VMEM((nh, rows, 2 * hd), BF),
            pltpu.VMEM((nh, 2, rows, 2 * hd), BF),
            pltpu.VMEM((nh, rows, hd), F32),
        ],
        mib=30,
        us=11,
    )


def store_gradient(at, dkv, w, nh):
    _, slots, twice = dkv.shape
    _, local, width = w.shape
    hd = twice // 2
    seg = slots // 4

    def body(at, ins, outs, _):
        dkv, w = ins
        keep, send = outs
        weights = []
        for h in range(nh):
            part = slice(h * hd, (h + 1) * hd)
            weights += [w[1][part], w[2][part]]
        weight = jnp.concatenate(weights, axis=0)
        for slot in (1, 3, 0, 2):
            rows = jnp.concatenate([dkv[h, slot * seg : (slot + 1) * seg, :] for h in range(nh)], axis=1)
            part = mm(rows, weight)
            if slot % 2 == 0:
                keep[slot // 2] = part
            else:
                send[slot // 2] = part.astype(BF)

    return launch(
        body,
        "store_grad",
        at,
        [near(dkv), near(w)],
        [shape(2, seg, width), shape(2, seg, width, dtype=BF)],
        us=2.6,
    )


def group_outs(width, columns, blocks, extra=0):
    if not blocks:
        return [shape(width, columns)]
    n, r = blocks
    return [shape(n * r + 3 * extra, columns, dtype=BF), shape(n, r, columns)]


def emit_group(at, grad, outs, blocks, first, columns):
    if not blocks:
        outs[0][:, first : first + columns] = grad[...]
        return
    n, r = blocks
    span = slice(first, first + columns)
    for b in range(n):
        theirs = pl.ds(pl.multiple_of((2 * b + 1 - at[4]) * r, 8), r)
        outs[0][b * r : (b + 1) * r, span] = grad[theirs, :].astype(BF)
        outs[1][b, :, span] = grad[pl.ds(pl.multiple_of((2 * b + at[4]) * r, 8), r), :]


def turned_product(out, left, right, step=256):
    if left.shape[1] % step:
        out[...] = mm(left[...], right[...], TN)
        return

    def some(i, _):
        span = pl.ds(pl.multiple_of(i * step, step), step)
        out[span, :] = mm(left[:, span], right[...], TN)
        return 0

    lax.fori_loop(0, left.shape[1] // step, some, 0)


def feed_grads(at, mid_mine, mid_other, dpre, dlast_mine, dlast_other, hidden, blocks):
    half, width = mid_mine.shape
    units = dpre.shape[1]

    def body(at, ins, outs, scratch):
        mid_mine, mid_other, dpre, dlast_mine, dlast_other, hidden = ins
        left, grad = scratch
        for i, (mine, other, right) in enumerate(((mid_mine, mid_other, dpre), (dlast_mine, dlast_other, hidden))):
            left[:half, :] = mine[...]
            left[half:, :] = other[...]
            turned_product(grad, left, right)
            emit_group(at, grad, outs, blocks, i * units, units)

    return launch(
        body,
        "feed_grads",
        at,
        [near(a) for a in (mid_mine, mid_other, dpre, dlast_mine, dlast_other, hidden)],
        group_outs(width, 2 * units, blocks),
        scratch=[pltpu.VMEM((2 * half, width), BF), pltpu.VMEM((width, units), F32)],
        us=4,
    )


def cross_grads(at, z_mine, z_other, mine, other, dquery, heads, shards, dkv, nh, blocks):
    half, width = mine.shape
    local = dquery.shape[1]
    hd = local // nh
    seg = shards[0].shape[0]

    def body(at, ins, outs, scratch):
        shards, (z_mine, z_other, mine, other, dquery, heads, dkv) = ins[0:4], ins[4:]
        (grad,) = scratch
        grad[...] = mm(mine[...], dquery[:half], TN) + mm(other[...], dquery[half:], TN)
        emit_group(at, grad, outs, blocks, 0, local)
        grad[...] = mm(z_mine[...], heads[:half], TN) + mm(z_other[...], heads[half:], TN)
        emit_group(at, grad, outs, blocks, 3 * local, local)
        both = None
        for slot, block in enumerate(shards):
            rows = jnp.concatenate([dkv[h, slot * seg : (slot + 1) * seg, :] for h in range(nh)], axis=1)
            part = mm(block[...], rows, TN)
            both = part if both is None else both + part
        for i in range(2):
            grad[...] = jnp.concatenate([both[:, (2 * h + i) * hd : (2 * h + i + 1) * hd] for h in range(nh)], axis=1)
            emit_group(at, grad, outs, blocks, (1 + i) * local, local)

    return launch(
        body,
        "cross_grads",
        at,
        [near(a) for a in (*shards, z_mine, z_other, mine, other, dquery, heads, dkv)],
        group_outs(width, 4 * local, blocks),
        scratch=[pltpu.VMEM((width, local), F32)],
        us=4,
    )


def self_out_grads(at, mine, other, flat, small, blocks):
    half, width = mine.shape
    local = flat.shape[1]
    cuts = width // local

    def body(at, ins, outs, scratch):
        mine, other, flat, third_sums, second_sums, first_sums, fc1_sum, head_sums = ins
        (grad,) = scratch
        own, distant = flat[rows_at(at[0], half), :], flat[rows_at(1 - at[0], half), :]
        grad[...] = mm(mine[...], own, TN) + mm(other[...], distant, TN)
        emit_group(at, grad, outs, blocks, 0, local)
        line = jnp.concatenate([head_sums[0:1], head_sums[1:2], jnp.zeros((1, width - 2 * local), F32)], axis=1)
        small = jnp.concatenate(
            [third_sums[0:3], second_sums[0:3], first_sums[0:3], fc1_sum[...], line, jnp.zeros((EXTRA - 11, width), F32)],
            axis=0,
        )
        small = jnp.concatenate([small[:, i * local : (i + 1) * local] for i in range(cuts)], axis=0)
        outs[-1][...] = small
        if blocks:
            outs[0][blocks[0] * blocks[1] :, :] = three_terms(small)

    return launch(
        body,
        "self_out_grads",
        at,
        [near(a) for a in (mine, other, flat, *small)],
        group_outs(width, local, blocks, cuts * EXTRA) + [shape(cuts * EXTRA, local)],
        scratch=[pltpu.VMEM((width, local), F32)],
        us=1,
    )


def first_back(at, dsecond, mine, other, total, gain):
    half, width = mine.shape

    def body(at, ins, outs, _):
        dsecond, mine, other, total, gain = ins
        dfirst, low, sums = outs
        value = dsecond[...] + (mine[...].astype(F32) + other[...].astype(F32))
        normed, inverse = norm_stats(total[...])
        result = norm_backward(value, normed, inverse, gain[0:1])
        dfirst[...] = result
        low[...] = result.astype(BF)
        counted = counted_rows(at, half)
        sums[...] = stacked_sums(value * normed * counted, value * counted, result * counted)

    ins = [near(a) for a in (dsecond, mine, other, total, gain)]
    outs = [shape(half, width), shape(half, width, dtype=BF), shape(8, width)]
    return launch(body, "first_back", at, ins, outs, us=1.8)


def self_backward(at, mine, other, tokens, w, wo, qkv, prob, mixed, nh, blocks):
    half, width = mine.shape
    rows = 2 * half
    local = wo.shape[0]
    hd = local // nh
    scale = hd**-0.5

    def body(at, ins, outs, scratch):
        mine, other, wo, qkv, prob, tok, w, mixed = ins
        send, keep = outs[0:2]
        group, extra = outs[2:-1], outs[-1]
        z, dqkv, grad = scratch
        own, distant = rows_at(at[0], half), rows_at(1 - at[0], half)
        z[own, :] = mine[...]
        z[distant, :] = other[...]
        dself = mm(z[...], wo[...], NT).astype(BF)
        v, k, q = qkv[2], qkv[1], qkv[0]
        dq, dk, dv = [], [], []
        for h in range(nh):
            part = slice(h * hd, (h + 1) * hd)
            weights_low = prob[h]
            weights = weights_low.astype(F32)
            weighed = weights * mm(dself[:, part], v[:, part], NT)
            dscore = (weighed - weights * jnp.sum(weighed, axis=1, keepdims=True)).astype(BF)
            dq.append(mm(dscore, k[:, part]))
            dk.append(mm(dscore, q[:, part], TN))
            dv.append(mm(weights_low, dself[:, part], TN))
        dquery = jnp.concatenate(dq, axis=1) * scale
        dvalue = jnp.concatenate(dv, axis=1)
        dqkv[0] = dquery.astype(BF)
        dqkv[1] = (jnp.concatenate(dk, axis=1) * scale).astype(BF)
        dqkv[2] = dvalue.astype(BF)
        x = tok[...]
        for i in range(3):
            grad[...] = mm(x, dqkv[i], TN)
            emit_group(at, grad, group, blocks, i * local, local)
        line = jnp.concatenate([column_sum(dquery), column_sum(dvalue), jnp.zeros((1, local), F32)], axis=1)
        small = jnp.concatenate([line, jnp.zeros((EXTRA - 1, 3 * local), F32)], axis=0)
        extra[...] = small
        if blocks:
            group[0][blocks[0] * blocks[1] :, :] = three_terms(small)
        send[half:, :] = mixed[...]
        for place, out in ((distant, send), (own, keep)):
            total = mm(dqkv[0, place, :], w[0]) + mm(dqkv[1, place, :], w[1]) + mm(dqkv[2, place, :], w[2])
            out[0:half, :] = total.astype(out.dtype)

    return launch(
        body,
        "self_bwd",
        at,
        [near(a) for a in (mine, other, wo, qkv, prob, tokens, w, mixed)],
        [shape(2 * half, width, dtype=BF), shape(half, width)]
        + group_outs(width, 3 * local, blocks, EXTRA)
        + [shape(EXTRA, 3 * local)],
        scratch=[
            pltpu.VMEM((rows, width), BF),
            pltpu.VMEM((3, rows, local), BF),
            pltpu.VMEM((width, local), F32),
        ],
        mib=20,
        us=6,
    )


def add_stage(at, keep, got, small, bit):
    n, rows, columns = keep.shape
    tail = 0 if small is None else 3 * small.shape[0]
    reach = small.shape[1] if tail else 0

    def body(at, ins, outs, _):
        keep, got = ins[:2]
        mine = at[bit]
        send, stay = outs[:2]
        for b in range(n // 2):
            for chosen, out in ((1 - mine, send), (mine, stay)):
                block = 2 * b + chosen
                value = keep[block] + got[pl.ds(pl.multiple_of(block * rows, 8), rows), :].astype(F32)
                if out is send:
                    send[b * rows : (b + 1) * rows, :] = value.astype(BF)
                else:
                    stay[b] = value
        if tail:
            total = ins[2][...] + from_terms(got[n * rows :, 0:reach])
            outs[2][...] = total
            send[n // 2 * rows :, 0:reach] = three_terms(total)
            if reach < columns:
                send[n // 2 * rows :, reach:] = jnp.zeros((tail, columns - reach), BF)

    ins = [near(keep), near(got)] + ([near(small)] if tail else [])
    outs = [shape(n // 2 * rows + tail, columns, dtype=BF), shape(n // 2, rows, columns)]
    if tail:
        outs.append(shape(small.shape[0], reach))
    return launch(body, "add_stage", at, ins, outs, us=1)


def last_stage(at, keep, got, small, parts):
    _, rows, columns = keep.shape
    each = columns // sum(count for count, _ in parts)
    reach = 0 if small is None else small.shape[1]

    def body(at, ins, outs, _):
        total = ins[0][0] + ins[1][0:rows].astype(F32)
        first = 0
        for out, (count, turned) in zip(outs, parts):
            if count == 1:
                value = total[:, first * each : (first + 1) * each]
                out[...] = value.T if turned else value
            else:
                for i in range(count):
                    out[i] = total[:, (first + i) * each : (first + i + 1) * each]
            first += count
        if reach:
            outs[-1][...] = ins[2][...] + from_terms(ins[1][rows:, 0:reach])

    outs = []
    for count, turned in parts:
        dims = (rows, each) if count == 1 else (count, rows, each)
        outs.append(shape(*(dims[::-1] if turned else dims)))
    ins = [near(keep), near(got)]
    if reach:
        ins.append(near(small))
        outs.append(shape(small.shape[0], reach))
    return launch(body, "last_stage", at, ins, outs, us=1)


def join_halves(at, mine, other):
    half, width = mine.shape
    skip = other.shape[0] - half

    def body(at, ins, outs, _):
        outs[0][rows_at(at[0], half), :] = ins[0][...]
        outs[0][rows_at(1 - at[0], half), :] = ins[1][...]

    out = shape(2 * half, width, dtype=mine.dtype)
    ins = [near(mine), near(other, lambda ref, at: ref.at[pl.ds(skip, half), :])]
    return launch(body, "join_halves", at, ins, [out])[0]


def flip(bit, size):
    return [(i, i ^ bit) for i in range(size)]


def butterfly(value, axis, size):
    bit = 1
    while bit < size:
        value = value + lax.ppermute(value, axis, flip(bit, size))
        bit *= 2
    return value


def on_device(
    tokens,
    store,
    summary_length,
    top_index,
    cotangent,
    self_qkv_weight,
    self_qv_bias,
    self_out_weight,
    self_out_bias,
    qkv_weight,
    qv_bias,
    out_weight,
    out_bias,
    fc1_weight,
    fc1_bias,
    fc2_weight,
    fc2_bias,
    norm_gain,
    norm_shift,
):
    rows, width = tokens.shape
    half = rows // 2
    nh = top_index.shape[1]
    local = qkv_weight.shape[2]
    units = fc1_weight.shape[1]
    seg = store.shape[1]
    wide = lax.axis_size("wide")
    place = lax.axis_index("narrow")
    doc = lax.axis_index("wide")
    core, across = place % 2, place // 2
    at = jnp.stack([core, across, place, summary_length[0], doc % 2, doc // 2 % 2, doc // 4]).astype(jnp.int32)
    blocks = (wide // 2, width // wide) if wide == 8 else None
    row = lambda v: v.reshape(1, -1)
    self_w = jnp.swapaxes(self_qkv_weight, 1, 2)
    cross_w = jnp.swapaxes(qkv_weight, 1, 2)

    def to_core(v):
        return lax.ppermute(v, "narrow", CORE)

    def to_across(v):
        return lax.ppermute(v, "narrow", ACROSS)

    def over(v, bit):
        return lax.ppermute(v, "wide", flip(bit, wide))

    def chip_sum(keep, send):
        return (keep + to_core(send).astype(F32)).astype(BF)

    store_x = to_across(store[0])
    qkv, prob, flat, send, keep = self_forward(at, tokens, self_w, self_qv_bias, self_out_weight, nh)
    mine = chip_sum(keep, send)
    other = to_across(mine)
    index = index_rows(top_index)
    bias_mine = make_mask(tie(at, mine), index, top_index.shape, seg, 128, 0)
    store_x, store_own = tie((store_x, store[0]), bias_mine)
    shards = [store_own, to_core(store_own), store_x, to_core(store_x)]
    bias_other = make_mask(tie(at, bias_mine), index, top_index.shape, seg, 128, 1)
    other = tie(other, bias_other)
    first_total, after, after_low = first_norm(at, mine, other, tokens, row(self_out_bias), norm_gain, norm_shift)
    after_other = to_core(after_low)

    keys, values = keys_values(tie(at, after_low), shards, cross_w, nh)
    keep, send, raised, inverse, query, heads = cross_forward(
        tie(at, keys), after_low, after_other, bias_mine, bias_other, keys, values, cross_w, qv_bias, out_weight, nh
    )
    mine = chip_sum(keep, send)
    second_total, mid_low = second_norm(at, after, mine, to_across(mine), row(out_bias), norm_gain, norm_shift)
    mid_other = to_core(mid_low)

    keep, send, hidden, slope = feed_up(at, mid_low, mid_other, fc1_weight, fc2_weight, row(fc1_bias))
    mine = chip_sum(keep, send)
    mixed_half, dlast, dlast_low, third_sums = third_norm(
        at, second_total, mine, to_across(mine), cotangent, row(fc2_bias), norm_gain, norm_shift
    )
    dlast_other = to_core(dlast_low)
    keep, send, dpre, fc1_sum = feed_down(at, dlast_low, dlast_other, fc1_weight, fc2_weight, slope)
    mine = chip_sum(keep, send)
    other = to_across(mine)
    feed_out = feed_grads(tie(at, mine), mid_low, mid_other, dpre, dlast_low, dlast_other, hidden, blocks)
    other = tie(other, feed_out[0])
    dsecond, z, second_sums = second_back(at, dlast, mine, other, second_total, norm_gain)
    z_other = to_core(z)

    keep, send, dquery, dkv, cross_sums = cross_backward(
        at, z, z_other, raised, inverse, query, keys, values, cross_w, out_weight, nh
    )
    mine = chip_sum(keep, send)
    other = to_across(mine)
    if blocks:
        feed_got = tie(over(feed_out[0], 1), mine)
        feed_send, feed_keep = add_stage(tie(at, mine), feed_out[1], feed_got, None, 5)
        feed_next = over(feed_send, 2)
        started = feed_send
    else:
        started = mine
    cross_out = cross_grads(
        tie(at, started), z, z_other, after_low, after_other, dquery, heads, shards, dkv, nh, blocks
    )
    store_keep, store_send = store_gradient(tie(at, cross_out[0]), dkv, cross_w, nh)
    other = tie(other, store_send)
    dfirst, dfirst_low, first_sums = first_back(at, dsecond, mine, other, first_total, norm_gain)
    dfirst_other = to_core(dfirst_low)
    store_close = to_core(tie(store_send, dfirst_low))

    *first_out, early_small = self_out_grads(
        at, dfirst_low, dfirst_other, flat, (third_sums, second_sums, first_sums, fc1_sum, cross_sums), blocks
    )
    store_distant = to_across((store_keep[1] + tie(store_close, early_small)[1].astype(F32)).astype(BF))
    if blocks:
        feed_send, feed_keep = add_stage(tie(at, early_small), feed_keep, feed_next, None, 6)
        cross_send, cross_keep = add_stage(tie(at, feed_send), cross_out[1], over(cross_out[0], 1), None, 5)
        started = cross_send
    else:
        started = early_small
    send, keep, *self_out, self_small = self_backward(
        tie(at, started), dfirst_low, dfirst_other, tokens, self_w, self_out_weight, qkv, prob, mixed_half, nh, blocks
    )
    close = to_core(send)
    mine = (keep + close[:half].astype(F32)).astype(BF)
    tokens_half = dfirst + (mine.astype(F32) + to_across(mine).astype(F32))
    tokens_grad = join_halves(at, tokens_half, to_core(tokens_half))
    mixed = join_halves(at, mixed_half, close)
    store_grad = (store_keep[0] + store_close[0].astype(F32) + store_distant.astype(F32))[None]

    if blocks:
        first_send, first_keep, early_small = add_stage(
            tie(at, mine), first_out[1], over(first_out[0], 1), early_small, 5
        )
        self_send, self_keep, self_small = add_stage(
            tie(at, first_send), self_out[1], over(self_out[0], 1), self_small, 5
        )
        cross_send, cross_keep = add_stage(tie(at, self_send, tokens_half), cross_keep, over(cross_send, 2), None, 6)
        first_send, first_keep, early_small = add_stage(
            tie(at, cross_send), first_keep, over(first_send, 2), early_small, 6
        )
        self_send, self_keep, self_small = add_stage(
            tie(at, first_send), self_keep, over(self_send, 2), self_small, 6
        )
        fc1_grad, fc2_grad = last_stage(tie(at, self_send), feed_keep, over(feed_send, 4), None, [(1, False), (1, False)])
        fc2_grad = fc2_grad.T
        self_out_grad, early_small = last_stage(
            tie(at, fc1_grad), first_keep, over(first_send, 4), early_small, [(1, True)]
        )
        qkv_grad, out_grad = last_stage(
            tie(at, early_small), cross_keep, over(cross_send, 4), None, [(3, False), (1, True)]
        )
        self_qkv_grad, self_small = last_stage(
            tie(at, out_grad), self_keep, over(self_send, 4), self_small, [(3, False)]
        )
    else:
        scatter = functools.partial(lax.psum_scatter, axis_name="wide", tiled=True)
        parts = lambda g: jnp.stack([g[:, i * local : (i + 1) * local] for i in range(3)])
        fc1_grad = scatter(feed_out[0][:, :units], scatter_dimension=0)
        fc2_grad = scatter(feed_out[0][:, units:].T, scatter_dimension=1)
        qkv_grad = scatter(parts(cross_out[0]), scatter_dimension=1)
        out_grad = scatter(cross_out[0][:, 3 * local :].T, scatter_dimension=1)
        self_qkv_grad = scatter(parts(self_out[0]), scatter_dimension=1)
        self_out_grad = scatter(first_out[0].T, scatter_dimension=1)
        early_small = butterfly(early_small, "wide", wide)
        self_small = butterfly(self_small, "wide", wide)
    lines = jnp.concatenate(
        [early_small[i * EXTRA : (i + 1) * EXTRA] for i in range(width // local)], axis=1
    )
    summed = butterfly(lines[:9], "narrow", 4)
    gain_last, shift_last, fc2_b, gain_mid, shift_mid, out_b, gain_first, shift_first, self_out_b = (
        summed[i] for i in range(9)
    )
    return (
        mixed,
        tokens_grad,
        store_grad,
        self_qkv_grad,
        self_small[0, : 2 * local].reshape(2, local),
        self_out_grad,
        self_out_b,
        qkv_grad,
        lines[10, : 2 * local].reshape(2, local),
        out_grad,
        out_b,
        fc1_grad,
        lines[9],
        fc2_grad,
        fc2_b,
        jnp.stack([gain_first, gain_mid, gain_last]),
        jnp.stack([shift_first, shift_mid, shift_last]),
    )


def solution(mesh):
    placed = (
        P("wide", None),
        P("wide", "narrow", None),
        P("wide"),
        P("wide", "narrow", None, None),
        P("wide", None),
        P(None, None, "narrow"),
        P(None, "narrow"),
        P("narrow", None),
        P(),
        P(None, None, "narrow"),
        P(None, "narrow"),
        P("narrow", None),
        P(),
        P(None, "narrow"),
        P("narrow"),
        P("narrow", None),
        P(),
        P(),
        P(),
    )
    return jax.shard_map(
        on_device,
        mesh=mesh,
        in_specs=placed,
        out_specs=(
            P("wide", None),
            P("wide", None),
            P("wide", "narrow", None),
            P(None, "wide", "narrow"),
            P(None, "narrow"),
            P("narrow", "wide"),
            P(),
            P(None, "wide", "narrow"),
            P(None, "narrow"),
            P("narrow", "wide"),
            P(),
            P("wide", "narrow"),
            P("narrow"),
            P("narrow", "wide"),
            P(),
            P(),
            P(),
        ),
        check_vma=False,
    )
```

```python
import functools

import jax
import jax.numpy as jnp
from jax import lax
from jax.experimental import pallas as pl
from jax.experimental.pallas import tpu as pltpu
from jax.sharding import PartitionSpec as P

F32 = jnp.float32
BF = jnp.bfloat16
NN = (((1,), (0,)), ((), ()))
NT = (((1,), (1,)), ((), ()))
TN = (((0,), (0,)), ((), ()))
EPS = 1e-05
PACE = 1.1e8
SELF_MIB = 60
EXTRA = 16

CORE = [(i, i ^ 1) for i in range(4)]
ACROSS = [(i, i ^ 2) for i in range(4)]


def mm(left, right, dims=NN):
    return lax.dot_general(left, right, dims, preferred_element_type=F32)


def shape(*dims, dtype=F32):
    return jax.ShapeDtypeStruct(dims, dtype)


def tie(value, *earlier):
    return lax.optimization_barrier((value, *earlier))[0]


class Operand:
    def __init__(self, source, buffer, sems, first, parts):
        self.buffer = buffer
        self.parts = parts
        if parts:
            self.copies = [
                pltpu.make_async_copy(source.at[i], buffer.at[i], sems.at[first + i]) for i in range(buffer.shape[0])
            ]
        else:
            self.copies = [pltpu.make_async_copy(source, buffer, sems.at[first])]
        self.waited = [False] * len(self.copies)
        for copy in self.copies:
            copy.start()

    def ready(self, part=None):
        for i, copy in enumerate(self.copies):
            if not self.waited[i] and (part is None or i == part):
                copy.wait()
                self.waited[i] = True

    @property
    def shape(self):
        return self.buffer.shape

    def __getitem__(self, at):
        self.ready(at if self.parts and isinstance(at, int) else None)
        return self.buffer[at]


class Result:
    def __init__(self, target, buffer, sems, first, parts):
        self.buffer = buffer
        if parts:
            self.copies = [
                pltpu.make_async_copy(buffer.at[i], target.at[i], sems.at[first + i]) for i in range(buffer.shape[0])
            ]
        else:
            self.copies = [pltpu.make_async_copy(buffer, target, sems.at[first])]
        self.started = [False] * len(self.copies)

    @property
    def shape(self):
        return self.buffer.shape

    @property
    def dtype(self):
        return self.buffer.dtype

    def __setitem__(self, at, value):
        self.buffer[at] = value

    def flush(self, part=0):
        self.copies[part].start()
        self.started[part] = True

    def finish(self):
        for i in range(len(self.copies)):
            if not self.started[i]:
                self.flush(i)
        for copy in self.copies:
            copy.wait()


def far(array, take=None, dims=None, parts=False):
    return ("far", array, take, tuple(dims or array.shape), parts)


def near(array, take=None):
    return ("near", array, take, None, False)


def raw(array):
    return ("raw", array, None, None, False)


def launch(body, name, at, ins, outs, scratch=(), mib=16, us=2.0):
    in_specs = [pl.BlockSpec(memory_space=pltpu.SMEM)]
    buffers, n_in, n_out = [], 0, 0
    for kind, array, _, dims, parts in ins:
        in_specs.append(pl.BlockSpec(memory_space=pltpu.VMEM if kind == "near" else pltpu.HBM))
        if kind == "far":
            buffers.append(pltpu.VMEM(dims, array.dtype))
            n_in += dims[0] if parts else 1
    out_specs, structs = [], []
    for out in outs:
        if isinstance(out, tuple):
            struct, parts = out
            out_specs.append(pl.BlockSpec(memory_space=pltpu.HBM))
            buffers.append(pltpu.VMEM(struct.shape, struct.dtype))
            n_out += struct.shape[0] if parts else 1
        else:
            struct = out
            out_specs.append(pl.BlockSpec(memory_space=pltpu.VMEM))
        structs.append(struct)
    n_buffers = len(buffers)
    sems = [pltpu.SemaphoreType.DMA((max(n, 1),)) for n in (n_in, n_out)]

    def kernel(at_ref, *refs):
        in_refs, out_refs = refs[: len(ins)], refs[len(ins) : len(ins) + len(outs)]
        rest = refs[len(ins) + len(outs) :]
        bufs, user, (in_sems, out_sems) = list(rest[:n_buffers]), rest[n_buffers:-2], rest[-2:]
        place, given = 0, []
        for ref, (kind, _, take, dims, parts) in zip(in_refs, ins):
            source = take(ref, at_ref) if take else ref
            if kind == "far":
                given.append(Operand(source, bufs.pop(0), in_sems, place, parts))
                place += dims[0] if parts else 1
            else:
                given.append(source)
        place, results = 0, []
        for ref, out in zip(out_refs, outs):
            if isinstance(out, tuple):
                results.append(Result(ref, bufs.pop(0), out_sems, place, out[1]))
                place += out[0].shape[0] if out[1] else 1
            else:
                results.append(ref)
        body(at_ref, given, results, user)
        for operand in given:
            if isinstance(operand, Operand):
                operand.ready()
        for result in results:
            if isinstance(result, Result):
                result.finish()

    return pl.pallas_call(
        kernel,
        in_specs=in_specs,
        out_specs=out_specs,
        out_shape=structs,
        scratch_shapes=buffers + list(scratch) + sems,
        compiler_params=pltpu.CompilerParams(vmem_limit_bytes=mib << 20),
        cost_estimate=pl.CostEstimate(flops=int(us * PACE), bytes_accessed=1000, transcendentals=0),
        name=name,
    )(at, *[entry[1] for entry in ins])


def norm_stats(value):
    centre = value - jnp.mean(value, axis=-1, keepdims=True)
    spread = jnp.mean(centre * centre, axis=-1, keepdims=True)
    inverse = lax.rsqrt(spread + EPS)
    return centre * inverse, inverse


def norm_backward(grad, normed, inverse, gain):
    scaled = grad * gain
    centred = scaled - jnp.mean(scaled, axis=-1, keepdims=True)
    return inverse * (centred - normed * jnp.mean(scaled * normed, axis=-1, keepdims=True))


def column_sum(value):
    return jnp.sum(value, axis=0, keepdims=True)


def erf(value):
    x = jnp.clip(value, -4.0, 4.0)
    y = x * x
    top = jnp.full_like(y, -2.72614225801306e-10)
    for factor in (
        2.77068142495902e-08,
        -2.10102402082508e-06,
        -5.69250639462346e-05,
        -7.34990630326855e-04,
        -2.95459980854025e-03,
        -1.60960333262415e-02,
    ):
        top = top * y + factor
    low = jnp.full_like(y, -1.45660718464996e-05)
    for factor in (
        -2.13374055278905e-04,
        -1.68282697438203e-03,
        -7.37332916720468e-03,
        -1.42647390514189e-02,
    ):
        low = low * y + factor
    return x * top / low


def three_terms(value):
    high = value.astype(BF)
    rest = value - high.astype(F32)
    middle = rest.astype(BF)
    return jnp.concatenate([high, middle, (rest - middle.astype(F32)).astype(BF)], axis=0)


def from_terms(stacked):
    rows = stacked.shape[0] // 3
    terms = stacked.astype(F32)
    return terms[:rows] + terms[rows : 2 * rows] + terms[2 * rows :]


def rows_at(place, rows):
    return pl.ds(pl.multiple_of(place * rows, rows), rows)


def self_forward(at, tokens, w, b, wo, nh):
    rows, width = tokens.shape
    local = w.shape[1]
    half = rows // 2
    hd = local // nh
    scale = hd**-0.5

    def body(at, ins, outs, _):
        tok, w, wo, b = ins
        qkv, prob, flat, send, keep = outs
        x = tok[...]
        q = (mm(x, w[0], NT) + b[0:1]).astype(BF)
        k = mm(x, w[1], NT).astype(BF)
        v = (mm(x, w[2], NT) + b[1:2]).astype(BF)
        for i, value in enumerate((q, k, v)):
            qkv[i] = value
            qkv.flush(i)
        row_ids = lax.broadcasted_iota(jnp.int32, (rows, rows), 0)
        key_ids = lax.broadcasted_iota(jnp.int32, (rows, rows), 1)
        allowed = (key_ids <= row_ids) & (key_ids < at[3])
        found = []
        for h in range(nh):
            part = slice(h * hd, (h + 1) * hd)
            scores = mm(q[:, part], k[:, part], NT) * scale
            scores = jnp.where(allowed, scores, -1e30)
            shifted = jnp.exp(scores - jnp.max(scores, axis=1, keepdims=True))
            weights = (shifted * (1.0 / jnp.sum(shifted, axis=1, keepdims=True))).astype(BF)
            prob[h] = weights
            prob.flush(h)
            found.append(mm(weights, v[:, part]).astype(BF))
        flat[...] = jnp.concatenate(found, axis=1)
        flat.flush()
        send[...] = mm(flat.buffer[rows_at(1 - at[0], half), :], wo[...]).astype(BF)
        send.flush()
        keep[...] = mm(flat.buffer[rows_at(at[0], half), :], wo[...])

    return launch(
        body,
        "self_fwd",
        at,
        [far(tokens), far(w, parts=True), far(wo), far(b)],
        [
            (shape(3, rows, local, dtype=BF), True),
            (shape(nh, rows, rows, dtype=BF), True),
            (shape(rows, local, dtype=BF), False),
            (shape(half, width, dtype=BF), False),
            (shape(half, width), False),
        ],
        mib=SELF_MIB,
        us=4,
    )


def first_norm(at, mine, other, tokens, bias, gain, shift):
    half, width = mine.shape

    def body(at, ins, outs, _):
        mine, other, tok, bias, gain, shift = ins
        total, after, low = outs
        value = tok[...].astype(F32) + (mine[...].astype(F32) + other[...].astype(F32)) + bias[...]
        total[...] = value
        normed, _ = norm_stats(value)
        result = normed * gain[0:1] + shift[0:1]
        after[...] = result
        low[...] = result.astype(BF)

    return launch(
        body,
        "first_norm",
        at,
        [
            near(mine),
            near(other),
            near(tokens, lambda ref, at: ref.at[rows_at(at[0], half), :]),
            near(bias),
            near(gain),
            near(shift),
        ],
        [shape(half, width), shape(half, width), shape(half, width, dtype=BF)],
        us=1.7,
    )


def index_rows(top_index):
    rows, nh, ns, keep = top_index.shape
    flat = top_index.reshape(rows, nh, ns, keep // 128, 128).transpose(0, 1, 3, 2, 4)
    return flat.reshape(rows * nh * ns * (keep // 128), 128)


def make_mask(at, flat, dims, seg, tile, turn):
    rows, nh, ns, keep = dims
    halves = keep // 128
    per_row = nh * ns * halves
    tiles = rows // 2 // tile
    columns = ns * seg
    blocks = columns // 128
    group = 32

    def body(at, ins, outs, _):
        (index,) = ins
        (bias,) = outs
        lane = lax.broadcasted_iota(jnp.int32, (group, 128), 1).astype(F32)
        lane_low = lane.astype(BF)
        empty = jnp.full((group, 128), -1.0, BF)
        own = at[2]
        steps = []
        step = 1
        while step <= seg - keep:
            steps.insert(0, step)
            step *= 2
        turns = steps + [(seg * s) % 128 for s in range(ns)]
        below = {s: lane_low < jnp.asarray(s, BF) for s in turns if 0 < s < 128}

        for t in range(tiles):
            index.ready(t)
            source = index.buffer.at[t]

            def one_group(g, _):
                for h in range(nh):
                    v = [empty] * blocks
                    for slot in range(ns):
                        first, turn = divmod(seg * slot, 128)
                        for c in range(halves):
                            start = g * (group * per_row) + h * ns * halves + c * ns + (own ^ slot)
                            found = jnp.concatenate(
                                [source[pl.ds(start + q * 8 * per_row, 8, stride=per_row), :] for q in range(group // 8)],
                                axis=0,
                            )
                            ahead = (found.astype(F32) - (lane + float(128 * c))).astype(BF)
                            at_block = first + c
                            if turn == 0:
                                v[at_block] = ahead
                            else:
                                turned = pltpu.roll(ahead, turn, axis=1)
                                v[at_block] = jnp.where(below[turn], v[at_block], turned)
                                v[at_block + 1] = jnp.where(below[turn], turned, v[at_block + 1])
                    for s in steps:
                        gap = jnp.asarray(s, BF)
                        moved = [x - gap for x in v]
                        stay = [jnp.where(x >= gap, empty, x) for x in v]
                        if s % 128 == 0:
                            hop = s // 128
                            v = stay[:hop] + [jnp.maximum(stay[i], moved[i - hop]) for i in range(hop, blocks)]
                        else:
                            turned = [pltpu.roll(x, s, axis=1) for x in moved]
                            v = [
                                jnp.maximum(stay[i], jnp.where(below[s], turned[i - 1], turned[i])) for i in range(blocks)
                            ]
                    for i in range(blocks):
                        bias[h, pl.ds(pl.multiple_of(t * tile + g * group, group), group), i * 128 : (i + 1) * 128] = v[
                            i
                        ] * jnp.asarray(1e30, BF)
                return 0

            lax.fori_loop(0, tile // group, one_group, 0)

    flat = flat.reshape(2 * tiles, tile * per_row, 128)
    return launch(
        body,
        "mask",
        at,
        [
            far(
                flat,
                lambda ref, at: ref.at[pl.ds((at[0] ^ turn) * tiles, tiles)],
                (tiles, tile * per_row, 128),
                parts=True,
            )
        ],
        [shape(nh, rows // 2, columns, dtype=BF)],
        us=10,
    )[0]


def keys_values(at, shards, w, nh):
    seg, width = shards[0].shape
    local = w.shape[1]
    hd = local // nh

    def body(at, ins, outs, _):
        for slot in range(4):
            x = ins[slot][...]
            span = slice(slot * seg, (slot + 1) * seg)
            for i, out in enumerate(outs):
                full = mm(x, ins[4][i + 1], NT)
                high = full.astype(BF)
                low = (full - high.astype(F32)).astype(BF)
                for h in range(nh):
                    part = slice(h * hd, (h + 1) * hd)
                    out[h, span, :] = jnp.concatenate([high[:, part], low[:, part]], axis=1)

    out = shape(nh, 4 * seg, 2 * hd, dtype=BF)
    return launch(body, "keys_values", at, [near(s) for s in shards] + [near(w)], [out, out], us=2)


def cross_forward(at, mine, other, bias_mine, bias_other, keys, values, w, b, wo, nh):
    half, width = mine.shape
    rows = 2 * half
    local = w.shape[1]
    hd = local // nh
    slots = keys.shape[1]
    scale = hd**-0.5

    def body(at, ins, outs, scratch):
        mine, other, wq, keys, bias_mine, bias_other, values, wo, b = ins
        keep, send, raised, inverse, query, heads = outs
        twice, found = scratch
        for r, x in enumerate((mine, other)):
            q = (mm(x[...], wq[0], NT) + b[0:1]).astype(BF)
            query[r * half : (r + 1) * half, :] = q
            scaled = q * jnp.asarray(scale, BF)
            for h in range(nh):
                part = scaled[:, h * hd : (h + 1) * hd]
                twice[h, r * half : (r + 1) * half, :] = jnp.concatenate([part, part], axis=1)

        def one_head(h, _):
            for r, bias in enumerate((bias_mine, bias_other)):
                span = slice(r * half, (r + 1) * half)
                scores = mm(twice[h, span, :], keys[h], NT) + bias[h].astype(F32)
                e = jnp.exp(scores - jnp.max(scores, axis=1, keepdims=True))
                total = 1.0 / jnp.sum(e, axis=1, keepdims=True)
                low = e.astype(BF)
                raised[h, span, :] = low
                inverse[h, span, :] = jnp.broadcast_to(total, (half, 128))
                both = mm(low, values[h])
                found[h, span, :] = (both[:, :hd] + both[:, hd:]) * total
            return 0

        lax.fori_loop(0, nh, one_head, 0)
        for r, target in enumerate((keep, send)):
            span = slice(r * half, (r + 1) * half)
            out = (jnp.concatenate([found[h, span, :] for h in range(nh)], axis=1) + b[1:2]).astype(BF)
            heads[span, :] = out
            target[...] = mm(out, wo[...]).astype(target.dtype)

    return launch(
        body,
        "cross_fwd",
        at,
        [near(a) for a in (mine, other, w, keys, bias_mine, bias_other, values, wo, b)],
        [
            shape(half, width),
            shape(half, width, dtype=BF),
            shape(nh, rows, slots, dtype=BF),
            shape(nh, rows, 128),
            shape(rows, local, dtype=BF),
            shape(rows, local, dtype=BF),
        ],
        scratch=[pltpu.VMEM((nh, rows, 2 * hd), BF), pltpu.VMEM((nh, rows, hd), F32)],
        mib=30,
        us=9,
    )


def counted_rows(at, half):
    rows = half // 2
    place = lax.broadcasted_iota(jnp.int32, (half, 1), 0)
    return ((place >= at[1] * rows) & (place < (at[1] + 1) * rows)).astype(F32)


def stacked_sums(*values):
    sums = [column_sum(value) for value in values]
    return jnp.concatenate(sums + [jnp.zeros((8 - len(sums), values[0].shape[1]), F32)], axis=0)


def second_norm(at, after, mine, other, bias, gain, shift):
    half, width = mine.shape

    def body(at, ins, outs, _):
        after, mine, other, bias, gain, shift = ins
        total, low = outs
        value = after[...] + (mine[...].astype(F32) + other[...].astype(F32)) + bias[...]
        total[...] = value
        normed, _ = norm_stats(value)
        low[...] = (normed * gain[1:2] + shift[1:2]).astype(BF)

    ins = [near(a) for a in (after, mine, other, bias, gain, shift)]
    return launch(body, "second_norm", at, ins, [shape(half, width), shape(half, width, dtype=BF)], us=1.5)


def feed_up(at, mine, other, f1, f2, b1):
    half, width = mine.shape
    units = f1.shape[1]

    def body(at, ins, outs, _):
        mine, other, f1, f2, b1 = ins
        keep, send, hidden, slope = outs
        for r, (x, target) in enumerate(((other, send), (mine, keep))):
            span = slice((1 - r) * half, (2 - r) * half)
            low, steep = gelu_pair(mm(x[...], f1[...]) + b1[...])
            hidden[span, :] = low
            slope[span, :] = steep
            target[...] = mm(low, f2[...]).astype(target.dtype)

    ins = [near(a) for a in (mine, other, f1, f2, b1)]
    outs = [
        shape(half, width),
        shape(half, width, dtype=BF),
        shape(2 * half, units, dtype=BF),
        shape(2 * half, units),
    ]
    return launch(body, "feed_up", at, ins, outs, us=4)


def third_norm(at, total, mine, other, cot, bias, gain, shift):
    half, width = mine.shape

    def body(at, ins, outs, _):
        total, mine, other, cot, bias, gain, shift = ins
        mixed, dlast_out, low, sums = outs
        normed_mid, _ = norm_stats(total[...])
        last = normed_mid * gain[1:2] + shift[1:2] + (mine[...].astype(F32) + other[...].astype(F32)) + bias[...]
        normed, inverse = norm_stats(last)
        first_row = at[0] * half
        live = (first_row + lax.broadcasted_iota(jnp.int32, (half, 1), 0) < at[3]).astype(F32)
        mixed[...] = ((normed * gain[2:3] + shift[2:3]) * live).astype(BF)
        delta = cot[...].astype(F32) * live
        dlast = norm_backward(delta, normed, inverse, gain[2:3])
        dlast_out[...] = dlast
        low[...] = dlast.astype(BF)
        counted = counted_rows(at, half)
        sums[...] = stacked_sums(delta * normed * counted, delta * counted, dlast * counted)

    ins = [
        near(total),
        near(mine),
        near(other),
        near(cot, lambda ref, at: ref.at[rows_at(at[0], half), :]),
        near(bias),
        near(gain),
        near(shift),
    ]
    outs = [shape(half, width, dtype=BF), shape(half, width), shape(half, width, dtype=BF), shape(8, width)]
    return launch(body, "third_norm", at, ins, outs, us=2.5)


def feed_down(at, mine, other, f1, f2, slope):
    half, width = mine.shape
    units = f1.shape[1]

    def body(at, ins, outs, _):
        mine, other, f1, f2, slope = ins
        keep, send, dpre, sums = outs
        total = jnp.zeros((1, units), F32)
        for r, (x, target) in enumerate(((other, send), (mine, keep))):
            span = slice((1 - r) * half, (2 - r) * half)
            grad = mm(x[...], f2[...], NT) * slope[span, :]
            total = total + column_sum(grad)
            low = grad.astype(BF)
            dpre[span, :] = low
            target[...] = mm(low, f1[...], NT).astype(target.dtype)
        sums[...] = total

    ins = [near(a) for a in (mine, other, f1, f2, slope)]
    outs = [
        shape(half, width),
        shape(half, width, dtype=BF),
        shape(2 * half, units, dtype=BF),
        shape(1, units),
    ]
    return launch(body, "feed_down", at, ins, outs, us=3)


def second_back(at, dlast, mine, other, total, gain):
    half, width = mine.shape

    def body(at, ins, outs, _):
        dlast, mine, other, total, gain = ins
        dsecond, low, sums = outs
        dmid = dlast[...] + (mine[...].astype(F32) + other[...].astype(F32))
        normed, inverse = norm_stats(total[...])
        result = norm_backward(dmid, normed, inverse, gain[1:2])
        dsecond[...] = result
        low[...] = result.astype(BF)
        counted = counted_rows(at, half)
        sums[...] = stacked_sums(dmid * normed * counted, dmid * counted, result * counted)

    ins = [near(a) for a in (dlast, mine, other, total, gain)]
    outs = [shape(half, width), shape(half, width, dtype=BF), shape(8, width)]
    return launch(body, "second_back", at, ins, outs, us=1.8)


def gelu_pair(pre):
    phi = 0.5 * (1.0 + erf(pre * 0.7071067811865476))
    return (pre * phi).astype(BF), phi + pre * (jnp.exp(pre * pre * -0.5) * 0.3989422804014327)


def cross_backward(at, z_mine, z_other, raised, inverse, query, keys, values, w, wo, nh):
    half, width = z_mine.shape
    rows = 2 * half
    local = w.shape[1]
    hd = local // nh
    slots = keys.shape[1]
    scale = hd**-0.5

    def body(at, ins, outs, scratch):
        z_halves, (wo, inverse, values, raised, query, keys, w) = ins[:2], ins[2:]
        keep, send, dquery, dkv, sums = outs
        douts, right, found = scratch
        zero = jnp.zeros((half, hd), BF)
        head_sum = jnp.zeros((1, local), F32)
        for r in range(2):
            span = slice(r * half, (r + 1) * half)
            dhead = mm(z_halves[r][...], wo[...], NT)
            head_sum = head_sum + column_sum(dhead)
            scaled = query[span, :] * jnp.asarray(scale, BF)
            for h in range(nh):
                part = slice(h * hd, (h + 1) * hd)
                dout = (dhead[:, part] * inverse[h, span, 0:1]).astype(BF)
                douts[h, span, :] = jnp.concatenate([dout, dout], axis=1)
                right[h, 0, span, :] = jnp.concatenate([scaled[:, part], zero], axis=1)
                right[h, 1, span, :] = jnp.concatenate([zero, dout], axis=1)

        def one_head(h, _):
            grad = None
            for r in range(2):
                span = slice(r * half, (r + 1) * half)
                dprob = mm(douts[h, span, :], values[h], NT)
                low = raised[h, span, :]
                e = low.astype(F32)
                weighed = e * dprob
                mean = jnp.sum(weighed, axis=1, keepdims=True) * inverse[h, span, 0:1]
                dscore = (weighed - e * mean).astype(BF)
                both = mm(dscore, keys[h])
                found[h, span, :] = both[:, :hd] + both[:, hd:]
                part = mm(dscore, right[h, 0, span, :], TN) + mm(low, right[h, 1, span, :], TN)
                grad = part if grad is None else grad + part
            dkv[h] = grad.astype(BF)
            return 0

        lax.fori_loop(0, nh, one_head, 0)
        query_sum = jnp.zeros((1, local), F32)
        for r, target in enumerate((keep, send)):
            span = slice(r * half, (r + 1) * half)
            dq = jnp.concatenate([found[h, span, :] for h in range(nh)], axis=1) * scale
            query_sum = query_sum + column_sum(dq)
            dq_low = dq.astype(BF)
            dquery[span, :] = dq_low
            target[...] = mm(dq_low, w[0]).astype(target.dtype)
        sums[...] = jnp.concatenate([query_sum, head_sum], axis=0)

    return launch(
        body,
        "cross_bwd",
        at,
        [near(a) for a in (z_mine, z_other, wo, inverse, values, raised, query, keys, w)],
        [
            shape(half, width),
            shape(half, width, dtype=BF),
            shape(rows, local, dtype=BF),
            shape(nh, slots, 2 * hd, dtype=BF),
            shape(2, local),
        ],
        scratch=[
            pltpu.VMEM((nh, rows, 2 * hd), BF),
            pltpu.VMEM((nh, 2, rows, 2 * hd), BF),
            pltpu.VMEM((nh, rows, hd), F32),
        ],
        mib=30,
        us=11,
    )


def store_gradient(at, dkv, w, nh):
    _, slots, twice = dkv.shape
    _, local, width = w.shape
    hd = twice // 2
    seg = slots // 4

    def body(at, ins, outs, _):
        dkv, w = ins
        keep, send = outs
        weights = []
        for h in range(nh):
            part = slice(h * hd, (h + 1) * hd)
            weights += [w[1][part], w[2][part]]
        weight = jnp.concatenate(weights, axis=0)
        for slot in (1, 3, 0, 2):
            rows = jnp.concatenate([dkv[h, slot * seg : (slot + 1) * seg, :] for h in range(nh)], axis=1)
            part = mm(rows, weight)
            if slot % 2 == 0:
                keep[slot // 2] = part
            else:
                send[slot // 2] = part.astype(BF)

    return launch(
        body,
        "store_grad",
        at,
        [near(dkv), near(w)],
        [shape(2, seg, width), shape(2, seg, width, dtype=BF)],
        us=2.6,
    )


def group_outs(width, columns, blocks, extra=0):
    if not blocks:
        return [shape(width, columns)]
    n, r = blocks
    return [shape(n * r + 3 * extra, columns, dtype=BF), shape(n, r, columns)]


def emit_group(at, grad, outs, blocks, first, columns, kept_first=None):
    if not blocks:
        outs[0][:, first : first + columns] = grad[...]
        return
    n, r = blocks
    kept_first = first if kept_first is None else kept_first
    span, kept = slice(first, first + columns), slice(kept_first, kept_first + columns)
    for b in range(n):
        theirs = pl.ds(pl.multiple_of((2 * b + 1 - at[4]) * r, 8), r)
        outs[0][b * r : (b + 1) * r, span] = grad[theirs, :].astype(BF)
        outs[1][b, :, kept] = grad[pl.ds(pl.multiple_of((2 * b + at[4]) * r, 8), r), :]


def turned_product(out, left, right, step=256):
    if left.shape[1] % step:
        out[...] = mm(left[...], right[...], TN)
        return

    def some(i, _):
        span = pl.ds(pl.multiple_of(i * step, step), step)
        out[span, :] = mm(left[:, span], right[...], TN)
        return 0

    lax.fori_loop(0, left.shape[1] // step, some, 0)


def feed_grads(at, mid_mine, mid_other, dpre, dlast_mine, dlast_other, hidden, blocks):
    half, width = mid_mine.shape
    units = dpre.shape[1]
    if blocks:
        n, r = blocks
        structs = [shape(n * r, 2 * units, dtype=BF), shape(n, r, 2 * units)]
    else:
        structs = [shape(width, units), shape(width, units)]

    def body(at, ins, outs, scratch):
        mid_mine, mid_other, dpre, dlast_mine, dlast_other, hidden = ins
        left, grad = scratch
        for i, (mine, other, right) in enumerate(((mid_mine, mid_other, dpre), (dlast_mine, dlast_other, hidden))):
            left[:half, :] = mine[...]
            left[half:, :] = other[...]
            turned_product(grad, left, right)
            emit_group(at, grad, outs if blocks else outs[i:], blocks, i * units if blocks else 0, units)

    return launch(
        body,
        "feed_grads",
        at,
        [near(a) for a in (mid_mine, mid_other, dpre, dlast_mine, dlast_other, hidden)],
        structs,
        scratch=[pltpu.VMEM((2 * half, width), BF), pltpu.VMEM((width, units), F32)],
        us=4,
    )


def cross_grads(at, z_mine, z_other, mine, other, dquery, heads, shards, dkv, nh, blocks):
    half, width = mine.shape
    local = dquery.shape[1]
    hd = local // nh
    seg = shards[0].shape[0]

    def body(at, ins, outs, scratch):
        shards, (z_mine, z_other, mine, other, dquery, heads, dkv) = ins[0:4], ins[4:]
        (grad,) = scratch
        grad[...] = mm(mine[...], dquery[:half], TN) + mm(other[...], dquery[half:], TN)
        emit_group(at, grad, outs, blocks, 0, local)
        grad[...] = mm(z_mine[...], heads[:half], TN) + mm(z_other[...], heads[half:], TN)
        emit_group(at, grad, outs, blocks, 3 * local, local)
        both = None
        for slot, block in enumerate(shards):
            rows = jnp.concatenate([dkv[h, slot * seg : (slot + 1) * seg, :] for h in range(nh)], axis=1)
            part = mm(block[...], rows, TN)
            both = part if both is None else both + part
        for i in range(2):
            grad[...] = jnp.concatenate([both[:, (2 * h + i) * hd : (2 * h + i + 1) * hd] for h in range(nh)], axis=1)
            emit_group(at, grad, outs, blocks, (1 + i) * local, local)

    return launch(
        body,
        "cross_grads",
        at,
        [near(a) for a in (*shards, z_mine, z_other, mine, other, dquery, heads, dkv)],
        group_outs(width, 4 * local, blocks),
        scratch=[pltpu.VMEM((width, local), F32)],
        us=4,
    )


def self_out_grads(at, mine, other, flat, small, blocks):
    half, width = mine.shape
    local = flat.shape[1]
    cuts = width // local

    def body(at, ins, outs, scratch):
        mine, other, flat, third_sums, second_sums, first_sums, fc1_sum, head_sums = ins
        (grad,) = scratch
        own, distant = flat[rows_at(at[0], half), :], flat[rows_at(1 - at[0], half), :]
        grad[...] = mm(mine[...], own, TN) + mm(other[...], distant, TN)
        emit_group(at, grad, outs, blocks, 0, local)
        line = jnp.concatenate([head_sums[0:1], head_sums[1:2], jnp.zeros((1, width - 2 * local), F32)], axis=1)
        small = jnp.concatenate(
            [third_sums[0:3], second_sums[0:3], first_sums[0:3], fc1_sum[...], line, jnp.zeros((EXTRA - 11, width), F32)],
            axis=0,
        )
        small = jnp.concatenate([small[:, i * local : (i + 1) * local] for i in range(cuts)], axis=0)
        outs[-1][...] = small
        if blocks:
            outs[0][blocks[0] * blocks[1] :, :] = three_terms(small)

    return launch(
        body,
        "self_out_grads",
        at,
        [near(a) for a in (mine, other, flat, *small)],
        group_outs(width, local, blocks, cuts * EXTRA) + [shape(cuts * EXTRA, local)],
        scratch=[pltpu.VMEM((width, local), F32)],
        us=1,
    )


def first_back(at, dsecond, mine, other, total, gain):
    half, width = mine.shape

    def body(at, ins, outs, _):
        dsecond, mine, other, total, gain = ins
        dfirst, low, sums = outs
        value = dsecond[...] + (mine[...].astype(F32) + other[...].astype(F32))
        normed, inverse = norm_stats(total[...])
        result = norm_backward(value, normed, inverse, gain[0:1])
        dfirst[...] = result
        low[...] = result.astype(BF)
        counted = counted_rows(at, half)
        sums[...] = stacked_sums(value * normed * counted, value * counted, result * counted)

    ins = [near(a) for a in (dsecond, mine, other, total, gain)]
    outs = [shape(half, width), shape(half, width, dtype=BF), shape(8, width)]
    return launch(body, "first_back", at, ins, outs, us=1.8)


def self_backward(at, mine, other, tokens, w, wo, qkv, prob, mixed, nh, blocks):
    half, width = mine.shape
    rows = 2 * half
    local = wo.shape[0]
    hd = local // nh
    scale = hd**-0.5

    def body(at, ins, outs, scratch):
        mine, other, wo, qkv, prob, tok, w, mixed = ins
        send, keep = outs[0:2]
        group, extra = outs[2:-1], outs[-1]
        z, dqkv, grad = scratch
        own, distant = rows_at(at[0], half), rows_at(1 - at[0], half)
        z[own, :] = mine[...]
        z[distant, :] = other[...]
        dself = mm(z[...], wo[...], NT).astype(BF)
        v, k, q = qkv[2], qkv[1], qkv[0]
        dq, dk, dv = [], [], []
        for h in range(nh):
            part = slice(h * hd, (h + 1) * hd)
            weights_low = prob[h]
            weights = weights_low.astype(F32)
            weighed = weights * mm(dself[:, part], v[:, part], NT)
            dscore = (weighed - weights * jnp.sum(weighed, axis=1, keepdims=True)).astype(BF)
            dq.append(mm(dscore, k[:, part]))
            dk.append(mm(dscore, q[:, part], TN))
            dv.append(mm(weights_low, dself[:, part], TN))
        dquery = jnp.concatenate(dq, axis=1) * scale
        dvalue = jnp.concatenate(dv, axis=1)
        dqkv[0] = dquery.astype(BF)
        dqkv[1] = (jnp.concatenate(dk, axis=1) * scale).astype(BF)
        dqkv[2] = dvalue.astype(BF)
        x = tok[...]
        for i in range(3):
            grad[...] = mm(x, dqkv[i], TN)
            emit_group(at, grad, group, blocks, i * local, local)
        line = jnp.concatenate([column_sum(dquery), column_sum(dvalue), jnp.zeros((1, local), F32)], axis=1)
        small = jnp.concatenate([line, jnp.zeros((EXTRA - 1, 3 * local), F32)], axis=0)
        extra[...] = small
        if blocks:
            group[0][blocks[0] * blocks[1] :, :] = three_terms(small)
        send[half:, :] = mixed[...]
        for place, out in ((distant, send), (own, keep)):
            total = mm(dqkv[0, place, :], w[0]) + mm(dqkv[1, place, :], w[1]) + mm(dqkv[2, place, :], w[2])
            out[0:half, :] = total.astype(out.dtype)

    return launch(
        body,
        "self_bwd",
        at,
        [near(a) for a in (mine, other, wo, qkv, prob, tokens, w, mixed)],
        [shape(2 * half, width, dtype=BF), shape(half, width)]
        + group_outs(width, 3 * local, blocks, EXTRA)
        + [shape(EXTRA, 3 * local)],
        scratch=[
            pltpu.VMEM((rows, width), BF),
            pltpu.VMEM((3, rows, local), BF),
            pltpu.VMEM((width, local), F32),
        ],
        mib=20,
        us=6,
    )


def add_stage(at, keep, got, small, bit):
    n, rows, columns = keep.shape
    tail = 0 if small is None else 3 * small.shape[0]
    reach = small.shape[1] if tail else 0

    got = got if isinstance(got, (tuple, list)) else (got,)
    each = columns // len(got)

    def body(at, ins, outs, _):
        keep, got_parts = ins[0], ins[1 : 1 + len(got)]
        mine = at[bit]
        send, stay = outs[:2]
        for b in range(n // 2):
            for chosen, out in ((1 - mine, send), (mine, stay)):
                block = 2 * b + chosen
                for i, part in enumerate(got_parts):
                    span = slice(i * each, (i + 1) * each)
                    value = keep[block, :, span] + part[pl.ds(pl.multiple_of(block * rows, 8), rows), :].astype(F32)
                    if out is send:
                        send[b * rows : (b + 1) * rows, span] = value.astype(BF)
                    else:
                        stay[b, :, span] = value
        if tail:
            total = ins[-1][...] + from_terms(got_parts[0][n * rows :, 0:reach])
            outs[2][...] = total
            send[n // 2 * rows :, 0:reach] = three_terms(total)
            if reach < columns:
                send[n // 2 * rows :, reach:] = jnp.zeros((tail, columns - reach), BF)

    ins = [near(keep)] + [near(part) for part in got] + ([near(small)] if tail else [])
    outs = [shape(n // 2 * rows + tail, columns, dtype=BF), shape(n // 2, rows, columns)]
    if tail:
        outs.append(shape(small.shape[0], reach))
    return launch(body, "add_stage", at, ins, outs, us=1)


def last_stage(at, keep, got, small, parts):
    _, rows, columns = keep.shape
    each = columns // sum(count for count, _ in parts)
    reach = 0 if small is None else small.shape[1]

    def body(at, ins, outs, _):
        total = ins[0][0] + ins[1][0:rows].astype(F32)
        first = 0
        for out, (count, turned) in zip(outs, parts):
            if count == 1:
                value = total[:, first * each : (first + 1) * each]
                out[...] = value.T if turned else value
            else:
                for i in range(count):
                    out[i] = total[:, (first + i) * each : (first + i + 1) * each]
            first += count
        if reach:
            outs[-1][...] = ins[2][...] + from_terms(ins[1][rows:, 0:reach])

    outs = []
    for count, turned in parts:
        dims = (rows, each) if count == 1 else (count, rows, each)
        outs.append(shape(*(dims[::-1] if turned else dims)))
    ins = [near(keep), near(got)]
    if reach:
        ins.append(near(small))
        outs.append(shape(small.shape[0], reach))
    return launch(body, "last_stage", at, ins, outs, us=1)


def join_halves(at, mine, other):
    half, width = mine.shape
    skip = other.shape[0] - half

    def body(at, ins, outs, _):
        outs[0][rows_at(at[0], half), :] = ins[0][...]
        outs[0][rows_at(1 - at[0], half), :] = ins[1][...]

    out = shape(2 * half, width, dtype=mine.dtype)
    ins = [near(mine), near(other, lambda ref, at: ref.at[pl.ds(skip, half), :])]
    return launch(body, "join_halves", at, ins, [out])[0]


def flip(bit, size):
    return [(i, i ^ bit) for i in range(size)]


def butterfly(value, axis, size):
    bit = 1
    while bit < size:
        value = value + lax.ppermute(value, axis, flip(bit, size))
        bit *= 2
    return value


def on_device(
    tokens,
    store,
    summary_length,
    top_index,
    cotangent,
    self_qkv_weight,
    self_qv_bias,
    self_out_weight,
    self_out_bias,
    qkv_weight,
    qv_bias,
    out_weight,
    out_bias,
    fc1_weight,
    fc1_bias,
    fc2_weight,
    fc2_bias,
    norm_gain,
    norm_shift,
):
    rows, width = tokens.shape
    half = rows // 2
    nh = top_index.shape[1]
    local = qkv_weight.shape[2]
    units = fc1_weight.shape[1]
    seg = store.shape[1]
    wide = lax.axis_size("wide")
    place = lax.axis_index("narrow")
    doc = lax.axis_index("wide")
    core, across = place % 2, place // 2
    at = jnp.stack([core, across, place, summary_length[0], doc % 2, doc // 2 % 2, doc // 4]).astype(jnp.int32)
    blocks = (wide // 2, width // wide) if wide == 8 else None
    row = lambda v: v.reshape(1, -1)
    self_w = jnp.swapaxes(self_qkv_weight, 1, 2)
    cross_w = jnp.swapaxes(qkv_weight, 1, 2)

    def to_core(v):
        return lax.ppermute(v, "narrow", CORE)

    def to_across(v):
        return lax.ppermute(v, "narrow", ACROSS)

    def over(v, bit):
        return lax.ppermute(v, "wide", flip(bit, wide))

    def chip_sum(keep, send):
        return (keep + to_core(send).astype(F32)).astype(BF)

    store_x = to_across(store[0])
    qkv, prob, flat, send, keep = self_forward(at, tokens, self_w, self_qv_bias, self_out_weight, nh)
    mine = chip_sum(keep, send)
    other = to_across(mine)
    index = index_rows(top_index)
    bias_mine = make_mask(tie(at, mine), index, top_index.shape, seg, 128, 0)
    store_x, store_own = tie((store_x, store[0]), bias_mine)
    shards = [store_own, to_core(store_own), store_x, to_core(store_x)]
    bias_other = make_mask(tie(at, bias_mine), index, top_index.shape, seg, 128, 1)
    other = tie(other, bias_other)
    first_total, after, after_low = first_norm(at, mine, other, tokens, row(self_out_bias), norm_gain, norm_shift)
    after_other = to_core(after_low)

    keys, values = keys_values(tie(at, after_low), shards, cross_w, nh)
    keep, send, raised, inverse, query, heads = cross_forward(
        tie(at, keys), after_low, after_other, bias_mine, bias_other, keys, values, cross_w, qv_bias, out_weight, nh
    )
    mine = chip_sum(keep, send)
    second_total, mid_low = second_norm(at, after, mine, to_across(mine), row(out_bias), norm_gain, norm_shift)
    mid_other = to_core(mid_low)

    keep, send, hidden, slope = feed_up(at, mid_low, mid_other, fc1_weight, fc2_weight, row(fc1_bias))
    mine = chip_sum(keep, send)
    mixed_half, dlast, dlast_low, third_sums = third_norm(
        at, second_total, mine, to_across(mine), cotangent, row(fc2_bias), norm_gain, norm_shift
    )
    dlast_other = to_core(dlast_low)
    keep, send, dpre, fc1_sum = feed_down(at, dlast_low, dlast_other, fc1_weight, fc2_weight, slope)
    mine = chip_sum(keep, send)
    other = to_across(mine)
    feed_out = feed_grads(tie(at, mine), mid_low, mid_other, dpre, dlast_low, dlast_other, hidden, blocks)
    other = tie(other, feed_out[0])
    dsecond, z, second_sums = second_back(at, dlast, mine, other, second_total, norm_gain)
    z_other = to_core(z)

    keep, send, dquery, dkv, cross_sums = cross_backward(
        at, z, z_other, raised, inverse, query, keys, values, cross_w, out_weight, nh
    )
    mine = chip_sum(keep, send)
    other = to_across(mine)
    cross_out = cross_grads(
        tie(at, mine), z, z_other, after_low, after_other, dquery, heads, shards, dkv, nh, blocks
    )
    started = cross_out[0]
    if blocks:
        feed_send, feed_keep = add_stage(tie(at, started), feed_out[1], over(feed_out[0], 1), None, 5)
        feed_next = over(feed_send, 2)
        started = feed_send
    store_keep, store_send = store_gradient(tie(at, started), dkv, cross_w, nh)
    other = tie(other, store_send)
    dfirst, dfirst_low, first_sums = first_back(at, dsecond, mine, other, first_total, norm_gain)
    dfirst_other = to_core(dfirst_low)
    store_close = to_core(tie(store_send, dfirst_other))
    started = dfirst_low

    *first_out, early_small = self_out_grads(
        tie(at, started), dfirst_low, dfirst_other, flat, (third_sums, second_sums, first_sums, fc1_sum, cross_sums), blocks
    )
    started = early_small
    if blocks:
        first_next = over(first_out[0], 1)
        cross_send, cross_keep = add_stage(tie(at, early_small), cross_out[1], over(cross_out[0], 1), None, 5)
        cross_next = over(cross_send, 2)
        started = cross_send
    send, keep, *self_out, self_small = self_backward(
        tie(at, started, store_close),
        dfirst_low,
        dfirst_other,
        tokens,
        self_w,
        self_out_weight,
        qkv,
        prob,
        mixed_half,
        nh,
        blocks,
    )
    if blocks:
        feed_send, feed_keep = add_stage(tie(at, self_small), feed_keep, feed_next, None, 6)
        feed_next = over(feed_send, 4)
        cross_send, cross_keep = add_stage(tie(at, feed_send), cross_keep, cross_next, None, 6)
        cross_next = over(cross_send, 4)
        first_send, first_keep, early_small = add_stage(tie(at, cross_send), first_out[1], first_next, early_small, 5)
        first_next = over(first_send, 2)
        self_next = over(self_out[0], 1)
        send = tie(send, first_send)
    close = to_core(send)
    mine = (keep + close[:half].astype(F32)).astype(BF)
    other = to_across(mine)
    if blocks:
        self_send, self_keep, self_small = add_stage(tie(at, mine), self_out[1], self_next, self_small, 5)
        self_next = over(self_send, 2)
        first_send, first_keep, early_small = add_stage(tie(at, self_send), first_keep, first_next, early_small, 6)
        first_next = over(first_send, 4)
        fc1_grad, fc2_grad = last_stage(tie(at, first_send), feed_keep, feed_next, None, [(1, False), (1, False)])
        other = tie(other, fc1_grad)
    store_distant = to_across(tie((store_keep[1] + store_close[1].astype(F32)).astype(BF), mine))
    tokens_half = dfirst + (mine.astype(F32) + other.astype(F32))
    tokens_other = to_core(tokens_half)
    mixed = join_halves(tie(at, tokens_half), mixed_half, close)
    if blocks:
        self_send, self_keep, self_small = add_stage(tie(at, mixed), self_keep, self_next, self_small, 6)
        self_next = over(self_send, 4)
        qkv_grad, out_grad = last_stage(tie(at, self_send), cross_keep, cross_next, None, [(3, False), (1, True)])
        tokens_other = tie(tokens_other, out_grad)
    tokens_grad = join_halves(at, tokens_half, tokens_other)
    if blocks:
        self_out_grad, early_small = last_stage(
            tie(at, tokens_grad), first_keep, first_next, early_small, [(1, True)]
        )
        store_distant = tie(store_distant, early_small)
    store_grad = (store_keep[0] + store_close[0].astype(F32) + store_distant.astype(F32))[None]

    if blocks:
        fc2_grad = fc2_grad.T
        self_qkv_grad, self_small = last_stage(
            tie(at, early_small), self_keep, self_next, self_small, [(3, False)]
        )
    else:
        scatter = functools.partial(lax.psum_scatter, axis_name="wide", tiled=True)
        parts = lambda g: jnp.stack([g[:, i * local : (i + 1) * local] for i in range(3)])
        fc1_grad = scatter(feed_out[0], scatter_dimension=0)
        fc2_grad = scatter(feed_out[1].T, scatter_dimension=1)
        qkv_grad = scatter(parts(cross_out[0]), scatter_dimension=1)
        out_grad = scatter(cross_out[0][:, 3 * local :].T, scatter_dimension=1)
        self_qkv_grad = scatter(parts(self_out[0]), scatter_dimension=1)
        self_out_grad = scatter(first_out[0].T, scatter_dimension=1)
        early_small = butterfly(early_small, "wide", wide)
        self_small = butterfly(self_small, "wide", wide)
    lines = jnp.concatenate(
        [early_small[i * EXTRA : (i + 1) * EXTRA] for i in range(width // local)], axis=1
    )
    summed = butterfly(lines[:9], "narrow", 4)
    gain_last, shift_last, fc2_b, gain_mid, shift_mid, out_b, gain_first, shift_first, self_out_b = (
        summed[i] for i in range(9)
    )
    return (
        mixed,
        tokens_grad,
        store_grad,
        self_qkv_grad,
        self_small[0, : 2 * local].reshape(2, local),
        self_out_grad,
        self_out_b,
        qkv_grad,
        lines[10, : 2 * local].reshape(2, local),
        out_grad,
        out_b,
        fc1_grad,
        lines[9],
        fc2_grad,
        fc2_b,
        jnp.stack([gain_first, gain_mid, gain_last]),
        jnp.stack([shift_first, shift_mid, shift_last]),
    )


def solution(mesh):
    placed = (
        P("wide", None),
        P("wide", "narrow", None),
        P("wide"),
        P("wide", "narrow", None, None),
        P("wide", None),
        P(None, None, "narrow"),
        P(None, "narrow"),
        P("narrow", None),
        P(),
        P(None, None, "narrow"),
        P(None, "narrow"),
        P("narrow", None),
        P(),
        P(None, "narrow"),
        P("narrow"),
        P("narrow", None),
        P(),
        P(),
        P(),
    )
    return jax.shard_map(
        on_device,
        mesh=mesh,
        in_specs=placed,
        out_specs=(
            P("wide", None),
            P("wide", None),
            P("wide", "narrow", None),
            P(None, "wide", "narrow"),
            P(None, "narrow"),
            P("narrow", "wide"),
            P(),
            P(None, "wide", "narrow"),
            P(None, "narrow"),
            P("narrow", "wide"),
            P(),
            P("wide", "narrow"),
            P("narrow"),
            P("narrow", "wide"),
            P(),
            P(),
            P(),
        ),
        check_vma=False,
    )
```

```python
import functools

import jax
import jax.numpy as jnp
from jax import lax
from jax.experimental import pallas as pl
from jax.experimental.pallas import tpu as pltpu
from jax.sharding import PartitionSpec as P

F32 = jnp.float32
BF = jnp.bfloat16
NN = (((1,), (0,)), ((), ()))
NT = (((1,), (1,)), ((), ()))
TN = (((0,), (0,)), ((), ()))
EPS = 1e-05
PACE = 1.1e8
SELF_MIB = 60
EXTRA = 16

CORE = [(i, i ^ 1) for i in range(4)]
ACROSS = [(i, i ^ 2) for i in range(4)]


def mm(left, right, dims=NN):
    return lax.dot_general(left, right, dims, preferred_element_type=F32)


def shape(*dims, dtype=F32):
    return jax.ShapeDtypeStruct(dims, dtype)


def tie(value, *earlier):
    return lax.optimization_barrier((value, *earlier))[0]


class Operand:
    def __init__(self, source, buffer, sems, first, parts):
        self.buffer = buffer
        self.parts = parts
        if parts:
            self.copies = [
                pltpu.make_async_copy(source.at[i], buffer.at[i], sems.at[first + i]) for i in range(buffer.shape[0])
            ]
        else:
            self.copies = [pltpu.make_async_copy(source, buffer, sems.at[first])]
        self.waited = [False] * len(self.copies)
        for copy in self.copies:
            copy.start()

    def ready(self, part=None):
        for i, copy in enumerate(self.copies):
            if not self.waited[i] and (part is None or i == part):
                copy.wait()
                self.waited[i] = True

    @property
    def shape(self):
        return self.buffer.shape

    def __getitem__(self, at):
        self.ready(at if self.parts and isinstance(at, int) else None)
        return self.buffer[at]


class Result:
    def __init__(self, target, buffer, sems, first, parts):
        self.buffer = buffer
        if parts:
            self.copies = [
                pltpu.make_async_copy(buffer.at[i], target.at[i], sems.at[first + i]) for i in range(buffer.shape[0])
            ]
        else:
            self.copies = [pltpu.make_async_copy(buffer, target, sems.at[first])]
        self.started = [False] * len(self.copies)

    @property
    def shape(self):
        return self.buffer.shape

    @property
    def dtype(self):
        return self.buffer.dtype

    def __setitem__(self, at, value):
        self.buffer[at] = value

    def flush(self, part=0):
        self.copies[part].start()
        self.started[part] = True

    def finish(self):
        for i in range(len(self.copies)):
            if not self.started[i]:
                self.flush(i)
        for copy in self.copies:
            copy.wait()


def far(array, take=None, dims=None, parts=False):
    return ("far", array, take, tuple(dims or array.shape), parts)


def near(array, take=None):
    return ("near", array, take, None, False)


def raw(array):
    return ("raw", array, None, None, False)


def launch(body, name, at, ins, outs, scratch=(), mib=16, us=2.0):
    in_specs = [pl.BlockSpec(memory_space=pltpu.SMEM)]
    buffers, n_in, n_out = [], 0, 0
    for kind, array, _, dims, parts in ins:
        in_specs.append(pl.BlockSpec(memory_space=pltpu.VMEM if kind == "near" else pltpu.HBM))
        if kind == "far":
            buffers.append(pltpu.VMEM(dims, array.dtype))
            n_in += dims[0] if parts else 1
    out_specs, structs = [], []
    for out in outs:
        if isinstance(out, tuple):
            struct, parts = out
            out_specs.append(pl.BlockSpec(memory_space=pltpu.HBM))
            buffers.append(pltpu.VMEM(struct.shape, struct.dtype))
            n_out += struct.shape[0] if parts else 1
        else:
            struct = out
            out_specs.append(pl.BlockSpec(memory_space=pltpu.VMEM))
        structs.append(struct)
    n_buffers = len(buffers)
    sems = [pltpu.SemaphoreType.DMA((max(n, 1),)) for n in (n_in, n_out)]

    def kernel(at_ref, *refs):
        in_refs, out_refs = refs[: len(ins)], refs[len(ins) : len(ins) + len(outs)]
        rest = refs[len(ins) + len(outs) :]
        bufs, user, (in_sems, out_sems) = list(rest[:n_buffers]), rest[n_buffers:-2], rest[-2:]
        place, given = 0, []
        for ref, (kind, _, take, dims, parts) in zip(in_refs, ins):
            source = take(ref, at_ref) if take else ref
            if kind == "far":
                given.append(Operand(source, bufs.pop(0), in_sems, place, parts))
                place += dims[0] if parts else 1
            else:
                given.append(source)
        place, results = 0, []
        for ref, out in zip(out_refs, outs):
            if isinstance(out, tuple):
                results.append(Result(ref, bufs.pop(0), out_sems, place, out[1]))
                place += out[0].shape[0] if out[1] else 1
            else:
                results.append(ref)
        body(at_ref, given, results, user)
        for operand in given:
            if isinstance(operand, Operand):
                operand.ready()
        for result in results:
            if isinstance(result, Result):
                result.finish()

    return pl.pallas_call(
        kernel,
        in_specs=in_specs,
        out_specs=out_specs,
        out_shape=structs,
        scratch_shapes=buffers + list(scratch) + sems,
        compiler_params=pltpu.CompilerParams(vmem_limit_bytes=mib << 20),
        cost_estimate=pl.CostEstimate(flops=int(us * PACE), bytes_accessed=1000, transcendentals=0),
        name=name,
    )(at, *[entry[1] for entry in ins])


def norm_stats(value):
    centre = value - jnp.mean(value, axis=-1, keepdims=True)
    spread = jnp.mean(centre * centre, axis=-1, keepdims=True)
    inverse = lax.rsqrt(spread + EPS)
    return centre * inverse, inverse


def norm_backward(grad, normed, inverse, gain):
    scaled = grad * gain
    centred = scaled - jnp.mean(scaled, axis=-1, keepdims=True)
    return inverse * (centred - normed * jnp.mean(scaled * normed, axis=-1, keepdims=True))


def column_sum(value):
    return jnp.sum(value, axis=0, keepdims=True)


def erf(value):
    x = jnp.clip(value, -4.0, 4.0)
    y = x * x
    top = jnp.full_like(y, -2.72614225801306e-10)
    for factor in (
        2.77068142495902e-08,
        -2.10102402082508e-06,
        -5.69250639462346e-05,
        -7.34990630326855e-04,
        -2.95459980854025e-03,
        -1.60960333262415e-02,
    ):
        top = top * y + factor
    low = jnp.full_like(y, -1.45660718464996e-05)
    for factor in (
        -2.13374055278905e-04,
        -1.68282697438203e-03,
        -7.37332916720468e-03,
        -1.42647390514189e-02,
    ):
        low = low * y + factor
    return x * top / low


def three_terms(value):
    high = value.astype(BF)
    rest = value - high.astype(F32)
    middle = rest.astype(BF)
    return jnp.concatenate([high, middle, (rest - middle.astype(F32)).astype(BF)], axis=0)


def from_terms(stacked):
    rows = stacked.shape[0] // 3
    terms = stacked.astype(F32)
    return terms[:rows] + terms[rows : 2 * rows] + terms[2 * rows :]


def rows_at(place, rows):
    return pl.ds(pl.multiple_of(place * rows, rows), rows)


def self_forward(at, tokens, w, b, wo, nh):
    rows, width = tokens.shape
    local = w.shape[1]
    half = rows // 2
    hd = local // nh
    scale = hd**-0.5

    def body(at, ins, outs, _):
        tok, w, wo, b = ins
        qkv, prob, flat, send, keep = outs
        x = tok[...]
        q = (mm(x, w[0], NT) + b[0:1]).astype(BF)
        k = mm(x, w[1], NT).astype(BF)
        v = (mm(x, w[2], NT) + b[1:2]).astype(BF)
        for i, value in enumerate((q, k, v)):
            qkv[i] = value
            qkv.flush(i)
        row_ids = lax.broadcasted_iota(jnp.int32, (rows, rows), 0)
        key_ids = lax.broadcasted_iota(jnp.int32, (rows, rows), 1)
        allowed = (key_ids <= row_ids) & (key_ids < at[3])
        found = []
        for h in range(nh):
            part = slice(h * hd, (h + 1) * hd)
            scores = mm(q[:, part], k[:, part], NT) * scale
            scores = jnp.where(allowed, scores, -1e30)
            shifted = jnp.exp(scores - jnp.max(scores, axis=1, keepdims=True))
            weights = (shifted * (1.0 / jnp.sum(shifted, axis=1, keepdims=True))).astype(BF)
            prob[h] = weights
            prob.flush(h)
            found.append(mm(weights, v[:, part]).astype(BF))
        flat[...] = jnp.concatenate(found, axis=1)
        flat.flush()
        send[...] = mm(flat.buffer[rows_at(1 - at[0], half), :], wo[...]).astype(BF)
        send.flush()
        keep[...] = mm(flat.buffer[rows_at(at[0], half), :], wo[...])

    return launch(
        body,
        "self_fwd",
        at,
        [far(tokens), far(w, parts=True), far(wo), far(b)],
        [
            (shape(3, rows, local, dtype=BF), True),
            (shape(nh, rows, rows, dtype=BF), True),
            (shape(rows, local, dtype=BF), False),
            (shape(half, width, dtype=BF), False),
            (shape(half, width), False),
        ],
        mib=SELF_MIB,
        us=4,
    )


def first_norm(at, mine, other, tokens, bias, gain, shift):
    half, width = mine.shape

    def body(at, ins, outs, _):
        mine, other, tok, bias, gain, shift = ins
        total, after, low = outs
        value = tok[...].astype(F32) + (mine[...].astype(F32) + other[...].astype(F32)) + bias[...]
        total[...] = value
        normed, _ = norm_stats(value)
        result = normed * gain[0:1] + shift[0:1]
        after[...] = result
        low[...] = result.astype(BF)

    return launch(
        body,
        "first_norm",
        at,
        [
            near(mine),
            near(other),
            near(tokens, lambda ref, at: ref.at[rows_at(at[0], half), :]),
            near(bias),
            near(gain),
            near(shift),
        ],
        [shape(half, width), shape(half, width), shape(half, width, dtype=BF)],
        us=1.7,
    )


def index_rows(top_index):
    rows, nh, ns, keep = top_index.shape
    flat = top_index.reshape(rows, nh, ns, keep // 128, 128).transpose(0, 1, 3, 2, 4)
    return flat.reshape(rows * nh * ns * (keep // 128), 128)


def make_mask(at, flat, dims, seg, tile, turn):
    rows, nh, ns, keep = dims
    halves = keep // 128
    per_row = nh * ns * halves
    tiles = rows // 2 // tile
    columns = ns * seg
    blocks = columns // 128
    group = 32

    def body(at, ins, outs, _):
        (index,) = ins
        (bias,) = outs
        lane = lax.broadcasted_iota(jnp.int32, (group, 128), 1).astype(F32)
        lane_low = lane.astype(BF)
        empty = jnp.full((group, 128), -1.0, BF)
        own = at[2]
        steps = []
        step = 1
        while step <= seg - keep:
            steps.insert(0, step)
            step *= 2
        turns = steps + [(seg * s) % 128 for s in range(ns)]
        below = {s: lane_low < jnp.asarray(s, BF) for s in turns if 0 < s < 128}

        for t in range(tiles):
            index.ready(t)
            source = index.buffer.at[t]

            def one_group(g, _):
                for h in range(nh):
                    v = [empty] * blocks
                    for slot in range(ns):
                        first, turn = divmod(seg * slot, 128)
                        for c in range(halves):
                            start = g * (group * per_row) + h * ns * halves + c * ns + (own ^ slot)
                            found = jnp.concatenate(
                                [source[pl.ds(start + q * 8 * per_row, 8, stride=per_row), :] for q in range(group // 8)],
                                axis=0,
                            )
                            ahead = (found.astype(F32) - (lane + float(128 * c))).astype(BF)
                            at_block = first + c
                            if turn == 0:
                                v[at_block] = ahead
                            else:
                                turned = pltpu.roll(ahead, turn, axis=1)
                                v[at_block] = jnp.where(below[turn], v[at_block], turned)
                                v[at_block + 1] = jnp.where(below[turn], turned, v[at_block + 1])
                    for s in steps:
                        gap = jnp.asarray(s, BF)
                        moved = [x - gap for x in v]
                        stay = [jnp.where(x >= gap, empty, x) for x in v]
                        if s % 128 == 0:
                            hop = s // 128
                            v = stay[:hop] + [jnp.maximum(stay[i], moved[i - hop]) for i in range(hop, blocks)]
                        else:
                            turned = [pltpu.roll(x, s, axis=1) for x in moved]
                            v = [
                                jnp.maximum(stay[i], jnp.where(below[s], turned[i - 1], turned[i])) for i in range(blocks)
                            ]
                    for i in range(blocks):
                        bias[h, pl.ds(pl.multiple_of(t * tile + g * group, group), group), i * 128 : (i + 1) * 128] = v[
                            i
                        ] * jnp.asarray(1e30, BF)
                return 0

            lax.fori_loop(0, tile // group, one_group, 0)

    flat = flat.reshape(2 * tiles, tile * per_row, 128)
    return launch(
        body,
        "mask",
        at,
        [
            far(
                flat,
                lambda ref, at: ref.at[pl.ds((at[0] ^ turn) * tiles, tiles)],
                (tiles, tile * per_row, 128),
                parts=True,
            )
        ],
        [shape(nh, rows // 2, columns, dtype=BF)],
        us=10,
    )[0]


def keys_values(at, shards, w, nh):
    seg, width = shards[0].shape
    local = w.shape[1]
    hd = local // nh

    def body(at, ins, outs, _):
        for slot in range(4):
            x = ins[slot][...]
            span = slice(slot * seg, (slot + 1) * seg)
            for i, out in enumerate(outs):
                full = mm(x, ins[4][i + 1], NT)
                high = full.astype(BF)
                low = (full - high.astype(F32)).astype(BF)
                for h in range(nh):
                    part = slice(h * hd, (h + 1) * hd)
                    out[h, span, :] = jnp.concatenate([high[:, part], low[:, part]], axis=1)

    out = shape(nh, 4 * seg, 2 * hd, dtype=BF)
    return launch(body, "keys_values", at, [near(s) for s in shards] + [near(w)], [out, out], us=2)


def cross_forward(at, mine, other, bias_mine, bias_other, keys, values, w, b, wo, nh):
    half, width = mine.shape
    rows = 2 * half
    local = w.shape[1]
    hd = local // nh
    slots = keys.shape[1]
    scale = hd**-0.5

    def body(at, ins, outs, scratch):
        mine, other, wq, keys, bias_mine, bias_other, values, wo, b = ins
        keep, send, raised, inverse, query, heads = outs
        twice, found = scratch
        for r, x in enumerate((mine, other)):
            q = (mm(x[...], wq[0], NT) + b[0:1]).astype(BF)
            query[r * half : (r + 1) * half, :] = q
            scaled = q * jnp.asarray(scale, BF)
            for h in range(nh):
                part = scaled[:, h * hd : (h + 1) * hd]
                twice[h, r * half : (r + 1) * half, :] = jnp.concatenate([part, part], axis=1)

        def one_head(h, _):
            for r, bias in enumerate((bias_mine, bias_other)):
                span = slice(r * half, (r + 1) * half)
                scores = mm(twice[h, span, :], keys[h], NT) + bias[h].astype(F32)
                e = jnp.exp(scores - jnp.max(scores, axis=1, keepdims=True))
                total = 1.0 / jnp.sum(e, axis=1, keepdims=True)
                low = e.astype(BF)
                raised[h, span, :] = low
                inverse[h, span, :] = jnp.broadcast_to(total, (half, 128))
                both = mm(low, values[h])
                found[h, span, :] = (both[:, :hd] + both[:, hd:]) * total
            return 0

        lax.fori_loop(0, nh, one_head, 0)
        for r, target in enumerate((keep, send)):
            span = slice(r * half, (r + 1) * half)
            out = (jnp.concatenate([found[h, span, :] for h in range(nh)], axis=1) + b[1:2]).astype(BF)
            heads[span, :] = out
            target[...] = mm(out, wo[...]).astype(target.dtype)

    return launch(
        body,
        "cross_fwd",
        at,
        [near(a) for a in (mine, other, w, keys, bias_mine, bias_other, values, wo, b)],
        [
            shape(half, width),
            shape(half, width, dtype=BF),
            shape(nh, rows, slots, dtype=BF),
            shape(nh, rows, 128),
            shape(rows, local, dtype=BF),
            shape(rows, local, dtype=BF),
        ],
        scratch=[pltpu.VMEM((nh, rows, 2 * hd), BF), pltpu.VMEM((nh, rows, hd), F32)],
        mib=30,
        us=9,
    )


def counted_rows(at, half):
    rows = half // 2
    place = lax.broadcasted_iota(jnp.int32, (half, 1), 0)
    return ((place >= at[1] * rows) & (place < (at[1] + 1) * rows)).astype(F32)


def stacked_sums(*values):
    sums = [column_sum(value) for value in values]
    return jnp.concatenate(sums + [jnp.zeros((8 - len(sums), values[0].shape[1]), F32)], axis=0)


def second_norm(at, after, mine, other, bias, gain, shift):
    half, width = mine.shape

    def body(at, ins, outs, _):
        after, mine, other, bias, gain, shift = ins
        total, low = outs
        value = after[...] + (mine[...].astype(F32) + other[...].astype(F32)) + bias[...]
        total[...] = value
        normed, _ = norm_stats(value)
        low[...] = (normed * gain[1:2] + shift[1:2]).astype(BF)

    ins = [near(a) for a in (after, mine, other, bias, gain, shift)]
    return launch(body, "second_norm", at, ins, [shape(half, width), shape(half, width, dtype=BF)], us=1.5)


def feed_up(at, mine, other, f1, f2, b1):
    half, width = mine.shape
    units = f1.shape[1]

    def body(at, ins, outs, _):
        mine, other, f1, f2, b1 = ins
        keep, send, hidden, slope = outs
        for r, (x, target) in enumerate(((other, send), (mine, keep))):
            span = slice((1 - r) * half, (2 - r) * half)
            low, steep = gelu_pair(mm(x[...], f1[...]) + b1[...])
            hidden[span, :] = low
            slope[span, :] = steep
            target[...] = mm(low, f2[...]).astype(target.dtype)

    ins = [near(a) for a in (mine, other, f1, f2, b1)]
    outs = [
        shape(half, width),
        shape(half, width, dtype=BF),
        shape(2 * half, units, dtype=BF),
        shape(2 * half, units),
    ]
    return launch(body, "feed_up", at, ins, outs, us=4)


def third_norm(at, total, mine, other, cot, bias, gain, shift):
    half, width = mine.shape

    def body(at, ins, outs, _):
        total, mine, other, cot, bias, gain, shift = ins
        mixed, dlast_out, low, sums = outs
        normed_mid, _ = norm_stats(total[...])
        last = normed_mid * gain[1:2] + shift[1:2] + (mine[...].astype(F32) + other[...].astype(F32)) + bias[...]
        normed, inverse = norm_stats(last)
        first_row = at[0] * half
        live = (first_row + lax.broadcasted_iota(jnp.int32, (half, 1), 0) < at[3]).astype(F32)
        mixed[...] = ((normed * gain[2:3] + shift[2:3]) * live).astype(BF)
        delta = cot[...].astype(F32) * live
        dlast = norm_backward(delta, normed, inverse, gain[2:3])
        dlast_out[...] = dlast
        low[...] = dlast.astype(BF)
        counted = counted_rows(at, half)
        sums[...] = stacked_sums(delta * normed * counted, delta * counted, dlast * counted)

    ins = [
        near(total),
        near(mine),
        near(other),
        near(cot, lambda ref, at: ref.at[rows_at(at[0], half), :]),
        near(bias),
        near(gain),
        near(shift),
    ]
    outs = [shape(half, width, dtype=BF), shape(half, width), shape(half, width, dtype=BF), shape(8, width)]
    return launch(body, "third_norm", at, ins, outs, us=2.5)


def feed_down(at, mine, other, f1, f2, slope):
    half, width = mine.shape
    units = f1.shape[1]

    def body(at, ins, outs, _):
        mine, other, f1, f2, slope = ins
        keep, send, dpre, sums = outs
        total = jnp.zeros((1, units), F32)
        for r, (x, target) in enumerate(((other, send), (mine, keep))):
            span = slice((1 - r) * half, (2 - r) * half)
            grad = mm(x[...], f2[...], NT) * slope[span, :]
            total = total + column_sum(grad)
            low = grad.astype(BF)
            dpre[span, :] = low
            target[...] = mm(low, f1[...], NT).astype(target.dtype)
        sums[...] = total

    ins = [near(a) for a in (mine, other, f1, f2, slope)]
    outs = [
        shape(half, width),
        shape(half, width, dtype=BF),
        shape(2 * half, units, dtype=BF),
        shape(1, units),
    ]
    return launch(body, "feed_down", at, ins, outs, us=3)


def second_back(at, dlast, mine, other, total, gain):
    half, width = mine.shape

    def body(at, ins, outs, _):
        dlast, mine, other, total, gain = ins
        dsecond, low, sums = outs
        dmid = dlast[...] + (mine[...].astype(F32) + other[...].astype(F32))
        normed, inverse = norm_stats(total[...])
        result = norm_backward(dmid, normed, inverse, gain[1:2])
        dsecond[...] = result
        low[...] = result.astype(BF)
        counted = counted_rows(at, half)
        sums[...] = stacked_sums(dmid * normed * counted, dmid * counted, result * counted)

    ins = [near(a) for a in (dlast, mine, other, total, gain)]
    outs = [shape(half, width), shape(half, width, dtype=BF), shape(8, width)]
    return launch(body, "second_back", at, ins, outs, us=1.8)


def gelu_pair(pre):
    phi = 0.5 * (1.0 + erf(pre * 0.7071067811865476))
    return (pre * phi).astype(BF), phi + pre * (jnp.exp(pre * pre * -0.5) * 0.3989422804014327)


def cross_backward(at, z_mine, z_other, raised, inverse, query, keys, values, w, wo, nh):
    half, width = z_mine.shape
    rows = 2 * half
    local = w.shape[1]
    hd = local // nh
    slots = keys.shape[1]
    scale = hd**-0.5

    def body(at, ins, outs, scratch):
        z_halves, (wo, inverse, values, raised, query, keys, w) = ins[:2], ins[2:]
        keep, send, dquery, dkv, sums = outs
        douts, right, found = scratch
        zero = jnp.zeros((half, hd), BF)
        head_sum = jnp.zeros((1, local), F32)
        for r in range(2):
            span = slice(r * half, (r + 1) * half)
            dhead = mm(z_halves[r][...], wo[...], NT)
            head_sum = head_sum + column_sum(dhead)
            scaled = query[span, :] * jnp.asarray(scale, BF)
            for h in range(nh):
                part = slice(h * hd, (h + 1) * hd)
                dout = (dhead[:, part] * inverse[h, span, 0:1]).astype(BF)
                douts[h, span, :] = jnp.concatenate([dout, dout], axis=1)
                right[h, 0, span, :] = jnp.concatenate([scaled[:, part], zero], axis=1)
                right[h, 1, span, :] = jnp.concatenate([zero, dout], axis=1)

        def one_head(h, _):
            grad = None
            for r in range(2):
                span = slice(r * half, (r + 1) * half)
                dprob = mm(douts[h, span, :], values[h], NT)
                low = raised[h, span, :]
                e = low.astype(F32)
                weighed = e * dprob
                mean = jnp.sum(weighed, axis=1, keepdims=True) * inverse[h, span, 0:1]
                dscore = (weighed - e * mean).astype(BF)
                both = mm(dscore, keys[h])
                found[h, span, :] = both[:, :hd] + both[:, hd:]
                part = mm(dscore, right[h, 0, span, :], TN) + mm(low, right[h, 1, span, :], TN)
                grad = part if grad is None else grad + part
            dkv[h] = grad.astype(BF)
            return 0

        lax.fori_loop(0, nh, one_head, 0)
        query_sum = jnp.zeros((1, local), F32)
        for r, target in enumerate((keep, send)):
            span = slice(r * half, (r + 1) * half)
            dq = jnp.concatenate([found[h, span, :] for h in range(nh)], axis=1) * scale
            query_sum = query_sum + column_sum(dq)
            dq_low = dq.astype(BF)
            dquery[span, :] = dq_low
            target[...] = mm(dq_low, w[0]).astype(target.dtype)
        sums[...] = jnp.concatenate([query_sum, head_sum], axis=0)

    return launch(
        body,
        "cross_bwd",
        at,
        [near(a) for a in (z_mine, z_other, wo, inverse, values, raised, query, keys, w)],
        [
            shape(half, width),
            shape(half, width, dtype=BF),
            shape(rows, local, dtype=BF),
            shape(nh, slots, 2 * hd, dtype=BF),
            shape(2, local),
        ],
        scratch=[
            pltpu.VMEM((nh, rows, 2 * hd), BF),
            pltpu.VMEM((nh, 2, rows, 2 * hd), BF),
            pltpu.VMEM((nh, rows, hd), F32),
        ],
        mib=30,
        us=11,
    )


def store_gradient(at, dkv, w, nh):
    _, slots, twice = dkv.shape
    _, local, width = w.shape
    hd = twice // 2
    seg = slots // 4

    def body(at, ins, outs, _):
        dkv, w = ins
        keep, send = outs
        weights = []
        for h in range(nh):
            part = slice(h * hd, (h + 1) * hd)
            weights += [w[1][part], w[2][part]]
        weight = jnp.concatenate(weights, axis=0)
        for slot in (1, 3, 0, 2):
            rows = jnp.concatenate([dkv[h, slot * seg : (slot + 1) * seg, :] for h in range(nh)], axis=1)
            part = mm(rows, weight)
            if slot % 2 == 0:
                keep[slot // 2] = part
            else:
                send[slot // 2] = part.astype(BF)

    return launch(
        body,
        "store_grad",
        at,
        [near(dkv), near(w)],
        [shape(2, seg, width), shape(2, seg, width, dtype=BF)],
        us=2.6,
    )


def group_outs(width, columns, blocks, extra=0):
    if not blocks:
        return [shape(width, columns)]
    n, r = blocks
    return [shape(n * r + 3 * extra, columns, dtype=BF), shape(n, r, columns)]


def emit_group(at, grad, outs, blocks, first, columns, kept_first=None):
    if not blocks:
        outs[0][:, first : first + columns] = grad[...]
        return
    n, r = blocks
    kept_first = first if kept_first is None else kept_first
    span, kept = slice(first, first + columns), slice(kept_first, kept_first + columns)
    for b in range(n):
        theirs = pl.ds(pl.multiple_of((2 * b + 1 - at[4]) * r, 8), r)
        outs[0][b * r : (b + 1) * r, span] = grad[theirs, :].astype(BF)
        outs[1][b, :, kept] = grad[pl.ds(pl.multiple_of((2 * b + at[4]) * r, 8), r), :]


def turned_product(out, left, right, step=256):
    if left.shape[1] % step:
        out[...] = mm(left[...], right[...], TN)
        return

    def some(i, _):
        span = pl.ds(pl.multiple_of(i * step, step), step)
        out[span, :] = mm(left[:, span], right[...], TN)
        return 0

    lax.fori_loop(0, left.shape[1] // step, some, 0)


def feed_grads(at, mid_mine, mid_other, dpre, dlast_mine, dlast_other, hidden, blocks):
    half, width = mid_mine.shape
    units = dpre.shape[1]
    if blocks:
        n, r = blocks
        structs = [shape(n * r, 2 * units, dtype=BF), shape(n, r, 2 * units)]
    else:
        structs = [shape(width, units), shape(width, units)]

    def body(at, ins, outs, scratch):
        mid_mine, mid_other, dpre, dlast_mine, dlast_other, hidden = ins
        left, grad = scratch
        for i, (mine, other, right) in enumerate(((mid_mine, mid_other, dpre), (dlast_mine, dlast_other, hidden))):
            left[:half, :] = mine[...]
            left[half:, :] = other[...]
            turned_product(grad, left, right)
            emit_group(at, grad, outs if blocks else outs[i:], blocks, i * units if blocks else 0, units)

    return launch(
        body,
        "feed_grads",
        at,
        [near(a) for a in (mid_mine, mid_other, dpre, dlast_mine, dlast_other, hidden)],
        structs,
        scratch=[pltpu.VMEM((2 * half, width), BF), pltpu.VMEM((width, units), F32)],
        us=4,
    )


def cross_grads(at, z_mine, z_other, mine, other, dquery, heads, shards, dkv, nh, blocks):
    half, width = mine.shape
    local = dquery.shape[1]
    hd = local // nh
    seg = shards[0].shape[0]

    def body(at, ins, outs, scratch):
        shards, (z_mine, z_other, mine, other, dquery, heads, dkv) = ins[0:4], ins[4:]
        (grad,) = scratch
        grad[...] = mm(mine[...], dquery[:half], TN) + mm(other[...], dquery[half:], TN)
        emit_group(at, grad, outs, blocks, 0, local)
        grad[...] = mm(z_mine[...], heads[:half], TN) + mm(z_other[...], heads[half:], TN)
        emit_group(at, grad, outs, blocks, 3 * local, local)
        both = None
        for slot, block in enumerate(shards):
            rows = jnp.concatenate([dkv[h, slot * seg : (slot + 1) * seg, :] for h in range(nh)], axis=1)
            part = mm(block[...], rows, TN)
            both = part if both is None else both + part
        for i in range(2):
            grad[...] = jnp.concatenate([both[:, (2 * h + i) * hd : (2 * h + i + 1) * hd] for h in range(nh)], axis=1)
            emit_group(at, grad, outs, blocks, (1 + i) * local, local)

    return launch(
        body,
        "cross_grads",
        at,
        [near(a) for a in (*shards, z_mine, z_other, mine, other, dquery, heads, dkv)],
        group_outs(width, 4 * local, blocks),
        scratch=[pltpu.VMEM((width, local), F32)],
        us=4,
    )


def self_out_grads(at, mine, other, flat, small, blocks):
    half, width = mine.shape
    local = flat.shape[1]
    cuts = width // local

    def body(at, ins, outs, scratch):
        mine, other, flat, third_sums, second_sums, first_sums, fc1_sum, head_sums = ins
        (grad,) = scratch
        own, distant = flat[rows_at(at[0], half), :], flat[rows_at(1 - at[0], half), :]
        grad[...] = mm(mine[...], own, TN) + mm(other[...], distant, TN)
        emit_group(at, grad, outs, blocks, 0, local)
        line = jnp.concatenate([head_sums[0:1], head_sums[1:2], jnp.zeros((1, width - 2 * local), F32)], axis=1)
        small = jnp.concatenate(
            [third_sums[0:3], second_sums[0:3], first_sums[0:3], fc1_sum[...], line, jnp.zeros((EXTRA - 11, width), F32)],
            axis=0,
        )
        small = jnp.concatenate([small[:, i * local : (i + 1) * local] for i in range(cuts)], axis=0)
        outs[-1][...] = small
        if blocks:
            outs[0][blocks[0] * blocks[1] :, :] = three_terms(small)

    return launch(
        body,
        "self_out_grads",
        at,
        [near(a) for a in (mine, other, flat, *small)],
        group_outs(width, local, blocks, cuts * EXTRA) + [shape(cuts * EXTRA, local)],
        scratch=[pltpu.VMEM((width, local), F32)],
        us=1,
    )


def first_back(at, dsecond, mine, other, total, gain):
    half, width = mine.shape

    def body(at, ins, outs, _):
        dsecond, mine, other, total, gain = ins
        dfirst, low, sums = outs
        value = dsecond[...] + (mine[...].astype(F32) + other[...].astype(F32))
        normed, inverse = norm_stats(total[...])
        result = norm_backward(value, normed, inverse, gain[0:1])
        dfirst[...] = result
        low[...] = result.astype(BF)
        counted = counted_rows(at, half)
        sums[...] = stacked_sums(value * normed * counted, value * counted, result * counted)

    ins = [near(a) for a in (dsecond, mine, other, total, gain)]
    outs = [shape(half, width), shape(half, width, dtype=BF), shape(8, width)]
    return launch(body, "first_back", at, ins, outs, us=1.8)


def self_backward(at, mine, other, tokens, w, wo, qkv, prob, mixed, nh, blocks):
    half, width = mine.shape
    rows = 2 * half
    local = wo.shape[0]
    hd = local // nh
    scale = hd**-0.5

    def body(at, ins, outs, scratch):
        mine, other, wo, qkv, prob, tok, w, mixed = ins
        send, keep = outs[0:2]
        group, extra = outs[2:-1], outs[-1]
        z, dqkv, grad = scratch
        own, distant = rows_at(at[0], half), rows_at(1 - at[0], half)
        z[own, :] = mine[...]
        z[distant, :] = other[...]
        dself = mm(z[...], wo[...], NT).astype(BF)
        v, k, q = qkv[2], qkv[1], qkv[0]
        dq, dk, dv = [], [], []
        for h in range(nh):
            part = slice(h * hd, (h + 1) * hd)
            weights_low = prob[h]
            weights = weights_low.astype(F32)
            weighed = weights * mm(dself[:, part], v[:, part], NT)
            dscore = (weighed - weights * jnp.sum(weighed, axis=1, keepdims=True)).astype(BF)
            dq.append(mm(dscore, k[:, part]))
            dk.append(mm(dscore, q[:, part], TN))
            dv.append(mm(weights_low, dself[:, part], TN))
        dquery = jnp.concatenate(dq, axis=1) * scale
        dvalue = jnp.concatenate(dv, axis=1)
        dqkv[0] = dquery.astype(BF)
        dqkv[1] = (jnp.concatenate(dk, axis=1) * scale).astype(BF)
        dqkv[2] = dvalue.astype(BF)
        x = tok[...]
        for i in range(3):
            grad[...] = mm(x, dqkv[i], TN)
            emit_group(at, grad, group, blocks, i * local, local)
        line = jnp.concatenate([column_sum(dquery), column_sum(dvalue), jnp.zeros((1, local), F32)], axis=1)
        small = jnp.concatenate([line, jnp.zeros((EXTRA - 1, 3 * local), F32)], axis=0)
        extra[...] = small
        if blocks:
            group[0][blocks[0] * blocks[1] :, :] = three_terms(small)
        send[half:, :] = mixed[...]
        for place, out in ((distant, send), (own, keep)):
            total = mm(dqkv[0, place, :], w[0]) + mm(dqkv[1, place, :], w[1]) + mm(dqkv[2, place, :], w[2])
            out[0:half, :] = total.astype(out.dtype)

    return launch(
        body,
        "self_bwd",
        at,
        [near(a) for a in (mine, other, wo, qkv, prob, tokens, w, mixed)],
        [shape(2 * half, width, dtype=BF), shape(half, width)]
        + group_outs(width, 3 * local, blocks, EXTRA)
        + [shape(EXTRA, 3 * local)],
        scratch=[
            pltpu.VMEM((rows, width), BF),
            pltpu.VMEM((3, rows, local), BF),
            pltpu.VMEM((width, local), F32),
        ],
        mib=20,
        us=6,
    )


def add_stage(at, keep, got, small, bit):
    n, rows, columns = keep.shape
    tail = 0 if small is None else 3 * small.shape[0]
    reach = small.shape[1] if tail else 0

    got = got if isinstance(got, (tuple, list)) else (got,)
    each = columns // len(got)

    def body(at, ins, outs, _):
        keep, got_parts = ins[0], ins[1 : 1 + len(got)]
        mine = at[bit]
        send, stay = outs[:2]
        for b in range(n // 2):
            for chosen, out in ((1 - mine, send), (mine, stay)):
                block = 2 * b + chosen
                for i, part in enumerate(got_parts):
                    span = slice(i * each, (i + 1) * each)
                    value = keep[block, :, span] + part[pl.ds(pl.multiple_of(block * rows, 8), rows), :].astype(F32)
                    if out is send:
                        send[b * rows : (b + 1) * rows, span] = value.astype(BF)
                    else:
                        stay[b, :, span] = value
        if tail:
            total = ins[-1][...] + from_terms(got_parts[0][n * rows :, 0:reach])
            outs[2][...] = total
            send[n // 2 * rows :, 0:reach] = three_terms(total)
            if reach < columns:
                send[n // 2 * rows :, reach:] = jnp.zeros((tail, columns - reach), BF)

    ins = [near(keep)] + [near(part) for part in got] + ([near(small)] if tail else [])
    outs = [shape(n // 2 * rows + tail, columns, dtype=BF), shape(n // 2, rows, columns)]
    if tail:
        outs.append(shape(small.shape[0], reach))
    return launch(body, "add_stage", at, ins, outs, us=1)


def last_stage(at, keep, got, small, parts):
    _, rows, columns = keep.shape
    each = columns // sum(count for count, _ in parts)
    reach = 0 if small is None else small.shape[1]

    def body(at, ins, outs, _):
        total = ins[0][0] + ins[1][0:rows].astype(F32)
        first = 0
        for out, (count, turned) in zip(outs, parts):
            if count == 1:
                value = total[:, first * each : (first + 1) * each]
                out[...] = value.T if turned else value
            else:
                for i in range(count):
                    out[i] = total[:, (first + i) * each : (first + i + 1) * each]
            first += count
        if reach:
            outs[-1][...] = ins[2][...] + from_terms(ins[1][rows:, 0:reach])

    outs = []
    for count, turned in parts:
        dims = (rows, each) if count == 1 else (count, rows, each)
        outs.append(shape(*(dims[::-1] if turned else dims)))
    ins = [near(keep), near(got)]
    if reach:
        ins.append(near(small))
        outs.append(shape(small.shape[0], reach))
    return launch(body, "last_stage", at, ins, outs, us=1)


def join_halves(at, mine, other):
    half, width = mine.shape
    skip = other.shape[0] - half

    def body(at, ins, outs, _):
        outs[0][rows_at(at[0], half), :] = ins[0][...]
        outs[0][rows_at(1 - at[0], half), :] = ins[1][...]

    out = shape(2 * half, width, dtype=mine.dtype)
    ins = [near(mine), near(other, lambda ref, at: ref.at[pl.ds(skip, half), :])]
    return launch(body, "join_halves", at, ins, [out])[0]


def flip(bit, size):
    return [(i, i ^ bit) for i in range(size)]


def butterfly(value, axis, size):
    bit = 1
    while bit < size:
        value = value + lax.ppermute(value, axis, flip(bit, size))
        bit *= 2
    return value


def on_device(
    tokens,
    store,
    summary_length,
    top_index,
    cotangent,
    self_qkv_weight,
    self_qv_bias,
    self_out_weight,
    self_out_bias,
    qkv_weight,
    qv_bias,
    out_weight,
    out_bias,
    fc1_weight,
    fc1_bias,
    fc2_weight,
    fc2_bias,
    norm_gain,
    norm_shift,
):
    rows, width = tokens.shape
    half = rows // 2
    nh = top_index.shape[1]
    local = qkv_weight.shape[2]
    units = fc1_weight.shape[1]
    seg = store.shape[1]
    wide = lax.axis_size("wide")
    place = lax.axis_index("narrow")
    doc = lax.axis_index("wide")
    core, across = place % 2, place // 2
    at = jnp.stack([core, across, place, summary_length[0], doc % 2, doc // 2 % 2, doc // 4]).astype(jnp.int32)
    blocks = (wide // 2, width // wide) if wide == 8 else None
    row = lambda v: v.reshape(1, -1)
    self_w = jnp.swapaxes(self_qkv_weight, 1, 2)
    cross_w = jnp.swapaxes(qkv_weight, 1, 2)

    def to_core(v):
        return lax.ppermute(v, "narrow", CORE)

    def to_across(v):
        return lax.ppermute(v, "narrow", ACROSS)

    def over(v, bit):
        return lax.ppermute(v, "wide", flip(bit, wide))

    def chip_sum(keep, send):
        return (keep + to_core(send).astype(F32)).astype(BF)

    store_x = to_across(store[0])
    qkv, prob, flat, send, keep = self_forward(at, tokens, self_w, self_qv_bias, self_out_weight, nh)
    mine = chip_sum(keep, send)
    other = to_across(mine)
    index = index_rows(top_index)
    bias_mine = make_mask(tie(at, mine), index, top_index.shape, seg, 128, 0)
    store_x, store_own = tie((store_x, store[0]), bias_mine)
    shards = [store_own, to_core(store_own), store_x, to_core(store_x)]
    bias_other = make_mask(tie(at, bias_mine), index, top_index.shape, seg, 128, 1)
    other = tie(other, bias_other)
    first_total, after, after_low = first_norm(at, mine, other, tokens, row(self_out_bias), norm_gain, norm_shift)
    after_other = to_core(after_low)

    keys, values = keys_values(tie(at, after_low), shards, cross_w, nh)
    keep, send, raised, inverse, query, heads = cross_forward(
        tie(at, keys), after_low, after_other, bias_mine, bias_other, keys, values, cross_w, qv_bias, out_weight, nh
    )
    mine = chip_sum(keep, send)
    second_total, mid_low = second_norm(at, after, mine, to_across(mine), row(out_bias), norm_gain, norm_shift)
    mid_other = to_core(mid_low)

    keep, send, hidden, slope = feed_up(at, mid_low, mid_other, fc1_weight, fc2_weight, row(fc1_bias))
    mine = chip_sum(keep, send)
    mixed_half, dlast, dlast_low, third_sums = third_norm(
        at, second_total, mine, to_across(mine), cotangent, row(fc2_bias), norm_gain, norm_shift
    )
    dlast_other = to_core(dlast_low)
    keep, send, dpre, fc1_sum = feed_down(at, dlast_low, dlast_other, fc1_weight, fc2_weight, slope)
    mine = chip_sum(keep, send)
    other = to_across(mine)
    feed_out = feed_grads(tie(at, mine), mid_low, mid_other, dpre, dlast_low, dlast_other, hidden, blocks)
    other = tie(other, feed_out[0])
    dsecond, z, second_sums = second_back(at, dlast, mine, other, second_total, norm_gain)
    z_other = to_core(z)

    keep, send, dquery, dkv, cross_sums = cross_backward(
        at, z, z_other, raised, inverse, query, keys, values, cross_w, out_weight, nh
    )
    mine = chip_sum(keep, send)
    other = to_across(mine)
    cross_out = cross_grads(
        tie(at, mine), z, z_other, after_low, after_other, dquery, heads, shards, dkv, nh, blocks
    )
    started = cross_out[0]
    if blocks:
        feed_send, feed_keep = add_stage(tie(at, started), feed_out[1], over(feed_out[0], 1), None, 5)
        feed_next = over(feed_send, 2)
        started = feed_send
    store_keep, store_send = store_gradient(tie(at, started), dkv, cross_w, nh)
    other = tie(other, store_send)
    dfirst, dfirst_low, first_sums = first_back(at, dsecond, mine, other, first_total, norm_gain)
    dfirst_other = to_core(dfirst_low)
    store_close = to_core(tie(store_send, dfirst_other))
    started = dfirst_low

    *first_out, early_small = self_out_grads(
        tie(at, started), dfirst_low, dfirst_other, flat, (third_sums, second_sums, first_sums, fc1_sum, cross_sums), blocks
    )
    send, keep, *self_out, self_small = self_backward(
        tie(at, early_small, store_close),
        dfirst_low,
        dfirst_other,
        tokens,
        self_w,
        self_out_weight,
        qkv,
        prob,
        mixed_half,
        nh,
        blocks,
    )
    if blocks:
        first_next, self_next, cross_next = over(first_out[0], 1), over(self_out[0], 1), over(cross_out[0], 1)
        feed_send, feed_keep = add_stage(tie(at, self_small), feed_keep, feed_next, None, 6)
        feed_next = over(feed_send, 4)
        cross_send, cross_keep = add_stage(tie(at, feed_send), cross_out[1], cross_next, None, 5)
        cross_next = over(cross_send, 2)
        first_send, first_keep, early_small = add_stage(tie(at, cross_send), first_out[1], first_next, early_small, 5)
        first_next = over(first_send, 2)
        send = tie(send, first_send)
    close = to_core(send)
    mine = (keep + close[:half].astype(F32)).astype(BF)
    other = to_across(mine)
    if blocks:
        cross_send, cross_keep = add_stage(tie(at, mine), cross_keep, cross_next, None, 6)
        cross_next = over(cross_send, 4)
        self_send, self_keep, self_small = add_stage(tie(at, cross_send), self_out[1], self_next, self_small, 5)
        self_next = over(self_send, 2)
        fc1_grad, fc2_grad = last_stage(tie(at, self_send), feed_keep, feed_next, None, [(1, False), (1, False)])
        first_send, first_keep, early_small = add_stage(tie(at, fc1_grad), first_keep, first_next, early_small, 6)
        first_next = over(first_send, 4)
        other = tie(other, first_send)
    store_distant = to_across(tie((store_keep[1] + store_close[1].astype(F32)).astype(BF), other))
    tokens_half = dfirst + (mine.astype(F32) + other.astype(F32))
    tokens_other = to_core(tokens_half)
    mixed = join_halves(tie(at, tokens_half), mixed_half, close)
    if blocks:
        self_send, self_keep, self_small = add_stage(tie(at, mixed), self_keep, self_next, self_small, 6)
        self_next = over(self_send, 4)
        qkv_grad, out_grad = last_stage(tie(at, self_send), cross_keep, cross_next, None, [(3, False), (1, True)])
        tokens_other = tie(tokens_other, out_grad)
    tokens_grad = join_halves(at, tokens_half, tokens_other)
    if blocks:
        self_out_grad, early_small = last_stage(
            tie(at, tokens_grad), first_keep, first_next, early_small, [(1, True)]
        )
        store_distant = tie(store_distant, early_small)
    store_grad = (store_keep[0] + store_close[0].astype(F32) + store_distant.astype(F32))[None]

    if blocks:
        fc2_grad = fc2_grad.T
        self_qkv_grad, self_small = last_stage(
            tie(at, early_small), self_keep, self_next, self_small, [(3, False)]
        )
    else:
        scatter = functools.partial(lax.psum_scatter, axis_name="wide", tiled=True)
        parts = lambda g: jnp.stack([g[:, i * local : (i + 1) * local] for i in range(3)])
        fc1_grad = scatter(feed_out[0], scatter_dimension=0)
        fc2_grad = scatter(feed_out[1].T, scatter_dimension=1)
        qkv_grad = scatter(parts(cross_out[0]), scatter_dimension=1)
        out_grad = scatter(cross_out[0][:, 3 * local :].T, scatter_dimension=1)
        self_qkv_grad = scatter(parts(self_out[0]), scatter_dimension=1)
        self_out_grad = scatter(first_out[0].T, scatter_dimension=1)
        early_small = butterfly(early_small, "wide", wide)
        self_small = butterfly(self_small, "wide", wide)
    lines = jnp.concatenate(
        [early_small[i * EXTRA : (i + 1) * EXTRA] for i in range(width // local)], axis=1
    )
    summed = butterfly(lines[:9], "narrow", 4)
    gain_last, shift_last, fc2_b, gain_mid, shift_mid, out_b, gain_first, shift_first, self_out_b = (
        summed[i] for i in range(9)
    )
    return (
        mixed,
        tokens_grad,
        store_grad,
        self_qkv_grad,
        self_small[0, : 2 * local].reshape(2, local),
        self_out_grad,
        self_out_b,
        qkv_grad,
        lines[10, : 2 * local].reshape(2, local),
        out_grad,
        out_b,
        fc1_grad,
        lines[9],
        fc2_grad,
        fc2_b,
        jnp.stack([gain_first, gain_mid, gain_last]),
        jnp.stack([shift_first, shift_mid, shift_last]),
    )


def solution(mesh):
    placed = (
        P("wide", None),
        P("wide", "narrow", None),
        P("wide"),
        P("wide", "narrow", None, None),
        P("wide", None),
        P(None, None, "narrow"),
        P(None, "narrow"),
        P("narrow", None),
        P(),
        P(None, None, "narrow"),
        P(None, "narrow"),
        P("narrow", None),
        P(),
        P(None, "narrow"),
        P("narrow"),
        P("narrow", None),
        P(),
        P(),
        P(),
    )
    return jax.shard_map(
        on_device,
        mesh=mesh,
        in_specs=placed,
        out_specs=(
            P("wide", None),
            P("wide", None),
            P("wide", "narrow", None),
            P(None, "wide", "narrow"),
            P(None, "narrow"),
            P("narrow", "wide"),
            P(),
            P(None, "wide", "narrow"),
            P(None, "narrow"),
            P("narrow", "wide"),
            P(),
            P("wide", "narrow"),
            P("narrow"),
            P("narrow", "wide"),
            P(),
            P(),
            P(),
        ),
        check_vma=False,
    )
```

```python
import functools

import jax
import jax.numpy as jnp
from jax import lax
from jax.experimental import pallas as pl
from jax.experimental.pallas import tpu as pltpu
from jax.sharding import PartitionSpec as P

F32 = jnp.float32
BF = jnp.bfloat16
NN = (((1,), (0,)), ((), ()))
NT = (((1,), (1,)), ((), ()))
TN = (((0,), (0,)), ((), ()))
EPS = 1e-05
PACE = 1.1e8
SELF_MIB = 60
EXTRA = 16

CORE = [(i, i ^ 1) for i in range(4)]
ACROSS = [(i, i ^ 2) for i in range(4)]


def mm(left, right, dims=NN):
    return lax.dot_general(left, right, dims, preferred_element_type=F32)


def shape(*dims, dtype=F32):
    return jax.ShapeDtypeStruct(dims, dtype)


def tie(value, *earlier):
    return lax.optimization_barrier((value, *earlier))[0]


class Operand:
    def __init__(self, source, buffer, sems, first, parts):
        self.buffer = buffer
        self.parts = parts
        if parts:
            self.copies = [
                pltpu.make_async_copy(source.at[i], buffer.at[i], sems.at[first + i]) for i in range(buffer.shape[0])
            ]
        else:
            self.copies = [pltpu.make_async_copy(source, buffer, sems.at[first])]
        self.waited = [False] * len(self.copies)
        for copy in self.copies:
            copy.start()

    def ready(self, part=None):
        for i, copy in enumerate(self.copies):
            if not self.waited[i] and (part is None or i == part):
                copy.wait()
                self.waited[i] = True

    @property
    def shape(self):
        return self.buffer.shape

    def __getitem__(self, at):
        self.ready(at if self.parts and isinstance(at, int) else None)
        return self.buffer[at]


class Result:
    def __init__(self, target, buffer, sems, first, parts):
        self.buffer = buffer
        if parts:
            self.copies = [
                pltpu.make_async_copy(buffer.at[i], target.at[i], sems.at[first + i]) for i in range(buffer.shape[0])
            ]
        else:
            self.copies = [pltpu.make_async_copy(buffer, target, sems.at[first])]
        self.started = [False] * len(self.copies)

    @property
    def shape(self):
        return self.buffer.shape

    @property
    def dtype(self):
        return self.buffer.dtype

    def __setitem__(self, at, value):
        self.buffer[at] = value

    def flush(self, part=0):
        self.copies[part].start()
        self.started[part] = True

    def finish(self):
        for i in range(len(self.copies)):
            if not self.started[i]:
                self.flush(i)
        for copy in self.copies:
            copy.wait()


def far(array, take=None, dims=None, parts=False):
    return ("far", array, take, tuple(dims or array.shape), parts)


def near(array, take=None):
    return ("near", array, take, None, False)


def raw(array):
    return ("raw", array, None, None, False)


def launch(body, name, at, ins, outs, scratch=(), mib=16, us=2.0):
    in_specs = [pl.BlockSpec(memory_space=pltpu.SMEM)]
    buffers, n_in, n_out = [], 0, 0
    for kind, array, _, dims, parts in ins:
        in_specs.append(pl.BlockSpec(memory_space=pltpu.VMEM if kind == "near" else pltpu.HBM))
        if kind == "far":
            buffers.append(pltpu.VMEM(dims, array.dtype))
            n_in += dims[0] if parts else 1
    out_specs, structs = [], []
    for out in outs:
        if isinstance(out, tuple):
            struct, parts = out
            out_specs.append(pl.BlockSpec(memory_space=pltpu.HBM))
            buffers.append(pltpu.VMEM(struct.shape, struct.dtype))
            n_out += struct.shape[0] if parts else 1
        else:
            struct = out
            out_specs.append(pl.BlockSpec(memory_space=pltpu.VMEM))
        structs.append(struct)
    n_buffers = len(buffers)
    sems = [pltpu.SemaphoreType.DMA((max(n, 1),)) for n in (n_in, n_out)]

    def kernel(at_ref, *refs):
        in_refs, out_refs = refs[: len(ins)], refs[len(ins) : len(ins) + len(outs)]
        rest = refs[len(ins) + len(outs) :]
        bufs, user, (in_sems, out_sems) = list(rest[:n_buffers]), rest[n_buffers:-2], rest[-2:]
        place, given = 0, []
        for ref, (kind, _, take, dims, parts) in zip(in_refs, ins):
            source = take(ref, at_ref) if take else ref
            if kind == "far":
                given.append(Operand(source, bufs.pop(0), in_sems, place, parts))
                place += dims[0] if parts else 1
            else:
                given.append(source)
        place, results = 0, []
        for ref, out in zip(out_refs, outs):
            if isinstance(out, tuple):
                results.append(Result(ref, bufs.pop(0), out_sems, place, out[1]))
                place += out[0].shape[0] if out[1] else 1
            else:
                results.append(ref)
        body(at_ref, given, results, user)
        for operand in given:
            if isinstance(operand, Operand):
                operand.ready()
        for result in results:
            if isinstance(result, Result):
                result.finish()

    return pl.pallas_call(
        kernel,
        in_specs=in_specs,
        out_specs=out_specs,
        out_shape=structs,
        scratch_shapes=buffers + list(scratch) + sems,
        compiler_params=pltpu.CompilerParams(vmem_limit_bytes=mib << 20),
        cost_estimate=pl.CostEstimate(flops=int(us * PACE), bytes_accessed=1000, transcendentals=0),
        name=name,
    )(at, *[entry[1] for entry in ins])


def norm_stats(value):
    centre = value - jnp.mean(value, axis=-1, keepdims=True)
    spread = jnp.mean(centre * centre, axis=-1, keepdims=True)
    inverse = lax.rsqrt(spread + EPS)
    return centre * inverse, inverse


def norm_backward(grad, normed, inverse, gain):
    scaled = grad * gain
    centred = scaled - jnp.mean(scaled, axis=-1, keepdims=True)
    return inverse * (centred - normed * jnp.mean(scaled * normed, axis=-1, keepdims=True))


def column_sum(value):
    return jnp.sum(value, axis=0, keepdims=True)


def erf(value):
    x = jnp.clip(value, -4.0, 4.0)
    y = x * x
    top = jnp.full_like(y, -2.72614225801306e-10)
    for factor in (
        2.77068142495902e-08,
        -2.10102402082508e-06,
        -5.69250639462346e-05,
        -7.34990630326855e-04,
        -2.95459980854025e-03,
        -1.60960333262415e-02,
    ):
        top = top * y + factor
    low = jnp.full_like(y, -1.45660718464996e-05)
    for factor in (
        -2.13374055278905e-04,
        -1.68282697438203e-03,
        -7.37332916720468e-03,
        -1.42647390514189e-02,
    ):
        low = low * y + factor
    return x * top / low


def two_terms(value):
    high = value.astype(BF)
    return jnp.concatenate([high, (value - high.astype(F32)).astype(BF)], axis=0)


def from_terms(stacked):
    rows = stacked.shape[0] // 2
    terms = stacked.astype(F32)
    return terms[:rows] + terms[rows:]


def rows_at(place, rows):
    return pl.ds(pl.multiple_of(place * rows, rows), rows)


def self_forward(at, tokens, w, b, wo, nh):
    rows, width = tokens.shape
    local = w.shape[1]
    half = rows // 2
    hd = local // nh
    scale = hd**-0.5

    def body(at, ins, outs, _):
        tok, w, wo, b = ins
        qkv, prob, flat, send, keep = outs
        x = tok[...]
        q = (mm(x, w[0], NT) + b[0:1]).astype(BF)
        k = mm(x, w[1], NT).astype(BF)
        v = (mm(x, w[2], NT) + b[1:2]).astype(BF)
        for i, value in enumerate((q, k, v)):
            qkv[i] = value
            qkv.flush(i)
        row_ids = lax.broadcasted_iota(jnp.int32, (rows, rows), 0)
        key_ids = lax.broadcasted_iota(jnp.int32, (rows, rows), 1)
        allowed = (key_ids <= row_ids) & (key_ids < at[3])
        found = []
        for h in range(nh):
            part = slice(h * hd, (h + 1) * hd)
            scores = mm(q[:, part], k[:, part], NT) * scale
            scores = jnp.where(allowed, scores, -1e30)
            shifted = jnp.exp(scores - jnp.max(scores, axis=1, keepdims=True))
            weights = (shifted * (1.0 / jnp.sum(shifted, axis=1, keepdims=True))).astype(BF)
            prob[h] = weights
            prob.flush(h)
            found.append(mm(weights, v[:, part]).astype(BF))
        flat[...] = jnp.concatenate(found, axis=1)
        flat.flush()
        send[...] = mm(flat.buffer[rows_at(1 - at[0], half), :], wo[...]).astype(BF)
        send.flush()
        keep[...] = mm(flat.buffer[rows_at(at[0], half), :], wo[...])

    return launch(
        body,
        "self_fwd",
        at,
        [far(tokens), far(w, parts=True), far(wo), far(b)],
        [
            (shape(3, rows, local, dtype=BF), True),
            (shape(nh, rows, rows, dtype=BF), True),
            (shape(rows, local, dtype=BF), False),
            (shape(half, width, dtype=BF), False),
            (shape(half, width), False),
        ],
        mib=SELF_MIB,
        us=4,
    )


def first_norm(at, mine, other, tokens, bias, gain, shift):
    half, width = mine.shape

    def body(at, ins, outs, _):
        mine, other, tok, bias, gain, shift = ins
        total, after, low = outs
        value = tok[...].astype(F32) + (mine[...].astype(F32) + other[...].astype(F32)) + bias[...]
        total[...] = value
        normed, _ = norm_stats(value)
        result = normed * gain[0:1] + shift[0:1]
        after[...] = result
        low[...] = result.astype(BF)

    return launch(
        body,
        "first_norm",
        at,
        [
            near(mine),
            near(other),
            near(tokens, lambda ref, at: ref.at[rows_at(at[0], half), :]),
            near(bias),
            near(gain),
            near(shift),
        ],
        [shape(half, width), shape(half, width), shape(half, width, dtype=BF)],
        us=1.7,
    )


def index_rows(top_index):
    rows, nh, ns, keep = top_index.shape
    flat = top_index.reshape(rows, nh, ns, keep // 128, 128).transpose(0, 1, 3, 2, 4)
    return flat.reshape(rows * nh * ns * (keep // 128), 128)


def make_mask(at, flat, dims, seg, tile, turn):
    rows, nh, ns, keep = dims
    halves = keep // 128
    per_row = nh * ns * halves
    tiles = rows // 2 // tile
    columns = ns * seg
    blocks = columns // 128
    group = 32

    def body(at, ins, outs, _):
        (index,) = ins
        (bias,) = outs
        lane = lax.broadcasted_iota(jnp.int32, (group, 128), 1).astype(F32)
        lane_low = lane.astype(BF)
        empty = jnp.full((group, 128), -1.0, BF)
        own = at[2]
        steps = []
        step = 1
        while step <= seg - keep:
            steps.insert(0, step)
            step *= 2
        turns = steps + [(seg * s) % 128 for s in range(ns)]
        below = {s: lane_low < jnp.asarray(s, BF) for s in turns if 0 < s < 128}

        for t in range(tiles):
            index.ready(t)
            source = index.buffer.at[t]

            def one_group(g, _):
                for h in range(nh):
                    v = [empty] * blocks
                    for slot in range(ns):
                        first, turn = divmod(seg * slot, 128)
                        for c in range(halves):
                            start = g * (group * per_row) + h * ns * halves + c * ns + (own ^ slot)
                            found = jnp.concatenate(
                                [source[pl.ds(start + q * 8 * per_row, 8, stride=per_row), :] for q in range(group // 8)],
                                axis=0,
                            )
                            ahead = (found.astype(F32) - (lane + float(128 * c))).astype(BF)
                            at_block = first + c
                            if turn == 0:
                                v[at_block] = ahead
                            else:
                                turned = pltpu.roll(ahead, turn, axis=1)
                                v[at_block] = jnp.where(below[turn], v[at_block], turned)
                                v[at_block + 1] = jnp.where(below[turn], turned, v[at_block + 1])
                    for s in steps:
                        gap = jnp.asarray(s, BF)
                        moved = [x - gap for x in v]
                        stay = [jnp.where(x >= gap, empty, x) for x in v]
                        if s % 128 == 0:
                            hop = s // 128
                            v = stay[:hop] + [jnp.maximum(stay[i], moved[i - hop]) for i in range(hop, blocks)]
                        else:
                            turned = [pltpu.roll(x, s, axis=1) for x in moved]
                            v = [
                                jnp.maximum(stay[i], jnp.where(below[s], turned[i - 1], turned[i])) for i in range(blocks)
                            ]
                    for i in range(blocks):
                        bias[h, pl.ds(pl.multiple_of(t * tile + g * group, group), group), i * 128 : (i + 1) * 128] = v[
                            i
                        ] * jnp.asarray(1e30, BF)
                return 0

            lax.fori_loop(0, tile // group, one_group, 0)

    flat = flat.reshape(2 * tiles, tile * per_row, 128)
    return launch(
        body,
        "mask",
        at,
        [
            far(
                flat,
                lambda ref, at: ref.at[pl.ds((at[0] ^ turn) * tiles, tiles)],
                (tiles, tile * per_row, 128),
                parts=True,
            )
        ],
        [shape(nh, rows // 2, columns, dtype=BF)],
        us=10,
    )[0]


def keys_values(at, shards, w, nh):
    seg, width = shards[0].shape
    local = w.shape[1]
    hd = local // nh

    def body(at, ins, outs, _):
        for slot in range(4):
            x = ins[slot][...]
            span = slice(slot * seg, (slot + 1) * seg)
            for i, out in enumerate(outs):
                full = mm(x, ins[4][i + 1], NT)
                high = full.astype(BF)
                low = (full - high.astype(F32)).astype(BF)
                for h in range(nh):
                    part = slice(h * hd, (h + 1) * hd)
                    out[h, span, :] = jnp.concatenate([high[:, part], low[:, part]], axis=1)

    out = shape(nh, 4 * seg, 2 * hd, dtype=BF)
    return launch(body, "keys_values", at, [near(s) for s in shards] + [near(w)], [out, out], us=2)


def cross_forward(at, mine, other, bias_mine, bias_other, keys, values, w, b, wo, nh):
    half, width = mine.shape
    rows = 2 * half
    local = w.shape[1]
    hd = local // nh
    slots = keys.shape[1]
    scale = hd**-0.5

    def body(at, ins, outs, scratch):
        mine, other, wq, keys, bias_mine, bias_other, values, wo, b = ins
        keep, send, raised, inverse, query, heads = outs
        twice, found = scratch
        for r, x in enumerate((mine, other)):
            q = (mm(x[...], wq[0], NT) + b[0:1]).astype(BF)
            query[r * half : (r + 1) * half, :] = q
            scaled = q * jnp.asarray(scale, BF)
            for h in range(nh):
                part = scaled[:, h * hd : (h + 1) * hd]
                twice[h, r * half : (r + 1) * half, :] = jnp.concatenate([part, part], axis=1)

        def one_head(h, _):
            for r, bias in enumerate((bias_mine, bias_other)):
                span = slice(r * half, (r + 1) * half)
                scores = mm(twice[h, span, :], keys[h], NT) + bias[h].astype(F32)
                e = jnp.exp(scores - jnp.max(scores, axis=1, keepdims=True))
                total = 1.0 / jnp.sum(e, axis=1, keepdims=True)
                low = e.astype(BF)
                raised[h, span, :] = low
                inverse[h, span, :] = jnp.broadcast_to(total, (half, 128))
                both = mm(low, values[h])
                found[h, span, :] = (both[:, :hd] + both[:, hd:]) * total
            return 0

        lax.fori_loop(0, nh, one_head, 0)
        for r, target in enumerate((keep, send)):
            span = slice(r * half, (r + 1) * half)
            out = (jnp.concatenate([found[h, span, :] for h in range(nh)], axis=1) + b[1:2]).astype(BF)
            heads[span, :] = out
            target[...] = mm(out, wo[...]).astype(target.dtype)

    return launch(
        body,
        "cross_fwd",
        at,
        [near(a) for a in (mine, other, w, keys, bias_mine, bias_other, values, wo, b)],
        [
            shape(half, width),
            shape(half, width, dtype=BF),
            shape(nh, rows, slots, dtype=BF),
            shape(nh, rows, 128),
            shape(rows, local, dtype=BF),
            shape(rows, local, dtype=BF),
        ],
        scratch=[pltpu.VMEM((nh, rows, 2 * hd), BF), pltpu.VMEM((nh, rows, hd), F32)],
        mib=30,
        us=9,
    )


def counted_rows(at, half):
    rows = half // 2
    place = lax.broadcasted_iota(jnp.int32, (half, 1), 0)
    return ((place >= at[1] * rows) & (place < (at[1] + 1) * rows)).astype(F32)


def stacked_sums(*values):
    sums = [column_sum(value) for value in values]
    return jnp.concatenate(sums + [jnp.zeros((8 - len(sums), values[0].shape[1]), F32)], axis=0)


def second_norm(at, after, mine, other, bias, gain, shift):
    half, width = mine.shape

    def body(at, ins, outs, _):
        after, mine, other, bias, gain, shift = ins
        total, low = outs
        value = after[...] + (mine[...].astype(F32) + other[...].astype(F32)) + bias[...]
        total[...] = value
        normed, _ = norm_stats(value)
        low[...] = (normed * gain[1:2] + shift[1:2]).astype(BF)

    ins = [near(a) for a in (after, mine, other, bias, gain, shift)]
    return launch(body, "second_norm", at, ins, [shape(half, width), shape(half, width, dtype=BF)], us=1.5)


def feed_up(at, mine, other, f1, f2, b1):
    half, width = mine.shape
    units = f1.shape[1]

    def body(at, ins, outs, _):
        mine, other, f1, f2, b1 = ins
        keep, send, hidden, slope = outs
        for r, (x, target) in enumerate(((other, send), (mine, keep))):
            span = slice((1 - r) * half, (2 - r) * half)
            low, steep = gelu_pair(mm(x[...], f1[...]) + b1[...])
            hidden[span, :] = low
            slope[span, :] = steep
            target[...] = mm(low, f2[...]).astype(target.dtype)

    ins = [near(a) for a in (mine, other, f1, f2, b1)]
    outs = [
        shape(half, width),
        shape(half, width, dtype=BF),
        shape(2 * half, units, dtype=BF),
        shape(2 * half, units),
    ]
    return launch(body, "feed_up", at, ins, outs, us=4)


def third_norm(at, total, mine, other, cot, bias, gain, shift):
    half, width = mine.shape

    def body(at, ins, outs, _):
        total, mine, other, cot, bias, gain, shift = ins
        mixed, dlast_out, low, sums = outs
        normed_mid, _ = norm_stats(total[...])
        last = normed_mid * gain[1:2] + shift[1:2] + (mine[...].astype(F32) + other[...].astype(F32)) + bias[...]
        normed, inverse = norm_stats(last)
        first_row = at[0] * half
        live = (first_row + lax.broadcasted_iota(jnp.int32, (half, 1), 0) < at[3]).astype(F32)
        mixed[...] = ((normed * gain[2:3] + shift[2:3]) * live).astype(BF)
        delta = cot[...].astype(F32) * live
        dlast = norm_backward(delta, normed, inverse, gain[2:3])
        dlast_out[...] = dlast
        low[...] = dlast.astype(BF)
        counted = counted_rows(at, half)
        sums[...] = stacked_sums(delta * normed * counted, delta * counted, dlast * counted)

    ins = [
        near(total),
        near(mine),
        near(other),
        near(cot, lambda ref, at: ref.at[rows_at(at[0], half), :]),
        near(bias),
        near(gain),
        near(shift),
    ]
    outs = [shape(half, width, dtype=BF), shape(half, width), shape(half, width, dtype=BF), shape(8, width)]
    return launch(body, "third_norm", at, ins, outs, us=2.5)


def feed_down(at, mine, other, f1, f2, slope):
    half, width = mine.shape
    units = f1.shape[1]

    def body(at, ins, outs, _):
        mine, other, f1, f2, slope = ins
        keep, send, dpre, sums = outs
        total = jnp.zeros((1, units), F32)
        for r, (x, target) in enumerate(((other, send), (mine, keep))):
            span = slice((1 - r) * half, (2 - r) * half)
            grad = mm(x[...], f2[...], NT) * slope[span, :]
            total = total + column_sum(grad)
            low = grad.astype(BF)
            dpre[span, :] = low
            target[...] = mm(low, f1[...], NT).astype(target.dtype)
        sums[...] = total

    ins = [near(a) for a in (mine, other, f1, f2, slope)]
    outs = [
        shape(half, width),
        shape(half, width, dtype=BF),
        shape(2 * half, units, dtype=BF),
        shape(1, units),
    ]
    return launch(body, "feed_down", at, ins, outs, us=3)


def second_back(at, dlast, mine, other, total, gain):
    half, width = mine.shape

    def body(at, ins, outs, _):
        dlast, mine, other, total, gain = ins
        dsecond, low, sums = outs
        dmid = dlast[...] + (mine[...].astype(F32) + other[...].astype(F32))
        normed, inverse = norm_stats(total[...])
        result = norm_backward(dmid, normed, inverse, gain[1:2])
        dsecond[...] = result
        low[...] = result.astype(BF)
        counted = counted_rows(at, half)
        sums[...] = stacked_sums(dmid * normed * counted, dmid * counted, result * counted)

    ins = [near(a) for a in (dlast, mine, other, total, gain)]
    outs = [shape(half, width), shape(half, width, dtype=BF), shape(8, width)]
    return launch(body, "second_back", at, ins, outs, us=1.8)


def gelu_pair(pre):
    phi = 0.5 * (1.0 + erf(pre * 0.7071067811865476))
    return (pre * phi).astype(BF), phi + pre * (jnp.exp(pre * pre * -0.5) * 0.3989422804014327)


def cross_backward(at, z_mine, z_other, raised, inverse, query, keys, values, w, wo, nh):
    half, width = z_mine.shape
    rows = 2 * half
    local = w.shape[1]
    hd = local // nh
    slots = keys.shape[1]
    scale = hd**-0.5

    def body(at, ins, outs, scratch):
        z_halves, (wo, inverse, values, raised, query, keys, w) = ins[:2], ins[2:]
        keep, send, dquery, dkv, sums = outs
        douts, right, found = scratch
        zero = jnp.zeros((half, hd), BF)
        head_sum = jnp.zeros((1, local), F32)
        for r in range(2):
            span = slice(r * half, (r + 1) * half)
            dhead = mm(z_halves[r][...], wo[...], NT)
            head_sum = head_sum + column_sum(dhead)
            scaled = query[span, :] * jnp.asarray(scale, BF)
            for h in range(nh):
                part = slice(h * hd, (h + 1) * hd)
                dout = (dhead[:, part] * inverse[h, span, 0:1]).astype(BF)
                douts[h, span, :] = jnp.concatenate([dout, dout], axis=1)
                right[h, 0, span, :] = jnp.concatenate([scaled[:, part], zero], axis=1)
                right[h, 1, span, :] = jnp.concatenate([zero, dout], axis=1)

        def one_head(h, _):
            grad = None
            for r in range(2):
                span = slice(r * half, (r + 1) * half)
                dprob = mm(douts[h, span, :], values[h], NT)
                low = raised[h, span, :]
                e = low.astype(F32)
                weighed = e * dprob
                mean = jnp.sum(weighed, axis=1, keepdims=True) * inverse[h, span, 0:1]
                dscore = (weighed - e * mean).astype(BF)
                both = mm(dscore, keys[h])
                found[h, span, :] = both[:, :hd] + both[:, hd:]
                part = mm(dscore, right[h, 0, span, :], TN) + mm(low, right[h, 1, span, :], TN)
                grad = part if grad is None else grad + part
            dkv[h] = grad.astype(BF)
            return 0

        lax.fori_loop(0, nh, one_head, 0)
        query_sum = jnp.zeros((1, local), F32)
        for r, target in enumerate((keep, send)):
            span = slice(r * half, (r + 1) * half)
            dq = jnp.concatenate([found[h, span, :] for h in range(nh)], axis=1) * scale
            query_sum = query_sum + column_sum(dq)
            dq_low = dq.astype(BF)
            dquery[span, :] = dq_low
            target[...] = mm(dq_low, w[0]).astype(target.dtype)
        sums[...] = jnp.concatenate([query_sum, head_sum], axis=0)

    return launch(
        body,
        "cross_bwd",
        at,
        [near(a) for a in (z_mine, z_other, wo, inverse, values, raised, query, keys, w)],
        [
            shape(half, width),
            shape(half, width, dtype=BF),
            shape(rows, local, dtype=BF),
            shape(nh, slots, 2 * hd, dtype=BF),
            shape(2, local),
        ],
        scratch=[
            pltpu.VMEM((nh, rows, 2 * hd), BF),
            pltpu.VMEM((nh, 2, rows, 2 * hd), BF),
            pltpu.VMEM((nh, rows, hd), F32),
        ],
        mib=30,
        us=11,
    )


def store_gradient(at, dkv, w, nh):
    _, slots, twice = dkv.shape
    _, local, width = w.shape
    hd = twice // 2
    seg = slots // 4

    def body(at, ins, outs, _):
        dkv, w = ins
        keep, send = outs
        weights = []
        for h in range(nh):
            part = slice(h * hd, (h + 1) * hd)
            weights += [w[1][part], w[2][part]]
        weight = jnp.concatenate(weights, axis=0)
        for slot in (1, 3, 0, 2):
            rows = jnp.concatenate([dkv[h, slot * seg : (slot + 1) * seg, :] for h in range(nh)], axis=1)
            part = mm(rows, weight)
            if slot % 2 == 0:
                keep[slot // 2] = part
            else:
                send[slot // 2] = part.astype(BF)

    return launch(
        body,
        "store_grad",
        at,
        [near(dkv), near(w)],
        [shape(2, seg, width), shape(2, seg, width, dtype=BF)],
        us=2.6,
    )


def group_outs(width, columns, blocks):
    if not blocks:
        return [shape(width, columns)]
    n, r = blocks
    return [shape(n * r, columns, dtype=BF), shape(n, r, columns)]


def emit_group(at, grad, outs, blocks, first, columns, kept_first=None):
    if not blocks:
        outs[0][:, first : first + columns] = grad[...]
        return
    n, r = blocks
    kept_first = first if kept_first is None else kept_first
    span, kept = slice(first, first + columns), slice(kept_first, kept_first + columns)
    for b in range(n):
        theirs = pl.ds(pl.multiple_of((2 * b + 1 - at[4]) * r, 8), r)
        outs[0][b * r : (b + 1) * r, span] = grad[theirs, :].astype(BF)
        outs[1][b, :, kept] = grad[pl.ds(pl.multiple_of((2 * b + at[4]) * r, 8), r), :]


def turned_product(out, left, right, step=256):
    if left.shape[1] % step:
        out[...] = mm(left[...], right[...], TN)
        return

    def some(i, _):
        span = pl.ds(pl.multiple_of(i * step, step), step)
        out[span, :] = mm(left[:, span], right[...], TN)
        return 0

    lax.fori_loop(0, left.shape[1] // step, some, 0)


def feed_grads(at, mid_mine, mid_other, dpre, dlast_mine, dlast_other, hidden, blocks):
    half, width = mid_mine.shape
    units = dpre.shape[1]
    if blocks:
        n, r = blocks
        structs = [shape(n * r, 2 * units, dtype=BF), shape(n, r, 2 * units)]
    else:
        structs = [shape(width, units), shape(width, units)]

    def body(at, ins, outs, scratch):
        mid_mine, mid_other, dpre, dlast_mine, dlast_other, hidden = ins
        left, grad = scratch
        for i, (mine, other, right) in enumerate(((mid_mine, mid_other, dpre), (dlast_mine, dlast_other, hidden))):
            left[:half, :] = mine[...]
            left[half:, :] = other[...]
            turned_product(grad, left, right)
            emit_group(at, grad, outs if blocks else outs[i:], blocks, i * units if blocks else 0, units)

    return launch(
        body,
        "feed_grads",
        at,
        [near(a) for a in (mid_mine, mid_other, dpre, dlast_mine, dlast_other, hidden)],
        structs,
        scratch=[pltpu.VMEM((2 * half, width), BF), pltpu.VMEM((width, units), F32)],
        us=4,
    )


def cross_grads(at, z_mine, z_other, mine, other, dquery, heads, shards, dkv, nh, blocks):
    half, width = mine.shape
    local = dquery.shape[1]
    hd = local // nh
    seg = shards[0].shape[0]

    def body(at, ins, outs, scratch):
        shards, (z_mine, z_other, mine, other, dquery, heads, dkv) = ins[0:4], ins[4:]
        (grad,) = scratch
        grad[...] = mm(mine[...], dquery[:half], TN) + mm(other[...], dquery[half:], TN)
        emit_group(at, grad, outs, blocks, 0, local)
        grad[...] = mm(z_mine[...], heads[:half], TN) + mm(z_other[...], heads[half:], TN)
        emit_group(at, grad, outs, blocks, 3 * local, local)
        both = None
        for slot, block in enumerate(shards):
            rows = jnp.concatenate([dkv[h, slot * seg : (slot + 1) * seg, :] for h in range(nh)], axis=1)
            part = mm(block[...], rows, TN)
            both = part if both is None else both + part
        for i in range(2):
            grad[...] = jnp.concatenate([both[:, (2 * h + i) * hd : (2 * h + i + 1) * hd] for h in range(nh)], axis=1)
            emit_group(at, grad, outs, blocks, (1 + i) * local, local)

    return launch(
        body,
        "cross_grads",
        at,
        [near(a) for a in (*shards, z_mine, z_other, mine, other, dquery, heads, dkv)],
        group_outs(width, 4 * local, blocks),
        scratch=[pltpu.VMEM((width, local), F32)],
        us=4,
    )


def first_back(at, dsecond, mine, other, total, gain):
    half, width = mine.shape

    def body(at, ins, outs, _):
        dsecond, mine, other, total, gain = ins
        dfirst, low, sums = outs
        value = dsecond[...] + (mine[...].astype(F32) + other[...].astype(F32))
        normed, inverse = norm_stats(total[...])
        result = norm_backward(value, normed, inverse, gain[0:1])
        dfirst[...] = result
        low[...] = result.astype(BF)
        counted = counted_rows(at, half)
        sums[...] = stacked_sums(value * normed * counted, value * counted, result * counted)

    ins = [near(a) for a in (dsecond, mine, other, total, gain)]
    outs = [shape(half, width), shape(half, width, dtype=BF), shape(8, width)]
    return launch(body, "first_back", at, ins, outs, us=1.8)


def self_backward(at, mine, other, tokens, w, wo, qkv, prob, flat, mixed, sums, nh, blocks):
    half, width = mine.shape
    rows = 2 * half
    local = wo.shape[0]
    hd = local // nh
    scale = hd**-0.5

    def body(at, ins, outs, scratch):
        mine, other, wo, qkv, prob, tok, w, mixed, flat = ins[:9]
        third_sums, second_sums, first_sums, fc1_sum, head_sums = ins[9:]
        send, keep = outs[0:2]
        group, extra = outs[2:-1], outs[-1]
        z, dqkv, grad = scratch
        own, distant = rows_at(at[0], half), rows_at(1 - at[0], half)
        z[own, :] = mine[...]
        z[distant, :] = other[...]
        dself = mm(z[...], wo[...], NT).astype(BF)
        v, k, q = qkv[2], qkv[1], qkv[0]
        dq, dk, dv = [], [], []
        for h in range(nh):
            part = slice(h * hd, (h + 1) * hd)
            weights_low = prob[h]
            weights = weights_low.astype(F32)
            weighed = weights * mm(dself[:, part], v[:, part], NT)
            dscore = (weighed - weights * jnp.sum(weighed, axis=1, keepdims=True)).astype(BF)
            dq.append(mm(dscore, k[:, part]))
            dk.append(mm(dscore, q[:, part], TN))
            dv.append(mm(weights_low, dself[:, part], TN))
        dquery = jnp.concatenate(dq, axis=1) * scale
        dvalue = jnp.concatenate(dv, axis=1)
        dqkv[0] = dquery.astype(BF)
        dqkv[1] = (jnp.concatenate(dk, axis=1) * scale).astype(BF)
        dqkv[2] = dvalue.astype(BF)
        x = tok[...]
        for i in range(3):
            grad[...] = mm(x, dqkv[i], TN)
            emit_group(at, grad, group, blocks, i * local, local)
        grad[...] = mm(z[...], flat[...], TN)
        emit_group(at, grad, group, blocks, 3 * local, local)
        pad = jnp.zeros((1, width - 2 * local), F32)
        extra[...] = jnp.concatenate(
            [
                third_sums[0:3],
                second_sums[0:3],
                first_sums[0:3],
                fc1_sum[...],
                jnp.concatenate([head_sums[0:1], head_sums[1:2], pad], axis=1),
                jnp.concatenate([column_sum(dquery), column_sum(dvalue), pad], axis=1),
                jnp.zeros((EXTRA - 12, width), F32),
            ],
            axis=0,
        )
        send[half:, :] = mixed[...]
        for place, out in ((distant, send), (own, keep)):
            total = mm(dqkv[0, place, :], w[0]) + mm(dqkv[1, place, :], w[1]) + mm(dqkv[2, place, :], w[2])
            out[0:half, :] = total.astype(out.dtype)

    return launch(
        body,
        "self_bwd",
        at,
        [near(a) for a in (mine, other, wo, qkv, prob, tokens, w, mixed, flat, *sums)],
        [shape(2 * half, width, dtype=BF), shape(half, width)]
        + group_outs(width, 4 * local, blocks)
        + [shape(EXTRA, width)],
        scratch=[
            pltpu.VMEM((rows, width), BF),
            pltpu.VMEM((3, rows, local), BF),
            pltpu.VMEM((width, local), F32),
        ],
        mib=20,
        us=6,
    )


def add_stage(at, keep, got, small, bit, apart=False):
    n, rows, _ = keep[0].shape
    starts = [0]
    for part in keep:
        starts.append(starts[-1] + part.shape[2])
    columns = starts[-1]
    tail = 0 if small is None else 2 * small.shape[0]
    reach = small.shape[1] if tail else 0

    def body(at, ins, outs, _):
        keeps, gots = ins[: len(keep)], ins[len(keep) : len(keep) + len(got)]
        mine = at[bit]
        send, stay = outs[:2]
        for b in range(n // 2):
            for chosen, out in ((1 - mine, send), (mine, stay)):
                block = 2 * b + chosen
                for i, part in enumerate(keeps):
                    span = slice(starts[i], starts[i + 1])
                    source, first = (gots[i], 0) if len(got) == len(keep) else (gots[0], starts[i])
                    arrived = source[
                        pl.ds(pl.multiple_of(block * rows, 8), rows), first : first + starts[i + 1] - starts[i]
                    ]
                    value = part[block] + arrived.astype(F32)
                    if out is send:
                        send[b * rows : (b + 1) * rows, span] = value.astype(BF)
                    else:
                        stay[b, :, span] = value
        if tail:
            total = ins[-1][...]
            if not apart:
                total = total + from_terms(gots[0][n * rows :, 0:reach])
            outs[2][...] = total
            send[n // 2 * rows :, 0:reach] = two_terms(total)
            if reach < columns:
                send[n // 2 * rows :, reach:] = jnp.zeros((tail, columns - reach), BF)

    ins = [near(part) for part in (*keep, *got)] + ([near(small)] if tail else [])
    outs = [shape(n // 2 * rows + tail, columns, dtype=BF), shape(n // 2, rows, columns)]
    if tail:
        outs.append(shape(small.shape[0], reach))
    return launch(body, "add_stage", at, ins, outs, us=1)


def last_stage(at, keep, got, small, parts):
    _, rows, columns = keep.shape
    each = columns // sum(count for count, _ in parts)
    reach = 0 if small is None else small.shape[1]

    def body(at, ins, outs, _):
        total = ins[0][0] + ins[1][0:rows].astype(F32)
        first = 0
        for out, (count, turned) in zip(outs, parts):
            if count == 1:
                value = total[:, first * each : (first + 1) * each]
                out[...] = value.T if turned else value
            else:
                for i in range(count):
                    out[i] = total[:, (first + i) * each : (first + i + 1) * each]
            first += count
        if reach:
            outs[-1][...] = ins[2][...] + from_terms(ins[1][rows:, 0:reach])

    outs = []
    for count, turned in parts:
        dims = (rows, each) if count == 1 else (count, rows, each)
        outs.append(shape(*(dims[::-1] if turned else dims)))
    ins = [near(keep), near(got)]
    if reach:
        ins.append(near(small))
        outs.append(shape(small.shape[0], reach))
    return launch(body, "last_stage", at, ins, outs, us=1)


def join_halves(at, mine, other):
    half, width = mine.shape
    skip = other.shape[0] - half

    def body(at, ins, outs, _):
        outs[0][rows_at(at[0], half), :] = ins[0][...]
        outs[0][rows_at(1 - at[0], half), :] = ins[1][...]

    out = shape(2 * half, width, dtype=mine.dtype)
    ins = [near(mine), near(other, lambda ref, at: ref.at[pl.ds(skip, half), :])]
    return launch(body, "join_halves", at, ins, [out])[0]


def flip(bit, size):
    return [(i, i ^ bit) for i in range(size)]


def butterfly(value, axis, size):
    bit = 1
    while bit < size:
        value = value + lax.ppermute(value, axis, flip(bit, size))
        bit *= 2
    return value


def on_device(
    tokens,
    store,
    summary_length,
    top_index,
    cotangent,
    self_qkv_weight,
    self_qv_bias,
    self_out_weight,
    self_out_bias,
    qkv_weight,
    qv_bias,
    out_weight,
    out_bias,
    fc1_weight,
    fc1_bias,
    fc2_weight,
    fc2_bias,
    norm_gain,
    norm_shift,
):
    rows, width = tokens.shape
    half = rows // 2
    nh = top_index.shape[1]
    local = qkv_weight.shape[2]
    units = fc1_weight.shape[1]
    seg = store.shape[1]
    wide = lax.axis_size("wide")
    place = lax.axis_index("narrow")
    doc = lax.axis_index("wide")
    core, across = place % 2, place // 2
    at = jnp.stack([core, across, place, summary_length[0], doc % 2, doc // 2 % 2, doc // 4]).astype(jnp.int32)
    blocks = (wide // 2, width // wide) if wide == 8 else None
    row = lambda v: v.reshape(1, -1)
    self_w = jnp.swapaxes(self_qkv_weight, 1, 2)
    cross_w = jnp.swapaxes(qkv_weight, 1, 2)

    def to_core(v):
        return lax.ppermute(v, "narrow", CORE)

    def to_across(v):
        return lax.ppermute(v, "narrow", ACROSS)

    def over(v, bit):
        return lax.ppermute(v, "wide", flip(bit, wide))

    def chip_sum(keep, send):
        return (keep + to_core(send).astype(F32)).astype(BF)

    store_x = to_across(store[0])
    qkv, prob, flat, send, keep = self_forward(at, tokens, self_w, self_qv_bias, self_out_weight, nh)
    mine = chip_sum(keep, send)
    other = to_across(mine)
    index = index_rows(top_index)
    bias_mine = make_mask(tie(at, mine), index, top_index.shape, seg, 128, 0)
    store_x, store_own = tie((store_x, store[0]), bias_mine)
    shards = [store_own, to_core(store_own), store_x, to_core(store_x)]
    bias_other = make_mask(tie(at, bias_mine), index, top_index.shape, seg, 128, 1)
    other = tie(other, bias_other)
    first_total, after, after_low = first_norm(at, mine, other, tokens, row(self_out_bias), norm_gain, norm_shift)
    after_other = to_core(after_low)

    keys, values = keys_values(tie(at, after_low), shards, cross_w, nh)
    keep, send, raised, inverse, query, heads = cross_forward(
        tie(at, keys), after_low, after_other, bias_mine, bias_other, keys, values, cross_w, qv_bias, out_weight, nh
    )
    mine = chip_sum(keep, send)
    second_total, mid_low = second_norm(at, after, mine, to_across(mine), row(out_bias), norm_gain, norm_shift)
    mid_other = to_core(mid_low)

    keep, send, hidden, slope = feed_up(at, mid_low, mid_other, fc1_weight, fc2_weight, row(fc1_bias))
    mine = chip_sum(keep, send)
    mixed_half, dlast, dlast_low, third_sums = third_norm(
        at, second_total, mine, to_across(mine), cotangent, row(fc2_bias), norm_gain, norm_shift
    )
    dlast_other = to_core(dlast_low)
    keep, send, dpre, fc1_sum = feed_down(at, dlast_low, dlast_other, fc1_weight, fc2_weight, slope)
    mine = chip_sum(keep, send)
    other = to_across(mine)
    feed_out = feed_grads(tie(at, mine), mid_low, mid_other, dpre, dlast_low, dlast_other, hidden, blocks)
    other = tie(other, feed_out[0])
    dsecond, z, second_sums = second_back(at, dlast, mine, other, second_total, norm_gain)
    z_other = to_core(z)

    keep, send, dquery, dkv, cross_sums = cross_backward(
        at, z, z_other, raised, inverse, query, keys, values, cross_w, out_weight, nh
    )
    mine = chip_sum(keep, send)
    other = to_across(mine)
    cross_out = cross_grads(
        tie(at, mine), z, z_other, after_low, after_other, dquery, heads, shards, dkv, nh, blocks
    )
    started = cross_out[0]
    if blocks:
        feed_send, feed_keep = add_stage(tie(at, started), [feed_out[1]], [over(feed_out[0], 1)], None, 5)
        feed_next = over(feed_send, 2)
        started = feed_send
    store_keep, store_send = store_gradient(tie(at, started), dkv, cross_w, nh)
    other = tie(other, store_send)
    dfirst, dfirst_low, first_sums = first_back(at, dsecond, mine, other, first_total, norm_gain)
    dfirst_other = to_core(dfirst_low)
    store_close = to_core(tie(store_send, dfirst_other))
    started = dfirst_low

    send, keep, *self_out, small = self_backward(
        tie(at, dfirst_other, store_close),
        dfirst_low,
        dfirst_other,
        tokens,
        self_w,
        self_out_weight,
        qkv,
        prob,
        flat,
        mixed_half,
        (third_sums, second_sums, first_sums, fc1_sum, cross_sums),
        nh,
        blocks,
    )
    small_rows = butterfly(small[:9], "narrow", 4)
    if blocks:
        cross_got = tie(over(cross_out[0], 1), small)
        feed_send, feed_keep = add_stage(tie(at, cross_got), [feed_keep], [feed_next], None, 6)
        feed_next = over(feed_send, 4)
        send = tie(send, feed_send)
    close = to_core(send)
    mine = (keep + close[:half].astype(F32)).astype(BF)
    other = to_across(mine)
    small = jnp.concatenate([tie(small_rows, mine), small[9:]], axis=0)
    if blocks:
        small = small + over(small, 1)
        later = tie(at, small)
        both_send, both_keep, small = add_stage(
            later, [cross_out[1], self_out[1]], [cross_got, over(self_out[0], 1)], small, 5, True
        )
        both_next = over(both_send, 2)
        other = tie(other, both_send)
    tokens_half = dfirst + (mine.astype(F32) + other.astype(F32))
    tokens_other = to_core(tokens_half)
    store_distant = to_across(tie((store_keep[1] + store_close[1].astype(F32)).astype(BF), other))
    mixed = join_halves(tie(at, tokens_half), mixed_half, close)
    if blocks:
        fc1_grad, fc2_grad = last_stage(tie(at, mixed), feed_keep, feed_next, None, [(1, False), (1, False)])
        fc2_grad = fc2_grad.T
        tokens_other = tie(tokens_other, fc1_grad)
    tokens_grad = join_halves(at, tokens_half, tokens_other)
    if blocks:
        both_send, both_keep, small = add_stage(tie(at, tokens_grad), [both_keep], [both_next], small, 6)
        both_next = over(both_send, 4)
        store_distant = tie(store_distant, both_send)
    store_grad = (store_keep[0] + store_close[0].astype(F32) + store_distant.astype(F32))[None]

    if blocks:
        qkv_grad, out_grad, self_qkv_grad, self_out_grad, small = last_stage(
            tie(at, store_grad), both_keep, both_next, small, [(3, False), (1, True), (3, False), (1, True)]
        )
    else:
        scatter = functools.partial(lax.psum_scatter, axis_name="wide", tiled=True)
        parts = lambda g: jnp.stack([g[:, i * local : (i + 1) * local] for i in range(3)])
        fc1_grad = scatter(feed_out[0], scatter_dimension=0)
        fc2_grad = scatter(feed_out[1].T, scatter_dimension=1)
        qkv_grad = scatter(parts(cross_out[0]), scatter_dimension=1)
        out_grad = scatter(cross_out[0][:, 3 * local :].T, scatter_dimension=1)
        self_qkv_grad = scatter(parts(self_out[0]), scatter_dimension=1)
        self_out_grad = scatter(self_out[0][:, 3 * local :].T, scatter_dimension=1)
        small = butterfly(small, "wide", wide)
    gain_last, shift_last, fc2_b, gain_mid, shift_mid, out_b, gain_first, shift_first, self_out_b = (
        small[i] for i in range(9)
    )
    return (
        mixed,
        tokens_grad,
        store_grad,
        self_qkv_grad,
        small[11, : 2 * local].reshape(2, local),
        self_out_grad,
        self_out_b,
        qkv_grad,
        small[10, : 2 * local].reshape(2, local),
        out_grad,
        out_b,
        fc1_grad,
        small[9],
        fc2_grad,
        fc2_b,
        jnp.stack([gain_first, gain_mid, gain_last]),
        jnp.stack([shift_first, shift_mid, shift_last]),
    )


def solution(mesh):
    placed = (
        P("wide", None),
        P("wide", "narrow", None),
        P("wide"),
        P("wide", "narrow", None, None),
        P("wide", None),
        P(None, None, "narrow"),
        P(None, "narrow"),
        P("narrow", None),
        P(),
        P(None, None, "narrow"),
        P(None, "narrow"),
        P("narrow", None),
        P(),
        P(None, "narrow"),
        P("narrow"),
        P("narrow", None),
        P(),
        P(),
        P(),
    )
    return jax.shard_map(
        on_device,
        mesh=mesh,
        in_specs=placed,
        out_specs=(
            P("wide", None),
            P("wide", None),
            P("wide", "narrow", None),
            P(None, "wide", "narrow"),
            P(None, "narrow"),
            P("narrow", "wide"),
            P(),
            P(None, "wide", "narrow"),
            P(None, "narrow"),
            P("narrow", "wide"),
            P(),
            P("wide", "narrow"),
            P("narrow"),
            P("narrow", "wide"),
            P(),
            P(),
            P(),
        ),
        check_vma=False,
    )
```

```python
import functools

import jax
import jax.numpy as jnp
from jax import lax
from jax.experimental import pallas as pl
from jax.experimental.pallas import tpu as pltpu
from jax.sharding import PartitionSpec as P

F32 = jnp.float32
BF = jnp.bfloat16
NN = (((1,), (0,)), ((), ()))
NT = (((1,), (1,)), ((), ()))
TN = (((0,), (0,)), ((), ()))
EPS = 1e-05
PACE = 1.1e8
SELF_MIB = 60
EXTRA = 16

CORE = [(i, i ^ 1) for i in range(4)]
ACROSS = [(i, i ^ 2) for i in range(4)]


def mm(left, right, dims=NN):
    return lax.dot_general(left, right, dims, preferred_element_type=F32)


def shape(*dims, dtype=F32):
    return jax.ShapeDtypeStruct(dims, dtype)


def tie(value, *earlier):
    return lax.optimization_barrier((value, *earlier))[0]


class Operand:
    def __init__(self, source, buffer, sems, first, parts):
        self.buffer = buffer
        self.parts = parts
        if parts:
            self.copies = [
                pltpu.make_async_copy(source.at[i], buffer.at[i], sems.at[first + i]) for i in range(buffer.shape[0])
            ]
        else:
            self.copies = [pltpu.make_async_copy(source, buffer, sems.at[first])]
        self.waited = [False] * len(self.copies)
        for copy in self.copies:
            copy.start()

    def ready(self, part=None):
        for i, copy in enumerate(self.copies):
            if not self.waited[i] and (part is None or i == part):
                copy.wait()
                self.waited[i] = True

    @property
    def shape(self):
        return self.buffer.shape

    def __getitem__(self, at):
        self.ready(at if self.parts and isinstance(at, int) else None)
        return self.buffer[at]


class Result:
    def __init__(self, target, buffer, sems, first, parts):
        self.buffer = buffer
        if parts:
            self.copies = [
                pltpu.make_async_copy(buffer.at[i], target.at[i], sems.at[first + i]) for i in range(buffer.shape[0])
            ]
        else:
            self.copies = [pltpu.make_async_copy(buffer, target, sems.at[first])]
        self.started = [False] * len(self.copies)

    @property
    def shape(self):
        return self.buffer.shape

    @property
    def dtype(self):
        return self.buffer.dtype

    def __setitem__(self, at, value):
        self.buffer[at] = value

    def flush(self, part=0):
        self.copies[part].start()
        self.started[part] = True

    def finish(self):
        for i in range(len(self.copies)):
            if not self.started[i]:
                self.flush(i)
        for copy in self.copies:
            copy.wait()


def far(array, take=None, dims=None, parts=False):
    return ("far", array, take, tuple(dims or array.shape), parts)


def near(array, take=None):
    return ("near", array, take, None, False)


def raw(array):
    return ("raw", array, None, None, False)


def launch(body, name, at, ins, outs, scratch=(), mib=16, us=2.0):
    in_specs = [pl.BlockSpec(memory_space=pltpu.SMEM)]
    buffers, n_in, n_out = [], 0, 0
    for kind, array, _, dims, parts in ins:
        in_specs.append(pl.BlockSpec(memory_space=pltpu.VMEM if kind == "near" else pltpu.HBM))
        if kind == "far":
            buffers.append(pltpu.VMEM(dims, array.dtype))
            n_in += dims[0] if parts else 1
    out_specs, structs = [], []
    for out in outs:
        if isinstance(out, tuple):
            struct, parts = out
            out_specs.append(pl.BlockSpec(memory_space=pltpu.HBM))
            buffers.append(pltpu.VMEM(struct.shape, struct.dtype))
            n_out += struct.shape[0] if parts else 1
        else:
            struct = out
            out_specs.append(pl.BlockSpec(memory_space=pltpu.VMEM))
        structs.append(struct)
    n_buffers = len(buffers)
    sems = [pltpu.SemaphoreType.DMA((max(n, 1),)) for n in (n_in, n_out)]

    def kernel(at_ref, *refs):
        in_refs, out_refs = refs[: len(ins)], refs[len(ins) : len(ins) + len(outs)]
        rest = refs[len(ins) + len(outs) :]
        bufs, user, (in_sems, out_sems) = list(rest[:n_buffers]), rest[n_buffers:-2], rest[-2:]
        place, given = 0, []
        for ref, (kind, _, take, dims, parts) in zip(in_refs, ins):
            source = take(ref, at_ref) if take else ref
            if kind == "far":
                given.append(Operand(source, bufs.pop(0), in_sems, place, parts))
                place += dims[0] if parts else 1
            else:
                given.append(source)
        place, results = 0, []
        for ref, out in zip(out_refs, outs):
            if isinstance(out, tuple):
                results.append(Result(ref, bufs.pop(0), out_sems, place, out[1]))
                place += out[0].shape[0] if out[1] else 1
            else:
                results.append(ref)
        body(at_ref, given, results, user)
        for operand in given:
            if isinstance(operand, Operand):
                operand.ready()
        for result in results:
            if isinstance(result, Result):
                result.finish()

    return pl.pallas_call(
        kernel,
        in_specs=in_specs,
        out_specs=out_specs,
        out_shape=structs,
        scratch_shapes=buffers + list(scratch) + sems,
        compiler_params=pltpu.CompilerParams(vmem_limit_bytes=mib << 20),
        cost_estimate=pl.CostEstimate(flops=int(us * PACE), bytes_accessed=1000, transcendentals=0),
        name=name,
    )(at, *[entry[1] for entry in ins])


def norm_stats(value):
    centre = value - jnp.mean(value, axis=-1, keepdims=True)
    spread = jnp.mean(centre * centre, axis=-1, keepdims=True)
    inverse = lax.rsqrt(spread + EPS)
    return centre * inverse, inverse


def norm_backward(grad, normed, inverse, gain):
    scaled = grad * gain
    centred = scaled - jnp.mean(scaled, axis=-1, keepdims=True)
    return inverse * (centred - normed * jnp.mean(scaled * normed, axis=-1, keepdims=True))


def column_sum(value):
    return jnp.sum(value, axis=0, keepdims=True)


def erf(value):
    x = jnp.clip(value, -4.0, 4.0)
    y = x * x
    top = jnp.full_like(y, -2.72614225801306e-10)
    for factor in (
        2.77068142495902e-08,
        -2.10102402082508e-06,
        -5.69250639462346e-05,
        -7.34990630326855e-04,
        -2.95459980854025e-03,
        -1.60960333262415e-02,
    ):
        top = top * y + factor
    low = jnp.full_like(y, -1.45660718464996e-05)
    for factor in (
        -2.13374055278905e-04,
        -1.68282697438203e-03,
        -7.37332916720468e-03,
        -1.42647390514189e-02,
    ):
        low = low * y + factor
    return x * top / low


def two_terms(value):
    high = value.astype(BF)
    return jnp.concatenate([high, (value - high.astype(F32)).astype(BF)], axis=0)


def from_terms(stacked):
    rows = stacked.shape[0] // 2
    terms = stacked.astype(F32)
    return terms[:rows] + terms[rows:]


def rows_at(place, rows):
    return pl.ds(pl.multiple_of(place * rows, rows), rows)


def self_forward(at, tokens, w, b, wo, nh):
    rows, width = tokens.shape
    local = w.shape[1]
    half = rows // 2
    hd = local // nh
    scale = hd**-0.5

    def body(at, ins, outs, _):
        tok, w, wo, b = ins
        qkv, prob, flat, send, keep = outs
        x = tok[...]
        q = (mm(x, w[0], NT) + b[0:1]).astype(BF)
        k = mm(x, w[1], NT).astype(BF)
        v = (mm(x, w[2], NT) + b[1:2]).astype(BF)
        for i, value in enumerate((q, k, v)):
            qkv[i] = value
            qkv.flush(i)
        row_ids = lax.broadcasted_iota(jnp.int32, (rows, rows), 0)
        key_ids = lax.broadcasted_iota(jnp.int32, (rows, rows), 1)
        allowed = (key_ids <= row_ids) & (key_ids < at[3])
        found = []
        for h in range(nh):
            part = slice(h * hd, (h + 1) * hd)
            scores = mm(q[:, part], k[:, part], NT) * scale
            scores = jnp.where(allowed, scores, -1e30)
            shifted = jnp.exp(scores - jnp.max(scores, axis=1, keepdims=True))
            weights = (shifted * (1.0 / jnp.sum(shifted, axis=1, keepdims=True))).astype(BF)
            prob[h] = weights
            prob.flush(h)
            found.append(mm(weights, v[:, part]).astype(BF))
        flat[...] = jnp.concatenate(found, axis=1)
        flat.flush()
        send[...] = mm(flat.buffer[rows_at(1 - at[0], half), :], wo[...]).astype(BF)
        send.flush()
        keep[...] = mm(flat.buffer[rows_at(at[0], half), :], wo[...])

    return launch(
        body,
        "self_fwd",
        at,
        [far(tokens), far(w, parts=True), far(wo), far(b)],
        [
            (shape(3, rows, local, dtype=BF), True),
            (shape(nh, rows, rows, dtype=BF), True),
            (shape(rows, local, dtype=BF), False),
            (shape(half, width, dtype=BF), False),
            (shape(half, width), False),
        ],
        mib=SELF_MIB,
        us=4,
    )


def first_norm(at, mine, other, tokens, bias, gain, shift):
    half, width = mine.shape

    def body(at, ins, outs, _):
        mine, other, tok, bias, gain, shift = ins
        total, after, low = outs
        value = tok[...].astype(F32) + (mine[...].astype(F32) + other[...].astype(F32)) + bias[...]
        total[...] = value
        normed, _ = norm_stats(value)
        result = normed * gain[0:1] + shift[0:1]
        after[...] = result
        low[...] = result.astype(BF)

    return launch(
        body,
        "first_norm",
        at,
        [
            near(mine),
            near(other),
            near(tokens, lambda ref, at: ref.at[rows_at(at[0], half), :]),
            near(bias),
            near(gain),
            near(shift),
        ],
        [shape(half, width), shape(half, width), shape(half, width, dtype=BF)],
        us=1.7,
    )


def index_rows(top_index):
    rows, nh, ns, keep = top_index.shape
    flat = top_index.reshape(rows, nh, ns, keep // 128, 128).transpose(0, 1, 3, 2, 4)
    return flat.reshape(rows * nh * ns * (keep // 128), 128)


def make_mask(at, flat, dims, seg, tile, turn):
    rows, nh, ns, keep = dims
    halves = keep // 128
    per_row = nh * ns * halves
    tiles = rows // 2 // tile
    columns = ns * seg
    blocks = columns // 128
    group = 32

    def body(at, ins, outs, _):
        (index,) = ins
        (bias,) = outs
        lane = lax.broadcasted_iota(jnp.int32, (group, 128), 1).astype(F32)
        lane_low = lane.astype(BF)
        empty = jnp.full((group, 128), -1.0, BF)
        own = at[2]
        steps = []
        step = 1
        while step <= seg - keep:
            steps.insert(0, step)
            step *= 2
        turns = steps + [(seg * s) % 128 for s in range(ns)]
        below = {s: lane_low < jnp.asarray(s, BF) for s in turns if 0 < s < 128}

        for t in range(tiles):
            index.ready(t)
            source = index.buffer.at[t]

            def one_group(g, _):
                for h in range(nh):
                    v = [empty] * blocks
                    for slot in range(ns):
                        first, turn = divmod(seg * slot, 128)
                        for c in range(halves):
                            start = g * (group * per_row) + h * ns * halves + c * ns + (own ^ slot)
                            found = jnp.concatenate(
                                [source[pl.ds(start + q * 8 * per_row, 8, stride=per_row), :] for q in range(group // 8)],
                                axis=0,
                            )
                            ahead = (found.astype(F32) - (lane + float(128 * c))).astype(BF)
                            at_block = first + c
                            if turn == 0:
                                v[at_block] = ahead
                            else:
                                turned = pltpu.roll(ahead, turn, axis=1)
                                v[at_block] = jnp.where(below[turn], v[at_block], turned)
                                v[at_block + 1] = jnp.where(below[turn], turned, v[at_block + 1])
                    for s in steps:
                        gap = jnp.asarray(s, BF)
                        moved = [x - gap for x in v]
                        stay = [jnp.where(x >= gap, empty, x) for x in v]
                        if s % 128 == 0:
                            hop = s // 128
                            v = stay[:hop] + [jnp.maximum(stay[i], moved[i - hop]) for i in range(hop, blocks)]
                        else:
                            turned = [pltpu.roll(x, s, axis=1) for x in moved]
                            v = [
                                jnp.maximum(stay[i], jnp.where(below[s], turned[i - 1], turned[i])) for i in range(blocks)
                            ]
                    for i in range(blocks):
                        bias[h, pl.ds(pl.multiple_of(t * tile + g * group, group), group), i * 128 : (i + 1) * 128] = v[
                            i
                        ] * jnp.asarray(1e30, BF)
                return 0

            lax.fori_loop(0, tile // group, one_group, 0)

    flat = flat.reshape(2 * tiles, tile * per_row, 128)
    return launch(
        body,
        "mask",
        at,
        [
            far(
                flat,
                lambda ref, at: ref.at[pl.ds((at[0] ^ turn) * tiles, tiles)],
                (tiles, tile * per_row, 128),
                parts=True,
            )
        ],
        [shape(nh, rows // 2, columns, dtype=BF)],
        us=10,
    )[0]


def keys_values(at, shards, w, nh):
    seg, width = shards[0].shape
    local = w.shape[1]
    hd = local // nh

    def body(at, ins, outs, _):
        for slot in range(4):
            x = ins[slot][...]
            span = slice(slot * seg, (slot + 1) * seg)
            for i, out in enumerate(outs):
                full = mm(x, ins[4][i + 1], NT)
                high = full.astype(BF)
                low = (full - high.astype(F32)).astype(BF)
                for h in range(nh):
                    part = slice(h * hd, (h + 1) * hd)
                    out[h, span, :] = jnp.concatenate([high[:, part], low[:, part]], axis=1)

    out = shape(nh, 4 * seg, 2 * hd, dtype=BF)
    return launch(body, "keys_values", at, [near(s) for s in shards] + [near(w)], [out, out], us=2)


def cross_forward(at, mine, other, bias_mine, bias_other, keys, values, w, b, wo, nh):
    half, width = mine.shape
    rows = 2 * half
    local = w.shape[1]
    hd = local // nh
    slots = keys.shape[1]
    scale = hd**-0.5

    def body(at, ins, outs, scratch):
        mine, other, wq, keys, bias_mine, bias_other, values, wo, b = ins
        keep, send, raised, inverse, query, heads = outs
        twice, found = scratch
        for r, x in enumerate((mine, other)):
            q = (mm(x[...], wq[0], NT) + b[0:1]).astype(BF)
            query[r * half : (r + 1) * half, :] = q
            scaled = q * jnp.asarray(scale, BF)
            for h in range(nh):
                part = scaled[:, h * hd : (h + 1) * hd]
                twice[h, r * half : (r + 1) * half, :] = jnp.concatenate([part, part], axis=1)

        def one_head(h, _):
            for r, bias in enumerate((bias_mine, bias_other)):
                span = slice(r * half, (r + 1) * half)
                scores = mm(twice[h, span, :], keys[h], NT) + bias[h].astype(F32)
                e = jnp.exp(scores - jnp.max(scores, axis=1, keepdims=True))
                total = 1.0 / jnp.sum(e, axis=1, keepdims=True)
                low = e.astype(BF)
                raised[h, span, :] = low
                inverse[h, span, :] = jnp.broadcast_to(total, (half, 128))
                both = mm(low, values[h])
                found[h, span, :] = (both[:, :hd] + both[:, hd:]) * total
            return 0

        lax.fori_loop(0, nh, one_head, 0)
        for r, target in enumerate((keep, send)):
            span = slice(r * half, (r + 1) * half)
            out = (jnp.concatenate([found[h, span, :] for h in range(nh)], axis=1) + b[1:2]).astype(BF)
            heads[span, :] = out
            target[...] = mm(out, wo[...]).astype(target.dtype)

    return launch(
        body,
        "cross_fwd",
        at,
        [near(a) for a in (mine, other, w, keys, bias_mine, bias_other, values, wo, b)],
        [
            shape(half, width),
            shape(half, width, dtype=BF),
            shape(nh, rows, slots, dtype=BF),
            shape(nh, rows, 128),
            shape(rows, local, dtype=BF),
            shape(rows, local, dtype=BF),
        ],
        scratch=[pltpu.VMEM((nh, rows, 2 * hd), BF), pltpu.VMEM((nh, rows, hd), F32)],
        mib=30,
        us=9,
    )


def counted_rows(at, half):
    rows = half // 2
    place = lax.broadcasted_iota(jnp.int32, (half, 1), 0)
    return ((place >= at[1] * rows) & (place < (at[1] + 1) * rows)).astype(F32)


def stacked_sums(*values):
    sums = [column_sum(value) for value in values]
    return jnp.concatenate(sums + [jnp.zeros((8 - len(sums), values[0].shape[1]), F32)], axis=0)


def second_norm(at, after, mine, other, bias, gain, shift):
    half, width = mine.shape

    def body(at, ins, outs, _):
        after, mine, other, bias, gain, shift = ins
        total, low = outs
        value = after[...] + (mine[...].astype(F32) + other[...].astype(F32)) + bias[...]
        total[...] = value
        normed, _ = norm_stats(value)
        low[...] = (normed * gain[1:2] + shift[1:2]).astype(BF)

    ins = [near(a) for a in (after, mine, other, bias, gain, shift)]
    return launch(body, "second_norm", at, ins, [shape(half, width), shape(half, width, dtype=BF)], us=1.5)


def feed_up(at, mine, other, f1, f2, b1):
    half, width = mine.shape
    units = f1.shape[1]

    def body(at, ins, outs, _):
        mine, other, f1, f2, b1 = ins
        keep, send, hidden, slope = outs
        for r, (x, target) in enumerate(((other, send), (mine, keep))):
            span = slice((1 - r) * half, (2 - r) * half)
            low, steep = gelu_pair(mm(x[...], f1[...]) + b1[...])
            hidden[span, :] = low
            slope[span, :] = steep
            target[...] = mm(low, f2[...]).astype(target.dtype)

    ins = [near(a) for a in (mine, other, f1, f2, b1)]
    outs = [
        shape(half, width),
        shape(half, width, dtype=BF),
        shape(2 * half, units, dtype=BF),
        shape(2 * half, units),
    ]
    return launch(body, "feed_up", at, ins, outs, us=4)


def third_norm(at, total, mine, other, cot, bias, gain, shift):
    half, width = mine.shape

    def body(at, ins, outs, _):
        total, mine, other, cot, bias, gain, shift = ins
        mixed, dlast_out, low, sums = outs
        normed_mid, _ = norm_stats(total[...])
        last = normed_mid * gain[1:2] + shift[1:2] + (mine[...].astype(F32) + other[...].astype(F32)) + bias[...]
        normed, inverse = norm_stats(last)
        first_row = at[0] * half
        live = (first_row + lax.broadcasted_iota(jnp.int32, (half, 1), 0) < at[3]).astype(F32)
        mixed[...] = ((normed * gain[2:3] + shift[2:3]) * live).astype(BF)
        delta = cot[...].astype(F32) * live
        dlast = norm_backward(delta, normed, inverse, gain[2:3])
        dlast_out[...] = dlast
        low[...] = dlast.astype(BF)
        counted = counted_rows(at, half)
        sums[...] = stacked_sums(delta * normed * counted, delta * counted, dlast * counted)

    ins = [
        near(total),
        near(mine),
        near(other),
        near(cot, lambda ref, at: ref.at[rows_at(at[0], half), :]),
        near(bias),
        near(gain),
        near(shift),
    ]
    outs = [shape(half, width, dtype=BF), shape(half, width), shape(half, width, dtype=BF), shape(8, width)]
    return launch(body, "third_norm", at, ins, outs, us=2.5)


def feed_down(at, mine, other, f1, f2, slope):
    half, width = mine.shape
    units = f1.shape[1]

    def body(at, ins, outs, _):
        mine, other, f1, f2, slope = ins
        keep, send, dpre, sums = outs
        total = jnp.zeros((1, units), F32)
        for r, (x, target) in enumerate(((other, send), (mine, keep))):
            span = slice((1 - r) * half, (2 - r) * half)
            grad = mm(x[...], f2[...], NT) * slope[span, :]
            total = total + column_sum(grad)
            low = grad.astype(BF)
            dpre[span, :] = low
            target[...] = mm(low, f1[...], NT).astype(target.dtype)
        sums[...] = total

    ins = [near(a) for a in (mine, other, f1, f2, slope)]
    outs = [
        shape(half, width),
        shape(half, width, dtype=BF),
        shape(2 * half, units, dtype=BF),
        shape(1, units),
    ]
    return launch(body, "feed_down", at, ins, outs, us=3)


def second_back(at, dlast, mine, other, total, gain):
    half, width = mine.shape

    def body(at, ins, outs, _):
        dlast, mine, other, total, gain = ins
        dsecond, low, sums = outs
        dmid = dlast[...] + (mine[...].astype(F32) + other[...].astype(F32))
        normed, inverse = norm_stats(total[...])
        result = norm_backward(dmid, normed, inverse, gain[1:2])
        dsecond[...] = result
        low[...] = result.astype(BF)
        counted = counted_rows(at, half)
        sums[...] = stacked_sums(dmid * normed * counted, dmid * counted, result * counted)

    ins = [near(a) for a in (dlast, mine, other, total, gain)]
    outs = [shape(half, width), shape(half, width, dtype=BF), shape(8, width)]
    return launch(body, "second_back", at, ins, outs, us=1.8)


def gelu_pair(pre):
    phi = 0.5 * (1.0 + erf(pre * 0.7071067811865476))
    return (pre * phi).astype(BF), phi + pre * (jnp.exp(pre * pre * -0.5) * 0.3989422804014327)


def cross_backward(at, z_mine, z_other, raised, inverse, query, keys, values, w, wo, nh):
    half, width = z_mine.shape
    rows = 2 * half
    local = w.shape[1]
    hd = local // nh
    slots = keys.shape[1]
    scale = hd**-0.5

    def body(at, ins, outs, scratch):
        z_halves, (wo, inverse, values, raised, query, keys, w) = ins[:2], ins[2:]
        keep, send, dquery, dkv, sums = outs
        douts, right, found = scratch
        zero = jnp.zeros((half, hd), BF)
        head_sum = jnp.zeros((1, local), F32)
        for r in range(2):
            span = slice(r * half, (r + 1) * half)
            dhead = mm(z_halves[r][...], wo[...], NT)
            head_sum = head_sum + column_sum(dhead)
            scaled = query[span, :] * jnp.asarray(scale, BF)
            for h in range(nh):
                part = slice(h * hd, (h + 1) * hd)
                dout = (dhead[:, part] * inverse[h, span, 0:1]).astype(BF)
                douts[h, span, :] = jnp.concatenate([dout, dout], axis=1)
                right[h, 0, span, :] = jnp.concatenate([scaled[:, part], zero], axis=1)
                right[h, 1, span, :] = jnp.concatenate([zero, dout], axis=1)

        def one_head(h, _):
            grad = None
            for r in range(2):
                span = slice(r * half, (r + 1) * half)
                dprob = mm(douts[h, span, :], values[h], NT)
                low = raised[h, span, :]
                e = low.astype(F32)
                weighed = e * dprob
                mean = jnp.sum(weighed, axis=1, keepdims=True) * inverse[h, span, 0:1]
                dscore = (weighed - e * mean).astype(BF)
                both = mm(dscore, keys[h])
                found[h, span, :] = both[:, :hd] + both[:, hd:]
                part = mm(dscore, right[h, 0, span, :], TN) + mm(low, right[h, 1, span, :], TN)
                grad = part if grad is None else grad + part
            dkv[h] = grad.astype(BF)
            return 0

        lax.fori_loop(0, nh, one_head, 0)
        query_sum = jnp.zeros((1, local), F32)
        for r, target in enumerate((keep, send)):
            span = slice(r * half, (r + 1) * half)
            dq = jnp.concatenate([found[h, span, :] for h in range(nh)], axis=1) * scale
            query_sum = query_sum + column_sum(dq)
            dq_low = dq.astype(BF)
            dquery[span, :] = dq_low
            target[...] = mm(dq_low, w[0]).astype(target.dtype)
        sums[...] = jnp.concatenate([query_sum, head_sum], axis=0)

    return launch(
        body,
        "cross_bwd",
        at,
        [near(a) for a in (z_mine, z_other, wo, inverse, values, raised, query, keys, w)],
        [
            shape(half, width),
            shape(half, width, dtype=BF),
            shape(rows, local, dtype=BF),
            shape(nh, slots, 2 * hd, dtype=BF),
            shape(2, local),
        ],
        scratch=[
            pltpu.VMEM((nh, rows, 2 * hd), BF),
            pltpu.VMEM((nh, 2, rows, 2 * hd), BF),
            pltpu.VMEM((nh, rows, hd), F32),
        ],
        mib=30,
        us=11,
    )


def store_gradient(at, dkv, w, nh):
    _, slots, twice = dkv.shape
    _, local, width = w.shape
    hd = twice // 2
    seg = slots // 4

    def body(at, ins, outs, _):
        dkv, w = ins
        keep, send = outs
        weights = []
        for h in range(nh):
            part = slice(h * hd, (h + 1) * hd)
            weights += [w[1][part], w[2][part]]
        weight = jnp.concatenate(weights, axis=0)
        for slot in (1, 3, 0, 2):
            rows = jnp.concatenate([dkv[h, slot * seg : (slot + 1) * seg, :] for h in range(nh)], axis=1)
            part = mm(rows, weight)
            if slot % 2 == 0:
                keep[slot // 2] = part
            else:
                send[slot // 2] = part.astype(BF)

    return launch(
        body,
        "store_grad",
        at,
        [near(dkv), near(w)],
        [shape(2, seg, width), shape(2, seg, width, dtype=BF)],
        us=2.6,
    )


def group_outs(width, columns, blocks):
    if not blocks:
        return [shape(width, columns)]
    n, r = blocks
    return [shape(n * r, columns, dtype=BF), shape(n, r, columns)]


def emit_group(at, grad, outs, blocks, first, columns, kept_first=None):
    if not blocks:
        outs[0][:, first : first + columns] = grad[...]
        return
    n, r = blocks
    kept_first = first if kept_first is None else kept_first
    span, kept = slice(first, first + columns), slice(kept_first, kept_first + columns)
    for b in range(n):
        theirs = pl.ds(pl.multiple_of((2 * b + 1 - at[4]) * r, 8), r)
        outs[0][b * r : (b + 1) * r, span] = grad[theirs, :].astype(BF)
        outs[1][b, :, kept] = grad[pl.ds(pl.multiple_of((2 * b + at[4]) * r, 8), r), :]


def turned_product(out, left, right, step=256):
    if left.shape[1] % step:
        out[...] = mm(left[...], right[...], TN)
        return

    def some(i, _):
        span = pl.ds(pl.multiple_of(i * step, step), step)
        out[span, :] = mm(left[:, span], right[...], TN)
        return 0

    lax.fori_loop(0, left.shape[1] // step, some, 0)


def feed_grads(at, mid_mine, mid_other, dpre, dlast_mine, dlast_other, hidden, blocks):
    half, width = mid_mine.shape
    units = dpre.shape[1]
    if blocks:
        n, r = blocks
        structs = [shape(n * r, 2 * units, dtype=BF), shape(n, r, 2 * units)]
    else:
        structs = [shape(width, units), shape(width, units)]

    def body(at, ins, outs, scratch):
        mid_mine, mid_other, dpre, dlast_mine, dlast_other, hidden = ins
        left, grad = scratch
        for i, (mine, other, right) in enumerate(((mid_mine, mid_other, dpre), (dlast_mine, dlast_other, hidden))):
            left[:half, :] = mine[...]
            left[half:, :] = other[...]
            turned_product(grad, left, right)
            emit_group(at, grad, outs if blocks else outs[i:], blocks, i * units if blocks else 0, units)

    return launch(
        body,
        "feed_grads",
        at,
        [near(a) for a in (mid_mine, mid_other, dpre, dlast_mine, dlast_other, hidden)],
        structs,
        scratch=[pltpu.VMEM((2 * half, width), BF), pltpu.VMEM((width, units), F32)],
        us=4,
    )


def cross_grads(at, z_mine, z_other, mine, other, dquery, heads, shards, dkv, nh, blocks):
    half, width = mine.shape
    local = dquery.shape[1]
    hd = local // nh
    seg = shards[0].shape[0]

    def body(at, ins, outs, scratch):
        shards, (z_mine, z_other, mine, other, dquery, heads, dkv) = ins[0:4], ins[4:]
        (grad,) = scratch
        grad[...] = mm(mine[...], dquery[:half], TN) + mm(other[...], dquery[half:], TN)
        emit_group(at, grad, outs, blocks, 0, local)
        grad[...] = mm(z_mine[...], heads[:half], TN) + mm(z_other[...], heads[half:], TN)
        emit_group(at, grad, outs, blocks, 3 * local, local)
        both = None
        for slot, block in enumerate(shards):
            rows = jnp.concatenate([dkv[h, slot * seg : (slot + 1) * seg, :] for h in range(nh)], axis=1)
            part = mm(block[...], rows, TN)
            both = part if both is None else both + part
        for i in range(2):
            grad[...] = jnp.concatenate([both[:, (2 * h + i) * hd : (2 * h + i + 1) * hd] for h in range(nh)], axis=1)
            emit_group(at, grad, outs, blocks, (1 + i) * local, local)

    return launch(
        body,
        "cross_grads",
        at,
        [near(a) for a in (*shards, z_mine, z_other, mine, other, dquery, heads, dkv)],
        group_outs(width, 4 * local, blocks),
        scratch=[pltpu.VMEM((width, local), F32)],
        us=4,
    )


def first_back(at, dsecond, mine, other, total, gain):
    half, width = mine.shape

    def body(at, ins, outs, _):
        dsecond, mine, other, total, gain = ins
        dfirst, low, sums = outs
        value = dsecond[...] + (mine[...].astype(F32) + other[...].astype(F32))
        normed, inverse = norm_stats(total[...])
        result = norm_backward(value, normed, inverse, gain[0:1])
        dfirst[...] = result
        low[...] = result.astype(BF)
        counted = counted_rows(at, half)
        sums[...] = stacked_sums(value * normed * counted, value * counted, result * counted)

    ins = [near(a) for a in (dsecond, mine, other, total, gain)]
    outs = [shape(half, width), shape(half, width, dtype=BF), shape(8, width)]
    return launch(body, "first_back", at, ins, outs, us=1.8)


def self_backward(at, mine, other, tokens, w, wo, qkv, prob, flat, mixed, sums, nh, blocks):
    half, width = mine.shape
    rows = 2 * half
    local = wo.shape[0]
    hd = local // nh
    scale = hd**-0.5

    def body(at, ins, outs, scratch):
        mine, other, wo, qkv, prob, tok, w, mixed, flat = ins[:9]
        third_sums, second_sums, first_sums, fc1_sum, head_sums = ins[9:]
        send, keep = outs[0:2]
        group, extra = outs[2:-1], outs[-1]
        z, dqkv, grad = scratch
        own, distant = rows_at(at[0], half), rows_at(1 - at[0], half)
        z[own, :] = mine[...]
        z[distant, :] = other[...]
        dself = mm(z[...], wo[...], NT).astype(BF)
        v, k, q = qkv[2], qkv[1], qkv[0]
        dq, dk, dv = [], [], []
        for h in range(nh):
            part = slice(h * hd, (h + 1) * hd)
            weights_low = prob[h]
            weights = weights_low.astype(F32)
            weighed = weights * mm(dself[:, part], v[:, part], NT)
            dscore = (weighed - weights * jnp.sum(weighed, axis=1, keepdims=True)).astype(BF)
            dq.append(mm(dscore, k[:, part]))
            dk.append(mm(dscore, q[:, part], TN))
            dv.append(mm(weights_low, dself[:, part], TN))
        dquery = jnp.concatenate(dq, axis=1) * scale
        dvalue = jnp.concatenate(dv, axis=1)
        dqkv[0] = dquery.astype(BF)
        dqkv[1] = (jnp.concatenate(dk, axis=1) * scale).astype(BF)
        dqkv[2] = dvalue.astype(BF)
        x = tok[...]
        for i in range(3):
            grad[...] = mm(x, dqkv[i], TN)
            emit_group(at, grad, group, blocks, i * local, local)
        grad[...] = mm(z[...], flat[...], TN)
        emit_group(at, grad, group, blocks, 3 * local, local)
        pad = jnp.zeros((1, width - 2 * local), F32)
        extra[...] = jnp.concatenate(
            [
                third_sums[0:3],
                second_sums[0:3],
                first_sums[0:3],
                fc1_sum[...],
                jnp.concatenate([head_sums[0:1], head_sums[1:2], pad], axis=1),
                jnp.concatenate([column_sum(dquery), column_sum(dvalue), pad], axis=1),
                jnp.zeros((EXTRA - 12, width), F32),
            ],
            axis=0,
        )
        send[half:, :] = mixed[...]
        for place, out in ((distant, send), (own, keep)):
            total = mm(dqkv[0, place, :], w[0]) + mm(dqkv[1, place, :], w[1]) + mm(dqkv[2, place, :], w[2])
            out[0:half, :] = total.astype(out.dtype)

    return launch(
        body,
        "self_bwd",
        at,
        [near(a) for a in (mine, other, wo, qkv, prob, tokens, w, mixed, flat, *sums)],
        [shape(2 * half, width, dtype=BF), shape(half, width)]
        + group_outs(width, 4 * local, blocks)
        + [shape(EXTRA, width)],
        scratch=[
            pltpu.VMEM((rows, width), BF),
            pltpu.VMEM((3, rows, local), BF),
            pltpu.VMEM((width, local), F32),
        ],
        mib=20,
        us=6,
    )


def add_stage(at, keep, got, small, bit, apart=False):
    n, rows, _ = keep[0].shape
    starts = [0]
    for part in keep:
        starts.append(starts[-1] + part.shape[2])
    columns = starts[-1]
    tail = 0 if small is None else 2 * small.shape[0]
    reach = small.shape[1] if tail else 0

    def body(at, ins, outs, _):
        keeps, gots = ins[: len(keep)], ins[len(keep) : len(keep) + len(got)]
        mine = at[bit]
        send, stay = outs[:2]
        for b in range(n // 2):
            for chosen, out in ((1 - mine, send), (mine, stay)):
                block = 2 * b + chosen
                for i, part in enumerate(keeps):
                    span = slice(starts[i], starts[i + 1])
                    source, first = (gots[i], 0) if len(got) == len(keep) else (gots[0], starts[i])
                    arrived = source[
                        pl.ds(pl.multiple_of(block * rows, 8), rows), first : first + starts[i + 1] - starts[i]
                    ]
                    value = part[block] + arrived.astype(F32)
                    if out is send:
                        send[b * rows : (b + 1) * rows, span] = value.astype(BF)
                    else:
                        stay[b, :, span] = value
        if tail:
            total = ins[-1][...]
            if not apart:
                total = total + from_terms(gots[0][n * rows :, 0:reach])
            outs[2][...] = total
            send[n // 2 * rows :, 0:reach] = two_terms(total)
            if reach < columns:
                send[n // 2 * rows :, reach:] = jnp.zeros((tail, columns - reach), BF)

    ins = [near(part) for part in (*keep, *got)] + ([near(small)] if tail else [])
    outs = [shape(n // 2 * rows + tail, columns, dtype=BF), shape(n // 2, rows, columns)]
    if tail:
        outs.append(shape(small.shape[0], reach))
    return launch(body, "add_stage", at, ins, outs, us=1)


def last_stage(at, keep, got, small, parts):
    _, rows, columns = keep.shape
    each = columns // sum(count for count, _ in parts)
    reach = 0 if small is None else small.shape[1]

    def body(at, ins, outs, _):
        total = ins[0][0] + ins[1][0:rows].astype(F32)
        first = 0
        for out, (count, turned) in zip(outs, parts):
            if count == 1:
                value = total[:, first * each : (first + 1) * each]
                out[...] = value.T if turned else value
            else:
                for i in range(count):
                    out[i] = total[:, (first + i) * each : (first + i + 1) * each]
            first += count
        if reach:
            outs[-1][...] = ins[2][...] + from_terms(ins[1][rows:, 0:reach])

    outs = []
    for count, turned in parts:
        dims = (rows, each) if count == 1 else (count, rows, each)
        outs.append(shape(*(dims[::-1] if turned else dims)))
    ins = [near(keep), near(got)]
    if reach:
        ins.append(near(small))
        outs.append(shape(small.shape[0], reach))
    return launch(body, "last_stage", at, ins, outs, us=1)


def join_halves(at, mine, other):
    half, width = mine.shape
    skip = other.shape[0] - half

    def body(at, ins, outs, _):
        outs[0][rows_at(at[0], half), :] = ins[0][...]
        outs[0][rows_at(1 - at[0], half), :] = ins[1][...]

    out = shape(2 * half, width, dtype=mine.dtype)
    ins = [near(mine), near(other, lambda ref, at: ref.at[pl.ds(skip, half), :])]
    return launch(body, "join_halves", at, ins, [out])[0]


def flip(bit, size):
    return [(i, i ^ bit) for i in range(size)]


def butterfly(value, axis, size):
    bit = 1
    while bit < size:
        value = value + lax.ppermute(value, axis, flip(bit, size))
        bit *= 2
    return value


def on_device(
    tokens,
    store,
    summary_length,
    top_index,
    cotangent,
    self_qkv_weight,
    self_qv_bias,
    self_out_weight,
    self_out_bias,
    qkv_weight,
    qv_bias,
    out_weight,
    out_bias,
    fc1_weight,
    fc1_bias,
    fc2_weight,
    fc2_bias,
    norm_gain,
    norm_shift,
):
    rows, width = tokens.shape
    half = rows // 2
    nh = top_index.shape[1]
    local = qkv_weight.shape[2]
    units = fc1_weight.shape[1]
    seg = store.shape[1]
    wide = lax.axis_size("wide")
    place = lax.axis_index("narrow")
    doc = lax.axis_index("wide")
    core, across = place % 2, place // 2
    at = jnp.stack([core, across, place, summary_length[0], doc % 2, doc // 2 % 2, doc // 4]).astype(jnp.int32)
    blocks = (wide // 2, width // wide) if wide == 8 else None
    row = lambda v: v.reshape(1, -1)
    self_w = jnp.swapaxes(self_qkv_weight, 1, 2)
    cross_w = jnp.swapaxes(qkv_weight, 1, 2)

    def to_core(v):
        return lax.ppermute(v, "narrow", CORE)

    def to_across(v):
        return lax.ppermute(v, "narrow", ACROSS)

    def over(v, bit):
        return lax.ppermute(v, "wide", flip(bit, wide))

    def chip_sum(keep, send):
        return (keep + to_core(send).astype(F32)).astype(BF)

    store_x = to_across(store[0])
    qkv, prob, flat, send, keep = self_forward(at, tokens, self_w, self_qv_bias, self_out_weight, nh)
    mine = chip_sum(keep, send)
    other = to_across(mine)
    index = index_rows(top_index)
    bias_mine = make_mask(tie(at, mine), index, top_index.shape, seg, 128, 0)
    store_x, store_own = tie((store_x, store[0]), bias_mine)
    shards = [store_own, to_core(store_own), store_x, to_core(store_x)]
    bias_other = make_mask(tie(at, bias_mine), index, top_index.shape, seg, 128, 1)
    other = tie(other, bias_other)
    first_total, after, after_low = first_norm(at, mine, other, tokens, row(self_out_bias), norm_gain, norm_shift)
    after_other = to_core(after_low)

    keys, values = keys_values(tie(at, after_low), shards, cross_w, nh)
    keep, send, raised, inverse, query, heads = cross_forward(
        tie(at, keys), after_low, after_other, bias_mine, bias_other, keys, values, cross_w, qv_bias, out_weight, nh
    )
    mine = chip_sum(keep, send)
    second_total, mid_low = second_norm(at, after, mine, to_across(mine), row(out_bias), norm_gain, norm_shift)
    mid_other = to_core(mid_low)

    keep, send, hidden, slope = feed_up(at, mid_low, mid_other, fc1_weight, fc2_weight, row(fc1_bias))
    mine = chip_sum(keep, send)
    mixed_half, dlast, dlast_low, third_sums = third_norm(
        at, second_total, mine, to_across(mine), cotangent, row(fc2_bias), norm_gain, norm_shift
    )
    dlast_other = to_core(dlast_low)
    keep, send, dpre, fc1_sum = feed_down(at, dlast_low, dlast_other, fc1_weight, fc2_weight, slope)
    mine = chip_sum(keep, send)
    other = to_across(mine)
    feed_out = feed_grads(tie(at, mine), mid_low, mid_other, dpre, dlast_low, dlast_other, hidden, blocks)
    other = tie(other, feed_out[0])
    dsecond, z, second_sums = second_back(at, dlast, mine, other, second_total, norm_gain)
    z_other = to_core(z)

    keep, send, dquery, dkv, cross_sums = cross_backward(
        at, z, z_other, raised, inverse, query, keys, values, cross_w, out_weight, nh
    )
    mine = chip_sum(keep, send)
    other = to_across(mine)
    cross_out = cross_grads(
        tie(at, mine), z, z_other, after_low, after_other, dquery, heads, shards, dkv, nh, blocks
    )
    started = cross_out[0]
    if blocks:
        feed_send, feed_keep = add_stage(tie(at, started), [feed_out[1]], [over(feed_out[0], 1)], None, 5)
        feed_next = over(feed_send, 2)
        started = feed_send
    store_keep, store_send = store_gradient(tie(at, started), dkv, cross_w, nh)
    other = tie(other, store_send)
    dfirst, dfirst_low, first_sums = first_back(at, dsecond, mine, other, first_total, norm_gain)
    dfirst_other = to_core(dfirst_low)
    store_close = to_core(tie(store_send, dfirst_other))
    started = dfirst_low

    send, keep, *self_out, small = self_backward(
        tie(at, dfirst_other, store_close),
        dfirst_low,
        dfirst_other,
        tokens,
        self_w,
        self_out_weight,
        qkv,
        prob,
        flat,
        mixed_half,
        (third_sums, second_sums, first_sums, fc1_sum, cross_sums),
        nh,
        blocks,
    )
    if blocks:
        cross_got = tie(over(cross_out[0], 1), small)
        feed_send, feed_keep = add_stage(tie(at, cross_got), [feed_keep], [feed_next], None, 6)
        feed_next = over(feed_send, 4)
        send = tie(send, feed_send)
    close = to_core(send)
    mine = (keep + close[:half].astype(F32)).astype(BF)
    other = to_across(mine)
    started = mine
    if blocks:
        fc1_grad, fc2_grad = last_stage(tie(at, mine), feed_keep, feed_next, None, [(1, False), (1, False)])
        fc2_grad = fc2_grad.T
        both_send, both_keep = add_stage(
            tie(at, fc1_grad), [cross_out[1], self_out[1]], [cross_got, over(self_out[0], 1)], None, 5
        )
        both_next = over(both_send, 2)
        started = both_send
    other, small = tie((other, small), started)
    tokens_half = dfirst + (mine.astype(F32) + other.astype(F32))
    tokens_other = to_core(tokens_half)
    small = jnp.concatenate([butterfly(small[:9], "narrow", 4), small[9:]], axis=0)
    store_distant = to_across(tie((store_keep[1] + store_close[1].astype(F32)).astype(BF), small))
    small = butterfly(small, "wide", wide)
    mixed = join_halves(tie(at, tokens_half), mixed_half, close)
    tokens_grad = join_halves(at, tokens_half, tie(tokens_other, mixed))
    if blocks:
        both_send, both_keep = add_stage(tie(at, tokens_grad), [both_keep], [both_next], None, 6)
        both_next = over(both_send, 4)
        store_distant, small = tie((store_distant, small), both_send)
    store_grad = (store_keep[0] + store_close[0].astype(F32) + store_distant.astype(F32))[None]
    (
        (gain_last, shift_last, fc2_b, gain_mid, shift_mid, out_b, gain_first, shift_first, self_out_b),
        fc1_b,
        cross_line,
        self_line,
    ) = (tuple(small[i] for i in range(9)), small[9], small[10], small[11])
    gain_grad = jnp.stack([gain_first, gain_mid, gain_last])
    shift_grad = jnp.stack([shift_first, shift_mid, shift_last])
    qv_grad, self_qv_grad = cross_line[: 2 * local].reshape(2, local), self_line[: 2 * local].reshape(2, local)

    if blocks:
        qkv_grad, out_grad, self_qkv_grad, self_out_grad = last_stage(
            tie(at, store_grad, gain_grad, shift_grad, qv_grad, self_qv_grad, fc1_b, fc2_b, out_b, self_out_b),
            both_keep,
            both_next,
            None,
            [(3, False), (1, True), (3, False), (1, True)],
        )
    else:
        scatter = functools.partial(lax.psum_scatter, axis_name="wide", tiled=True)
        parts = lambda g: jnp.stack([g[:, i * local : (i + 1) * local] for i in range(3)])
        fc1_grad = scatter(feed_out[0], scatter_dimension=0)
        fc2_grad = scatter(feed_out[1].T, scatter_dimension=1)
        qkv_grad = scatter(parts(cross_out[0]), scatter_dimension=1)
        out_grad = scatter(cross_out[0][:, 3 * local :].T, scatter_dimension=1)
        self_qkv_grad = scatter(parts(self_out[0]), scatter_dimension=1)
        self_out_grad = scatter(self_out[0][:, 3 * local :].T, scatter_dimension=1)
    return (
        mixed,
        tokens_grad,
        store_grad,
        self_qkv_grad,
        self_qv_grad,
        self_out_grad,
        self_out_b,
        qkv_grad,
        qv_grad,
        out_grad,
        out_b,
        fc1_grad,
        fc1_b,
        fc2_grad,
        fc2_b,
        gain_grad,
        shift_grad,
    )


def solution(mesh):
    placed = (
        P("wide", None),
        P("wide", "narrow", None),
        P("wide"),
        P("wide", "narrow", None, None),
        P("wide", None),
        P(None, None, "narrow"),
        P(None, "narrow"),
        P("narrow", None),
        P(),
        P(None, None, "narrow"),
        P(None, "narrow"),
        P("narrow", None),
        P(),
        P(None, "narrow"),
        P("narrow"),
        P("narrow", None),
        P(),
        P(),
        P(),
    )
    return jax.shard_map(
        on_device,
        mesh=mesh,
        in_specs=placed,
        out_specs=(
            P("wide", None),
            P("wide", None),
            P("wide", "narrow", None),
            P(None, "wide", "narrow"),
            P(None, "narrow"),
            P("narrow", "wide"),
            P(),
            P(None, "wide", "narrow"),
            P(None, "narrow"),
            P("narrow", "wide"),
            P(),
            P("wide", "narrow"),
            P("narrow"),
            P("narrow", "wide"),
            P(),
            P(),
            P(),
        ),
        check_vma=False,
    )
```

```python
import functools

import jax
import jax.numpy as jnp
from jax import lax
from jax.experimental import pallas as pl
from jax.experimental.pallas import tpu as pltpu
from jax.sharding import PartitionSpec as P

F32 = jnp.float32
BF = jnp.bfloat16
NN = (((1,), (0,)), ((), ()))
NT = (((1,), (1,)), ((), ()))
TN = (((0,), (0,)), ((), ()))
EPS = 1e-05
PACE = 1.1e8
SELF_MIB = 60
EXTRA = 16

CORE = [(i, i ^ 1) for i in range(4)]
ACROSS = [(i, i ^ 2) for i in range(4)]


def mm(left, right, dims=NN):
    return lax.dot_general(left, right, dims, preferred_element_type=F32)


def shape(*dims, dtype=F32):
    return jax.ShapeDtypeStruct(dims, dtype)


def tie(value, *earlier):
    return lax.optimization_barrier((value, *earlier))[0]


class Operand:
    def __init__(self, source, buffer, sems, first, parts):
        self.buffer = buffer
        self.parts = parts
        if parts:
            self.copies = [
                pltpu.make_async_copy(source.at[i], buffer.at[i], sems.at[first + i]) for i in range(buffer.shape[0])
            ]
        else:
            self.copies = [pltpu.make_async_copy(source, buffer, sems.at[first])]
        self.waited = [False] * len(self.copies)
        for copy in self.copies:
            copy.start()

    def ready(self, part=None):
        for i, copy in enumerate(self.copies):
            if not self.waited[i] and (part is None or i == part):
                copy.wait()
                self.waited[i] = True

    @property
    def shape(self):
        return self.buffer.shape

    def __getitem__(self, at):
        self.ready(at if self.parts and isinstance(at, int) else None)
        return self.buffer[at]


class Result:
    def __init__(self, target, buffer, sems, first, parts):
        self.buffer = buffer
        if parts:
            self.copies = [
                pltpu.make_async_copy(buffer.at[i], target.at[i], sems.at[first + i]) for i in range(buffer.shape[0])
            ]
        else:
            self.copies = [pltpu.make_async_copy(buffer, target, sems.at[first])]
        self.started = [False] * len(self.copies)

    @property
    def shape(self):
        return self.buffer.shape

    @property
    def dtype(self):
        return self.buffer.dtype

    def __setitem__(self, at, value):
        self.buffer[at] = value

    def flush(self, part=0):
        self.copies[part].start()
        self.started[part] = True

    def finish(self):
        for i in range(len(self.copies)):
            if not self.started[i]:
                self.flush(i)
        for copy in self.copies:
            copy.wait()


def far(array, take=None, dims=None, parts=False):
    return ("far", array, take, tuple(dims or array.shape), parts)


def near(array, take=None):
    return ("near", array, take, None, False)


def raw(array):
    return ("raw", array, None, None, False)


def launch(body, name, at, ins, outs, scratch=(), mib=16, us=2.0):
    in_specs = [pl.BlockSpec(memory_space=pltpu.SMEM)]
    buffers, n_in, n_out = [], 0, 0
    for kind, array, _, dims, parts in ins:
        in_specs.append(pl.BlockSpec(memory_space=pltpu.VMEM if kind == "near" else pltpu.HBM))
        if kind == "far":
            buffers.append(pltpu.VMEM(dims, array.dtype))
            n_in += dims[0] if parts else 1
    out_specs, structs = [], []
    for out in outs:
        if isinstance(out, tuple):
            struct, parts = out
            out_specs.append(pl.BlockSpec(memory_space=pltpu.HBM))
            buffers.append(pltpu.VMEM(struct.shape, struct.dtype))
            n_out += struct.shape[0] if parts else 1
        else:
            struct = out
            out_specs.append(pl.BlockSpec(memory_space=pltpu.VMEM))
        structs.append(struct)
    n_buffers = len(buffers)
    sems = [pltpu.SemaphoreType.DMA((max(n, 1),)) for n in (n_in, n_out)]

    def kernel(at_ref, *refs):
        in_refs, out_refs = refs[: len(ins)], refs[len(ins) : len(ins) + len(outs)]
        rest = refs[len(ins) + len(outs) :]
        bufs, user, (in_sems, out_sems) = list(rest[:n_buffers]), rest[n_buffers:-2], rest[-2:]
        place, given = 0, []
        for ref, (kind, _, take, dims, parts) in zip(in_refs, ins):
            source = take(ref, at_ref) if take else ref
            if kind == "far":
                given.append(Operand(source, bufs.pop(0), in_sems, place, parts))
                place += dims[0] if parts else 1
            else:
                given.append(source)
        place, results = 0, []
        for ref, out in zip(out_refs, outs):
            if isinstance(out, tuple):
                results.append(Result(ref, bufs.pop(0), out_sems, place, out[1]))
                place += out[0].shape[0] if out[1] else 1
            else:
                results.append(ref)
        body(at_ref, given, results, user)
        for operand in given:
            if isinstance(operand, Operand):
                operand.ready()
        for result in results:
            if isinstance(result, Result):
                result.finish()

    return pl.pallas_call(
        kernel,
        in_specs=in_specs,
        out_specs=out_specs,
        out_shape=structs,
        scratch_shapes=buffers + list(scratch) + sems,
        compiler_params=pltpu.CompilerParams(vmem_limit_bytes=mib << 20),
        cost_estimate=pl.CostEstimate(flops=int(us * PACE), bytes_accessed=1000, transcendentals=0),
        name=name,
    )(at, *[entry[1] for entry in ins])


def norm_stats(value):
    centre = value - jnp.mean(value, axis=-1, keepdims=True)
    spread = jnp.mean(centre * centre, axis=-1, keepdims=True)
    inverse = lax.rsqrt(spread + EPS)
    return centre * inverse, inverse


def norm_backward(grad, normed, inverse, gain):
    scaled = grad * gain
    centred = scaled - jnp.mean(scaled, axis=-1, keepdims=True)
    return inverse * (centred - normed * jnp.mean(scaled * normed, axis=-1, keepdims=True))


def column_sum(value):
    return jnp.sum(value, axis=0, keepdims=True)


def erf(value):
    x = jnp.clip(value, -4.0, 4.0)
    y = x * x
    top = jnp.full_like(y, -2.72614225801306e-10)
    for factor in (
        2.77068142495902e-08,
        -2.10102402082508e-06,
        -5.69250639462346e-05,
        -7.34990630326855e-04,
        -2.95459980854025e-03,
        -1.60960333262415e-02,
    ):
        top = top * y + factor
    low = jnp.full_like(y, -1.45660718464996e-05)
    for factor in (
        -2.13374055278905e-04,
        -1.68282697438203e-03,
        -7.37332916720468e-03,
        -1.42647390514189e-02,
    ):
        low = low * y + factor
    return x * top / low


def two_terms(value):
    high = value.astype(BF)
    return jnp.concatenate([high, (value - high.astype(F32)).astype(BF)], axis=0)


def from_terms(stacked):
    rows = stacked.shape[0] // 2
    terms = stacked.astype(F32)
    return terms[:rows] + terms[rows:]


def rows_at(place, rows):
    return pl.ds(pl.multiple_of(place * rows, rows), rows)


def self_forward(at, tokens, w, b, wo, nh):
    rows, width = tokens.shape
    local = w.shape[1]
    half = rows // 2
    hd = local // nh
    scale = hd**-0.5

    def body(at, ins, outs, _):
        tok, w, wo, b = ins
        qkv, prob, flat, send, keep = outs
        x = tok[...]
        q = (mm(x, w[0], NT) + b[0:1]).astype(BF)
        k = mm(x, w[1], NT).astype(BF)
        v = (mm(x, w[2], NT) + b[1:2]).astype(BF)
        for i, value in enumerate((q, k, v)):
            qkv[i] = value
            qkv.flush(i)
        row_ids = lax.broadcasted_iota(jnp.int32, (rows, rows), 0)
        key_ids = lax.broadcasted_iota(jnp.int32, (rows, rows), 1)
        allowed = (key_ids <= row_ids) & (key_ids < at[3])
        found = []
        for h in range(nh):
            part = slice(h * hd, (h + 1) * hd)
            scores = mm(q[:, part], k[:, part], NT) * scale
            scores = jnp.where(allowed, scores, -1e30)
            shifted = jnp.exp(scores - jnp.max(scores, axis=1, keepdims=True))
            weights = (shifted * (1.0 / jnp.sum(shifted, axis=1, keepdims=True))).astype(BF)
            prob[h] = weights
            prob.flush(h)
            found.append(mm(weights, v[:, part]).astype(BF))
        flat[...] = jnp.concatenate(found, axis=1)
        flat.flush()
        send[...] = mm(flat.buffer[rows_at(1 - at[0], half), :], wo[...]).astype(BF)
        send.flush()
        keep[...] = mm(flat.buffer[rows_at(at[0], half), :], wo[...])

    return launch(
        body,
        "self_fwd",
        at,
        [far(tokens), far(w, parts=True), far(wo), far(b)],
        [
            (shape(3, rows, local, dtype=BF), True),
            (shape(nh, rows, rows, dtype=BF), True),
            (shape(rows, local, dtype=BF), False),
            (shape(half, width, dtype=BF), False),
            (shape(half, width), False),
        ],
        mib=SELF_MIB,
        us=4,
    )


def first_norm(at, mine, other, tokens, bias, gain, shift):
    half, width = mine.shape

    def body(at, ins, outs, _):
        mine, other, tok, bias, gain, shift = ins
        total, after, low = outs
        value = tok[...].astype(F32) + (mine[...].astype(F32) + other[...].astype(F32)) + bias[...]
        total[...] = value
        normed, _ = norm_stats(value)
        result = normed * gain[0:1] + shift[0:1]
        after[...] = result
        low[...] = result.astype(BF)

    return launch(
        body,
        "first_norm",
        at,
        [
            near(mine),
            near(other),
            near(tokens, lambda ref, at: ref.at[rows_at(at[0], half), :]),
            near(bias),
            near(gain),
            near(shift),
        ],
        [shape(half, width), shape(half, width), shape(half, width, dtype=BF)],
        us=1.7,
    )


def index_rows(top_index):
    rows, nh, ns, keep = top_index.shape
    flat = top_index.reshape(rows, nh, ns, keep // 128, 128).transpose(0, 1, 3, 2, 4)
    return flat.reshape(rows * nh * ns * (keep // 128), 128)


def make_mask(at, flat, dims, seg, tile, turn):
    rows, nh, ns, keep = dims
    halves = keep // 128
    per_row = nh * ns * halves
    tiles = rows // 2 // tile
    columns = ns * seg
    blocks = columns // 128
    group = 32

    def body(at, ins, outs, _):
        (index,) = ins
        (bias,) = outs
        lane = lax.broadcasted_iota(jnp.int32, (group, 128), 1).astype(F32)
        lane_low = lane.astype(BF)
        empty = jnp.full((group, 128), -1.0, BF)
        own = at[2]
        steps = []
        step = 1
        while step <= seg - keep:
            steps.insert(0, step)
            step *= 2
        turns = steps + [(seg * s) % 128 for s in range(ns)]
        below = {s: lane_low < jnp.asarray(s, BF) for s in turns if 0 < s < 128}

        for t in range(tiles):
            index.ready(t)
            source = index.buffer.at[t]

            def one_group(g, _):
                for h in range(nh):
                    v = [empty] * blocks
                    for slot in range(ns):
                        first, turn = divmod(seg * slot, 128)
                        for c in range(halves):
                            start = g * (group * per_row) + h * ns * halves + c * ns + (own ^ slot)
                            found = jnp.concatenate(
                                [source[pl.ds(start + q * 8 * per_row, 8, stride=per_row), :] for q in range(group // 8)],
                                axis=0,
                            )
                            ahead = (found.astype(F32) - (lane + float(128 * c))).astype(BF)
                            at_block = first + c
                            if turn == 0:
                                v[at_block] = ahead
                            else:
                                turned = pltpu.roll(ahead, turn, axis=1)
                                v[at_block] = jnp.where(below[turn], v[at_block], turned)
                                v[at_block + 1] = jnp.where(below[turn], turned, v[at_block + 1])
                    for s in steps:
                        gap = jnp.asarray(s, BF)
                        moved = [x - gap for x in v]
                        stay = [jnp.where(x >= gap, empty, x) for x in v]
                        if s % 128 == 0:
                            hop = s // 128
                            v = stay[:hop] + [jnp.maximum(stay[i], moved[i - hop]) for i in range(hop, blocks)]
                        else:
                            turned = [pltpu.roll(x, s, axis=1) for x in moved]
                            v = [
                                jnp.maximum(stay[i], jnp.where(below[s], turned[i - 1], turned[i])) for i in range(blocks)
                            ]
                    for i in range(blocks):
                        bias[h, pl.ds(pl.multiple_of(t * tile + g * group, group), group), i * 128 : (i + 1) * 128] = v[
                            i
                        ] * jnp.asarray(1e30, BF)
                return 0

            lax.fori_loop(0, tile // group, one_group, 0)

    flat = flat.reshape(2 * tiles, tile * per_row, 128)
    return launch(
        body,
        "mask",
        at,
        [
            far(
                flat,
                lambda ref, at: ref.at[pl.ds((at[0] ^ turn) * tiles, tiles)],
                (tiles, tile * per_row, 128),
                parts=True,
            )
        ],
        [shape(nh, rows // 2, columns, dtype=BF)],
        us=10,
    )[0]


def keys_values(at, shards, w, nh):
    seg, width = shards[0].shape
    local = w.shape[1]
    hd = local // nh

    def body(at, ins, outs, _):
        for slot in range(4):
            x = ins[slot][...]
            span = slice(slot * seg, (slot + 1) * seg)
            for i, out in enumerate(outs):
                full = mm(x, ins[4][i + 1], NT)
                high = full.astype(BF)
                low = (full - high.astype(F32)).astype(BF)
                for h in range(nh):
                    part = slice(h * hd, (h + 1) * hd)
                    out[h, span, :] = jnp.concatenate([high[:, part], low[:, part]], axis=1)

    out = shape(nh, 4 * seg, 2 * hd, dtype=BF)
    return launch(body, "keys_values", at, [near(s) for s in shards] + [near(w)], [out, out], us=2)


def cross_forward(at, mine, other, bias_mine, bias_other, keys, values, w, b, wo, nh):
    half, width = mine.shape
    rows = 2 * half
    local = w.shape[1]
    hd = local // nh
    slots = keys.shape[1]
    scale = hd**-0.5

    def body(at, ins, outs, scratch):
        mine, other, wq, keys, bias_mine, bias_other, values, wo, b = ins
        keep, send, raised, inverse, query, heads = outs
        twice, found = scratch
        for r, x in enumerate((mine, other)):
            q = (mm(x[...], wq[0], NT) + b[0:1]).astype(BF)
            query[r * half : (r + 1) * half, :] = q
            scaled = q * jnp.asarray(scale, BF)
            for h in range(nh):
                part = scaled[:, h * hd : (h + 1) * hd]
                twice[h, r * half : (r + 1) * half, :] = jnp.concatenate([part, part], axis=1)

        def one_head(h, _):
            for r, bias in enumerate((bias_mine, bias_other)):
                span = slice(r * half, (r + 1) * half)
                scores = mm(twice[h, span, :], keys[h], NT) + bias[h].astype(F32)
                e = jnp.exp(scores - jnp.max(scores, axis=1, keepdims=True))
                total = 1.0 / jnp.sum(e, axis=1, keepdims=True)
                low = e.astype(BF)
                raised[h, span, :] = low
                inverse[h, span, :] = jnp.broadcast_to(total, (half, 128))
                both = mm(low, values[h])
                found[h, span, :] = (both[:, :hd] + both[:, hd:]) * total
            return 0

        lax.fori_loop(0, nh, one_head, 0)
        for r, target in enumerate((keep, send)):
            span = slice(r * half, (r + 1) * half)
            out = (jnp.concatenate([found[h, span, :] for h in range(nh)], axis=1) + b[1:2]).astype(BF)
            heads[span, :] = out
            target[...] = mm(out, wo[...]).astype(target.dtype)

    return launch(
        body,
        "cross_fwd",
        at,
        [near(a) for a in (mine, other, w, keys, bias_mine, bias_other, values, wo, b)],
        [
            shape(half, width),
            shape(half, width, dtype=BF),
            shape(nh, rows, slots, dtype=BF),
            shape(nh, rows, 128),
            shape(rows, local, dtype=BF),
            shape(rows, local, dtype=BF),
        ],
        scratch=[pltpu.VMEM((nh, rows, 2 * hd), BF), pltpu.VMEM((nh, rows, hd), F32)],
        mib=30,
        us=9,
    )


def stacked_sums(*values):
    sums = [column_sum(value) for value in values]
    return jnp.concatenate(sums + [jnp.zeros((8 - len(sums), values[0].shape[1]), F32)], axis=0)


def second_norm(at, after, mine, other, bias, gain, shift):
    half, width = mine.shape

    def body(at, ins, outs, _):
        after, mine, other, bias, gain, shift = ins
        total, low = outs
        value = after[...] + (mine[...].astype(F32) + other[...].astype(F32)) + bias[...]
        total[...] = value
        normed, _ = norm_stats(value)
        low[...] = (normed * gain[1:2] + shift[1:2]).astype(BF)

    ins = [near(a) for a in (after, mine, other, bias, gain, shift)]
    return launch(body, "second_norm", at, ins, [shape(half, width), shape(half, width, dtype=BF)], us=1.5)


def feed_up(at, mine, other, f1, f2, b1):
    half, width = mine.shape
    units = f1.shape[1]

    def body(at, ins, outs, _):
        mine, other, f1, f2, b1 = ins
        keep, send, hidden, slope = outs
        for r, (x, target) in enumerate(((other, send), (mine, keep))):
            span = slice((1 - r) * half, (2 - r) * half)
            low, steep = gelu_pair(mm(x[...], f1[...]) + b1[...])
            hidden[span, :] = low
            slope[span, :] = steep
            target[...] = mm(low, f2[...]).astype(target.dtype)

    ins = [near(a) for a in (mine, other, f1, f2, b1)]
    outs = [
        shape(half, width),
        shape(half, width, dtype=BF),
        shape(2 * half, units, dtype=BF),
        shape(2 * half, units),
    ]
    return launch(body, "feed_up", at, ins, outs, us=4)


def third_norm(at, total, mine, other, cot, bias, gain, shift):
    half, width = mine.shape

    def body(at, ins, outs, _):
        total, mine, other, cot, bias, gain, shift = ins
        mixed, dlast_out, low, sums = outs
        normed_mid, _ = norm_stats(total[...])
        last = normed_mid * gain[1:2] + shift[1:2] + (mine[...].astype(F32) + other[...].astype(F32)) + bias[...]
        normed, inverse = norm_stats(last)
        first_row = at[0] * half
        live = (first_row + lax.broadcasted_iota(jnp.int32, (half, 1), 0) < at[3]).astype(F32)
        mixed[...] = ((normed * gain[2:3] + shift[2:3]) * live).astype(BF)
        delta = cot[...].astype(F32) * live
        dlast = norm_backward(delta, normed, inverse, gain[2:3])
        dlast_out[...] = dlast
        low[...] = dlast.astype(BF)
        sums[...] = stacked_sums(delta * normed, delta, dlast)

    ins = [
        near(total),
        near(mine),
        near(other),
        near(cot, lambda ref, at: ref.at[rows_at(at[0], half), :]),
        near(bias),
        near(gain),
        near(shift),
    ]
    outs = [shape(half, width, dtype=BF), shape(half, width), shape(half, width, dtype=BF), shape(8, width)]
    return launch(body, "third_norm", at, ins, outs, us=2.5)


def feed_down(at, mine, other, f1, f2, slope):
    half, width = mine.shape
    units = f1.shape[1]

    def body(at, ins, outs, _):
        mine, other, f1, f2, slope = ins
        keep, send, dpre, sums = outs
        total = jnp.zeros((1, units), F32)
        for r, (x, target) in enumerate(((other, send), (mine, keep))):
            span = slice((1 - r) * half, (2 - r) * half)
            grad = mm(x[...], f2[...], NT) * slope[span, :]
            total = total + column_sum(grad)
            low = grad.astype(BF)
            dpre[span, :] = low
            target[...] = mm(low, f1[...], NT).astype(target.dtype)
        sums[...] = total

    ins = [near(a) for a in (mine, other, f1, f2, slope)]
    outs = [
        shape(half, width),
        shape(half, width, dtype=BF),
        shape(2 * half, units, dtype=BF),
        shape(1, units),
    ]
    return launch(body, "feed_down", at, ins, outs, us=3)


def second_back(at, dlast, mine, other, total, gain):
    half, width = mine.shape

    def body(at, ins, outs, _):
        dlast, mine, other, total, gain = ins
        dsecond, low, sums = outs
        dmid = dlast[...] + (mine[...].astype(F32) + other[...].astype(F32))
        normed, inverse = norm_stats(total[...])
        result = norm_backward(dmid, normed, inverse, gain[1:2])
        dsecond[...] = result
        low[...] = result.astype(BF)
        sums[...] = stacked_sums(dmid * normed, dmid, result)

    ins = [near(a) for a in (dlast, mine, other, total, gain)]
    outs = [shape(half, width), shape(half, width, dtype=BF), shape(8, width)]
    return launch(body, "second_back", at, ins, outs, us=1.8)


def gelu_pair(pre):
    phi = 0.5 * (1.0 + erf(pre * 0.7071067811865476))
    return (pre * phi).astype(BF), phi + pre * (jnp.exp(pre * pre * -0.5) * 0.3989422804014327)


def cross_backward(at, z_mine, z_other, raised, inverse, query, keys, values, w, wo, nh):
    half, width = z_mine.shape
    rows = 2 * half
    local = w.shape[1]
    hd = local // nh
    slots = keys.shape[1]
    scale = hd**-0.5

    def body(at, ins, outs, scratch):
        z_halves, (wo, inverse, values, raised, query, keys, w) = ins[:2], ins[2:]
        keep, send, dquery, dkv, sums = outs
        douts, right, found = scratch
        zero = jnp.zeros((half, hd), BF)
        head_sum = jnp.zeros((1, local), F32)
        for r in range(2):
            span = slice(r * half, (r + 1) * half)
            dhead = mm(z_halves[r][...], wo[...], NT)
            head_sum = head_sum + column_sum(dhead)
            scaled = query[span, :] * jnp.asarray(scale, BF)
            for h in range(nh):
                part = slice(h * hd, (h + 1) * hd)
                dout = (dhead[:, part] * inverse[h, span, 0:1]).astype(BF)
                douts[h, span, :] = jnp.concatenate([dout, dout], axis=1)
                right[h, 0, span, :] = jnp.concatenate([scaled[:, part], zero], axis=1)
                right[h, 1, span, :] = jnp.concatenate([zero, dout], axis=1)

        def one_head(h, _):
            grad = None
            for r in range(2):
                span = slice(r * half, (r + 1) * half)
                dprob = mm(douts[h, span, :], values[h], NT)
                low = raised[h, span, :]
                e = low.astype(F32)
                weighed = e * dprob
                mean = jnp.sum(weighed, axis=1, keepdims=True) * inverse[h, span, 0:1]
                dscore = (weighed - e * mean).astype(BF)
                both = mm(dscore, keys[h])
                found[h, span, :] = both[:, :hd] + both[:, hd:]
                part = mm(dscore, right[h, 0, span, :], TN) + mm(low, right[h, 1, span, :], TN)
                grad = part if grad is None else grad + part
            dkv[h] = grad.astype(BF)
            return 0

        lax.fori_loop(0, nh, one_head, 0)
        query_sum = jnp.zeros((1, local), F32)
        for r, target in enumerate((keep, send)):
            span = slice(r * half, (r + 1) * half)
            dq = jnp.concatenate([found[h, span, :] for h in range(nh)], axis=1) * scale
            query_sum = query_sum + column_sum(dq)
            dq_low = dq.astype(BF)
            dquery[span, :] = dq_low
            target[...] = mm(dq_low, w[0]).astype(target.dtype)
        sums[...] = jnp.concatenate([query_sum, head_sum], axis=0)

    return launch(
        body,
        "cross_bwd",
        at,
        [near(a) for a in (z_mine, z_other, wo, inverse, values, raised, query, keys, w)],
        [
            shape(half, width),
            shape(half, width, dtype=BF),
            shape(rows, local, dtype=BF),
            shape(nh, slots, 2 * hd, dtype=BF),
            shape(2, local),
        ],
        scratch=[
            pltpu.VMEM((nh, rows, 2 * hd), BF),
            pltpu.VMEM((nh, 2, rows, 2 * hd), BF),
            pltpu.VMEM((nh, rows, hd), F32),
        ],
        mib=30,
        us=11,
    )


def store_gradient(at, dkv, w, nh):
    _, slots, twice = dkv.shape
    _, local, width = w.shape
    hd = twice // 2
    seg = slots // 4

    def body(at, ins, outs, _):
        dkv, w = ins
        keep, send = outs
        weights = []
        for h in range(nh):
            part = slice(h * hd, (h + 1) * hd)
            weights += [w[1][part], w[2][part]]
        weight = jnp.concatenate(weights, axis=0)
        for slot in (1, 3, 0, 2):
            rows = jnp.concatenate([dkv[h, slot * seg : (slot + 1) * seg, :] for h in range(nh)], axis=1)
            part = mm(rows, weight)
            if slot % 2 == 0:
                keep[slot // 2] = part
            else:
                send[slot // 2] = part.astype(BF)

    return launch(
        body,
        "store_grad",
        at,
        [near(dkv), near(w)],
        [shape(2, seg, width), shape(2, seg, width, dtype=BF)],
        us=2.6,
    )


def group_outs(width, columns, blocks, tail=0):
    if not blocks:
        return [shape(width, columns)]
    n, r = blocks
    return [shape(n * r + tail, columns, dtype=BF), shape(n, r, columns)]


def emit_group(at, grad, outs, blocks, first, columns, kept_first=None):
    if not blocks:
        outs[0][:, first : first + columns] = grad[...]
        return
    n, r = blocks
    kept_first = first if kept_first is None else kept_first
    span, kept = slice(first, first + columns), slice(kept_first, kept_first + columns)
    for b in range(n):
        theirs = pl.ds(pl.multiple_of((2 * b + 1 - at[4]) * r, 8), r)
        outs[0][b * r : (b + 1) * r, span] = grad[theirs, :].astype(BF)
        outs[1][b, :, kept] = grad[pl.ds(pl.multiple_of((2 * b + at[4]) * r, 8), r), :]


def turned_product(out, left, right, step=256):
    if left.shape[1] % step:
        out[...] = mm(left[...], right[...], TN)
        return

    def some(i, _):
        span = pl.ds(pl.multiple_of(i * step, step), step)
        out[span, :] = mm(left[:, span], right[...], TN)
        return 0

    lax.fori_loop(0, left.shape[1] // step, some, 0)


def feed_grads(at, mid_mine, mid_other, dpre, dlast_mine, dlast_other, hidden, blocks):
    half, width = mid_mine.shape
    units = dpre.shape[1]
    if blocks:
        n, r = blocks
        structs = [shape(n * r, 2 * units, dtype=BF), shape(n, r, 2 * units)]
    else:
        structs = [shape(width, units), shape(width, units)]

    def body(at, ins, outs, scratch):
        mid_mine, mid_other, dpre, dlast_mine, dlast_other, hidden = ins
        left, grad = scratch
        for i, (mine, other, right) in enumerate(((mid_mine, mid_other, dpre), (dlast_mine, dlast_other, hidden))):
            left[:half, :] = mine[...]
            left[half:, :] = other[...]
            turned_product(grad, left, right)
            emit_group(at, grad, outs if blocks else outs[i:], blocks, i * units if blocks else 0, units)

    return launch(
        body,
        "feed_grads",
        at,
        [near(a) for a in (mid_mine, mid_other, dpre, dlast_mine, dlast_other, hidden)],
        structs,
        scratch=[pltpu.VMEM((2 * half, width), BF), pltpu.VMEM((width, units), F32)],
        us=4,
    )


def cross_grads(at, z_mine, z_other, mine, other, dquery, heads, shards, dkv, nh, blocks):
    half, width = mine.shape
    local = dquery.shape[1]
    hd = local // nh
    seg = shards[0].shape[0]

    def body(at, ins, outs, scratch):
        shards, (z_mine, z_other, mine, other, dquery, heads, dkv) = ins[0:4], ins[4:]
        (grad,) = scratch
        grad[...] = mm(mine[...], dquery[:half], TN) + mm(other[...], dquery[half:], TN)
        emit_group(at, grad, outs, blocks, 0, local)
        grad[...] = mm(z_mine[...], heads[:half], TN) + mm(z_other[...], heads[half:], TN)
        emit_group(at, grad, outs, blocks, 3 * local, local)
        both = None
        for slot, block in enumerate(shards):
            rows = jnp.concatenate([dkv[h, slot * seg : (slot + 1) * seg, :] for h in range(nh)], axis=1)
            part = mm(block[...], rows, TN)
            both = part if both is None else both + part
        for i in range(2):
            grad[...] = jnp.concatenate([both[:, (2 * h + i) * hd : (2 * h + i + 1) * hd] for h in range(nh)], axis=1)
            emit_group(at, grad, outs, blocks, (1 + i) * local, local)

    return launch(
        body,
        "cross_grads",
        at,
        [near(a) for a in (*shards, z_mine, z_other, mine, other, dquery, heads, dkv)],
        group_outs(width, 4 * local, blocks),
        scratch=[pltpu.VMEM((width, local), F32)],
        us=4,
    )


def first_back(at, dsecond, mine, other, total, gain):
    half, width = mine.shape

    def body(at, ins, outs, _):
        dsecond, mine, other, total, gain = ins
        dfirst, low, sums = outs
        value = dsecond[...] + (mine[...].astype(F32) + other[...].astype(F32))
        normed, inverse = norm_stats(total[...])
        result = norm_backward(value, normed, inverse, gain[0:1])
        dfirst[...] = result
        low[...] = result.astype(BF)
        sums[...] = stacked_sums(value * normed, value, result)

    ins = [near(a) for a in (dsecond, mine, other, total, gain)]
    outs = [shape(half, width), shape(half, width, dtype=BF), shape(8, width)]
    return launch(body, "first_back", at, ins, outs, us=1.8)


def self_backward(at, mine, other, tokens, w, wo, qkv, prob, flat, mixed, sums, nh, blocks):
    half, width = mine.shape
    rows = 2 * half
    local = wo.shape[0]
    hd = local // nh
    scale = hd**-0.5

    def body(at, ins, outs, scratch):
        mine, other, wo, qkv, prob, tok, w, mixed, flat = ins[:9]
        third_sums, second_sums, first_sums, third_other, second_other, first_other, fc1_sum, head_sums = ins[9:]
        send, keep = outs[0:2]
        group, extra = outs[2:-1], outs[-1]
        z, dqkv, grad = scratch
        own, distant = rows_at(at[0], half), rows_at(1 - at[0], half)
        z[own, :] = mine[...]
        z[distant, :] = other[...]
        dself = mm(z[...], wo[...], NT).astype(BF)
        v, k, q = qkv[2], qkv[1], qkv[0]
        dq, dk, dv = [], [], []
        for h in range(nh):
            part = slice(h * hd, (h + 1) * hd)
            weights_low = prob[h]
            weights = weights_low.astype(F32)
            weighed = weights * mm(dself[:, part], v[:, part], NT)
            dscore = (weighed - weights * jnp.sum(weighed, axis=1, keepdims=True)).astype(BF)
            dq.append(mm(dscore, k[:, part]))
            dk.append(mm(dscore, q[:, part], TN))
            dv.append(mm(weights_low, dself[:, part], TN))
        dquery = jnp.concatenate(dq, axis=1) * scale
        dvalue = jnp.concatenate(dv, axis=1)
        dqkv[0] = dquery.astype(BF)
        dqkv[1] = (jnp.concatenate(dk, axis=1) * scale).astype(BF)
        dqkv[2] = dvalue.astype(BF)
        x = tok[...]
        for i in range(3):
            grad[...] = mm(x, dqkv[i], TN)
            emit_group(at, grad, group, blocks, i * local, local)
        grad[...] = mm(z[...], flat[...], TN)
        emit_group(at, grad, group, blocks, 3 * local, local)
        pad = jnp.zeros((1, width - 2 * local), F32)
        small = jnp.concatenate(
            [
                third_sums[0:3] + third_other[0:3],
                second_sums[0:3] + second_other[0:3],
                first_sums[0:3] + first_other[0:3],
                fc1_sum[...],
                jnp.concatenate([head_sums[0:1], head_sums[1:2], pad], axis=1),
                jnp.concatenate([column_sum(dquery), column_sum(dvalue), pad], axis=1),
                jnp.zeros((EXTRA - 12, width), F32),
            ],
            axis=0,
        )
        extra[...] = small
        if blocks:
            group[0][blocks[0] * blocks[1] :, :] = two_terms(small)
        send[half:, :] = mixed[...]
        for place, out in ((distant, send), (own, keep)):
            total = mm(dqkv[0, place, :], w[0]) + mm(dqkv[1, place, :], w[1]) + mm(dqkv[2, place, :], w[2])
            out[0:half, :] = total.astype(out.dtype)

    return launch(
        body,
        "self_bwd",
        at,
        [near(a) for a in (mine, other, wo, qkv, prob, tokens, w, mixed, flat, *sums)],
        [shape(2 * half, width, dtype=BF), shape(half, width)]
        + group_outs(width, 4 * local, blocks, 2 * EXTRA)
        + [shape(EXTRA, width)],
        scratch=[
            pltpu.VMEM((rows, width), BF),
            pltpu.VMEM((3, rows, local), BF),
            pltpu.VMEM((width, local), F32),
        ],
        mib=20,
        us=6,
    )


def fold_lines(value, columns):
    rows, width = value.shape
    times = columns // width
    each = rows // times
    return value if times == 1 else jnp.concatenate([value[i * each : (i + 1) * each] for i in range(times)], axis=1)


def unfold_lines(value, width):
    times = value.shape[1] // width
    return (
        value
        if times == 1
        else jnp.concatenate([value[:, i * width : (i + 1) * width] for i in range(times)], axis=0)
    )


def add_stage(at, keep, got, small, bit):
    n, rows, _ = keep[0].shape
    starts = [0]
    for part in keep:
        starts.append(starts[-1] + part.shape[2])
    columns = starts[-1]
    tail = 0 if small is None else 2 * small.shape[0] * small.shape[1] // columns

    def body(at, ins, outs, _):
        keeps, gots = ins[: len(keep)], ins[len(keep) : len(keep) + len(got)]
        mine = at[bit]
        send, stay = outs[:2]
        for b in range(n // 2):
            for chosen, out in ((1 - mine, send), (mine, stay)):
                block = 2 * b + chosen
                for i, part in enumerate(keeps):
                    span = slice(starts[i], starts[i + 1])
                    source, first = (gots[i], 0) if len(got) == len(keep) else (gots[0], starts[i])
                    arrived = source[
                        pl.ds(pl.multiple_of(block * rows, 8), rows), first : first + starts[i + 1] - starts[i]
                    ]
                    value = part[block] + arrived.astype(F32)
                    if out is send:
                        send[b * rows : (b + 1) * rows, span] = value.astype(BF)
                    else:
                        stay[b, :, span] = value
        if tail:
            total = ins[-1][...] + unfold_lines(from_terms(gots[-1][n * rows :, :]), small.shape[1])
            outs[2][...] = total
            send[n // 2 * rows :, :] = two_terms(fold_lines(total, columns))

    ins = [near(part) for part in (*keep, *got)] + ([near(small)] if tail else [])
    outs = [shape(n // 2 * rows + tail, columns, dtype=BF), shape(n // 2, rows, columns)]
    if tail:
        outs.append(shape(*small.shape))
    return launch(body, "add_stage", at, ins, outs, us=1)


def last_stage(at, keep, got, small, parts):
    _, rows, columns = keep.shape
    each = columns // sum(count for count, _ in parts)
    reach = 0 if small is None else small.shape[1]

    def body(at, ins, outs, _):
        total = ins[0][0] + ins[1][0:rows].astype(F32)
        first = 0
        for out, (count, turned) in zip(outs, parts):
            if count == 1:
                value = total[:, first * each : (first + 1) * each]
                out[...] = value.T if turned else value
            else:
                for i in range(count):
                    out[i] = total[:, (first + i) * each : (first + i + 1) * each]
            first += count
        if reach:
            outs[-1][...] = ins[2][...] + unfold_lines(from_terms(ins[1][rows:, :]), reach)

    outs = []
    for count, turned in parts:
        dims = (rows, each) if count == 1 else (count, rows, each)
        outs.append(shape(*(dims[::-1] if turned else dims)))
    ins = [near(keep), near(got)]
    if reach:
        ins.append(near(small))
        outs.append(shape(small.shape[0], reach))
    return launch(body, "last_stage", at, ins, outs, us=1)


def join_halves(at, mine, other):
    half, width = mine.shape
    skip = other.shape[0] - half

    def body(at, ins, outs, _):
        outs[0][rows_at(at[0], half), :] = ins[0][...]
        outs[0][rows_at(1 - at[0], half), :] = ins[1][...]

    out = shape(2 * half, width, dtype=mine.dtype)
    ins = [near(mine), near(other, lambda ref, at: ref.at[pl.ds(skip, half), :])]
    return launch(body, "join_halves", at, ins, [out])[0]


def flip(bit, size):
    return [(i, i ^ bit) for i in range(size)]


def butterfly(value, axis, size):
    bit = 1
    while bit < size:
        value = value + lax.ppermute(value, axis, flip(bit, size))
        bit *= 2
    return value


def on_device(
    tokens,
    store,
    summary_length,
    top_index,
    cotangent,
    self_qkv_weight,
    self_qv_bias,
    self_out_weight,
    self_out_bias,
    qkv_weight,
    qv_bias,
    out_weight,
    out_bias,
    fc1_weight,
    fc1_bias,
    fc2_weight,
    fc2_bias,
    norm_gain,
    norm_shift,
):
    rows, width = tokens.shape
    half = rows // 2
    nh = top_index.shape[1]
    local = qkv_weight.shape[2]
    units = fc1_weight.shape[1]
    seg = store.shape[1]
    wide = lax.axis_size("wide")
    place = lax.axis_index("narrow")
    doc = lax.axis_index("wide")
    core, across = place % 2, place // 2
    at = jnp.stack([core, across, place, summary_length[0], doc % 2, doc // 2 % 2, doc // 4]).astype(jnp.int32)
    blocks = (wide // 2, width // wide) if wide == 8 else None
    row = lambda v: v.reshape(1, -1)
    self_w = jnp.swapaxes(self_qkv_weight, 1, 2)
    cross_w = jnp.swapaxes(qkv_weight, 1, 2)

    def to_core(v):
        return lax.ppermute(v, "narrow", CORE)

    def to_across(v):
        return lax.ppermute(v, "narrow", ACROSS)

    def over(v, bit):
        return lax.ppermute(v, "wide", flip(bit, wide))

    def chip_sum(keep, send):
        return (keep + to_core(send).astype(F32)).astype(BF)

    store_x = to_across(store[0])
    qkv, prob, flat, send, keep = self_forward(at, tokens, self_w, self_qv_bias, self_out_weight, nh)
    mine = chip_sum(keep, send)
    other = to_across(mine)
    index = index_rows(top_index)
    bias_mine = make_mask(tie(at, mine), index, top_index.shape, seg, 128, 0)
    store_x, store_own = tie((store_x, store[0]), bias_mine)
    shards = [store_own, to_core(store_own), store_x, to_core(store_x)]
    bias_other = make_mask(tie(at, bias_mine), index, top_index.shape, seg, 128, 1)
    other = tie(other, bias_other)
    first_total, after, after_low = first_norm(at, mine, other, tokens, row(self_out_bias), norm_gain, norm_shift)
    after_other = to_core(after_low)

    keys, values = keys_values(tie(at, after_low), shards, cross_w, nh)
    keep, send, raised, inverse, query, heads = cross_forward(
        tie(at, keys), after_low, after_other, bias_mine, bias_other, keys, values, cross_w, qv_bias, out_weight, nh
    )
    mine = chip_sum(keep, send)
    second_total, mid_low = second_norm(at, after, mine, to_across(mine), row(out_bias), norm_gain, norm_shift)
    mid_other = to_core(mid_low)

    keep, send, hidden, slope = feed_up(at, mid_low, mid_other, fc1_weight, fc2_weight, row(fc1_bias))
    mine = chip_sum(keep, send)
    mixed_half, dlast, dlast_low, third_sums = third_norm(
        at, second_total, mine, to_across(mine), cotangent, row(fc2_bias), norm_gain, norm_shift
    )
    dlast_other, third_other = to_core(dlast_low), to_core(third_sums)
    keep, send, dpre, fc1_sum = feed_down(at, dlast_low, dlast_other, fc1_weight, fc2_weight, slope)
    mine = chip_sum(keep, send)
    other = to_across(mine)
    feed_out = feed_grads(tie(at, mine), mid_low, mid_other, dpre, dlast_low, dlast_other, hidden, blocks)
    other = tie(other, feed_out[0])
    dsecond, z, second_sums = second_back(at, dlast, mine, other, second_total, norm_gain)
    z_other, second_other = to_core(z), to_core(second_sums)

    keep, send, dquery, dkv, cross_sums = cross_backward(
        at, z, z_other, raised, inverse, query, keys, values, cross_w, out_weight, nh
    )
    mine = chip_sum(keep, send)
    other = to_across(mine)
    cross_out = cross_grads(
        tie(at, mine), z, z_other, after_low, after_other, dquery, heads, shards, dkv, nh, blocks
    )
    started = cross_out[0]
    if blocks:
        feed_send, feed_keep = add_stage(tie(at, started), [feed_out[1]], [over(feed_out[0], 1)], None, 5)
        feed_next = over(feed_send, 2)
        started = feed_send
    store_keep, store_send = store_gradient(tie(at, started), dkv, cross_w, nh)
    other = tie(other, store_send)
    dfirst, dfirst_low, first_sums = first_back(at, dsecond, mine, other, first_total, norm_gain)
    dfirst_other, first_other = to_core(dfirst_low), to_core(first_sums)
    store_close = to_core(tie(store_send, dfirst_other))
    started = dfirst_low

    send, keep, *self_out, small = self_backward(
        tie(at, dfirst_other, store_close),
        dfirst_low,
        dfirst_other,
        tokens,
        self_w,
        self_out_weight,
        qkv,
        prob,
        flat,
        mixed_half,
        (third_sums, second_sums, first_sums, third_other, second_other, first_other, fc1_sum, cross_sums),
        nh,
        blocks,
    )
    if blocks:
        cross_got = tie(over(cross_out[0], 1), small)
        feed_send, feed_keep = add_stage(tie(at, cross_got), [feed_keep], [feed_next], None, 6)
        feed_next = over(feed_send, 4)
        fc1_grad, fc2_grad = last_stage(tie(at, feed_send), feed_keep, feed_next, None, [(1, False), (1, False)])
        fc2_grad = fc2_grad.T
        both_send, both_keep, small = add_stage(
            tie(at, fc1_grad), [cross_out[1], self_out[1]], [cross_got, over(self_out[0], 1)], small, 5
        )
        both_next = over(both_send, 2)
        send = tie(send, both_send)
    close = to_core(send)
    mine = (keep + close[:half].astype(F32)).astype(BF)
    other = to_across(mine)
    if blocks:
        both_send, both_keep, small = add_stage(tie(at, mine), [both_keep], [both_next], small, 6)
        both_next = over(both_send, 4)
        other = tie(other, both_send)
    tokens_half = dfirst + (mine.astype(F32) + other.astype(F32))
    tokens_other = to_core(tokens_half)
    mixed = join_halves(tie(at, tokens_half), mixed_half, close)
    store_distant = to_across(tie((store_keep[1] + store_close[1].astype(F32)).astype(BF), mine))
    tokens_grad = join_halves(at, tokens_half, tie(tokens_other, mixed))
    store_distant = tie(store_distant, tokens_grad)
    store_grad = (store_keep[0] + store_close[0].astype(F32) + store_distant.astype(F32))[None]

    if blocks:
        qkv_grad, out_grad, self_qkv_grad, self_out_grad, small = last_stage(
            tie(at, store_grad), both_keep, both_next, small, [(3, False), (1, True), (3, False), (1, True)]
        )
    else:
        scatter = functools.partial(lax.psum_scatter, axis_name="wide", tiled=True)
        parts = lambda g: jnp.stack([g[:, i * local : (i + 1) * local] for i in range(3)])
        fc1_grad = scatter(feed_out[0], scatter_dimension=0)
        fc2_grad = scatter(feed_out[1].T, scatter_dimension=1)
        qkv_grad = scatter(parts(cross_out[0]), scatter_dimension=1)
        out_grad = scatter(cross_out[0][:, 3 * local :].T, scatter_dimension=1)
        self_qkv_grad = scatter(parts(self_out[0]), scatter_dimension=1)
        self_out_grad = scatter(self_out[0][:, 3 * local :].T, scatter_dimension=1)
        small = butterfly(small, "wide", wide)
    gain_last, shift_last, fc2_b, gain_mid, shift_mid, out_b, gain_first, shift_first, self_out_b = (
        small[i] for i in range(9)
    )
    return (
        mixed,
        tokens_grad,
        store_grad,
        self_qkv_grad,
        small[11, : 2 * local].reshape(2, local),
        self_out_grad,
        self_out_b,
        qkv_grad,
        small[10, : 2 * local].reshape(2, local),
        out_grad,
        out_b,
        fc1_grad,
        small[9],
        fc2_grad,
        fc2_b,
        jnp.stack([gain_first, gain_mid, gain_last]),
        jnp.stack([shift_first, shift_mid, shift_last]),
    )


def solution(mesh):
    placed = (
        P("wide", None),
        P("wide", "narrow", None),
        P("wide"),
        P("wide", "narrow", None, None),
        P("wide", None),
        P(None, None, "narrow"),
        P(None, "narrow"),
        P("narrow", None),
        P(),
        P(None, None, "narrow"),
        P(None, "narrow"),
        P("narrow", None),
        P(),
        P(None, "narrow"),
        P("narrow"),
        P("narrow", None),
        P(),
        P(),
        P(),
    )
    return jax.shard_map(
        on_device,
        mesh=mesh,
        in_specs=placed,
        out_specs=(
            P("wide", None),
            P("wide", None),
            P("wide", "narrow", None),
            P(None, "wide", "narrow"),
            P(None, "narrow"),
            P("narrow", "wide"),
            P(),
            P(None, "wide", "narrow"),
            P(None, "narrow"),
            P("narrow", "wide"),
            P(),
            P("wide", "narrow"),
            P("narrow"),
            P("narrow", "wide"),
            P(),
            P(),
            P(),
        ),
        check_vma=False,
    )
```

```python
import functools

import jax
import jax.numpy as jnp
from jax import lax
from jax.experimental import pallas as pl
from jax.experimental.pallas import tpu as pltpu
from jax.sharding import PartitionSpec as P

F32 = jnp.float32
BF = jnp.bfloat16
NN = (((1,), (0,)), ((), ()))
NT = (((1,), (1,)), ((), ()))
TN = (((0,), (0,)), ((), ()))
EPS = 1e-05
PACE = 1.1e8
SELF_MIB = 60
EXTRA = 16

CORE = [(i, i ^ 1) for i in range(4)]
ACROSS = [(i, i ^ 2) for i in range(4)]


def mm(left, right, dims=NN):
    return lax.dot_general(left, right, dims, preferred_element_type=F32)


def shape(*dims, dtype=F32):
    return jax.ShapeDtypeStruct(dims, dtype)


def tie(value, *earlier):
    return lax.optimization_barrier((value, *earlier))[0]


class Operand:
    def __init__(self, source, buffer, sems, first, parts):
        self.buffer = buffer
        self.parts = parts
        if parts:
            self.copies = [
                pltpu.make_async_copy(source.at[i], buffer.at[i], sems.at[first + i]) for i in range(buffer.shape[0])
            ]
        else:
            self.copies = [pltpu.make_async_copy(source, buffer, sems.at[first])]
        self.waited = [False] * len(self.copies)
        for copy in self.copies:
            copy.start()

    def ready(self, part=None):
        for i, copy in enumerate(self.copies):
            if not self.waited[i] and (part is None or i == part):
                copy.wait()
                self.waited[i] = True

    @property
    def shape(self):
        return self.buffer.shape

    def __getitem__(self, at):
        self.ready(at if self.parts and isinstance(at, int) else None)
        return self.buffer[at]


class Result:
    def __init__(self, target, buffer, sems, first, parts):
        self.buffer = buffer
        if parts:
            self.copies = [
                pltpu.make_async_copy(buffer.at[i], target.at[i], sems.at[first + i]) for i in range(buffer.shape[0])
            ]
        else:
            self.copies = [pltpu.make_async_copy(buffer, target, sems.at[first])]
        self.started = [False] * len(self.copies)

    @property
    def shape(self):
        return self.buffer.shape

    @property
    def dtype(self):
        return self.buffer.dtype

    def __setitem__(self, at, value):
        self.buffer[at] = value

    def flush(self, part=0):
        self.copies[part].start()
        self.started[part] = True

    def finish(self):
        for i in range(len(self.copies)):
            if not self.started[i]:
                self.flush(i)
        for copy in self.copies:
            copy.wait()


def far(array, take=None, dims=None, parts=False):
    return ("far", array, take, tuple(dims or array.shape), parts)


def near(array, take=None):
    return ("near", array, take, None, False)


def raw(array):
    return ("raw", array, None, None, False)


def launch(body, name, at, ins, outs, scratch=(), mib=16, us=2.0):
    in_specs = [pl.BlockSpec(memory_space=pltpu.SMEM)]
    buffers, n_in, n_out = [], 0, 0
    for kind, array, _, dims, parts in ins:
        in_specs.append(pl.BlockSpec(memory_space=pltpu.VMEM if kind == "near" else pltpu.HBM))
        if kind == "far":
            buffers.append(pltpu.VMEM(dims, array.dtype))
            n_in += dims[0] if parts else 1
    out_specs, structs = [], []
    for out in outs:
        if isinstance(out, tuple):
            struct, parts = out
            out_specs.append(pl.BlockSpec(memory_space=pltpu.HBM))
            buffers.append(pltpu.VMEM(struct.shape, struct.dtype))
            n_out += struct.shape[0] if parts else 1
        else:
            struct = out
            out_specs.append(pl.BlockSpec(memory_space=pltpu.VMEM))
        structs.append(struct)
    n_buffers = len(buffers)
    sems = [pltpu.SemaphoreType.DMA((max(n, 1),)) for n in (n_in, n_out)]

    def kernel(at_ref, *refs):
        in_refs, out_refs = refs[: len(ins)], refs[len(ins) : len(ins) + len(outs)]
        rest = refs[len(ins) + len(outs) :]
        bufs, user, (in_sems, out_sems) = list(rest[:n_buffers]), rest[n_buffers:-2], rest[-2:]
        place, given = 0, []
        for ref, (kind, _, take, dims, parts) in zip(in_refs, ins):
            source = take(ref, at_ref) if take else ref
            if kind == "far":
                given.append(Operand(source, bufs.pop(0), in_sems, place, parts))
                place += dims[0] if parts else 1
            else:
                given.append(source)
        place, results = 0, []
        for ref, out in zip(out_refs, outs):
            if isinstance(out, tuple):
                results.append(Result(ref, bufs.pop(0), out_sems, place, out[1]))
                place += out[0].shape[0] if out[1] else 1
            else:
                results.append(ref)
        body(at_ref, given, results, user)
        for operand in given:
            if isinstance(operand, Operand):
                operand.ready()
        for result in results:
            if isinstance(result, Result):
                result.finish()

    return pl.pallas_call(
        kernel,
        in_specs=in_specs,
        out_specs=out_specs,
        out_shape=structs,
        scratch_shapes=buffers + list(scratch) + sems,
        compiler_params=pltpu.CompilerParams(vmem_limit_bytes=mib << 20),
        cost_estimate=pl.CostEstimate(flops=int(us * PACE), bytes_accessed=1000, transcendentals=0),
        name=name,
    )(at, *[entry[1] for entry in ins])


def norm_stats(value):
    centre = value - jnp.mean(value, axis=-1, keepdims=True)
    spread = jnp.mean(centre * centre, axis=-1, keepdims=True)
    inverse = lax.rsqrt(spread + EPS)
    return centre * inverse, inverse


def norm_backward(grad, normed, inverse, gain):
    scaled = grad * gain
    centred = scaled - jnp.mean(scaled, axis=-1, keepdims=True)
    return inverse * (centred - normed * jnp.mean(scaled * normed, axis=-1, keepdims=True))


def column_sum(value):
    return jnp.sum(value, axis=0, keepdims=True)


def erf(value):
    x = jnp.clip(value, -4.0, 4.0)
    y = x * x
    top = jnp.full_like(y, -2.72614225801306e-10)
    for factor in (
        2.77068142495902e-08,
        -2.10102402082508e-06,
        -5.69250639462346e-05,
        -7.34990630326855e-04,
        -2.95459980854025e-03,
        -1.60960333262415e-02,
    ):
        top = top * y + factor
    low = jnp.full_like(y, -1.45660718464996e-05)
    for factor in (
        -2.13374055278905e-04,
        -1.68282697438203e-03,
        -7.37332916720468e-03,
        -1.42647390514189e-02,
    ):
        low = low * y + factor
    return x * top / low


def two_terms(value):
    high = value.astype(BF)
    return jnp.concatenate([high, (value - high.astype(F32)).astype(BF)], axis=0)


def from_terms(stacked):
    rows = stacked.shape[0] // 2
    terms = stacked.astype(F32)
    return terms[:rows] + terms[rows:]


def rows_at(place, rows):
    return pl.ds(pl.multiple_of(place * rows, rows), rows)


def self_forward(at, tokens, w, b, wo, nh):
    rows, width = tokens.shape
    local = w.shape[1]
    half = rows // 2
    hd = local // nh
    scale = hd**-0.5

    def body(at, ins, outs, _):
        tok, w, wo, b = ins
        qkv, prob, flat, send, keep = outs
        x = tok[...]
        q = (mm(x, w[0], NT) + b[0:1]).astype(BF)
        k = mm(x, w[1], NT).astype(BF)
        v = (mm(x, w[2], NT) + b[1:2]).astype(BF)
        for i, value in enumerate((q, k, v)):
            qkv[i] = value
            qkv.flush(i)
        row_ids = lax.broadcasted_iota(jnp.int32, (rows, rows), 0)
        key_ids = lax.broadcasted_iota(jnp.int32, (rows, rows), 1)
        allowed = (key_ids <= row_ids) & (key_ids < at[3])
        found = []
        for h in range(nh):
            part = slice(h * hd, (h + 1) * hd)
            scores = mm(q[:, part], k[:, part], NT) * scale
            scores = jnp.where(allowed, scores, -1e30)
            shifted = jnp.exp(scores - jnp.max(scores, axis=1, keepdims=True))
            weights = (shifted * (1.0 / jnp.sum(shifted, axis=1, keepdims=True))).astype(BF)
            prob[h] = weights
            prob.flush(h)
            found.append(mm(weights, v[:, part]).astype(BF))
        flat[...] = jnp.concatenate(found, axis=1)
        flat.flush()
        send[...] = mm(flat.buffer[rows_at(1 - at[0], half), :], wo[...]).astype(BF)
        send.flush()
        keep[...] = mm(flat.buffer[rows_at(at[0], half), :], wo[...])

    return launch(
        body,
        "self_fwd",
        at,
        [far(tokens), far(w, parts=True), far(wo), far(b)],
        [
            (shape(3, rows, local, dtype=BF), True),
            (shape(nh, rows, rows, dtype=BF), True),
            (shape(rows, local, dtype=BF), False),
            (shape(half, width, dtype=BF), False),
            (shape(half, width), False),
        ],
        mib=SELF_MIB,
        us=4,
    )


def first_norm(at, mine, other, tokens, bias, gain, shift):
    half, width = mine.shape

    def body(at, ins, outs, _):
        mine, other, tok, bias, gain, shift = ins
        total, after, low = outs
        value = tok[...].astype(F32) + (mine[...].astype(F32) + other[...].astype(F32)) + bias[...]
        total[...] = value
        normed, _ = norm_stats(value)
        result = normed * gain[0:1] + shift[0:1]
        after[...] = result
        low[...] = result.astype(BF)

    return launch(
        body,
        "first_norm",
        at,
        [
            near(mine),
            near(other),
            near(tokens, lambda ref, at: ref.at[rows_at(at[0], half), :]),
            near(bias),
            near(gain),
            near(shift),
        ],
        [shape(half, width), shape(half, width), shape(half, width, dtype=BF)],
        us=1.7,
    )


def index_rows(top_index):
    rows, nh, ns, keep = top_index.shape
    flat = top_index.reshape(rows, nh, ns, keep // 128, 128).transpose(0, 1, 3, 2, 4)
    return flat.reshape(rows * nh * ns * (keep // 128), 128)


def make_mask(at, flat, dims, seg, tile, turn):
    rows, nh, ns, keep = dims
    halves = keep // 128
    per_row = nh * ns * halves
    tiles = rows // 2 // tile
    columns = ns * seg
    blocks = columns // 128
    group = 32

    def body(at, ins, outs, _):
        (index,) = ins
        (bias,) = outs
        lane = lax.broadcasted_iota(jnp.int32, (group, 128), 1).astype(F32)
        lane_low = lane.astype(BF)
        empty = jnp.full((group, 128), -1.0, BF)
        own = at[2]
        steps = []
        step = 1
        while step <= seg - keep:
            steps.insert(0, step)
            step *= 2
        turns = steps + [(seg * s) % 128 for s in range(ns)]
        below = {s: lane_low < jnp.asarray(s, BF) for s in turns if 0 < s < 128}

        for t in range(tiles):
            index.ready(t)
            source = index.buffer.at[t]

            def one_group(g, _):
                for h in range(nh):
                    v = [empty] * blocks
                    for slot in range(ns):
                        first, turn = divmod(seg * slot, 128)
                        for c in range(halves):
                            start = g * (group * per_row) + h * ns * halves + c * ns + (own ^ slot)
                            found = jnp.concatenate(
                                [source[pl.ds(start + q * 8 * per_row, 8, stride=per_row), :] for q in range(group // 8)],
                                axis=0,
                            )
                            ahead = (found.astype(F32) - (lane + float(128 * c))).astype(BF)
                            at_block = first + c
                            if turn == 0:
                                v[at_block] = ahead
                            else:
                                turned = pltpu.roll(ahead, turn, axis=1)
                                v[at_block] = jnp.where(below[turn], v[at_block], turned)
                                v[at_block + 1] = jnp.where(below[turn], turned, v[at_block + 1])
                    for s in steps:
                        gap = jnp.asarray(s, BF)
                        moved = [x - gap for x in v]
                        stay = [jnp.where(x >= gap, empty, x) for x in v]
                        if s % 128 == 0:
                            hop = s // 128
                            v = stay[:hop] + [jnp.maximum(stay[i], moved[i - hop]) for i in range(hop, blocks)]
                        else:
                            turned = [pltpu.roll(x, s, axis=1) for x in moved]
                            v = [
                                jnp.maximum(stay[i], jnp.where(below[s], turned[i - 1], turned[i])) for i in range(blocks)
                            ]
                    for i in range(blocks):
                        bias[h, pl.ds(pl.multiple_of(t * tile + g * group, group), group), i * 128 : (i + 1) * 128] = v[
                            i
                        ] * jnp.asarray(1e30, BF)
                return 0

            lax.fori_loop(0, tile // group, one_group, 0)

    flat = flat.reshape(2 * tiles, tile * per_row, 128)
    return launch(
        body,
        "mask",
        at,
        [
            far(
                flat,
                lambda ref, at: ref.at[pl.ds((at[0] ^ turn) * tiles, tiles)],
                (tiles, tile * per_row, 128),
                parts=True,
            )
        ],
        [shape(nh, rows // 2, columns, dtype=BF)],
        us=10,
    )[0]


def keys_values(at, shards, w, nh):
    seg, width = shards[0].shape
    local = w.shape[1]
    hd = local // nh

    def body(at, ins, outs, _):
        for slot in range(4):
            x = ins[slot][...]
            span = slice(slot * seg, (slot + 1) * seg)
            for i, out in enumerate(outs):
                full = mm(x, ins[4][i + 1], NT)
                high = full.astype(BF)
                low = (full - high.astype(F32)).astype(BF)
                for h in range(nh):
                    part = slice(h * hd, (h + 1) * hd)
                    out[h, span, :] = jnp.concatenate([high[:, part], low[:, part]], axis=1)

    out = shape(nh, 4 * seg, 2 * hd, dtype=BF)
    return launch(body, "keys_values", at, [near(s) for s in shards] + [near(w)], [out, out], us=2)


def cross_forward(at, mine, other, bias_mine, bias_other, keys, values, w, b, wo, nh):
    half, width = mine.shape
    rows = 2 * half
    local = w.shape[1]
    hd = local // nh
    slots = keys.shape[1]
    scale = hd**-0.5

    def body(at, ins, outs, scratch):
        mine, other, wq, keys, bias_mine, bias_other, values, wo, b = ins
        keep, send, raised, inverse, query, heads = outs
        twice, found = scratch
        for r, x in enumerate((mine, other)):
            q = (mm(x[...], wq[0], NT) + b[0:1]).astype(BF)
            query[r * half : (r + 1) * half, :] = q
            scaled = q * jnp.asarray(scale, BF)
            for h in range(nh):
                part = scaled[:, h * hd : (h + 1) * hd]
                twice[h, r * half : (r + 1) * half, :] = jnp.concatenate([part, part], axis=1)

        def one_head(h, _):
            for r, bias in enumerate((bias_mine, bias_other)):
                span = slice(r * half, (r + 1) * half)
                scores = mm(twice[h, span, :], keys[h], NT) + bias[h].astype(F32)
                e = jnp.exp(scores - jnp.max(scores, axis=1, keepdims=True))
                total = 1.0 / jnp.sum(e, axis=1, keepdims=True)
                low = e.astype(BF)
                raised[h, span, :] = low
                inverse[h, span, :] = jnp.broadcast_to(total, (half, 128))
                both = mm(low, values[h])
                found[h, span, :] = (both[:, :hd] + both[:, hd:]) * total
            return 0

        lax.fori_loop(0, nh, one_head, 0)
        for r, target in enumerate((keep, send)):
            span = slice(r * half, (r + 1) * half)
            out = (jnp.concatenate([found[h, span, :] for h in range(nh)], axis=1) + b[1:2]).astype(BF)
            heads[span, :] = out
            target[...] = mm(out, wo[...]).astype(target.dtype)

    return launch(
        body,
        "cross_fwd",
        at,
        [near(a) for a in (mine, other, w, keys, bias_mine, bias_other, values, wo, b)],
        [
            shape(half, width),
            shape(half, width, dtype=BF),
            shape(nh, rows, slots, dtype=BF),
            shape(nh, rows, 128),
            shape(rows, local, dtype=BF),
            shape(rows, local, dtype=BF),
        ],
        scratch=[pltpu.VMEM((nh, rows, 2 * hd), BF), pltpu.VMEM((nh, rows, hd), F32)],
        mib=30,
        us=9,
    )


def stacked_sums(*values):
    sums = [column_sum(value) for value in values]
    return jnp.concatenate(sums + [jnp.zeros((8 - len(sums), values[0].shape[1]), F32)], axis=0)


def second_norm(at, after, mine, other, bias, gain, shift):
    half, width = mine.shape

    def body(at, ins, outs, _):
        after, mine, other, bias, gain, shift = ins
        total, low = outs
        value = after[...] + (mine[...].astype(F32) + other[...].astype(F32)) + bias[...]
        total[...] = value
        normed, _ = norm_stats(value)
        low[...] = (normed * gain[1:2] + shift[1:2]).astype(BF)

    ins = [near(a) for a in (after, mine, other, bias, gain, shift)]
    return launch(body, "second_norm", at, ins, [shape(half, width), shape(half, width, dtype=BF)], us=1.5)


def feed_up(at, mine, other, f1, f2, b1):
    half, width = mine.shape
    units = f1.shape[1]

    def body(at, ins, outs, _):
        mine, other, f1, f2, b1 = ins
        keep, send, hidden, slope = outs
        for r, (x, target) in enumerate(((other, send), (mine, keep))):
            span = slice((1 - r) * half, (2 - r) * half)
            low, steep = gelu_pair(mm(x[...], f1[...]) + b1[...])
            hidden[span, :] = low
            slope[span, :] = steep
            target[...] = mm(low, f2[...]).astype(target.dtype)

    ins = [near(a) for a in (mine, other, f1, f2, b1)]
    outs = [
        shape(half, width),
        shape(half, width, dtype=BF),
        shape(2 * half, units, dtype=BF),
        shape(2 * half, units),
    ]
    return launch(body, "feed_up", at, ins, outs, us=4)


def third_norm(at, total, mine, other, cot, bias, gain, shift):
    half, width = mine.shape

    def body(at, ins, outs, _):
        total, mine, other, cot, bias, gain, shift = ins
        mixed, dlast_out, low, sums = outs
        normed_mid, _ = norm_stats(total[...])
        last = normed_mid * gain[1:2] + shift[1:2] + (mine[...].astype(F32) + other[...].astype(F32)) + bias[...]
        normed, inverse = norm_stats(last)
        first_row = at[0] * half
        live = (first_row + lax.broadcasted_iota(jnp.int32, (half, 1), 0) < at[3]).astype(F32)
        mixed[...] = ((normed * gain[2:3] + shift[2:3]) * live).astype(BF)
        delta = cot[...].astype(F32) * live
        dlast = norm_backward(delta, normed, inverse, gain[2:3])
        dlast_out[...] = dlast
        low[...] = dlast.astype(BF)
        sums[...] = stacked_sums(delta * normed, delta, dlast)

    ins = [
        near(total),
        near(mine),
        near(other),
        near(cot, lambda ref, at: ref.at[rows_at(at[0], half), :]),
        near(bias),
        near(gain),
        near(shift),
    ]
    outs = [shape(half, width, dtype=BF), shape(half, width), shape(half, width, dtype=BF), shape(8, width)]
    return launch(body, "third_norm", at, ins, outs, us=2.5)


def feed_down(at, mine, other, f1, f2, slope):
    half, width = mine.shape
    units = f1.shape[1]

    def body(at, ins, outs, _):
        mine, other, f1, f2, slope = ins
        keep, send, dpre, sums = outs
        total = jnp.zeros((1, units), F32)
        for r, (x, target) in enumerate(((other, send), (mine, keep))):
            span = slice((1 - r) * half, (2 - r) * half)
            grad = mm(x[...], f2[...], NT) * slope[span, :]
            total = total + column_sum(grad)
            low = grad.astype(BF)
            dpre[span, :] = low
            target[...] = mm(low, f1[...], NT).astype(target.dtype)
        sums[...] = total

    ins = [near(a) for a in (mine, other, f1, f2, slope)]
    outs = [
        shape(half, width),
        shape(half, width, dtype=BF),
        shape(2 * half, units, dtype=BF),
        shape(1, units),
    ]
    return launch(body, "feed_down", at, ins, outs, us=3)


def second_back(at, dlast, mine, other, total, gain):
    half, width = mine.shape

    def body(at, ins, outs, _):
        dlast, mine, other, total, gain = ins
        dsecond, low, sums = outs
        dmid = dlast[...] + (mine[...].astype(F32) + other[...].astype(F32))
        normed, inverse = norm_stats(total[...])
        result = norm_backward(dmid, normed, inverse, gain[1:2])
        dsecond[...] = result
        low[...] = result.astype(BF)
        sums[...] = stacked_sums(dmid * normed, dmid, result)

    ins = [near(a) for a in (dlast, mine, other, total, gain)]
    outs = [shape(half, width), shape(half, width, dtype=BF), shape(8, width)]
    return launch(body, "second_back", at, ins, outs, us=1.8)


def gelu_pair(pre):
    phi = 0.5 * (1.0 + erf(pre * 0.7071067811865476))
    return (pre * phi).astype(BF), phi + pre * (jnp.exp(pre * pre * -0.5) * 0.3989422804014327)


def cross_backward(at, z_mine, z_other, raised, inverse, query, keys, values, w, wo, nh):
    half, width = z_mine.shape
    rows = 2 * half
    local = w.shape[1]
    hd = local // nh
    slots = keys.shape[1]
    scale = hd**-0.5

    def body(at, ins, outs, scratch):
        z_halves, (wo, inverse, values, raised, query, keys, w) = ins[:2], ins[2:]
        keep, send, dquery, dkv, sums = outs
        douts, right, found = scratch
        zero = jnp.zeros((half, hd), BF)
        head_sum = jnp.zeros((1, local), F32)
        for r in range(2):
            span = slice(r * half, (r + 1) * half)
            dhead = mm(z_halves[r][...], wo[...], NT)
            head_sum = head_sum + column_sum(dhead)
            scaled = query[span, :] * jnp.asarray(scale, BF)
            for h in range(nh):
                part = slice(h * hd, (h + 1) * hd)
                dout = (dhead[:, part] * inverse[h, span, 0:1]).astype(BF)
                douts[h, span, :] = jnp.concatenate([dout, dout], axis=1)
                right[h, 0, span, :] = jnp.concatenate([scaled[:, part], zero], axis=1)
                right[h, 1, span, :] = jnp.concatenate([zero, dout], axis=1)

        def one_head(h, _):
            grad = None
            for r in range(2):
                span = slice(r * half, (r + 1) * half)
                dprob = mm(douts[h, span, :], values[h], NT)
                low = raised[h, span, :]
                e = low.astype(F32)
                weighed = e * dprob
                mean = jnp.sum(weighed, axis=1, keepdims=True) * inverse[h, span, 0:1]
                dscore = (weighed - e * mean).astype(BF)
                both = mm(dscore, keys[h])
                found[h, span, :] = both[:, :hd] + both[:, hd:]
                part = mm(right[h, 0, span, :], dscore, TN) + mm(right[h, 1, span, :], low, TN)
                grad = part if grad is None else grad + part
            dkv[h] = grad.astype(BF).T
            return 0

        lax.fori_loop(0, nh, one_head, 0)
        query_sum = jnp.zeros((1, local), F32)
        for r, target in enumerate((keep, send)):
            span = slice(r * half, (r + 1) * half)
            dq = jnp.concatenate([found[h, span, :] for h in range(nh)], axis=1) * scale
            query_sum = query_sum + column_sum(dq)
            dq_low = dq.astype(BF)
            dquery[span, :] = dq_low
            target[...] = mm(dq_low, w[0]).astype(target.dtype)
        sums[...] = jnp.concatenate([query_sum, head_sum], axis=0)

    return launch(
        body,
        "cross_bwd",
        at,
        [near(a) for a in (z_mine, z_other, wo, inverse, values, raised, query, keys, w)],
        [
            shape(half, width),
            shape(half, width, dtype=BF),
            shape(rows, local, dtype=BF),
            shape(nh, slots, 2 * hd, dtype=BF),
            shape(2, local),
        ],
        scratch=[
            pltpu.VMEM((nh, rows, 2 * hd), BF),
            pltpu.VMEM((nh, 2, rows, 2 * hd), BF),
            pltpu.VMEM((nh, rows, hd), F32),
        ],
        mib=30,
        us=11,
    )


def store_gradient(at, dkv, w, nh):
    _, slots, twice = dkv.shape
    _, local, width = w.shape
    hd = twice // 2
    seg = slots // 4

    def body(at, ins, outs, _):
        dkv, w = ins
        keep, send = outs
        weights = []
        for h in range(nh):
            part = slice(h * hd, (h + 1) * hd)
            weights += [w[1][part], w[2][part]]
        weight = jnp.concatenate(weights, axis=0)
        for slot in (1, 3, 0, 2):
            rows = jnp.concatenate([dkv[h, slot * seg : (slot + 1) * seg, :] for h in range(nh)], axis=1)
            part = mm(rows, weight)
            if slot % 2 == 0:
                keep[slot // 2] = part
            else:
                send[slot // 2] = part.astype(BF)

    return launch(
        body,
        "store_grad",
        at,
        [near(dkv), near(w)],
        [shape(2, seg, width), shape(2, seg, width, dtype=BF)],
        us=2.6,
    )


def group_outs(width, columns, blocks, tail=0):
    if not blocks:
        return [shape(width, columns)]
    n, r = blocks
    return [shape(n * r + tail, columns, dtype=BF), shape(n, r, columns)]


def emit_group(at, grad, outs, blocks, first, columns, kept_first=None):
    if not blocks:
        outs[0][:, first : first + columns] = grad[...]
        return
    n, r = blocks
    kept_first = first if kept_first is None else kept_first
    span, kept = slice(first, first + columns), slice(kept_first, kept_first + columns)
    for b in range(n):
        theirs = pl.ds(pl.multiple_of((2 * b + 1 - at[4]) * r, 8), r)
        outs[0][b * r : (b + 1) * r, span] = grad[theirs, :].astype(BF)
        outs[1][b, :, kept] = grad[pl.ds(pl.multiple_of((2 * b + at[4]) * r, 8), r), :]


def turned_product(out, left, right, step=256):
    if left.shape[1] % step:
        out[...] = mm(left[...], right[...], TN)
        return

    def some(i, _):
        span = pl.ds(pl.multiple_of(i * step, step), step)
        out[span, :] = mm(left[:, span], right[...], TN)
        return 0

    lax.fori_loop(0, left.shape[1] // step, some, 0)


def feed_grads(at, mid_mine, mid_other, dpre, dlast_mine, dlast_other, hidden, blocks):
    half, width = mid_mine.shape
    units = dpre.shape[1]
    if blocks:
        n, r = blocks
        structs = [shape(n * r, 2 * units, dtype=BF), shape(n, r, 2 * units)]
    else:
        structs = [shape(width, units), shape(width, units)]

    def body(at, ins, outs, scratch):
        mid_mine, mid_other, dpre, dlast_mine, dlast_other, hidden = ins
        left, grad = scratch
        for i, (mine, other, right) in enumerate(((mid_mine, mid_other, dpre), (dlast_mine, dlast_other, hidden))):
            left[:half, :] = mine[...]
            left[half:, :] = other[...]
            turned_product(grad, left, right)
            emit_group(at, grad, outs if blocks else outs[i:], blocks, i * units if blocks else 0, units)

    return launch(
        body,
        "feed_grads",
        at,
        [near(a) for a in (mid_mine, mid_other, dpre, dlast_mine, dlast_other, hidden)],
        structs,
        scratch=[pltpu.VMEM((2 * half, width), BF), pltpu.VMEM((width, units), F32)],
        us=4,
    )


def cross_grads(at, z_mine, z_other, mine, other, dquery, heads, shards, dkv, nh, blocks):
    half, width = mine.shape
    local = dquery.shape[1]
    hd = local // nh
    seg = shards[0].shape[0]

    def body(at, ins, outs, scratch):
        shards, (z_mine, z_other, mine, other, dquery, heads, dkv) = ins[0:4], ins[4:]
        (grad,) = scratch
        grad[...] = mm(mine[...], dquery[:half], TN) + mm(other[...], dquery[half:], TN)
        emit_group(at, grad, outs, blocks, 0, local)
        grad[...] = mm(z_mine[...], heads[:half], TN) + mm(z_other[...], heads[half:], TN)
        emit_group(at, grad, outs, blocks, 3 * local, local)
        both = None
        for slot, block in enumerate(shards):
            rows = jnp.concatenate([dkv[h, slot * seg : (slot + 1) * seg, :] for h in range(nh)], axis=1)
            part = mm(block[...], rows, TN)
            both = part if both is None else both + part
        for i in range(2):
            grad[...] = jnp.concatenate([both[:, (2 * h + i) * hd : (2 * h + i + 1) * hd] for h in range(nh)], axis=1)
            emit_group(at, grad, outs, blocks, (1 + i) * local, local)

    return launch(
        body,
        "cross_grads",
        at,
        [near(a) for a in (*shards, z_mine, z_other, mine, other, dquery, heads, dkv)],
        group_outs(width, 4 * local, blocks),
        scratch=[pltpu.VMEM((width, local), F32)],
        us=4,
    )


def first_back(at, dsecond, mine, other, total, gain):
    half, width = mine.shape

    def body(at, ins, outs, _):
        dsecond, mine, other, total, gain = ins
        dfirst, low, sums = outs
        value = dsecond[...] + (mine[...].astype(F32) + other[...].astype(F32))
        normed, inverse = norm_stats(total[...])
        result = norm_backward(value, normed, inverse, gain[0:1])
        dfirst[...] = result
        low[...] = result.astype(BF)
        sums[...] = stacked_sums(value * normed, value, result)

    ins = [near(a) for a in (dsecond, mine, other, total, gain)]
    outs = [shape(half, width), shape(half, width, dtype=BF), shape(8, width)]
    return launch(body, "first_back", at, ins, outs, us=1.8)


def self_backward(at, mine, other, tokens, w, wo, qkv, prob, flat, mixed, sums, nh, blocks):
    half, width = mine.shape
    rows = 2 * half
    local = wo.shape[0]
    hd = local // nh
    scale = hd**-0.5

    def body(at, ins, outs, scratch):
        mine, other, wo, qkv, prob, tok, w, mixed, flat = ins[:9]
        third_sums, second_sums, first_sums, third_other, second_other, first_other, fc1_sum, head_sums = ins[9:]
        send, keep = outs[0:2]
        group, extra = outs[2:-1], outs[-1]
        z, dqkv, grad = scratch
        own, distant = rows_at(at[0], half), rows_at(1 - at[0], half)
        z[own, :] = mine[...]
        z[distant, :] = other[...]
        dself = mm(z[...], wo[...], NT).astype(BF)
        v, k, q = qkv[2], qkv[1], qkv[0]
        dq, dk, dv = [], [], []
        for h in range(nh):
            part = slice(h * hd, (h + 1) * hd)
            weights_low = prob[h]
            weights = weights_low.astype(F32)
            weighed = weights * mm(dself[:, part], v[:, part], NT)
            dscore = (weighed - weights * jnp.sum(weighed, axis=1, keepdims=True)).astype(BF)
            dq.append(mm(dscore, k[:, part]))
            dk.append(mm(q[:, part], dscore, TN))
            dv.append(mm(dself[:, part], weights_low, TN))
        dquery = jnp.concatenate(dq, axis=1) * scale
        dvalue = jnp.concatenate(dv, axis=0).T
        dqkv[:, 0:local] = dquery.astype(BF)
        dqkv[:, local : 2 * local] = (jnp.concatenate(dk, axis=0) * scale).astype(BF).T
        dqkv[:, 2 * local :] = dvalue.astype(BF)
        x = tok[...]
        grad[:, 0 : 3 * local] = mm(x, dqkv[...], TN)
        grad[:, 3 * local :] = mm(z[...], flat[...], TN)
        emit_group(at, grad, group, blocks, 0, 4 * local)
        pad = jnp.zeros((1, width - 2 * local), F32)
        small = jnp.concatenate(
            [
                third_sums[0:3] + third_other[0:3],
                second_sums[0:3] + second_other[0:3],
                first_sums[0:3] + first_other[0:3],
                fc1_sum[...],
                jnp.concatenate([head_sums[0:1], head_sums[1:2], pad], axis=1),
                jnp.concatenate([column_sum(dquery), column_sum(dvalue), pad], axis=1),
                jnp.zeros((EXTRA - 12, width), F32),
            ],
            axis=0,
        )
        extra[...] = small
        if blocks:
            group[0][blocks[0] * blocks[1] :, :] = two_terms(small)
        send[half:, :] = mixed[...]
        for place, out in ((distant, send), (own, keep)):
            rows_now = dqkv[place, :]
            total = sum(mm(rows_now[:, i * local : (i + 1) * local], w[i]) for i in range(3))
            out[0:half, :] = total.astype(out.dtype)

    return launch(
        body,
        "self_bwd",
        at,
        [near(a) for a in (mine, other, wo, qkv, prob, tokens, w, mixed, flat, *sums)],
        [shape(2 * half, width, dtype=BF), shape(half, width)]
        + group_outs(width, 4 * local, blocks, 2 * EXTRA)
        + [shape(EXTRA, width)],
        scratch=[
            pltpu.VMEM((rows, width), BF),
            pltpu.VMEM((rows, 3 * local), BF),
            pltpu.VMEM((width, 4 * local), F32),
        ],
        mib=20,
        us=6,
    )


def fold_lines(value, columns):
    rows, width = value.shape
    times = columns // width
    each = rows // times
    return value if times == 1 else jnp.concatenate([value[i * each : (i + 1) * each] for i in range(times)], axis=1)


def unfold_lines(value, width):
    times = value.shape[1] // width
    return (
        value
        if times == 1
        else jnp.concatenate([value[:, i * width : (i + 1) * width] for i in range(times)], axis=0)
    )


def add_stage(at, keep, got, small, bit):
    n, rows, _ = keep[0].shape
    starts = [0]
    for part in keep:
        starts.append(starts[-1] + part.shape[2])
    columns = starts[-1]
    tail = 0 if small is None else 2 * small.shape[0] * small.shape[1] // columns

    def body(at, ins, outs, _):
        keeps, gots = ins[: len(keep)], ins[len(keep) : len(keep) + len(got)]
        mine = at[bit]
        send, stay = outs[:2]
        for b in range(n // 2):
            for chosen, out in ((1 - mine, send), (mine, stay)):
                block = 2 * b + chosen
                for i, part in enumerate(keeps):
                    span = slice(starts[i], starts[i + 1])
                    source, first = (gots[i], 0) if len(got) == len(keep) else (gots[0], starts[i])
                    arrived = source[
                        pl.ds(pl.multiple_of(block * rows, 8), rows), first : first + starts[i + 1] - starts[i]
                    ]
                    value = part[block] + arrived.astype(F32)
                    if out is send:
                        send[b * rows : (b + 1) * rows, span] = value.astype(BF)
                    else:
                        stay[b, :, span] = value
        if tail:
            total = ins[-1][...] + unfold_lines(from_terms(gots[-1][n * rows :, :]), small.shape[1])
            outs[2][...] = total
            send[n // 2 * rows :, :] = two_terms(fold_lines(total, columns))

    ins = [near(part) for part in (*keep, *got)] + ([near(small)] if tail else [])
    outs = [shape(n // 2 * rows + tail, columns, dtype=BF), shape(n // 2, rows, columns)]
    if tail:
        outs.append(shape(*small.shape))
    return launch(body, "add_stage", at, ins, outs, us=1)


def last_stage(at, keep, got, small, parts):
    _, rows, columns = keep.shape
    each = columns // sum(count for count, _ in parts)
    reach = 0 if small is None else small.shape[1]

    def body(at, ins, outs, _):
        total = ins[0][0] + ins[1][0:rows].astype(F32)
        first = 0
        for out, (count, turned) in zip(outs, parts):
            if count == 1:
                value = total[:, first * each : (first + 1) * each]
                out[...] = value.T if turned else value
            else:
                for i in range(count):
                    out[i] = total[:, (first + i) * each : (first + i + 1) * each]
            first += count
        if reach:
            value = ins[2][...] + unfold_lines(from_terms(ins[1][rows:, :]), reach)
            outs[-1][...] = value
            gains, shifts, cross_line, self_line = outs[-5:-1]
            gains[...] = jnp.concatenate([value[6:7], value[3:4], value[0:1]], axis=0)
            shifts[...] = jnp.concatenate([value[7:8], value[4:5], value[1:2]], axis=0)
            half = cross_line.shape[1]
            for line, row in ((cross_line, value[10:11]), (self_line, value[11:12])):
                line[...] = jnp.concatenate([row[:, :half], row[:, half : 2 * half]], axis=0)

    outs = []
    for count, turned in parts:
        dims = (rows, each) if count == 1 else (count, rows, each)
        outs.append(shape(*(dims[::-1] if turned else dims)))
    ins = [near(keep), near(got)]
    if reach:
        ins.append(near(small))
        outs += [shape(3, reach), shape(3, reach), shape(2, reach // 4), shape(2, reach // 4), shape(small.shape[0], reach)]
    return launch(body, "last_stage", at, ins, outs, us=1)


def join_halves(at, mine, other):
    half, width = mine.shape
    skip = other.shape[0] - half

    def body(at, ins, outs, _):
        outs[0][rows_at(at[0], half), :] = ins[0][...]
        outs[0][rows_at(1 - at[0], half), :] = ins[1][...]

    out = shape(2 * half, width, dtype=mine.dtype)
    ins = [near(mine), near(other, lambda ref, at: ref.at[pl.ds(skip, half), :])]
    return launch(body, "join_halves", at, ins, [out])[0]


def flip(bit, size):
    return [(i, i ^ bit) for i in range(size)]


def butterfly(value, axis, size):
    bit = 1
    while bit < size:
        value = value + lax.ppermute(value, axis, flip(bit, size))
        bit *= 2
    return value


def on_device(
    tokens,
    store,
    summary_length,
    top_index,
    cotangent,
    self_qkv_weight,
    self_qv_bias,
    self_out_weight,
    self_out_bias,
    qkv_weight,
    qv_bias,
    out_weight,
    out_bias,
    fc1_weight,
    fc1_bias,
    fc2_weight,
    fc2_bias,
    norm_gain,
    norm_shift,
):
    rows, width = tokens.shape
    half = rows // 2
    nh = top_index.shape[1]
    local = qkv_weight.shape[2]
    units = fc1_weight.shape[1]
    seg = store.shape[1]
    wide = lax.axis_size("wide")
    place = lax.axis_index("narrow")
    doc = lax.axis_index("wide")
    core, across = place % 2, place // 2
    at = jnp.stack([core, across, place, summary_length[0], doc % 2, doc // 2 % 2, doc // 4]).astype(jnp.int32)
    blocks = (wide // 2, width // wide) if wide == 8 else None
    row = lambda v: v.reshape(1, -1)
    self_w = jnp.swapaxes(self_qkv_weight, 1, 2)
    cross_w = jnp.swapaxes(qkv_weight, 1, 2)

    def to_core(v):
        return lax.ppermute(v, "narrow", CORE)

    def to_across(v):
        return lax.ppermute(v, "narrow", ACROSS)

    def over(v, bit):
        return lax.ppermute(v, "wide", flip(bit, wide))

    def chip_sum(keep, send):
        return (keep + to_core(send).astype(F32)).astype(BF)

    store_x = to_across(store[0])
    qkv, prob, flat, send, keep = self_forward(at, tokens, self_w, self_qv_bias, self_out_weight, nh)
    mine = chip_sum(keep, send)
    other = to_across(mine)
    index = index_rows(top_index)
    bias_mine = make_mask(tie(at, mine), index, top_index.shape, seg, 128, 0)
    store_x, store_own = tie((store_x, store[0]), bias_mine)
    shards = [store_own, to_core(store_own), store_x, to_core(store_x)]
    bias_other = make_mask(tie(at, bias_mine), index, top_index.shape, seg, 128, 1)
    other = tie(other, bias_other)
    first_total, after, after_low = first_norm(at, mine, other, tokens, row(self_out_bias), norm_gain, norm_shift)
    after_other = to_core(after_low)

    keys, values = keys_values(tie(at, after_low), shards, cross_w, nh)
    keep, send, raised, inverse, query, heads = cross_forward(
        tie(at, keys), after_low, after_other, bias_mine, bias_other, keys, values, cross_w, qv_bias, out_weight, nh
    )
    mine = chip_sum(keep, send)
    second_total, mid_low = second_norm(at, after, mine, to_across(mine), row(out_bias), norm_gain, norm_shift)
    mid_other = to_core(mid_low)

    keep, send, hidden, slope = feed_up(at, mid_low, mid_other, fc1_weight, fc2_weight, row(fc1_bias))
    mine = chip_sum(keep, send)
    mixed_half, dlast, dlast_low, third_sums = third_norm(
        at, second_total, mine, to_across(mine), cotangent, row(fc2_bias), norm_gain, norm_shift
    )
    dlast_other, third_other = to_core(dlast_low), to_core(third_sums)
    keep, send, dpre, fc1_sum = feed_down(at, dlast_low, dlast_other, fc1_weight, fc2_weight, slope)
    mine = chip_sum(keep, send)
    other = to_across(mine)
    feed_out = feed_grads(tie(at, mine), mid_low, mid_other, dpre, dlast_low, dlast_other, hidden, blocks)
    other = tie(other, feed_out[0])
    dsecond, z, second_sums = second_back(at, dlast, mine, other, second_total, norm_gain)
    z_other, second_other = to_core(z), to_core(second_sums)

    keep, send, dquery, dkv, cross_sums = cross_backward(
        at, z, z_other, raised, inverse, query, keys, values, cross_w, out_weight, nh
    )
    mine = chip_sum(keep, send)
    other = to_across(mine)
    cross_out = cross_grads(
        tie(at, mine), z, z_other, after_low, after_other, dquery, heads, shards, dkv, nh, blocks
    )
    started = cross_out[0]
    if blocks:
        feed_send, feed_keep = add_stage(tie(at, started), [feed_out[1]], [over(feed_out[0], 1)], None, 5)
        feed_next = over(feed_send, 2)
        started = feed_send
    store_keep, store_send = store_gradient(tie(at, started), dkv, cross_w, nh)
    other = tie(other, store_send)
    dfirst, dfirst_low, first_sums = first_back(at, dsecond, mine, other, first_total, norm_gain)
    dfirst_other, first_other = to_core(dfirst_low), to_core(first_sums)
    store_close = to_core(tie(store_send, dfirst_other))
    started = dfirst_low

    send, keep, *self_out, small = self_backward(
        tie(at, dfirst_other, store_close),
        dfirst_low,
        dfirst_other,
        tokens,
        self_w,
        self_out_weight,
        qkv,
        prob,
        flat,
        mixed_half,
        (third_sums, second_sums, first_sums, third_other, second_other, first_other, fc1_sum, cross_sums),
        nh,
        blocks,
    )
    if blocks:
        cross_got = tie(over(cross_out[0], 1), small)
        feed_send, feed_keep = add_stage(tie(at, cross_got), [feed_keep], [feed_next], None, 6)
        feed_next = over(feed_send, 4)
        fc1_grad, fc2_grad = last_stage(tie(at, feed_send), feed_keep, feed_next, None, [(1, False), (1, False)])
        fc2_grad = fc2_grad.T
        both_send, both_keep, small = add_stage(
            tie(at, fc1_grad), [cross_out[1], self_out[1]], [cross_got, over(self_out[0], 1)], small, 5
        )
        both_next = over(both_send, 2)
        send = tie(send, both_send)
    close = to_core(send)
    mine = (keep + close[:half].astype(F32)).astype(BF)
    other = to_across(mine)
    if blocks:
        both_send, both_keep, small = add_stage(tie(at, mine), [both_keep], [both_next], small, 6)
        both_next = over(both_send, 4)
        other = tie(other, both_send)
    tokens_half = dfirst + (mine.astype(F32) + other.astype(F32))
    tokens_other = to_core(tokens_half)
    mixed = join_halves(tie(at, tokens_half), mixed_half, close)
    store_distant = to_across(tie((store_keep[1] + store_close[1].astype(F32)).astype(BF), mine))
    tokens_grad = join_halves(at, tokens_half, tie(tokens_other, mixed))
    store_distant = tie(store_distant, tokens_grad)
    store_grad = (store_keep[0] + store_close[0].astype(F32) + store_distant.astype(F32))[None]

    if blocks:
        qkv_grad, out_grad, self_qkv_grad, self_out_grad, *lines, small = last_stage(
            tie(at, store_grad), both_keep, both_next, small, [(3, False), (1, True), (3, False), (1, True)]
        )
    else:
        scatter = functools.partial(lax.psum_scatter, axis_name="wide", tiled=True)
        parts = lambda g: jnp.stack([g[:, i * local : (i + 1) * local] for i in range(3)])
        fc1_grad = scatter(feed_out[0], scatter_dimension=0)
        fc2_grad = scatter(feed_out[1].T, scatter_dimension=1)
        qkv_grad = scatter(parts(cross_out[0]), scatter_dimension=1)
        out_grad = scatter(cross_out[0][:, 3 * local :].T, scatter_dimension=1)
        self_qkv_grad = scatter(parts(self_out[0]), scatter_dimension=1)
        self_out_grad = scatter(self_out[0][:, 3 * local :].T, scatter_dimension=1)
        small = butterfly(small, "wide", wide)
        lines = (
            jnp.stack([small[6], small[3], small[0]]),
            jnp.stack([small[7], small[4], small[1]]),
            small[10, : 2 * local].reshape(2, local),
            small[11, : 2 * local].reshape(2, local),
        )
    gain_grad, shift_grad, qv_grad, self_qv_grad = lines
    return (
        mixed,
        tokens_grad,
        store_grad,
        self_qkv_grad,
        self_qv_grad,
        self_out_grad,
        small[8],
        qkv_grad,
        qv_grad,
        out_grad,
        small[5],
        fc1_grad,
        small[9],
        fc2_grad,
        small[2],
        gain_grad,
        shift_grad,
    )


def solution(mesh):
    placed = (
        P("wide", None),
        P("wide", "narrow", None),
        P("wide"),
        P("wide", "narrow", None, None),
        P("wide", None),
        P(None, None, "narrow"),
        P(None, "narrow"),
        P("narrow", None),
        P(),
        P(None, None, "narrow"),
        P(None, "narrow"),
        P("narrow", None),
        P(),
        P(None, "narrow"),
        P("narrow"),
        P("narrow", None),
        P(),
        P(),
        P(),
    )
    return jax.shard_map(
        on_device,
        mesh=mesh,
        in_specs=placed,
        out_specs=(
            P("wide", None),
            P("wide", None),
            P("wide", "narrow", None),
            P(None, "wide", "narrow"),
            P(None, "narrow"),
            P("narrow", "wide"),
            P(),
            P(None, "wide", "narrow"),
            P(None, "narrow"),
            P("narrow", "wide"),
            P(),
            P("wide", "narrow"),
            P("narrow"),
            P("narrow", "wide"),
            P(),
            P(),
            P(),
        ),
        check_vma=False,
    )
```

```python
import functools

import jax
import jax.numpy as jnp
from jax import lax
from jax.experimental import pallas as pl
from jax.experimental.pallas import tpu as pltpu
from jax.sharding import PartitionSpec as P

F32 = jnp.float32
BF = jnp.bfloat16
NN = (((1,), (0,)), ((), ()))
NT = (((1,), (1,)), ((), ()))
TN = (((0,), (0,)), ((), ()))
EPS = 1e-05
PACE = 1.1e8
SELF_MIB = 60
EXTRA = 16

CORE = [(i, i ^ 1) for i in range(4)]
ACROSS = [(i, i ^ 2) for i in range(4)]


def mm(left, right, dims=NN):
    return lax.dot_general(left, right, dims, preferred_element_type=F32)


def shape(*dims, dtype=F32):
    return jax.ShapeDtypeStruct(dims, dtype)


def tie(value, *earlier):
    return lax.optimization_barrier((value, *earlier))[0]


class Operand:
    def __init__(self, source, buffer, sems, first, parts):
        self.buffer = buffer
        self.parts = parts
        if parts:
            self.copies = [
                pltpu.make_async_copy(source.at[i], buffer.at[i], sems.at[first + i]) for i in range(buffer.shape[0])
            ]
        else:
            self.copies = [pltpu.make_async_copy(source, buffer, sems.at[first])]
        self.waited = [False] * len(self.copies)
        for copy in self.copies:
            copy.start()

    def ready(self, part=None):
        for i, copy in enumerate(self.copies):
            if not self.waited[i] and (part is None or i == part):
                copy.wait()
                self.waited[i] = True

    @property
    def shape(self):
        return self.buffer.shape

    def __getitem__(self, at):
        self.ready(at if self.parts and isinstance(at, int) else None)
        return self.buffer[at]


class Result:
    def __init__(self, target, buffer, sems, first, parts):
        self.buffer = buffer
        if parts:
            self.copies = [
                pltpu.make_async_copy(buffer.at[i], target.at[i], sems.at[first + i]) for i in range(buffer.shape[0])
            ]
        else:
            self.copies = [pltpu.make_async_copy(buffer, target, sems.at[first])]
        self.started = [False] * len(self.copies)

    @property
    def shape(self):
        return self.buffer.shape

    @property
    def dtype(self):
        return self.buffer.dtype

    def __setitem__(self, at, value):
        self.buffer[at] = value

    def flush(self, part=0):
        self.copies[part].start()
        self.started[part] = True

    def finish(self):
        for i in range(len(self.copies)):
            if not self.started[i]:
                self.flush(i)
        for copy in self.copies:
            copy.wait()


def far(array, take=None, dims=None, parts=False):
    return ("far", array, take, tuple(dims or array.shape), parts)


def near(array, take=None):
    return ("near", array, take, None, False)


def raw(array):
    return ("raw", array, None, None, False)


def launch(body, name, at, ins, outs, scratch=(), mib=16, us=2.0):
    in_specs = [pl.BlockSpec(memory_space=pltpu.SMEM)]
    buffers, n_in, n_out = [], 0, 0
    for kind, array, _, dims, parts in ins:
        in_specs.append(pl.BlockSpec(memory_space=pltpu.VMEM if kind == "near" else pltpu.HBM))
        if kind == "far":
            buffers.append(pltpu.VMEM(dims, array.dtype))
            n_in += dims[0] if parts else 1
    out_specs, structs = [], []
    for out in outs:
        if isinstance(out, tuple):
            struct, parts = out
            out_specs.append(pl.BlockSpec(memory_space=pltpu.HBM))
            buffers.append(pltpu.VMEM(struct.shape, struct.dtype))
            n_out += struct.shape[0] if parts else 1
        else:
            struct = out
            out_specs.append(pl.BlockSpec(memory_space=pltpu.VMEM))
        structs.append(struct)
    n_buffers = len(buffers)
    sems = [pltpu.SemaphoreType.DMA((max(n, 1),)) for n in (n_in, n_out)]

    def kernel(at_ref, *refs):
        in_refs, out_refs = refs[: len(ins)], refs[len(ins) : len(ins) + len(outs)]
        rest = refs[len(ins) + len(outs) :]
        bufs, user, (in_sems, out_sems) = list(rest[:n_buffers]), rest[n_buffers:-2], rest[-2:]
        place, given = 0, []
        for ref, (kind, _, take, dims, parts) in zip(in_refs, ins):
            source = take(ref, at_ref) if take else ref
            if kind == "far":
                given.append(Operand(source, bufs.pop(0), in_sems, place, parts))
                place += dims[0] if parts else 1
            else:
                given.append(source)
        place, results = 0, []
        for ref, out in zip(out_refs, outs):
            if isinstance(out, tuple):
                results.append(Result(ref, bufs.pop(0), out_sems, place, out[1]))
                place += out[0].shape[0] if out[1] else 1
            else:
                results.append(ref)
        body(at_ref, given, results, user)
        for operand in given:
            if isinstance(operand, Operand):
                operand.ready()
        for result in results:
            if isinstance(result, Result):
                result.finish()

    return pl.pallas_call(
        kernel,
        in_specs=in_specs,
        out_specs=out_specs,
        out_shape=structs,
        scratch_shapes=buffers + list(scratch) + sems,
        compiler_params=pltpu.CompilerParams(vmem_limit_bytes=mib << 20),
        cost_estimate=pl.CostEstimate(flops=int(us * PACE), bytes_accessed=1000, transcendentals=0),
        name=name,
    )(at, *[entry[1] for entry in ins])


def norm_stats(value):
    centre = value - jnp.mean(value, axis=-1, keepdims=True)
    spread = jnp.mean(centre * centre, axis=-1, keepdims=True)
    inverse = lax.rsqrt(spread + EPS)
    return centre * inverse, inverse


def norm_backward(grad, normed, inverse, gain):
    scaled = grad * gain
    centred = scaled - jnp.mean(scaled, axis=-1, keepdims=True)
    return inverse * (centred - normed * jnp.mean(scaled * normed, axis=-1, keepdims=True))


def column_sum(value):
    return jnp.sum(value, axis=0, keepdims=True)


def erf(value):
    x = jnp.clip(value, -4.0, 4.0)
    y = x * x
    top = jnp.full_like(y, -2.72614225801306e-10)
    for factor in (
        2.77068142495902e-08,
        -2.10102402082508e-06,
        -5.69250639462346e-05,
        -7.34990630326855e-04,
        -2.95459980854025e-03,
        -1.60960333262415e-02,
    ):
        top = top * y + factor
    low = jnp.full_like(y, -1.45660718464996e-05)
    for factor in (
        -2.13374055278905e-04,
        -1.68282697438203e-03,
        -7.37332916720468e-03,
        -1.42647390514189e-02,
    ):
        low = low * y + factor
    return x * top / low


def two_terms(value):
    high = value.astype(BF)
    return jnp.concatenate([high, (value - high.astype(F32)).astype(BF)], axis=0)


def from_terms(stacked):
    rows = stacked.shape[0] // 2
    terms = stacked.astype(F32)
    return terms[:rows] + terms[rows:]


def rows_at(place, rows):
    return pl.ds(pl.multiple_of(place * rows, rows), rows)


def self_forward(at, tokens, w, b, wo, nh):
    rows, width = tokens.shape
    local = w.shape[1]
    half = rows // 2
    hd = local // nh
    scale = hd**-0.5

    def body(at, ins, outs, _):
        tok, w, wo, b = ins
        qkv, prob, flat, send, keep = outs
        x = tok[...]
        q = (mm(x, w[0], NT) + b[0:1]).astype(BF)
        k = mm(x, w[1], NT).astype(BF)
        v = (mm(x, w[2], NT) + b[1:2]).astype(BF)
        for i, value in enumerate((q, k, v)):
            qkv[i] = value
            qkv.flush(i)
        row_ids = lax.broadcasted_iota(jnp.int32, (rows, rows), 0)
        key_ids = lax.broadcasted_iota(jnp.int32, (rows, rows), 1)
        allowed = (key_ids <= row_ids) & (key_ids < at[3])
        found = []
        for h in range(nh):
            part = slice(h * hd, (h + 1) * hd)
            scores = mm(q[:, part], k[:, part], NT) * scale
            scores = jnp.where(allowed, scores, -1e30)
            shifted = jnp.exp(scores - jnp.max(scores, axis=1, keepdims=True))
            weights = (shifted * (1.0 / jnp.sum(shifted, axis=1, keepdims=True))).astype(BF)
            prob[h] = weights
            prob.flush(h)
            found.append(mm(weights, v[:, part]).astype(BF))
        flat[...] = jnp.concatenate(found, axis=1)
        flat.flush()
        send[...] = mm(flat.buffer[rows_at(1 - at[0], half), :], wo[...]).astype(BF)
        send.flush()
        keep[...] = mm(flat.buffer[rows_at(at[0], half), :], wo[...])

    return launch(
        body,
        "self_fwd",
        at,
        [far(tokens), far(w, parts=True), far(wo), far(b)],
        [
            (shape(3, rows, local, dtype=BF), True),
            (shape(nh, rows, rows, dtype=BF), True),
            (shape(rows, local, dtype=BF), False),
            (shape(half, width, dtype=BF), False),
            (shape(half, width), False),
        ],
        mib=SELF_MIB,
        us=4,
    )


def first_norm(at, mine, other, tokens, bias, gain, shift):
    half, width = mine.shape

    def body(at, ins, outs, _):
        mine, other, tok, bias, gain, shift = ins
        total, after, low = outs
        value = tok[...].astype(F32) + (mine[...].astype(F32) + other[...].astype(F32)) + bias[...]
        total[...] = value
        normed, _ = norm_stats(value)
        result = normed * gain[0:1] + shift[0:1]
        after[...] = result
        low[...] = result.astype(BF)

    return launch(
        body,
        "first_norm",
        at,
        [
            near(mine),
            near(other),
            near(tokens, lambda ref, at: ref.at[rows_at(at[0], half), :]),
            near(bias),
            near(gain),
            near(shift),
        ],
        [shape(half, width), shape(half, width), shape(half, width, dtype=BF)],
        us=1.7,
    )


def index_rows(top_index):
    rows, nh, ns, keep = top_index.shape
    flat = top_index.reshape(rows, nh, ns, keep // 128, 128).transpose(0, 1, 3, 2, 4)
    return flat.reshape(rows * nh * ns * (keep // 128), 128)


def make_mask(at, flat, dims, seg, tile, turn):
    rows, nh, ns, keep = dims
    halves = keep // 128
    per_row = nh * ns * halves
    tiles = rows // 2 // tile
    columns = ns * seg
    blocks = columns // 128
    group = 32

    def body(at, ins, outs, _):
        (index,) = ins
        (bias,) = outs
        lane = lax.broadcasted_iota(jnp.int32, (group, 128), 1).astype(F32)
        lane_low = lane.astype(BF)
        empty = jnp.full((group, 128), -1.0, BF)
        own = at[2]
        steps = []
        step = 1
        while step <= seg - keep:
            steps.insert(0, step)
            step *= 2
        turns = steps + [(seg * s) % 128 for s in range(ns)]
        below = {s: lane_low < jnp.asarray(s, BF) for s in turns if 0 < s < 128}

        for t in range(tiles):
            index.ready(t)
            source = index.buffer.at[t]

            def one_group(g, _):
                for h in range(nh):
                    v = [empty] * blocks
                    for slot in range(ns):
                        first, turn = divmod(seg * slot, 128)
                        for c in range(halves):
                            start = g * (group * per_row) + h * ns * halves + c * ns + (own ^ slot)
                            found = jnp.concatenate(
                                [source[pl.ds(start + q * 8 * per_row, 8, stride=per_row), :] for q in range(group // 8)],
                                axis=0,
                            )
                            ahead = (found.astype(F32) - (lane + float(128 * c))).astype(BF)
                            at_block = first + c
                            if turn == 0:
                                v[at_block] = ahead
                            else:
                                turned = pltpu.roll(ahead, turn, axis=1)
                                v[at_block] = jnp.where(below[turn], v[at_block], turned)
                                v[at_block + 1] = jnp.where(below[turn], turned, v[at_block + 1])
                    for s in steps:
                        gap = jnp.asarray(s, BF)
                        moved = [x - gap for x in v]
                        stay = [jnp.where(x >= gap, empty, x) for x in v]
                        if s % 128 == 0:
                            hop = s // 128
                            v = stay[:hop] + [jnp.maximum(stay[i], moved[i - hop]) for i in range(hop, blocks)]
                        else:
                            turned = [pltpu.roll(x, s, axis=1) for x in moved]
                            v = [
                                jnp.maximum(stay[i], jnp.where(below[s], turned[i - 1], turned[i])) for i in range(blocks)
                            ]
                    for i in range(blocks):
                        bias[h, pl.ds(pl.multiple_of(t * tile + g * group, group), group), i * 128 : (i + 1) * 128] = v[
                            i
                        ] * jnp.asarray(1e30, BF)
                return 0

            lax.fori_loop(0, tile // group, one_group, 0)

    flat = flat.reshape(2 * tiles, tile * per_row, 128)
    return launch(
        body,
        "mask",
        at,
        [
            far(
                flat,
                lambda ref, at: ref.at[pl.ds((at[0] ^ turn) * tiles, tiles)],
                (tiles, tile * per_row, 128),
                parts=True,
            )
        ],
        [shape(nh, rows // 2, columns, dtype=BF)],
        us=10,
    )[0]


def keys_values(at, shards, w, nh):
    seg, width = shards[0].shape
    local = w.shape[1]
    hd = local // nh

    def body(at, ins, outs, _):
        for slot in range(4):
            x = ins[slot][...]
            span = slice(slot * seg, (slot + 1) * seg)
            for i, out in enumerate(outs):
                full = mm(x, ins[4][i + 1], NT)
                high = full.astype(BF)
                low = (full - high.astype(F32)).astype(BF)
                for h in range(nh):
                    part = slice(h * hd, (h + 1) * hd)
                    out[h, span, :] = jnp.concatenate([high[:, part], low[:, part]], axis=1)

    out = shape(nh, 4 * seg, 2 * hd, dtype=BF)
    return launch(body, "keys_values", at, [near(s) for s in shards] + [near(w)], [out, out], us=2)


def cross_forward(at, mine, other, bias_mine, bias_other, keys, values, w, b, wo, nh):
    half, width = mine.shape
    rows = 2 * half
    local = w.shape[1]
    hd = local // nh
    slots = keys.shape[1]
    scale = hd**-0.5

    def body(at, ins, outs, scratch):
        mine, other, wq, keys, bias_mine, bias_other, values, wo, b = ins
        keep, send, raised, inverse, query, heads = outs
        twice, found = scratch
        for r, x in enumerate((mine, other)):
            q = (mm(x[...], wq[0], NT) + b[0:1]).astype(BF)
            query[r * half : (r + 1) * half, :] = q
            scaled = q * jnp.asarray(scale, BF)
            for h in range(nh):
                part = scaled[:, h * hd : (h + 1) * hd]
                twice[h, r * half : (r + 1) * half, :] = jnp.concatenate([part, part], axis=1)

        def one_head(h, _):
            for r, bias in enumerate((bias_mine, bias_other)):
                span = slice(r * half, (r + 1) * half)
                scores = mm(twice[h, span, :], keys[h], NT) + bias[h].astype(F32)
                e = jnp.exp(scores - jnp.max(scores, axis=1, keepdims=True))
                total = 1.0 / jnp.sum(e, axis=1, keepdims=True)
                low = e.astype(BF)
                raised[h, span, :] = low
                inverse[h, span, :] = jnp.broadcast_to(total, (half, 128))
                both = mm(low, values[h])
                found[h, span, :] = (both[:, :hd] + both[:, hd:]) * total
            return 0

        lax.fori_loop(0, nh, one_head, 0)
        for r, target in enumerate((keep, send)):
            span = slice(r * half, (r + 1) * half)
            out = (jnp.concatenate([found[h, span, :] for h in range(nh)], axis=1) + b[1:2]).astype(BF)
            heads[span, :] = out
            target[...] = mm(out, wo[...]).astype(target.dtype)

    return launch(
        body,
        "cross_fwd",
        at,
        [near(a) for a in (mine, other, w, keys, bias_mine, bias_other, values, wo, b)],
        [
            shape(half, width),
            shape(half, width, dtype=BF),
            shape(nh, rows, slots, dtype=BF),
            shape(nh, rows, 128),
            shape(rows, local, dtype=BF),
            shape(rows, local, dtype=BF),
        ],
        scratch=[pltpu.VMEM((nh, rows, 2 * hd), BF), pltpu.VMEM((nh, rows, hd), F32)],
        mib=30,
        us=9,
    )


def stacked_sums(*values):
    sums = [column_sum(value) for value in values]
    return jnp.concatenate(sums + [jnp.zeros((8 - len(sums), values[0].shape[1]), F32)], axis=0)


def second_norm(at, after, mine, other, bias, gain, shift):
    half, width = mine.shape

    def body(at, ins, outs, _):
        after, mine, other, bias, gain, shift = ins
        total, low = outs
        value = after[...] + (mine[...].astype(F32) + other[...].astype(F32)) + bias[...]
        total[...] = value
        normed, _ = norm_stats(value)
        low[...] = (normed * gain[1:2] + shift[1:2]).astype(BF)

    ins = [near(a) for a in (after, mine, other, bias, gain, shift)]
    return launch(body, "second_norm", at, ins, [shape(half, width), shape(half, width, dtype=BF)], us=1.5)


def feed_up(at, mine, other, f1, f2, b1):
    half, width = mine.shape
    units = f1.shape[1]

    def body(at, ins, outs, _):
        mine, other, f1, f2, b1 = ins
        keep, send, hidden, slope = outs
        for r, (x, target) in enumerate(((other, send), (mine, keep))):
            span = slice((1 - r) * half, (2 - r) * half)
            low, steep = gelu_pair(mm(x[...], f1[...]) + b1[...])
            hidden[span, :] = low
            slope[span, :] = steep
            target[...] = mm(low, f2[...]).astype(target.dtype)

    ins = [near(a) for a in (mine, other, f1, f2, b1)]
    outs = [
        shape(half, width),
        shape(half, width, dtype=BF),
        shape(2 * half, units, dtype=BF),
        shape(2 * half, units),
    ]
    return launch(body, "feed_up", at, ins, outs, us=4)


def third_norm(at, total, mine, other, cot, bias, gain, shift):
    half, width = mine.shape

    def body(at, ins, outs, _):
        total, mine, other, cot, bias, gain, shift = ins
        mixed, dlast_out, low, sums = outs
        normed_mid, _ = norm_stats(total[...])
        last = normed_mid * gain[1:2] + shift[1:2] + (mine[...].astype(F32) + other[...].astype(F32)) + bias[...]
        normed, inverse = norm_stats(last)
        first_row = at[0] * half
        live = (first_row + lax.broadcasted_iota(jnp.int32, (half, 1), 0) < at[3]).astype(F32)
        mixed[...] = ((normed * gain[2:3] + shift[2:3]) * live).astype(BF)
        delta = cot[...].astype(F32) * live
        dlast = norm_backward(delta, normed, inverse, gain[2:3])
        dlast_out[...] = dlast
        low[...] = dlast.astype(BF)
        sums[...] = stacked_sums(delta * normed, delta, dlast)

    ins = [
        near(total),
        near(mine),
        near(other),
        near(cot, lambda ref, at: ref.at[rows_at(at[0], half), :]),
        near(bias),
        near(gain),
        near(shift),
    ]
    outs = [shape(half, width, dtype=BF), shape(half, width), shape(half, width, dtype=BF), shape(8, width)]
    return launch(body, "third_norm", at, ins, outs, us=2.5)


def feed_down(at, mine, other, f1, f2, slope):
    half, width = mine.shape
    units = f1.shape[1]

    def body(at, ins, outs, _):
        mine, other, f1, f2, slope = ins
        keep, send, dpre, sums = outs
        total = jnp.zeros((1, units), F32)
        for r, (x, target) in enumerate(((other, send), (mine, keep))):
            span = slice((1 - r) * half, (2 - r) * half)
            grad = mm(x[...], f2[...], NT) * slope[span, :]
            total = total + column_sum(grad)
            low = grad.astype(BF)
            dpre[span, :] = low
            target[...] = mm(low, f1[...], NT).astype(target.dtype)
        sums[...] = total

    ins = [near(a) for a in (mine, other, f1, f2, slope)]
    outs = [
        shape(half, width),
        shape(half, width, dtype=BF),
        shape(2 * half, units, dtype=BF),
        shape(1, units),
    ]
    return launch(body, "feed_down", at, ins, outs, us=3)


def second_back(at, dlast, mine, other, total, gain):
    half, width = mine.shape

    def body(at, ins, outs, _):
        dlast, mine, other, total, gain = ins
        dsecond, low, sums = outs
        dmid = dlast[...] + (mine[...].astype(F32) + other[...].astype(F32))
        normed, inverse = norm_stats(total[...])
        result = norm_backward(dmid, normed, inverse, gain[1:2])
        dsecond[...] = result
        low[...] = result.astype(BF)
        sums[...] = stacked_sums(dmid * normed, dmid, result)

    ins = [near(a) for a in (dlast, mine, other, total, gain)]
    outs = [shape(half, width), shape(half, width, dtype=BF), shape(8, width)]
    return launch(body, "second_back", at, ins, outs, us=1.8)


def gelu_pair(pre):
    phi = 0.5 * (1.0 + erf(pre * 0.7071067811865476))
    return (pre * phi).astype(BF), phi + pre * (jnp.exp(pre * pre * -0.5) * 0.3989422804014327)


def cross_backward(at, z_mine, z_other, raised, inverse, query, keys, values, w, wo, nh):
    half, width = z_mine.shape
    rows = 2 * half
    local = w.shape[1]
    hd = local // nh
    slots = keys.shape[1]
    scale = hd**-0.5

    def body(at, ins, outs, scratch):
        z_halves, (wo, inverse, values, raised, query, keys, w) = ins[:2], ins[2:]
        keep, send, dquery, dkv, sums = outs
        douts, right, found = scratch
        zero = jnp.zeros((half, hd), BF)
        head_sum = jnp.zeros((1, local), F32)
        for r in range(2):
            span = slice(r * half, (r + 1) * half)
            dhead = mm(z_halves[r][...], wo[...], NT)
            head_sum = head_sum + column_sum(dhead)
            scaled = query[span, :] * jnp.asarray(scale, BF)
            for h in range(nh):
                part = slice(h * hd, (h + 1) * hd)
                dout = (dhead[:, part] * inverse[h, span, 0:1]).astype(BF)
                douts[h, span, :] = jnp.concatenate([dout, dout], axis=1)
                right[h, 0, span, :] = jnp.concatenate([scaled[:, part], zero], axis=1)
                right[h, 1, span, :] = jnp.concatenate([zero, dout], axis=1)

        def one_head(h, _):
            grad = None
            for r in range(2):
                span = slice(r * half, (r + 1) * half)
                dprob = mm(douts[h, span, :], values[h], NT)
                low = raised[h, span, :]
                e = low.astype(F32)
                weighed = e * dprob
                mean = jnp.sum(weighed, axis=1, keepdims=True) * inverse[h, span, 0:1]
                dscore = (weighed - e * mean).astype(BF)
                both = mm(dscore, keys[h])
                found[h, span, :] = both[:, :hd] + both[:, hd:]
                part = mm(right[h, 0, span, :], dscore, TN) + mm(right[h, 1, span, :], low, TN)
                grad = part if grad is None else grad + part
            dkv[h] = grad.astype(BF).T
            return 0

        lax.fori_loop(0, nh, one_head, 0)
        query_sum = jnp.zeros((1, local), F32)
        for r, target in enumerate((keep, send)):
            span = slice(r * half, (r + 1) * half)
            dq = jnp.concatenate([found[h, span, :] for h in range(nh)], axis=1) * scale
            query_sum = query_sum + column_sum(dq)
            dq_low = dq.astype(BF)
            dquery[span, :] = dq_low
            target[...] = mm(dq_low, w[0]).astype(target.dtype)
        sums[...] = jnp.concatenate([query_sum, head_sum], axis=0)

    return launch(
        body,
        "cross_bwd",
        at,
        [near(a) for a in (z_mine, z_other, wo, inverse, values, raised, query, keys, w)],
        [
            shape(half, width),
            shape(half, width, dtype=BF),
            shape(rows, local, dtype=BF),
            shape(nh, slots, 2 * hd, dtype=BF),
            shape(2, local),
        ],
        scratch=[
            pltpu.VMEM((nh, rows, 2 * hd), BF),
            pltpu.VMEM((nh, 2, rows, 2 * hd), BF),
            pltpu.VMEM((nh, rows, hd), F32),
        ],
        mib=30,
        us=11,
    )


def group_outs(width, columns, blocks, tail=0):
    if not blocks:
        return [shape(width, columns)]
    n, r = blocks
    return [shape(n * r + tail, columns, dtype=BF), shape(n, r, columns)]


def emit_group(at, grad, outs, blocks, first, columns, kept_first=None):
    if not blocks:
        outs[0][:, first : first + columns] = grad[...]
        return
    n, r = blocks
    kept_first = first if kept_first is None else kept_first
    span, kept = slice(first, first + columns), slice(kept_first, kept_first + columns)
    for b in range(n):
        theirs = pl.ds(pl.multiple_of((2 * b + 1 - at[4]) * r, 8), r)
        outs[0][b * r : (b + 1) * r, span] = grad[theirs, :].astype(BF)
        outs[1][b, :, kept] = grad[pl.ds(pl.multiple_of((2 * b + at[4]) * r, 8), r), :]


def turned_product(out, left, right, step=256):
    if left.shape[1] % step:
        out[...] = mm(left[...], right[...], TN)
        return

    def some(i, _):
        span = pl.ds(pl.multiple_of(i * step, step), step)
        out[span, :] = mm(left[:, span], right[...], TN)
        return 0

    lax.fori_loop(0, left.shape[1] // step, some, 0)


def feed_grads(at, mid_mine, mid_other, dpre, dlast_mine, dlast_other, hidden, blocks):
    half, width = mid_mine.shape
    units = dpre.shape[1]
    if blocks:
        n, r = blocks
        structs = [shape(n * r, 2 * units, dtype=BF), shape(n, r, 2 * units)]
    else:
        structs = [shape(width, units), shape(width, units)]

    def body(at, ins, outs, scratch):
        mid_mine, mid_other, dpre, dlast_mine, dlast_other, hidden = ins
        left, grad = scratch
        for i, (mine, other, right) in enumerate(((mid_mine, mid_other, dpre), (dlast_mine, dlast_other, hidden))):
            left[:half, :] = mine[...]
            left[half:, :] = other[...]
            turned_product(grad, left, right)
            emit_group(at, grad, outs if blocks else outs[i:], blocks, i * units if blocks else 0, units)

    return launch(
        body,
        "feed_grads",
        at,
        [near(a) for a in (mid_mine, mid_other, dpre, dlast_mine, dlast_other, hidden)],
        structs,
        scratch=[pltpu.VMEM((2 * half, width), BF), pltpu.VMEM((width, units), F32)],
        us=4,
    )


def cross_grads(at, z_mine, z_other, mine, other, dquery, heads, shards, dkv, w, nh, blocks):
    half, width = mine.shape
    local = dquery.shape[1]
    hd = local // nh
    seg = shards[0].shape[0]

    def body(at, ins, outs, scratch):
        shards, (dkv, w, z_mine, z_other, mine, other, dquery, heads) = ins[0:4], ins[4:]
        store_send, store_keep = outs[:2]
        group = outs[2:]
        (grad,) = scratch
        weights = []
        for h in range(nh):
            part = slice(h * hd, (h + 1) * hd)
            weights += [w[1][part], w[2][part]]
        weight = jnp.concatenate(weights, axis=0)
        both = None
        for slot, block in enumerate(shards):
            rows = jnp.concatenate([dkv[h, slot * seg : (slot + 1) * seg, :] for h in range(nh)], axis=1)
            found = mm(rows, weight)
            if slot % 2 == 0:
                store_keep[slot // 2] = found
            else:
                store_send[slot // 2] = found.astype(BF)
            part = mm(block[...], rows, TN)
            both = part if both is None else both + part
        for i in range(2):
            grad[...] = jnp.concatenate([both[:, (2 * h + i) * hd : (2 * h + i + 1) * hd] for h in range(nh)], axis=1)
            emit_group(at, grad, group, blocks, (1 + i) * local, local)
        grad[...] = mm(mine[...], dquery[:half], TN) + mm(other[...], dquery[half:], TN)
        emit_group(at, grad, group, blocks, 0, local)
        grad[...] = mm(z_mine[...], heads[:half], TN) + mm(z_other[...], heads[half:], TN)
        emit_group(at, grad, group, blocks, 3 * local, local)

    return launch(
        body,
        "cross_grads",
        at,
        [near(a) for a in (*shards, dkv, w, z_mine, z_other, mine, other, dquery, heads)],
        [shape(2, seg, width, dtype=BF), shape(2, seg, width)] + group_outs(width, 4 * local, blocks),
        scratch=[pltpu.VMEM((width, local), F32)],
        mib=24,
        us=5,
    )


def first_back(at, dsecond, mine, other, total, gain):
    half, width = mine.shape

    def body(at, ins, outs, _):
        dsecond, mine, other, total, gain = ins
        dfirst, low, sums = outs
        value = dsecond[...] + (mine[...].astype(F32) + other[...].astype(F32))
        normed, inverse = norm_stats(total[...])
        result = norm_backward(value, normed, inverse, gain[0:1])
        dfirst[...] = result
        low[...] = result.astype(BF)
        sums[...] = stacked_sums(value * normed, value, result)

    ins = [near(a) for a in (dsecond, mine, other, total, gain)]
    outs = [shape(half, width), shape(half, width, dtype=BF), shape(8, width)]
    return launch(body, "first_back", at, ins, outs, us=1.8)


def self_backward(at, mine, other, tokens, w, wo, qkv, prob, flat, mixed, sums, nh, blocks):
    half, width = mine.shape
    rows = 2 * half
    local = wo.shape[0]
    hd = local // nh
    scale = hd**-0.5

    def body(at, ins, outs, scratch):
        mine, other, wo, qkv, prob, tok, w, mixed, flat = ins[:9]
        third_sums, second_sums, first_sums, third_other, second_other, first_other, fc1_sum, head_sums = ins[9:]
        send, keep = outs[0:2]
        group, extra = outs[2:-1], outs[-1]
        z, dqkv, grad = scratch
        own, distant = rows_at(at[0], half), rows_at(1 - at[0], half)
        z[own, :] = mine[...]
        z[distant, :] = other[...]
        dself = mm(z[...], wo[...], NT).astype(BF)
        v, k, q = qkv[2], qkv[1], qkv[0]
        dq, dk, dv = [], [], []
        for h in range(nh):
            part = slice(h * hd, (h + 1) * hd)
            weights_low = prob[h]
            weights = weights_low.astype(F32)
            weighed = weights * mm(dself[:, part], v[:, part], NT)
            dscore = (weighed - weights * jnp.sum(weighed, axis=1, keepdims=True)).astype(BF)
            dq.append(mm(dscore, k[:, part]))
            dk.append(mm(q[:, part], dscore, TN))
            dv.append(mm(dself[:, part], weights_low, TN))
        dquery = jnp.concatenate(dq, axis=1) * scale
        dvalue = jnp.concatenate(dv, axis=0).T
        dqkv[:, 0:local] = dquery.astype(BF)
        dqkv[:, local : 2 * local] = (jnp.concatenate(dk, axis=0) * scale).astype(BF).T
        dqkv[:, 2 * local :] = dvalue.astype(BF)
        x = tok[...]
        grad[:, 0 : 3 * local] = mm(x, dqkv[...], TN)
        grad[:, 3 * local :] = mm(z[...], flat[...], TN)
        emit_group(at, grad, group, blocks, 0, 4 * local)
        pad = jnp.zeros((1, width - 2 * local), F32)
        small = jnp.concatenate(
            [
                third_sums[0:3] + third_other[0:3],
                second_sums[0:3] + second_other[0:3],
                first_sums[0:3] + first_other[0:3],
                fc1_sum[...],
                jnp.concatenate([head_sums[0:1], head_sums[1:2], pad], axis=1),
                jnp.concatenate([column_sum(dquery), column_sum(dvalue), pad], axis=1),
                jnp.zeros((EXTRA - 12, width), F32),
            ],
            axis=0,
        )
        extra[...] = small
        if blocks:
            group[0][blocks[0] * blocks[1] :, :] = two_terms(small)
        send[half:, :] = mixed[...]
        for place, out in ((distant, send), (own, keep)):
            rows_now = dqkv[place, :]
            total = sum(mm(rows_now[:, i * local : (i + 1) * local], w[i]) for i in range(3))
            out[0:half, :] = total.astype(out.dtype)

    return launch(
        body,
        "self_bwd",
        at,
        [near(a) for a in (mine, other, wo, qkv, prob, tokens, w, mixed, flat, *sums)],
        [shape(2 * half, width, dtype=BF), shape(half, width)]
        + group_outs(width, 4 * local, blocks, 2 * EXTRA)
        + [shape(EXTRA, width)],
        scratch=[
            pltpu.VMEM((rows, width), BF),
            pltpu.VMEM((rows, 3 * local), BF),
            pltpu.VMEM((width, 4 * local), F32),
        ],
        mib=20,
        us=6,
    )


def fold_lines(value, columns):
    rows, width = value.shape
    times = columns // width
    each = rows // times
    return value if times == 1 else jnp.concatenate([value[i * each : (i + 1) * each] for i in range(times)], axis=1)


def unfold_lines(value, width):
    times = value.shape[1] // width
    return (
        value
        if times == 1
        else jnp.concatenate([value[:, i * width : (i + 1) * width] for i in range(times)], axis=0)
    )


def add_stage(at, keep, got, small, bit):
    n, rows, _ = keep[0].shape
    starts = [0]
    for part in keep:
        starts.append(starts[-1] + part.shape[2])
    columns = starts[-1]
    tail = 0 if small is None else 2 * small.shape[0] * small.shape[1] // columns

    def body(at, ins, outs, _):
        keeps, gots = ins[: len(keep)], ins[len(keep) : len(keep) + len(got)]
        mine = at[bit]
        send, stay = outs[:2]
        for b in range(n // 2):
            for chosen, out in ((1 - mine, send), (mine, stay)):
                block = 2 * b + chosen
                for i, part in enumerate(keeps):
                    span = slice(starts[i], starts[i + 1])
                    source, first = (gots[i], 0) if len(got) == len(keep) else (gots[0], starts[i])
                    arrived = source[
                        pl.ds(pl.multiple_of(block * rows, 8), rows), first : first + starts[i + 1] - starts[i]
                    ]
                    value = part[block] + arrived.astype(F32)
                    if out is send:
                        send[b * rows : (b + 1) * rows, span] = value.astype(BF)
                    else:
                        stay[b, :, span] = value
        if tail:
            total = ins[-1][...] + unfold_lines(from_terms(gots[-1][n * rows :, :]), small.shape[1])
            outs[2][...] = total
            send[n // 2 * rows :, :] = two_terms(fold_lines(total, columns))

    ins = [near(part) for part in (*keep, *got)] + ([near(small)] if tail else [])
    outs = [shape(n // 2 * rows + tail, columns, dtype=BF), shape(n // 2, rows, columns)]
    if tail:
        outs.append(shape(*small.shape))
    return launch(body, "add_stage", at, ins, outs, us=1)


def last_stage(at, keep, got, small, parts):
    _, rows, columns = keep.shape
    each = columns // sum(count for count, _ in parts)
    reach = 0 if small is None else small.shape[1]

    def body(at, ins, outs, _):
        total = ins[0][0] + ins[1][0:rows].astype(F32)
        first = 0
        for out, (count, turned) in zip(outs, parts):
            if count == 1:
                value = total[:, first * each : (first + 1) * each]
                out[...] = value.T if turned else value
            else:
                for i in range(count):
                    out[i] = total[:, (first + i) * each : (first + i + 1) * each]
            first += count
        if reach:
            value = ins[2][...] + unfold_lines(from_terms(ins[1][rows:, :]), reach)
            outs[-1][...] = value
            gains, shifts, cross_line, self_line = outs[-5:-1]
            gains[...] = jnp.concatenate([value[6:7], value[3:4], value[0:1]], axis=0)
            shifts[...] = jnp.concatenate([value[7:8], value[4:5], value[1:2]], axis=0)
            half = cross_line.shape[1]
            for line, row in ((cross_line, value[10:11]), (self_line, value[11:12])):
                line[...] = jnp.concatenate([row[:, :half], row[:, half : 2 * half]], axis=0)

    outs = []
    for count, turned in parts:
        dims = (rows, each) if count == 1 else (count, rows, each)
        outs.append(shape(*(dims[::-1] if turned else dims)))
    ins = [near(keep), near(got)]
    if reach:
        ins.append(near(small))
        outs += [shape(3, reach), shape(3, reach), shape(2, reach // 4), shape(2, reach // 4), shape(small.shape[0], reach)]
    return launch(body, "last_stage", at, ins, outs, us=1)


def join_halves(at, mine, other):
    half, width = mine.shape
    skip = other.shape[0] - half

    def body(at, ins, outs, _):
        outs[0][rows_at(at[0], half), :] = ins[0][...]
        outs[0][rows_at(1 - at[0], half), :] = ins[1][...]

    out = shape(2 * half, width, dtype=mine.dtype)
    ins = [near(mine), near(other, lambda ref, at: ref.at[pl.ds(skip, half), :])]
    return launch(body, "join_halves", at, ins, [out])[0]


def flip(bit, size):
    return [(i, i ^ bit) for i in range(size)]


def butterfly(value, axis, size):
    bit = 1
    while bit < size:
        value = value + lax.ppermute(value, axis, flip(bit, size))
        bit *= 2
    return value


def on_device(
    tokens,
    store,
    summary_length,
    top_index,
    cotangent,
    self_qkv_weight,
    self_qv_bias,
    self_out_weight,
    self_out_bias,
    qkv_weight,
    qv_bias,
    out_weight,
    out_bias,
    fc1_weight,
    fc1_bias,
    fc2_weight,
    fc2_bias,
    norm_gain,
    norm_shift,
):
    rows, width = tokens.shape
    half = rows // 2
    nh = top_index.shape[1]
    local = qkv_weight.shape[2]
    units = fc1_weight.shape[1]
    seg = store.shape[1]
    wide = lax.axis_size("wide")
    place = lax.axis_index("narrow")
    doc = lax.axis_index("wide")
    core, across = place % 2, place // 2
    at = jnp.stack([core, across, place, summary_length[0], doc % 2, doc // 2 % 2, doc // 4]).astype(jnp.int32)
    blocks = (wide // 2, width // wide) if wide == 8 else None
    row = lambda v: v.reshape(1, -1)
    self_w = jnp.swapaxes(self_qkv_weight, 1, 2)
    cross_w = jnp.swapaxes(qkv_weight, 1, 2)

    def to_core(v):
        return lax.ppermute(v, "narrow", CORE)

    def to_across(v):
        return lax.ppermute(v, "narrow", ACROSS)

    def over(v, bit):
        return lax.ppermute(v, "wide", flip(bit, wide))

    def chip_sum(keep, send):
        return (keep + to_core(send).astype(F32)).astype(BF)

    store_x = to_across(store[0])
    qkv, prob, flat, send, keep = self_forward(at, tokens, self_w, self_qv_bias, self_out_weight, nh)
    mine = chip_sum(keep, send)
    other = to_across(mine)
    index = index_rows(top_index)
    bias_mine = make_mask(tie(at, mine), index, top_index.shape, seg, 128, 0)
    store_x, store_own = tie((store_x, store[0]), bias_mine)
    shards = [store_own, to_core(store_own), store_x, to_core(store_x)]
    bias_other = make_mask(tie(at, bias_mine), index, top_index.shape, seg, 128, 1)
    other = tie(other, bias_other)
    first_total, after, after_low = first_norm(at, mine, other, tokens, row(self_out_bias), norm_gain, norm_shift)
    after_other = to_core(after_low)

    keys, values = keys_values(tie(at, after_low), shards, cross_w, nh)
    keep, send, raised, inverse, query, heads = cross_forward(
        tie(at, keys), after_low, after_other, bias_mine, bias_other, keys, values, cross_w, qv_bias, out_weight, nh
    )
    mine = chip_sum(keep, send)
    second_total, mid_low = second_norm(at, after, mine, to_across(mine), row(out_bias), norm_gain, norm_shift)
    mid_other = to_core(mid_low)

    keep, send, hidden, slope = feed_up(at, mid_low, mid_other, fc1_weight, fc2_weight, row(fc1_bias))
    mine = chip_sum(keep, send)
    mixed_half, dlast, dlast_low, third_sums = third_norm(
        at, second_total, mine, to_across(mine), cotangent, row(fc2_bias), norm_gain, norm_shift
    )
    dlast_other, third_other = tie((to_core(dlast_low), to_core(third_sums)))
    keep, send, dpre, fc1_sum = feed_down(at, dlast_low, dlast_other, fc1_weight, fc2_weight, slope)
    mine = chip_sum(keep, send)
    other = to_across(mine)
    feed_out = feed_grads(tie(at, mine), mid_low, mid_other, dpre, dlast_low, dlast_other, hidden, blocks)
    other = tie(other, feed_out[0])
    dsecond, z, second_sums = second_back(at, dlast, mine, other, second_total, norm_gain)
    z_other, second_other = tie((to_core(z), to_core(second_sums)))

    keep, send, dquery, dkv, cross_sums = cross_backward(
        at, z, z_other, raised, inverse, query, keys, values, cross_w, out_weight, nh
    )
    mine = chip_sum(keep, send)
    other = to_across(mine)
    store_send, store_keep, *cross_out = cross_grads(
        tie(at, mine), z, z_other, after_low, after_other, dquery, heads, shards, dkv, cross_w, nh, blocks
    )
    started = store_send
    if blocks:
        feed_send, feed_keep = add_stage(tie(at, store_send), [feed_out[1]], [over(feed_out[0], 1)], None, 5)
        feed_next = over(feed_send, 2)
        started = feed_send
    other, store_send = tie((other, store_send), started)
    store_close = to_core(store_send)
    dfirst, dfirst_low, first_sums = first_back(at, dsecond, mine, other, first_total, norm_gain)
    dfirst_other, first_other = tie((to_core(dfirst_low), to_core(first_sums)))

    send, keep, *self_out, small = self_backward(
        tie(at, dfirst_other, store_close),
        dfirst_low,
        dfirst_other,
        tokens,
        self_w,
        self_out_weight,
        qkv,
        prob,
        flat,
        mixed_half,
        (third_sums, second_sums, first_sums, third_other, second_other, first_other, fc1_sum, cross_sums),
        nh,
        blocks,
    )
    if blocks:
        cross_got = tie(over(cross_out[0], 1), small)
        feed_send, feed_keep = add_stage(tie(at, cross_got), [feed_keep], [feed_next], None, 6)
        feed_next = over(feed_send, 4)
        fc1_grad, fc2_grad = last_stage(tie(at, feed_send), feed_keep, feed_next, None, [(1, False), (1, False)])
        fc2_grad = fc2_grad.T
        both_send, both_keep, small = add_stage(
            tie(at, fc1_grad), [cross_out[1], self_out[1]], [cross_got, over(self_out[0], 1)], small, 5
        )
        both_next = over(both_send, 2)
        send = tie(send, both_send)
    close = to_core(send)
    mine = (keep + close[:half].astype(F32)).astype(BF)
    other = to_across(mine)
    if blocks:
        both_send, both_keep, small = add_stage(tie(at, mine), [both_keep], [both_next], small, 6)
        both_next = over(both_send, 4)
        other = tie(other, both_send)
    tokens_half = dfirst + (mine.astype(F32) + other.astype(F32))
    tokens_other = to_core(tokens_half)
    mixed = join_halves(tie(at, tokens_half), mixed_half, close)
    store_distant = to_across(tie((store_keep[1] + store_close[1].astype(F32)).astype(BF), mine))
    tokens_grad = join_halves(at, tokens_half, tie(tokens_other, mixed))
    store_distant = tie(store_distant, tokens_grad)
    store_grad = (store_keep[0] + store_close[0].astype(F32) + store_distant.astype(F32))[None]

    if blocks:
        qkv_grad, out_grad, self_qkv_grad, self_out_grad, *lines, small = last_stage(
            tie(at, store_grad), both_keep, both_next, small, [(3, False), (1, True), (3, False), (1, True)]
        )
    else:
        scatter = functools.partial(lax.psum_scatter, axis_name="wide", tiled=True)
        parts = lambda g: jnp.stack([g[:, i * local : (i + 1) * local] for i in range(3)])
        fc1_grad = scatter(feed_out[0], scatter_dimension=0)
        fc2_grad = scatter(feed_out[1].T, scatter_dimension=1)
        qkv_grad = scatter(parts(cross_out[0]), scatter_dimension=1)
        out_grad = scatter(cross_out[0][:, 3 * local :].T, scatter_dimension=1)
        self_qkv_grad = scatter(parts(self_out[0]), scatter_dimension=1)
        self_out_grad = scatter(self_out[0][:, 3 * local :].T, scatter_dimension=1)
        small = butterfly(small, "wide", wide)
        lines = (
            jnp.stack([small[6], small[3], small[0]]),
            jnp.stack([small[7], small[4], small[1]]),
            small[10, : 2 * local].reshape(2, local),
            small[11, : 2 * local].reshape(2, local),
        )
    gain_grad, shift_grad, qv_grad, self_qv_grad = lines
    return (
        mixed,
        tokens_grad,
        store_grad,
        self_qkv_grad,
        self_qv_grad,
        self_out_grad,
        small[8],
        qkv_grad,
        qv_grad,
        out_grad,
        small[5],
        fc1_grad,
        small[9],
        fc2_grad,
        small[2],
        gain_grad,
        shift_grad,
    )


def solution(mesh):
    placed = (
        P("wide", None),
        P("wide", "narrow", None),
        P("wide"),
        P("wide", "narrow", None, None),
        P("wide", None),
        P(None, None, "narrow"),
        P(None, "narrow"),
        P("narrow", None),
        P(),
        P(None, None, "narrow"),
        P(None, "narrow"),
        P("narrow", None),
        P(),
        P(None, "narrow"),
        P("narrow"),
        P("narrow", None),
        P(),
        P(),
        P(),
    )
    return jax.shard_map(
        on_device,
        mesh=mesh,
        in_specs=placed,
        out_specs=(
            P("wide", None),
            P("wide", None),
            P("wide", "narrow", None),
            P(None, "wide", "narrow"),
            P(None, "narrow"),
            P("narrow", "wide"),
            P(),
            P(None, "wide", "narrow"),
            P(None, "narrow"),
            P("narrow", "wide"),
            P(),
            P("wide", "narrow"),
            P("narrow"),
            P("narrow", "wide"),
            P(),
            P(),
            P(),
        ),
        check_vma=False,
    )
```
